256 devices in a mesh: seq: 64 (over z, x, core), tp: 4 (over y).
Axes of the slice: x: 4, y: 4, z: 8, core: 2. Of those that a mesh axis runs over, the one named last changes fastest.
Arguments:
- tokens: bfloat16 [32768, 2048], P('seq', 'tp'), may hold values from -6 to 6
- norm_gain: float32 [2048], replicated, may hold values from 0.1 to 1.9
- w_query: bfloat16 [2048, 2048], P(None, 'tp'), may hold values from -0.125 to 0.125
- w_keyval: bfloat16 [2048, 256], replicated, may hold values from -0.125 to 0.125
- w_out: bfloat16 [2048, 2048], P('tp'), may hold values from -0.5 to 0.5
- span_lens: int32 [64], P('seq'), may hold values from 1 to 512, 24576 in all
- cached_lens: int32 [64], P('seq'), may hold values from 1 to 1536, 49152 in all
- old_table: int32 [64, 64], P('seq'), may hold values from 0 to 63, each once within a row
- new_table: int32 [64, 64], P('seq'), may hold values from 0 to 63, each once within a row
- old_cache: bfloat16 [4096, 32, 256], P('seq', 'tp'), may hold values from -720 to 720
Outputs:
- mixed: bfloat16 [32768, 2048], P('seq', 'tp')
- new_cache: bfloat16 [4096, 32, 256], P('seq', 'tp')
The draws below stay inside these ranges and needn't reach their ends.
Inputs may be any that keep to these rules, and one draw needn't show every extreme that they name: Request r's new tokens are the first span_lens[r] of its 512 rows. `old_table`: each row names every device once: each device holds exactly one block of every request. `new_table`: each row names every device once: each device receives exactly one block of every request.
All inputs are finite; a program needn't handle non-finite values. No bound on the sum of `span_lens` or of `cached_lens` on one device may be relied on, other than what follows from the above.
Results may differ from the reference program's by a relative error of at most 0.012.
The reference program's roundings to bfloat16 on the way count: a program that leaves them out, or rounds other values in their place, can miss the bound.
Values may be sent and summed in bfloat16 or wider, within the bound.
A program may use at most 128 MiB of HBM per device.

```python
import math
import jax
import jax.numpy as jnp
import numpy as np
from jax import lax

D = 2048
HEADS = 16
HD = 128
TOK_DEV = 512
CAP = 2048
REQS = 64
TOKENS = 32768
BLK = 32
SLOTS = 4096
N_SEQ = 64
N_TP = 4


def draw_old_cache(key, part):
    first = jax.random.fold_in(jax.random.fold_in(key, 17), 0)
    base = jnp.clip(jax.random.normal(first, (SLOTS, BLK, 2 * HD), jnp.float32), -6.0, 6.0)
    return base.astype(jnp.bfloat16)


def block_levels(rng, dims, cuts, smallest, high):
    level = 1.0
    for axis_at, parts in cuts:
        steps = jax.random.uniform(jax.random.fold_in(jax.random.fold_in(rng, 6), axis_at), (parts,), jnp.float32, smallest / len(cuts), high / len(cuts))
        level = level * jnp.repeat(jnp.exp(steps), dims[axis_at] // parts).reshape((-1,) + (1,) * (len(dims) - 1 - axis_at))
    return level


def length_profile(amount, total, limit, slope):
    portions = [(1 << 20) // math.isqrt(standing ** slope) + 1 for standing in range(2, amount + 1)]
    surplus, given = total - limit - (amount - 1), [1] * (amount - 1)
    while surplus > 0:
        movable = [i for i in range(amount - 1) if given[i] < limit]
        whole, budget = sum([portions[i] for i in movable]), surplus
        for i in movable:
            more = min(limit - given[i], max(1, budget * portions[i] // whole), surplus)
            given[i] = given[i] + more
            surplus = surplus - more
    return np.array([limit] + given)


def uneven(stream_key, count, total, limit, skew):
    if count == 2:
        one = jax.random.randint(stream_key, (), max(1, total - limit), min(limit, total - 1) + 1)
        return jnp.stack([one, total - one])
    sizes = jnp.asarray(length_profile(count, total, limit, skew), jnp.int32)
    couples = (count - 1) // 2
    source_of, receiver = sizes[1:1 + 2 * couples:2], sizes[2:2 + 2 * couples:2]
    margin = jnp.minimum(source_of - 1, limit - receiver)
    passed = jax.random.randint(jax.random.fold_in(stream_key, 1), (couples,), 0, 1 << 20) % (margin + 1)
    sizes = sizes.at[1:1 + 2 * couples:2].set(source_of - passed).at[2:2 + 2 * couples:2].set(receiver + passed)
    return sizes[jax.random.permutation(jax.random.fold_in(stream_key, 2), count)]


def bell_draw(rng, extent, width, limit, cuts=(), held_as=jnp.bfloat16):
    result = jax.random.normal(rng, extent, jnp.float32) * width
    if len(cuts) > 0:
        result = block_levels(rng, extent, cuts, -0.22, 0.18) * result
    return jnp.clip(result, min=-limit, max=limit).astype(held_as)


def setup_inputs(seed: int = 0) -> dict:
    splits = jax.random.split(jax.random.key(seed), 11)
    tokens = bell_draw(splits[0], (TOKENS, D), 1.0, 6.0, ((0, 64), (1, 4)))
    norm_gain = jnp.clip(1.0 + 0.18 * jax.random.normal(splits[1], (D,), jnp.float32), 0.1, 1.9)
    w_query = bell_draw(splits[2], (D, HEADS * HD), D ** -0.5, 0.125, ((1, 4),))
    w_keyval = bell_draw(splits[3], (D, 2 * HD), D ** -0.5, 0.125)
    w_out = bell_draw(splits[4], (HEADS * HD, D), HD ** -0.5, 0.5, ((0, 4),))
    span_lens = uneven(splits[5], REQS, REQS * TOK_DEV * 3 // 4, TOK_DEV, 1).astype(jnp.int32)
    cached_lens = uneven(splits[6], REQS, REQS * (CAP - TOK_DEV) // 2, CAP - TOK_DEV, 1).astype(jnp.int32)
    old_table = jax.vmap(lambda own: jax.random.permutation(own, N_SEQ))(jax.random.split(splits[7], REQS)).reshape((REQS, N_SEQ)).astype(jnp.int32)
    new_table = jax.vmap(lambda own: jax.random.permutation(own, N_SEQ))(jax.random.split(splits[8], REQS)).reshape((REQS, N_SEQ)).astype(jnp.int32)
    old_cache = draw_old_cache(jax.random.fold_in(splits[10], 71), 0)
    return {"tokens": tokens, "norm_gain": norm_gain, "w_query": w_query, "w_keyval": w_keyval, "w_out": w_out, "span_lens": span_lens, "cached_lens": cached_lens, "old_table": old_table, "new_table": new_table, "old_cache": old_cache}


EPSILON = 1e-05
MASKED = -1e+30

def normalize(rows, norm_gain):
    values = rows.astype(jnp.float32)
    average = lax.optimization_barrier(jnp.mean(values, axis=1, keepdims=True))
    centred = values - average
    spread = lax.optimization_barrier(jnp.mean(centred * centred, axis=1, keepdims=True))
    return (centred * lax.rsqrt(spread + EPSILON) * norm_gain.astype(jnp.float32)).astype(jnp.bfloat16)

def reference(tokens, norm_gain, w_query, w_keyval, w_out, span_lens, cached_lens, old_table, new_table, old_cache):
    normed = normalize(tokens, norm_gain)
    query = jnp.dot(normed, w_query, preferred_element_type=jnp.float32).astype(jnp.bfloat16)
    keyval = jnp.dot(normed, w_keyval, preferred_element_type=jnp.float32).astype(jnp.bfloat16)
    pool = old_cache.reshape(N_SEQ, N_SEQ, BLK, 2 * HD)
    requests = jnp.arange(N_SEQ).astype(jnp.int32)
    cached = pool[old_table, requests[:, None]].reshape(N_SEQ, CAP, 2 * HD)
    group_width = HEADS * HD // N_TP

    def attend(items):
        query_rows, keyval_rows, cache_rows, token_rows, held_len, span_len = items
        placed = lax.dynamic_update_slice(cache_rows, keyval_rows, (held_len.astype(jnp.int32), jnp.int32(0)))
        positions = lax.broadcasted_iota(jnp.int32, (CAP, 1), 0)
        fresh = jnp.where(positions < held_len + span_len, placed, jnp.zeros_like(placed))
        keys = fresh[:, :HD].astype(jnp.float32)
        values = fresh[:, HD:].astype(jnp.float32)
        query3 = query_rows.reshape(TOK_DEV, HEADS, HD).astype(jnp.float32)
        scores = jnp.einsum('thd,kd->htk', query3, keys) * HD ** (-0.5)
        row_pos = lax.broadcasted_iota(jnp.int32, (TOK_DEV, 1), 0)
        key_pos = lax.broadcasted_iota(jnp.int32, (1, CAP), 1)
        allowed = key_pos <= held_len + row_pos
        scores = jnp.where(allowed[None], scores, MASKED)
        top = lax.optimization_barrier(jnp.max(scores, axis=2, keepdims=True))
        weights = jnp.exp(scores - top)
        probs = (weights / lax.optimization_barrier(jnp.sum(weights, axis=2, keepdims=True))).astype(jnp.bfloat16)
        context = jnp.einsum('htk,kd->thd', probs.astype(jnp.float32), values).astype(jnp.bfloat16)
        context = context.reshape(TOK_DEV, HEADS * HD)
        total = token_rows.astype(jnp.float32)
        for group in range(N_TP):
            part = jnp.dot(context[:, group * group_width:(group + 1) * group_width], w_out[group * group_width:(group + 1) * group_width], preferred_element_type=jnp.float32).astype(jnp.bfloat16)
            part = lax.optimization_barrier(part)
            total = total + part.astype(jnp.float32)
        mixed_rows = jnp.where(row_pos < span_len, total, jnp.zeros_like(total)).astype(jnp.bfloat16)
        return (fresh, mixed_rows)
    fresh_all, mixed_all = lax.map(attend, (query.reshape(N_SEQ, TOK_DEV, HEADS * HD), keyval.reshape(N_SEQ, TOK_DEV, 2 * HD), cached, tokens.reshape(N_SEQ, TOK_DEV, D), cached_lens, span_lens))
    layout = jnp.zeros((N_SEQ, N_SEQ, BLK, 2 * HD), jnp.bfloat16)
    layout = layout.at[new_table, requests[:, None]].set(fresh_all.reshape(N_SEQ, N_SEQ, BLK, 2 * HD))
    return (mixed_all.reshape(TOKENS, D), layout.reshape(SLOTS, BLK, 2 * HD))
```

```python
import jax
import jax.numpy as jnp
from jax import lax
from jax.sharding import PartitionSpec as P

EPSILON = 1e-05
MASKED = -1e30


def normalize(rows, norm_gain):
    values = rows.astype(jnp.float32)
    average = jnp.mean(values, axis=1, keepdims=True)
    centred = values - average
    spread = jnp.mean(centred * centred, axis=1, keepdims=True)
    return (centred * lax.rsqrt(spread + EPSILON) * norm_gain).astype(jnp.bfloat16)


def body(
    tokens,
    norm_gain,
    w_query,
    w_keyval,
    w_out,
    span_lens,
    cached_lens,
    old_table,
    new_table,
    old_cache,
):
    groups = lax.axis_size("seq")
    tp_count = lax.axis_size("tp")
    tp_index = lax.axis_index("tp")
    holders = old_table[0]
    held_len = cached_lens[0]
    span_len = span_lens[0]
    tok_rows = tokens.shape[0]
    share = old_cache.shape[1]
    width = old_cache.shape[2]
    block_rows = share * tp_count
    capacity = groups * block_rows

    arrived = lax.all_to_all(old_cache, "seq", split_axis=0, concat_axis=0, tiled=True)
    cache_share = jnp.take(arrived, holders, axis=0)

    full_rows = lax.all_gather(tokens, "tp", axis=1, tiled=True)
    normed = normalize(full_rows, norm_gain)
    query = jnp.dot(normed, w_query, preferred_element_type=jnp.float32).astype(jnp.bfloat16)
    keyval = jnp.dot(normed, w_keyval, preferred_element_type=jnp.float32).astype(jnp.bfloat16)

    shifted = lax.dynamic_update_slice(
        jnp.zeros((capacity, width), jnp.bfloat16), keyval, (held_len, jnp.int32(0))
    )
    shifted_share = lax.dynamic_slice_in_dim(
        shifted.reshape(groups, block_rows, width), tp_index * share, share, 1
    )
    share_pos = (
        lax.broadcasted_iota(jnp.int32, (groups, share, 1), 0) * block_rows
        + tp_index * share
        + lax.broadcasted_iota(jnp.int32, (groups, share, 1), 1)
    )
    fresh_share = jnp.where(
        share_pos < held_len,
        cache_share,
        jnp.where(share_pos < held_len + span_len, shifted_share, jnp.zeros_like(shifted_share)),
    )
    targets = new_table[0]
    device_ids = lax.broadcasted_iota(jnp.int32, (groups, groups), 0)
    block_ids = lax.broadcasted_iota(jnp.int32, (groups, groups), 1)
    matches = targets[None, :] == device_ids
    sources = jnp.sum(jnp.where(matches, block_ids, 0), axis=1)
    new_cache = lax.all_to_all(
        jnp.take(fresh_share, sources, axis=0), "seq", split_axis=0, concat_axis=0, tiled=True
    )

    cached = lax.all_gather(cache_share, "tp", axis=1, tiled=True).reshape(capacity, width)
    positions = lax.broadcasted_iota(jnp.int32, (capacity, 1), 0)
    fresh = jnp.where(
        positions < held_len,
        cached,
        jnp.where(positions < held_len + span_len, shifted, jnp.zeros_like(shifted)),
    )
    head_size = width // 2
    keys = fresh[:, :head_size]
    values = fresh[:, head_size:]
    local_heads = query.shape[1] // head_size
    query3 = query.reshape(tok_rows, local_heads, head_size)
    scores = jnp.einsum(
        "thd,kd->htk", query3, keys, preferred_element_type=jnp.float32
    ) * head_size ** (-0.5)
    row_pos = lax.broadcasted_iota(jnp.int32, (tok_rows, 1), 0)
    key_pos = lax.broadcasted_iota(jnp.int32, (1, capacity), 1)
    allowed = key_pos <= held_len + row_pos
    scores = jnp.where(allowed[None], scores, MASKED)
    top = jnp.max(scores, axis=2, keepdims=True)
    weights = jnp.exp(scores - top)
    probs = (weights / jnp.sum(weights, axis=2, keepdims=True)).astype(jnp.bfloat16)
    context = jnp.einsum("htk,kd->thd", probs, values, preferred_element_type=jnp.float32).astype(
        jnp.bfloat16
    )
    context = context.reshape(tok_rows, local_heads * head_size)
    partial_out = jnp.dot(context, w_out, preferred_element_type=jnp.float32)
    summed = lax.psum_scatter(
        partial_out.astype(jnp.bfloat16), "tp", scatter_dimension=1, tiled=True
    ).astype(jnp.float32)
    total = tokens.astype(jnp.float32) + summed
    mixed = jnp.where(row_pos < span_len, total, jnp.zeros_like(total)).astype(jnp.bfloat16)
    return (mixed, new_cache)


def solution(mesh):
    in_specs = (
        P("seq", "tp"),
        P(),
        P(None, "tp"),
        P(),
        P("tp", None),
        P("seq"),
        P("seq"),
        P("seq", None),
        P("seq", None),
        P("seq", "tp", None),
    )
    out_specs = (P("seq", "tp"), P("seq", "tp", None))
    return jax.shard_map(body, mesh=mesh, in_specs=in_specs, out_specs=out_specs, check_vma=False)
```

```python
import functools

import jax
import jax.numpy as jnp
from jax import lax
from jax.experimental import pallas as pl
from jax.experimental.pallas import tpu as pltpu
from jax.sharding import PartitionSpec as P

EPSILON = 1e-05
MASKED = -1e30


def normalize(rows, norm_gain):
    values = rows.astype(jnp.float32)
    average = jnp.mean(values, axis=1, keepdims=True)
    centred = values - average
    spread = jnp.mean(centred * centred, axis=1, keepdims=True)
    return (centred * lax.rsqrt(spread + EPSILON) * norm_gain).astype(jnp.bfloat16)


def _exchange_kernel(axis, other, n, per_peer, x_ref, y_ref, send_sem, recv_sem, local_sem):
    me = lax.axis_index(axis)
    fixed = lax.axis_index(other)

    def dev(peer):
        return {axis: peer, other: fixed}

    barrier = pltpu.get_barrier_semaphore()

    def greet(k, carry):
        pl.semaphore_signal(
            barrier, inc=1, device_id=dev(lax.rem(me + k, n)), device_id_type=pl.DeviceIdType.MESH
        )
        return carry

    lax.fori_loop(1, n, greet, 0)
    pl.semaphore_wait(barrier, n - 1)

    def src_of(peer):
        return x_ref.at[peer] if per_peer else x_ref

    own = pltpu.make_async_copy(src_of(me), y_ref.at[me], local_sem)
    own.start()

    def outgoing(k):
        peer = lax.rem(me + k, n)
        return pltpu.make_async_remote_copy(
            src_ref=src_of(peer),
            dst_ref=y_ref.at[me],
            send_sem=send_sem.at[k],
            recv_sem=recv_sem.at[k],
            device_id=dev(peer),
            device_id_type=pl.DeviceIdType.MESH,
        )

    def incoming(k):
        sender = lax.rem(me + n - k, n)
        return pltpu.make_async_remote_copy(
            src_ref=src_of(me),
            dst_ref=y_ref.at[sender],
            send_sem=send_sem.at[k],
            recv_sem=recv_sem.at[k],
            device_id=dev(sender),
            device_id_type=pl.DeviceIdType.MESH,
        )

    def start(k, carry):
        outgoing(k).start()
        return carry

    lax.fori_loop(1, n, start, 0)

    def finish(k, carry):
        outgoing(k).wait_send()
        incoming(k).wait_recv()
        return carry

    lax.fori_loop(1, n, finish, 0)
    own.wait()


def exchange(x, axis, other, n, per_peer, cid):
    out_shape = x.shape[1:] if per_peer else x.shape
    return pl.pallas_call(
        functools.partial(_exchange_kernel, axis, other, n, per_peer),
        out_shape=jax.ShapeDtypeStruct((n,) + out_shape, x.dtype),
        in_specs=[pl.BlockSpec(memory_space=pl.ANY)],
        out_specs=pl.BlockSpec(memory_space=pl.ANY),
        scratch_shapes=[
            pltpu.SemaphoreType.DMA((n,)),
            pltpu.SemaphoreType.DMA((n,)),
            pltpu.SemaphoreType.DMA,
        ],
        compiler_params=pltpu.CompilerParams(collective_id=cid, has_side_effects=True),
    )(x)


def body(
    tokens,
    norm_gain,
    w_query,
    w_keyval,
    w_out,
    span_lens,
    cached_lens,
    old_table,
    new_table,
    old_cache,
):
    groups = lax.axis_size("seq")
    tp_count = lax.axis_size("tp")
    tp_index = lax.axis_index("tp")
    holders = old_table[0]
    held_len = cached_lens[0]
    span_len = span_lens[0]
    tok_rows, tok_cols = tokens.shape
    share = old_cache.shape[1]
    width = old_cache.shape[2]
    block_rows = share * tp_count
    capacity = groups * block_rows

    arrived = exchange(old_cache, "seq", "tp", groups, True, 0)
    cache_share = jnp.take(arrived, holders, axis=0)

    gathered = exchange(tokens, "tp", "seq", tp_count, False, 1)
    full_rows = gathered.transpose(1, 0, 2).reshape(tok_rows, tp_count * tok_cols)
    normed = normalize(full_rows, norm_gain)
    query = jnp.dot(normed, w_query, preferred_element_type=jnp.float32).astype(jnp.bfloat16)
    keyval = jnp.dot(normed, w_keyval, preferred_element_type=jnp.float32).astype(jnp.bfloat16)

    shifted = lax.dynamic_update_slice(
        jnp.zeros((capacity, width), jnp.bfloat16), keyval, (held_len, jnp.int32(0))
    )
    shifted_share = lax.dynamic_slice_in_dim(
        shifted.reshape(groups, block_rows, width), tp_index * share, share, 1
    )
    share_pos = (
        lax.broadcasted_iota(jnp.int32, (groups, share, 1), 0) * block_rows
        + tp_index * share
        + lax.broadcasted_iota(jnp.int32, (groups, share, 1), 1)
    )
    fresh_share = jnp.where(
        share_pos < held_len,
        cache_share,
        jnp.where(share_pos < held_len + span_len, shifted_share, jnp.zeros_like(shifted_share)),
    )
    targets = new_table[0]
    device_ids = lax.broadcasted_iota(jnp.int32, (groups, groups), 0)
    block_ids = lax.broadcasted_iota(jnp.int32, (groups, groups), 1)
    matches = targets[None, :] == device_ids
    sources = jnp.sum(jnp.where(matches, block_ids, 0), axis=1)
    new_cache = exchange(jnp.take(fresh_share, sources, axis=0), "seq", "tp", groups, True, 2)

    pieces = exchange(cache_share, "tp", "seq", tp_count, False, 3)
    cached = pieces.transpose(1, 0, 2, 3).reshape(capacity, width)
    positions = lax.broadcasted_iota(jnp.int32, (capacity, 1), 0)
    fresh = jnp.where(
        positions < held_len,
        cached,
        jnp.where(positions < held_len + span_len, shifted, jnp.zeros_like(shifted)),
    )
    head_size = width // 2
    keys = fresh[:, :head_size]
    values = fresh[:, head_size:]
    local_heads = query.shape[1] // head_size
    query3 = query.reshape(tok_rows, local_heads, head_size)
    scores = jnp.einsum(
        "thd,kd->htk", query3, keys, preferred_element_type=jnp.float32
    ) * head_size ** (-0.5)
    row_pos = lax.broadcasted_iota(jnp.int32, (tok_rows, 1), 0)
    key_pos = lax.broadcasted_iota(jnp.int32, (1, capacity), 1)
    allowed = key_pos <= held_len + row_pos
    scores = jnp.where(allowed[None], scores, MASKED)
    top = jnp.max(scores, axis=2, keepdims=True)
    weights = jnp.exp(scores - top)
    probs = (weights / jnp.sum(weights, axis=2, keepdims=True)).astype(jnp.bfloat16)
    context = jnp.einsum("htk,kd->thd", probs, values, preferred_element_type=jnp.float32).astype(
        jnp.bfloat16
    )
    context = context.reshape(tok_rows, local_heads * head_size)
    out_blocks = w_out.reshape(w_out.shape[0], tp_count, tok_cols)
    partial_out = jnp.einsum(
        "tk,kpn->ptn", context, out_blocks, preferred_element_type=jnp.float32
    ).astype(jnp.bfloat16)
    summed = exchange(partial_out, "tp", "seq", tp_count, True, 4).astype(jnp.float32)
    total = tokens.astype(jnp.float32) + jnp.sum(summed, axis=0)
    mixed = jnp.where(row_pos < span_len, total, jnp.zeros_like(total)).astype(jnp.bfloat16)
    return (mixed, new_cache)


def solution(mesh):
    in_specs = (
        P("seq", "tp"),
        P(),
        P(None, "tp"),
        P(),
        P("tp", None),
        P("seq"),
        P("seq"),
        P("seq", None),
        P("seq", None),
        P("seq", "tp", None),
    )
    out_specs = (P("seq", "tp"), P("seq", "tp", None))
    return jax.shard_map(body, mesh=mesh, in_specs=in_specs, out_specs=out_specs, check_vma=False)
```

```python
import functools

import jax
import jax.numpy as jnp
from jax import lax
from jax.experimental import pallas as pl
from jax.experimental.pallas import tpu as pltpu
from jax.sharding import PartitionSpec as P

EPSILON = 1e-05
MASKED = -1e30


def normalize(rows, norm_gain):
    values = rows.astype(jnp.float32)
    average = jnp.mean(values, axis=1, keepdims=True)
    centred = values - average
    spread = jnp.mean(centred * centred, axis=1, keepdims=True)
    return (centred * lax.rsqrt(spread + EPSILON) * norm_gain).astype(jnp.bfloat16)


MESH = pl.DeviceIdType.MESH


def _remote(src, dst, send, recv, dev):
    return pltpu.make_async_remote_copy(
        src_ref=src, dst_ref=dst, send_sem=send, recv_sem=recv, device_id=dev, device_id_type=MESH
    )


def _greet(nseq, s, t, left, right):
    barrier = pltpu.get_barrier_semaphore()

    def one(k, carry):
        pl.semaphore_signal(
            barrier, inc=1, device_id={"seq": lax.rem(s + k, nseq), "tp": t}, device_id_type=MESH
        )
        return carry

    lax.fori_loop(1, nseq, one, 0)
    for p in (left, right):
        pl.semaphore_signal(barrier, inc=1, device_id={"seq": s, "tp": p}, device_id_type=MESH)
    pl.semaphore_wait(barrier, nseq + 1)


def _seq_copies(nseq, s, t, src_ref, dst_ref, send, recv):
    def outgoing(k):
        peer = lax.rem(s + k, nseq)
        return _remote(src_ref.at[peer], dst_ref.at[s], send.at[k], recv.at[k],
                       {"seq": peer, "tp": t})

    def incoming(k):
        sender = lax.rem(s + nseq - k, nseq)
        return _remote(src_ref.at[s], dst_ref.at[sender], send.at[k], recv.at[k],
                       {"seq": sender, "tp": t})

    return outgoing, incoming


def _loop(n, fn):
    def step(k, carry):
        fn(k)
        return carry

    lax.fori_loop(1, n, step, 0)


def _in_kernel(nseq, ntp, tok_ref, cache_ref, tok_out, cache_out, tsend, trecv, csend, crecv,
               ssend, srecv, lsem):
    s = lax.axis_index("seq")
    t = lax.axis_index("tp")
    right = lax.rem(t + 1, ntp)
    left = lax.rem(t + ntp - 1, ntp)
    across = lax.rem(t + 2, ntp)
    rdev = {"seq": s, "tp": right}
    ldev = {"seq": s, "tp": left}
    rows, cols = tok_ref.shape
    half = rows // 2
    blocks = nseq // 2
    _greet(nseq, s, t, left, right)

    own_tok = pltpu.make_async_copy(tok_ref, tok_out.at[:, pl.ds(t * cols, cols)], lsem.at[0])
    own_tok.start()
    tok_r = _remote(tok_ref, tok_out.at[:, pl.ds(t * cols, cols)], tsend.at[0], trecv.at[0], rdev)
    tok_l = _remote(tok_ref, tok_out.at[:, pl.ds(t * cols, cols)], tsend.at[1], trecv.at[1], ldev)
    tok_r.start()
    tok_l.start()

    own_cache = pltpu.make_async_copy(cache_ref.at[s], cache_out.at[s, t], lsem.at[1])
    own_cache.start()
    seq_out, seq_in = _seq_copies(nseq, s, t, cache_ref, cache_out.at[:, t], ssend, srecv)
    _loop(nseq, lambda k: seq_out(k).start())

    _remote(tok_ref, tok_out.at[:, pl.ds(left * cols, cols)], tsend.at[0], trecv.at[0], ldev).wait_recv()
    fwd_r = _remote(tok_out.at[pl.ds(0, half), pl.ds(left * cols, cols)], tok_out.at[pl.ds(0, half), pl.ds(left * cols, cols)],
                    tsend.at[2], trecv.at[2], rdev)
    fwd_r.start()
    _remote(tok_ref, tok_out.at[:, pl.ds(right * cols, cols)], tsend.at[1], trecv.at[1], rdev).wait_recv()
    fwd_l = _remote(tok_out.at[pl.ds(half, half), pl.ds(right * cols, cols)], tok_out.at[pl.ds(half, half), pl.ds(right * cols, cols)],
                    tsend.at[3], trecv.at[3], ldev)
    fwd_l.start()

    _loop(nseq, lambda k: seq_in(k).wait_recv())
    own_cache.wait()
    mine = cache_out.at[:, t]
    cache_r = _remote(mine, mine, csend.at[0], crecv.at[0], rdev)
    cache_l = _remote(mine, mine, csend.at[1], crecv.at[1], ldev)
    cache_r.start()
    cache_l.start()
    _remote(mine, cache_out.at[:, left], csend.at[0], crecv.at[0], ldev).wait_recv()
    cfwd_r = _remote(cache_out.at[pl.ds(0, blocks), left], cache_out.at[pl.ds(0, blocks), left],
                     csend.at[2], crecv.at[2], rdev)
    cfwd_r.start()
    _remote(mine, cache_out.at[:, right], csend.at[1], crecv.at[1], rdev).wait_recv()
    cfwd_l = _remote(cache_out.at[pl.ds(blocks, blocks), right],
                     cache_out.at[pl.ds(blocks, blocks), right], csend.at[3], crecv.at[3], ldev)
    cfwd_l.start()

    _remote(tok_ref.at[pl.ds(0, half)], tok_out.at[pl.ds(0, half), pl.ds(across * cols, cols)], tsend.at[2], trecv.at[2], ldev).wait_recv()
    _remote(tok_ref.at[pl.ds(half, half)], tok_out.at[pl.ds(half, half), pl.ds(across * cols, cols)], tsend.at[3], trecv.at[3], rdev).wait_recv()
    _remote(cache_out.at[pl.ds(0, blocks), t], cache_out.at[pl.ds(0, blocks), across], csend.at[2], crecv.at[2], ldev).wait_recv()
    _remote(cache_out.at[pl.ds(blocks, blocks), t], cache_out.at[pl.ds(blocks, blocks), across], csend.at[3], crecv.at[3],
            rdev).wait_recv()
    for c in (tok_r, tok_l, fwd_r, fwd_l, cache_r, cache_l, cfwd_r, cfwd_l):
        c.wait_send()
    _loop(nseq, lambda k: seq_out(k).wait_send())
    own_tok.wait()


def gather_inputs(tokens, old_cache, nseq, ntp):
    rows, cols = tokens.shape
    _, share, width = old_cache.shape
    return pl.pallas_call(
        functools.partial(_in_kernel, nseq, ntp),
        out_shape=(
            jax.ShapeDtypeStruct((rows, ntp * cols), tokens.dtype),
            jax.ShapeDtypeStruct((nseq, ntp, share, width), old_cache.dtype),
        ),
        in_specs=[pl.BlockSpec(memory_space=pl.ANY)] * 2,
        out_specs=(pl.BlockSpec(memory_space=pl.ANY), pl.BlockSpec(memory_space=pl.ANY)),
        scratch_shapes=[
            pltpu.SemaphoreType.DMA((4,)),
            pltpu.SemaphoreType.DMA((4,)),
            pltpu.SemaphoreType.DMA((4,)),
            pltpu.SemaphoreType.DMA((4,)),
            pltpu.SemaphoreType.DMA((nseq,)),
            pltpu.SemaphoreType.DMA((nseq,)),
            pltpu.SemaphoreType.DMA((2,)),
        ],
        compiler_params=pltpu.CompilerParams(collective_id=0, has_side_effects=True),
    )(tokens, old_cache)


def _out_kernel(nseq, ntp, part_ref, share_ref, rs_out, new_out, stage, rsend, rrecv, ssend,
                srecv, lsem):
    s = lax.axis_index("seq")
    t = lax.axis_index("tp")
    right = lax.rem(t + 1, ntp)
    left = lax.rem(t + ntp - 1, ntp)
    across = lax.rem(t + 2, ntp)
    rdev = {"seq": s, "tp": right}
    ldev = {"seq": s, "tp": left}
    half = part_ref.shape[1] // 2
    _greet(nseq, s, t, left, right)

    own_part = pltpu.make_async_copy(part_ref.at[t], rs_out.at[t], lsem.at[0])
    own_part.start()
    own_new = pltpu.make_async_copy(share_ref.at[s], new_out.at[s], lsem.at[1])
    own_new.start()
    to_r = _remote(part_ref.at[right], rs_out.at[t], rsend.at[0], rrecv.at[0], rdev)
    to_l = _remote(part_ref.at[left], rs_out.at[t], rsend.at[1], rrecv.at[1], ldev)
    via_r = _remote(part_ref.at[across, pl.ds(0, half)], stage.at[0], rsend.at[2], rrecv.at[2], rdev)
    via_l = _remote(part_ref.at[across, pl.ds(half, half)], stage.at[1], rsend.at[3], rrecv.at[3],
                    ldev)
    for c in (to_r, to_l, via_r, via_l):
        c.start()
    seq_out, seq_in = _seq_copies(nseq, s, t, share_ref, new_out, ssend, srecv)
    _loop(nseq, lambda k: seq_out(k).start())

    _remote(part_ref.at[across, pl.ds(0, half)], stage.at[0], rsend.at[2], rrecv.at[2],
            ldev).wait_recv()
    fwd_r = _remote(stage.at[0], rs_out.at[left, pl.ds(0, half)], rsend.at[4], rrecv.at[4], rdev)
    fwd_r.start()
    _remote(part_ref.at[across, pl.ds(half, half)], stage.at[1], rsend.at[3], rrecv.at[3],
            rdev).wait_recv()
    fwd_l = _remote(stage.at[1], rs_out.at[right, pl.ds(half, half)], rsend.at[5], rrecv.at[5],
                    ldev)
    fwd_l.start()

    _remote(part_ref.at[t], rs_out.at[left], rsend.at[0], rrecv.at[0], ldev).wait_recv()
    _remote(part_ref.at[t], rs_out.at[right], rsend.at[1], rrecv.at[1], rdev).wait_recv()
    _remote(stage.at[0], rs_out.at[across, pl.ds(0, half)], rsend.at[4], rrecv.at[4],
            ldev).wait_recv()
    _remote(stage.at[1], rs_out.at[across, pl.ds(half, half)], rsend.at[5], rrecv.at[5],
            rdev).wait_recv()
    _loop(nseq, lambda k: seq_in(k).wait_recv())
    for c in (to_r, to_l, via_r, via_l, fwd_r, fwd_l):
        c.wait_send()
    _loop(nseq, lambda k: seq_out(k).wait_send())
    own_part.wait()
    own_new.wait()


def scatter_outputs(partial, share, nseq, ntp):
    _, rows, cols = partial.shape
    return pl.pallas_call(
        functools.partial(_out_kernel, nseq, ntp),
        out_shape=(
            jax.ShapeDtypeStruct(partial.shape, partial.dtype),
            jax.ShapeDtypeStruct(share.shape, share.dtype),
        ),
        in_specs=[pl.BlockSpec(memory_space=pl.ANY)] * 2,
        out_specs=(pl.BlockSpec(memory_space=pl.ANY), pl.BlockSpec(memory_space=pl.ANY)),
        scratch_shapes=[
            pltpu.VMEM((2, rows // 2, cols), partial.dtype),
            pltpu.SemaphoreType.DMA((6,)),
            pltpu.SemaphoreType.DMA((6,)),
            pltpu.SemaphoreType.DMA((nseq,)),
            pltpu.SemaphoreType.DMA((nseq,)),
            pltpu.SemaphoreType.DMA((2,)),
        ],
        compiler_params=pltpu.CompilerParams(collective_id=1, has_side_effects=True),
    )(partial, share)


def body(
    tokens,
    norm_gain,
    w_query,
    w_keyval,
    w_out,
    span_lens,
    cached_lens,
    old_table,
    new_table,
    old_cache,
):
    groups = lax.axis_size("seq")
    tp_count = lax.axis_size("tp")
    tp_index = lax.axis_index("tp")
    holders = old_table[0]
    held_len = cached_lens[0]
    span_len = span_lens[0]
    tok_rows, tok_cols = tokens.shape
    share = old_cache.shape[1]
    width = old_cache.shape[2]
    block_rows = share * tp_count
    capacity = groups * block_rows

    tok_all, cache_all = gather_inputs(tokens, old_cache, groups, tp_count)
    full_rows = tok_all
    normed = normalize(full_rows, norm_gain)
    query = jnp.dot(normed, w_query, preferred_element_type=jnp.float32).astype(jnp.bfloat16)
    keyval = jnp.dot(normed, w_keyval, preferred_element_type=jnp.float32).astype(jnp.bfloat16)

    cached = jnp.take(cache_all, holders, axis=0).reshape(capacity, width)
    shifted = lax.dynamic_update_slice(
        jnp.zeros((capacity, width), jnp.bfloat16), keyval, (held_len, jnp.int32(0))
    )
    positions = lax.broadcasted_iota(jnp.int32, (capacity, 1), 0)
    fresh = jnp.where(
        positions < held_len,
        cached,
        jnp.where(positions < held_len + span_len, shifted, jnp.zeros_like(shifted)),
    )
    fresh_share = lax.dynamic_slice_in_dim(
        fresh.reshape(groups, block_rows, width), tp_index * share, share, 1
    )
    targets = new_table[0]
    device_ids = lax.broadcasted_iota(jnp.int32, (groups, groups), 0)
    block_ids = lax.broadcasted_iota(jnp.int32, (groups, groups), 1)
    matches = targets[None, :] == device_ids
    sources = jnp.sum(jnp.where(matches, block_ids, 0), axis=1)
    sorted_share = jnp.take(fresh_share, sources, axis=0)
    head_size = width // 2
    keys = fresh[:, :head_size]
    values = fresh[:, head_size:]
    local_heads = query.shape[1] // head_size
    query3 = query.reshape(tok_rows, local_heads, head_size)
    scores = jnp.einsum(
        "thd,kd->htk", query3, keys, preferred_element_type=jnp.float32
    ) * head_size ** (-0.5)
    row_pos = lax.broadcasted_iota(jnp.int32, (tok_rows, 1), 0)
    key_pos = lax.broadcasted_iota(jnp.int32, (1, capacity), 1)
    allowed = key_pos <= held_len + row_pos
    scores = jnp.where(allowed[None], scores, MASKED)
    top = jnp.max(scores, axis=2, keepdims=True)
    weights = jnp.exp(scores - top)
    probs = (weights / jnp.sum(weights, axis=2, keepdims=True)).astype(jnp.bfloat16)
    context = jnp.einsum("htk,kd->thd", probs, values, preferred_element_type=jnp.float32).astype(
        jnp.bfloat16
    )
    context = context.reshape(tok_rows, local_heads * head_size)
    out_blocks = w_out.reshape(w_out.shape[0], tp_count, tok_cols)
    partial_out = jnp.einsum(
        "tk,kpn->ptn", context, out_blocks, preferred_element_type=jnp.float32
    ).astype(jnp.bfloat16)
    summed, new_cache = scatter_outputs(partial_out, sorted_share, groups, tp_count)
    summed = summed.astype(jnp.float32)
    total = tokens.astype(jnp.float32) + jnp.sum(summed, axis=0)
    mixed = jnp.where(row_pos < span_len, total, jnp.zeros_like(total)).astype(jnp.bfloat16)
    return (mixed, new_cache)


def solution(mesh):
    in_specs = (
        P("seq", "tp"),
        P(),
        P(None, "tp"),
        P(),
        P("tp", None),
        P("seq"),
        P("seq"),
        P("seq", None),
        P("seq", None),
        P("seq", "tp", None),
    )
    out_specs = (P("seq", "tp"), P("seq", "tp", None))
    return jax.shard_map(body, mesh=mesh, in_specs=in_specs, out_specs=out_specs, check_vma=False)
```

```python
import functools

import jax
import jax.numpy as jnp
from jax import lax
from jax.experimental import pallas as pl
from jax.experimental.pallas import tpu as pltpu
from jax.sharding import PartitionSpec as P

EPSILON = 1e-05
MASKED = -1e30


def normalize(rows, norm_gain):
    values = rows.astype(jnp.float32)
    average = jnp.mean(values, axis=1, keepdims=True)
    centred = values - average
    spread = jnp.mean(centred * centred, axis=1, keepdims=True)
    return (centred * lax.rsqrt(spread + EPSILON) * norm_gain).astype(jnp.bfloat16)


MESH = pl.DeviceIdType.MESH


def _remote(src, dst, send, recv, dev):
    return pltpu.make_async_remote_copy(
        src_ref=src, dst_ref=dst, send_sem=send, recv_sem=recv, device_id=dev, device_id_type=MESH
    )


def _greet(na, nb, s, t, left, right):
    barrier = pltpu.get_barrier_semaphore()
    a = s // nb
    b = s % nb

    def one_b(k, carry):
        pl.semaphore_signal(barrier, inc=1, device_id={"seq": a * nb + lax.rem(b + k, nb), "tp": t},
                            device_id_type=MESH)
        return carry

    def one_a(k, carry):
        pl.semaphore_signal(barrier, inc=1, device_id={"seq": lax.rem(a + k, na) * nb + b, "tp": t},
                            device_id_type=MESH)
        return carry

    lax.fori_loop(1, nb, one_b, 0)
    lax.fori_loop(1, na, one_a, 0)
    for p in (left, right):
        pl.semaphore_signal(barrier, inc=1, device_id={"seq": s, "tp": p}, device_id_type=MESH)
    pl.semaphore_wait(barrier, na + nb)


class SeqAllToAll:
    def __init__(self, na, nb, s, t, src, stage, dst, sems):
        self.na, self.nb, self.t, self.src, self.stage, self.dst = na, nb, t, src, stage, dst
        self.a = s // nb
        self.b = s % nb
        self.s1send, self.s1recv, self.s2send, self.s2recv, self.local = sems

    def _dev(self, a, b):
        return {"seq": a * self.nb + b, "tp": self.t}

    def _out1(self, k):
        peer = lax.rem(self.b + k, self.nb)
        return _remote(self.src.at[:, peer], self.stage.at[self.b], self.s1send.at[k],
                       self.s1recv.at[k], self._dev(self.a, peer))

    def _in1(self, k):
        sender = lax.rem(self.b + self.nb - k, self.nb)
        return _remote(self.src.at[:, self.b], self.stage.at[sender], self.s1send.at[k],
                       self.s1recv.at[k], self._dev(self.a, sender))

    def _out2(self, k):
        peer = lax.rem(self.a + k, self.na)
        return _remote(self.stage.at[:, peer], self.dst(self.a), self.s2send.at[k],
                       self.s2recv.at[k], self._dev(peer, self.b))

    def _in2(self, k):
        sender = lax.rem(self.a + self.na - k, self.na)
        return _remote(self.stage.at[:, self.a], self.dst(sender), self.s2send.at[k],
                       self.s2recv.at[k], self._dev(sender, self.b))

    def first(self):
        self.own1 = pltpu.make_async_copy(self.src.at[:, self.b], self.stage.at[self.b],
                                          self.local.at[0])
        self.own1.start()
        _loop(self.nb, lambda k: self._out1(k).start())

    def second(self):
        _loop(self.nb, lambda k: self._in1(k).wait_recv())
        self.own1.wait()
        self.own2 = pltpu.make_async_copy(self.stage.at[:, self.a], self.dst(self.a),
                                          self.local.at[1])
        self.own2.start()
        _loop(self.na, lambda k: self._out2(k).start())

    def arrived(self):
        _loop(self.na, lambda k: self._in2(k).wait_recv())
        self.own2.wait()

    def finish(self):
        _loop(self.nb, lambda k: self._out1(k).wait_send())
        _loop(self.na, lambda k: self._out2(k).wait_send())


def _seq_scratch(na, nb, share, width, dtype):
    return [
        pltpu.VMEM((nb, na, share, width), dtype),
        pltpu.SemaphoreType.DMA((nb,)),
        pltpu.SemaphoreType.DMA((nb,)),
        pltpu.SemaphoreType.DMA((na,)),
        pltpu.SemaphoreType.DMA((na,)),
        pltpu.SemaphoreType.DMA((2,)),
    ]


def _loop(n, fn):
    def step(k, carry):
        fn(k)
        return carry

    lax.fori_loop(1, n, step, 0)


def _in_kernel(na, nb, ntp, tok_ref, cache_ref, tok_out, cache_out, tsend, trecv, csend, crecv,
               lsem, stage, s1send, s1recv, s2send, s2recv, slocal):
    s = lax.axis_index("seq")
    t = lax.axis_index("tp")
    right = lax.rem(t + 1, ntp)
    left = lax.rem(t + ntp - 1, ntp)
    across = lax.rem(t + 2, ntp)
    rdev = {"seq": s, "tp": right}
    ldev = {"seq": s, "tp": left}
    rows, cols = tok_ref.shape
    half = rows // 2
    blocks = na * nb // 2
    _greet(na, nb, s, t, left, right)

    def tok_cols(p):
        return pl.ds(p * cols, cols)

    a2a = SeqAllToAll(na, nb, s, t, cache_ref, stage, lambda a_src: cache_out.at[a_src, :, t],
                      (s1send, s1recv, s2send, s2recv, slocal))
    a2a.first()

    own_tok = pltpu.make_async_copy(tok_ref, tok_out.at[:, tok_cols(t)], lsem.at[0])
    own_tok.start()
    tok_r = _remote(tok_ref, tok_out.at[:, tok_cols(t)], tsend.at[0], trecv.at[0], rdev)
    tok_l = _remote(tok_ref, tok_out.at[:, tok_cols(t)], tsend.at[1], trecv.at[1], ldev)
    tok_r.start()
    tok_l.start()

    a2a.second()

    _remote(tok_ref, tok_out.at[:, tok_cols(left)], tsend.at[0], trecv.at[0], ldev).wait_recv()
    fwd_r = _remote(tok_out.at[pl.ds(0, half), tok_cols(left)],
                    tok_out.at[pl.ds(0, half), tok_cols(left)], tsend.at[2], trecv.at[2], rdev)
    fwd_r.start()
    _remote(tok_ref, tok_out.at[:, tok_cols(right)], tsend.at[1], trecv.at[1], rdev).wait_recv()
    fwd_l = _remote(tok_out.at[pl.ds(half, half), tok_cols(right)],
                    tok_out.at[pl.ds(half, half), tok_cols(right)], tsend.at[3], trecv.at[3], ldev)
    fwd_l.start()

    a2a.arrived()
    flat = cache_out.reshape(na * nb, ntp, *cache_out.shape[3:])
    mine = flat.at[:, t]
    cache_r = _remote(mine, mine, csend.at[0], crecv.at[0], rdev)
    cache_l = _remote(mine, mine, csend.at[1], crecv.at[1], ldev)
    cache_r.start()
    cache_l.start()
    _remote(mine, flat.at[:, left], csend.at[0], crecv.at[0], ldev).wait_recv()
    cfwd_r = _remote(flat.at[pl.ds(0, blocks), left], flat.at[pl.ds(0, blocks), left],
                     csend.at[2], crecv.at[2], rdev)
    cfwd_r.start()
    _remote(mine, flat.at[:, right], csend.at[1], crecv.at[1], rdev).wait_recv()
    cfwd_l = _remote(flat.at[pl.ds(blocks, blocks), right], flat.at[pl.ds(blocks, blocks), right],
                     csend.at[3], crecv.at[3], ldev)
    cfwd_l.start()

    _remote(tok_ref.at[pl.ds(0, half)], tok_out.at[pl.ds(0, half), tok_cols(across)],
            tsend.at[2], trecv.at[2], ldev).wait_recv()
    _remote(tok_ref.at[pl.ds(half, half)], tok_out.at[pl.ds(half, half), tok_cols(across)],
            tsend.at[3], trecv.at[3], rdev).wait_recv()
    _remote(flat.at[pl.ds(0, blocks), t], flat.at[pl.ds(0, blocks), across],
            csend.at[2], crecv.at[2], ldev).wait_recv()
    _remote(flat.at[pl.ds(blocks, blocks), t], flat.at[pl.ds(blocks, blocks), across],
            csend.at[3], crecv.at[3], rdev).wait_recv()
    for c in (tok_r, tok_l, fwd_r, fwd_l, cache_r, cache_l, cfwd_r, cfwd_l):
        c.wait_send()
    a2a.finish()
    own_tok.wait()


def gather_inputs(tokens, old_cache, na, nb, ntp):
    rows, cols = tokens.shape
    _, share, width = old_cache.shape
    cache4 = old_cache.reshape(na, nb, share, width)
    return pl.pallas_call(
        functools.partial(_in_kernel, na, nb, ntp),
        out_shape=(
            jax.ShapeDtypeStruct((rows, ntp * cols), tokens.dtype),
            jax.ShapeDtypeStruct((na, nb, ntp, share, width), old_cache.dtype),
        ),
        in_specs=[pl.BlockSpec(memory_space=pl.ANY)] * 2,
        out_specs=(pl.BlockSpec(memory_space=pl.ANY), pl.BlockSpec(memory_space=pl.ANY)),
        scratch_shapes=[
            pltpu.SemaphoreType.DMA((4,)),
            pltpu.SemaphoreType.DMA((4,)),
            pltpu.SemaphoreType.DMA((4,)),
            pltpu.SemaphoreType.DMA((4,)),
            pltpu.SemaphoreType.DMA((2,)),
        ] + _seq_scratch(na, nb, share, width, old_cache.dtype),
        compiler_params=pltpu.CompilerParams(collective_id=0, has_side_effects=True),
    )(tokens, cache4)


def _out_kernel(na, nb, ntp, part_ref, share_ref, rs_out, new_out, stage_rs, rsend, rrecv, lsem,
                stage, s1send, s1recv, s2send, s2recv, slocal):
    s = lax.axis_index("seq")
    t = lax.axis_index("tp")
    right = lax.rem(t + 1, ntp)
    left = lax.rem(t + ntp - 1, ntp)
    across = lax.rem(t + 2, ntp)
    rdev = {"seq": s, "tp": right}
    ldev = {"seq": s, "tp": left}
    half = part_ref.shape[1] // 2
    _greet(na, nb, s, t, left, right)

    a2a = SeqAllToAll(na, nb, s, t, share_ref, stage, lambda a_src: new_out.at[a_src],
                      (s1send, s1recv, s2send, s2recv, slocal))
    a2a.first()

    own_part = pltpu.make_async_copy(part_ref.at[t], rs_out.at[t], lsem.at[0])
    own_part.start()
    to_r = _remote(part_ref.at[right], rs_out.at[t], rsend.at[0], rrecv.at[0], rdev)
    to_l = _remote(part_ref.at[left], rs_out.at[t], rsend.at[1], rrecv.at[1], ldev)
    via_r = _remote(part_ref.at[across, pl.ds(0, half)], stage_rs.at[0], rsend.at[2], rrecv.at[2],
                    rdev)
    via_l = _remote(part_ref.at[across, pl.ds(half, half)], stage_rs.at[1], rsend.at[3],
                    rrecv.at[3], ldev)
    for c in (to_r, to_l, via_r, via_l):
        c.start()

    a2a.second()

    _remote(part_ref.at[across, pl.ds(0, half)], stage_rs.at[0], rsend.at[2], rrecv.at[2],
            ldev).wait_recv()
    fwd_r = _remote(stage_rs.at[0], rs_out.at[left, pl.ds(0, half)], rsend.at[4], rrecv.at[4],
                    rdev)
    fwd_r.start()
    _remote(part_ref.at[across, pl.ds(half, half)], stage_rs.at[1], rsend.at[3], rrecv.at[3],
            rdev).wait_recv()
    fwd_l = _remote(stage_rs.at[1], rs_out.at[right, pl.ds(half, half)], rsend.at[5],
                    rrecv.at[5], ldev)
    fwd_l.start()

    a2a.arrived()
    _remote(part_ref.at[t], rs_out.at[left], rsend.at[0], rrecv.at[0], ldev).wait_recv()
    _remote(part_ref.at[t], rs_out.at[right], rsend.at[1], rrecv.at[1], rdev).wait_recv()
    _remote(stage_rs.at[0], rs_out.at[across, pl.ds(0, half)], rsend.at[4], rrecv.at[4],
            ldev).wait_recv()
    _remote(stage_rs.at[1], rs_out.at[across, pl.ds(half, half)], rsend.at[5], rrecv.at[5],
            rdev).wait_recv()
    for c in (to_r, to_l, via_r, via_l, fwd_r, fwd_l):
        c.wait_send()
    a2a.finish()
    own_part.wait()


def scatter_outputs(partial, share, na, nb, ntp):
    _, rows, cols = partial.shape
    _, block, width = share.shape
    share4 = share.reshape(na, nb, block, width)
    rs, new = pl.pallas_call(
        functools.partial(_out_kernel, na, nb, ntp),
        out_shape=(
            jax.ShapeDtypeStruct(partial.shape, partial.dtype),
            jax.ShapeDtypeStruct(share4.shape, share.dtype),
        ),
        in_specs=[pl.BlockSpec(memory_space=pl.ANY)] * 2,
        out_specs=(pl.BlockSpec(memory_space=pl.ANY), pl.BlockSpec(memory_space=pl.ANY)),
        scratch_shapes=[
            pltpu.VMEM((2, rows // 2, cols), partial.dtype),
            pltpu.SemaphoreType.DMA((6,)),
            pltpu.SemaphoreType.DMA((6,)),
            pltpu.SemaphoreType.DMA((1,)),
        ] + _seq_scratch(na, nb, block, width, share.dtype),
        compiler_params=pltpu.CompilerParams(collective_id=1, has_side_effects=True),
    )(partial, share4)
    return rs, new.reshape(share.shape)


def body(
    tokens,
    norm_gain,
    w_query,
    w_keyval,
    w_out,
    span_lens,
    cached_lens,
    old_table,
    new_table,
    old_cache,
):
    groups = lax.axis_size("seq")
    tp_count = lax.axis_size("tp")
    tp_index = lax.axis_index("tp")
    holders = old_table[0]
    held_len = cached_lens[0]
    span_len = span_lens[0]
    tok_rows, tok_cols = tokens.shape
    share = old_cache.shape[1]
    width = old_cache.shape[2]
    block_rows = share * tp_count
    capacity = groups * block_rows

    inner = min(groups, 8)
    outer = groups // inner
    tok_all, cache_all = gather_inputs(tokens, old_cache, outer, inner, tp_count)
    cache_all = cache_all.reshape(groups, tp_count, share, width)
    full_rows = tok_all
    normed = normalize(full_rows, norm_gain)
    query = jnp.dot(normed, w_query, preferred_element_type=jnp.float32).astype(jnp.bfloat16)
    keyval = jnp.dot(normed, w_keyval, preferred_element_type=jnp.float32).astype(jnp.bfloat16)

    cached = jnp.take(cache_all, holders, axis=0).reshape(capacity, width)
    shifted = lax.dynamic_update_slice(
        jnp.zeros((capacity, width), jnp.bfloat16), keyval, (held_len, jnp.int32(0))
    )
    positions = lax.broadcasted_iota(jnp.int32, (capacity, 1), 0)
    fresh = jnp.where(
        positions < held_len,
        cached,
        jnp.where(positions < held_len + span_len, shifted, jnp.zeros_like(shifted)),
    )
    fresh_share = lax.dynamic_slice_in_dim(
        fresh.reshape(groups, block_rows, width), tp_index * share, share, 1
    )
    targets = new_table[0]
    device_ids = lax.broadcasted_iota(jnp.int32, (groups, groups), 0)
    block_ids = lax.broadcasted_iota(jnp.int32, (groups, groups), 1)
    matches = targets[None, :] == device_ids
    sources = jnp.sum(jnp.where(matches, block_ids, 0), axis=1)
    sorted_share = jnp.take(fresh_share, sources, axis=0)
    head_size = width // 2
    keys = fresh[:, :head_size]
    values = fresh[:, head_size:]
    local_heads = query.shape[1] // head_size
    query3 = query.reshape(tok_rows, local_heads, head_size)
    scores = jnp.einsum(
        "thd,kd->htk", query3, keys, preferred_element_type=jnp.float32
    ) * head_size ** (-0.5)
    row_pos = lax.broadcasted_iota(jnp.int32, (tok_rows, 1), 0)
    key_pos = lax.broadcasted_iota(jnp.int32, (1, capacity), 1)
    allowed = key_pos <= held_len + row_pos
    scores = jnp.where(allowed[None], scores, MASKED)
    top = jnp.max(scores, axis=2, keepdims=True)
    weights = jnp.exp(scores - top)
    probs = (weights / jnp.sum(weights, axis=2, keepdims=True)).astype(jnp.bfloat16)
    context = jnp.einsum("htk,kd->thd", probs, values, preferred_element_type=jnp.float32).astype(
        jnp.bfloat16
    )
    context = context.reshape(tok_rows, local_heads * head_size)
    out_blocks = w_out.reshape(w_out.shape[0], tp_count, tok_cols)
    partial_out = jnp.einsum(
        "tk,kpn->ptn", context, out_blocks, preferred_element_type=jnp.float32
    ).astype(jnp.bfloat16)
    summed, new_cache = scatter_outputs(partial_out, sorted_share, outer, inner, tp_count)
    summed = summed.astype(jnp.float32)
    total = tokens.astype(jnp.float32) + jnp.sum(summed, axis=0)
    mixed = jnp.where(row_pos < span_len, total, jnp.zeros_like(total)).astype(jnp.bfloat16)
    return (mixed, new_cache)


def solution(mesh):
    in_specs = (
        P("seq", "tp"),
        P(),
        P(None, "tp"),
        P(),
        P("tp", None),
        P("seq"),
        P("seq"),
        P("seq", None),
        P("seq", None),
        P("seq", "tp", None),
    )
    out_specs = (P("seq", "tp"), P("seq", "tp", None))
    return jax.shard_map(body, mesh=mesh, in_specs=in_specs, out_specs=out_specs, check_vma=False)
```

```python
import functools

import jax
import jax.numpy as jnp
from jax import lax
from jax.experimental import pallas as pl
from jax.experimental.pallas import tpu as pltpu
from jax.sharding import PartitionSpec as P

EPSILON = 1e-05
MASKED = -1e30


def normalize(rows, norm_gain):
    values = rows.astype(jnp.float32)
    average = jnp.mean(values, axis=1, keepdims=True)
    centred = values - average
    spread = jnp.mean(centred * centred, axis=1, keepdims=True)
    return (centred * lax.rsqrt(spread + EPSILON) * norm_gain).astype(jnp.bfloat16)


MESH = pl.DeviceIdType.MESH


def _remote(src, dst, send, recv, dev):
    return pltpu.make_async_remote_copy(
        src_ref=src, dst_ref=dst, send_sem=send, recv_sem=recv, device_id=dev, device_id_type=MESH
    )


def _greet(na, nb, s, t, left, right):
    barrier = pltpu.get_barrier_semaphore()
    a = s // nb
    b = s % nb

    def one_b(k, carry):
        pl.semaphore_signal(barrier, inc=1, device_id={"seq": a * nb + lax.rem(b + k, nb), "tp": t},
                            device_id_type=MESH)
        return carry

    def one_a(k, carry):
        pl.semaphore_signal(barrier, inc=1, device_id={"seq": lax.rem(a + k, na) * nb + b, "tp": t},
                            device_id_type=MESH)
        return carry

    lax.fori_loop(1, nb, one_b, 0)
    lax.fori_loop(1, na, one_a, 0)
    for p in (left, right):
        pl.semaphore_signal(barrier, inc=1, device_id={"seq": s, "tp": p}, device_id_type=MESH)
    pl.semaphore_wait(barrier, na + nb)


class SeqAllToAll:
    def __init__(self, na, nb, s, t, src, stage, dst, sems):
        self.na, self.nb, self.t, self.src, self.stage, self.dst = na, nb, t, src, stage, dst
        self.a = s // nb
        self.b = s % nb
        self.s1send, self.s1recv, self.s2send, self.s2recv, self.local = sems

    def _dev(self, a, b):
        return {"seq": a * self.nb + b, "tp": self.t}

    def _out1(self, k):
        peer = lax.rem(self.b + k, self.nb)
        return _remote(self.src.at[:, peer], self.stage.at[self.b], self.s1send.at[k],
                       self.s1recv.at[k], self._dev(self.a, peer))

    def _in1(self, k):
        sender = lax.rem(self.b + self.nb - k, self.nb)
        return _remote(self.src.at[:, self.b], self.stage.at[sender], self.s1send.at[k],
                       self.s1recv.at[k], self._dev(self.a, sender))

    def _out2(self, k):
        peer = lax.rem(self.a + k, self.na)
        return _remote(self.stage.at[:, peer], self.dst(self.a), self.s2send.at[k],
                       self.s2recv.at[k], self._dev(peer, self.b))

    def _in2(self, k):
        sender = lax.rem(self.a + self.na - k, self.na)
        return _remote(self.stage.at[:, self.a], self.dst(sender), self.s2send.at[k],
                       self.s2recv.at[k], self._dev(sender, self.b))

    def first(self):
        self.own1 = pltpu.make_async_copy(self.src.at[:, self.b], self.stage.at[self.b],
                                          self.local.at[0])
        self.own1.start()
        _loop(self.nb, lambda k: self._out1(k).start())

    def second(self):
        _loop(self.nb, lambda k: self._in1(k).wait_recv())
        self.own1.wait()
        self.own2 = pltpu.make_async_copy(self.stage.at[:, self.a], self.dst(self.a),
                                          self.local.at[1])
        self.own2.start()
        _loop(self.na, lambda k: self._out2(k).start())

    def arrived(self):
        _loop(self.na, lambda k: self._in2(k).wait_recv())
        self.own2.wait()

    def finish(self):
        _loop(self.nb, lambda k: self._out1(k).wait_send())
        _loop(self.na, lambda k: self._out2(k).wait_send())


def _seq_scratch(na, nb, share, width, dtype):
    return [
        pltpu.VMEM((nb, na, share, width), dtype),
        pltpu.SemaphoreType.DMA((nb,)),
        pltpu.SemaphoreType.DMA((nb,)),
        pltpu.SemaphoreType.DMA((na,)),
        pltpu.SemaphoreType.DMA((na,)),
        pltpu.SemaphoreType.DMA((2,)),
    ]


def _loop(n, fn):
    def step(k, carry):
        fn(k)
        return carry

    lax.fori_loop(1, n, step, 0)


def _in_kernel(na, nb, ntp, tok_ref, cache_ref, tok_out, cache_out, tsend, trecv, csend, crecv,
               lsem, stage, s1send, s1recv, s2send, s2recv, slocal):
    s = lax.axis_index("seq")
    t = lax.axis_index("tp")
    right = lax.rem(t + 1, ntp)
    left = lax.rem(t + ntp - 1, ntp)
    across = lax.rem(t + 2, ntp)
    rdev = {"seq": s, "tp": right}
    ldev = {"seq": s, "tp": left}
    rows, cols = tok_ref.shape
    half = rows // 2
    blocks = na * nb // 2
    _greet(na, nb, s, t, left, right)

    def tok_cols(p):
        return pl.ds(p * cols, cols)

    a2a = SeqAllToAll(na, nb, s, t, cache_ref, stage, lambda a_src: cache_out.at[a_src, :, t],
                      (s1send, s1recv, s2send, s2recv, slocal))
    a2a.first()

    own_tok = pltpu.make_async_copy(tok_ref, tok_out.at[:, tok_cols(t)], lsem.at[0])
    own_tok.start()
    tok_r = _remote(tok_ref, tok_out.at[:, tok_cols(t)], tsend.at[0], trecv.at[0], rdev)
    tok_l = _remote(tok_ref, tok_out.at[:, tok_cols(t)], tsend.at[1], trecv.at[1], ldev)
    tok_r.start()
    tok_l.start()

    a2a.second()

    _remote(tok_ref, tok_out.at[:, tok_cols(left)], tsend.at[0], trecv.at[0], ldev).wait_recv()
    fwd_r = _remote(tok_out.at[pl.ds(0, half), tok_cols(left)],
                    tok_out.at[pl.ds(0, half), tok_cols(left)], tsend.at[2], trecv.at[2], rdev)
    fwd_r.start()
    _remote(tok_ref, tok_out.at[:, tok_cols(right)], tsend.at[1], trecv.at[1], rdev).wait_recv()
    fwd_l = _remote(tok_out.at[pl.ds(half, half), tok_cols(right)],
                    tok_out.at[pl.ds(half, half), tok_cols(right)], tsend.at[3], trecv.at[3], ldev)
    fwd_l.start()

    a2a.arrived()
    flat = cache_out.reshape(na * nb, ntp, *cache_out.shape[3:])
    mine = flat.at[:, t]
    cache_r = _remote(mine, mine, csend.at[0], crecv.at[0], rdev)
    cache_l = _remote(mine, mine, csend.at[1], crecv.at[1], ldev)
    cache_r.start()
    cache_l.start()
    _remote(mine, flat.at[:, left], csend.at[0], crecv.at[0], ldev).wait_recv()
    cfwd_r = _remote(flat.at[pl.ds(0, blocks), left], flat.at[pl.ds(0, blocks), left],
                     csend.at[2], crecv.at[2], rdev)
    cfwd_r.start()
    _remote(mine, flat.at[:, right], csend.at[1], crecv.at[1], rdev).wait_recv()
    cfwd_l = _remote(flat.at[pl.ds(blocks, blocks), right], flat.at[pl.ds(blocks, blocks), right],
                     csend.at[3], crecv.at[3], ldev)
    cfwd_l.start()

    _remote(tok_ref.at[pl.ds(0, half)], tok_out.at[pl.ds(0, half), tok_cols(across)],
            tsend.at[2], trecv.at[2], ldev).wait_recv()
    _remote(tok_ref.at[pl.ds(half, half)], tok_out.at[pl.ds(half, half), tok_cols(across)],
            tsend.at[3], trecv.at[3], rdev).wait_recv()
    _remote(flat.at[pl.ds(0, blocks), t], flat.at[pl.ds(0, blocks), across],
            csend.at[2], crecv.at[2], ldev).wait_recv()
    _remote(flat.at[pl.ds(blocks, blocks), t], flat.at[pl.ds(blocks, blocks), across],
            csend.at[3], crecv.at[3], rdev).wait_recv()
    for c in (tok_r, tok_l, fwd_r, fwd_l, cache_r, cache_l, cfwd_r, cfwd_l):
        c.wait_send()
    a2a.finish()
    own_tok.wait()


def gather_inputs(tokens, old_cache, na, nb, ntp):
    rows, cols = tokens.shape
    _, share, width = old_cache.shape
    cache4 = old_cache.reshape(na, nb, share, width)
    return pl.pallas_call(
        functools.partial(_in_kernel, na, nb, ntp),
        out_shape=(
            jax.ShapeDtypeStruct((rows, ntp * cols), tokens.dtype),
            jax.ShapeDtypeStruct((na, nb, ntp, share, width), old_cache.dtype),
        ),
        in_specs=[pl.BlockSpec(memory_space=pl.ANY)] * 2,
        out_specs=(pl.BlockSpec(memory_space=pl.ANY), pl.BlockSpec(memory_space=pl.ANY)),
        scratch_shapes=[
            pltpu.SemaphoreType.DMA((4,)),
            pltpu.SemaphoreType.DMA((4,)),
            pltpu.SemaphoreType.DMA((4,)),
            pltpu.SemaphoreType.DMA((4,)),
            pltpu.SemaphoreType.DMA((2,)),
        ] + _seq_scratch(na, nb, share, width, old_cache.dtype),
        compiler_params=pltpu.CompilerParams(collective_id=0, has_side_effects=True),
    )(tokens, cache4)


def _out_kernel(na, nb, ntp, part_ref, share_ref, rs_out, new_out, stage_rs, rsend, rrecv, lsem,
                stage, s1send, s1recv, s2send, s2recv, slocal):
    s = lax.axis_index("seq")
    t = lax.axis_index("tp")
    right = lax.rem(t + 1, ntp)
    left = lax.rem(t + ntp - 1, ntp)
    across = lax.rem(t + 2, ntp)
    rdev = {"seq": s, "tp": right}
    ldev = {"seq": s, "tp": left}
    half = part_ref.shape[1] // 2
    _greet(na, nb, s, t, left, right)

    a2a = SeqAllToAll(na, nb, s, t, share_ref, stage, lambda a_src: new_out.at[a_src],
                      (s1send, s1recv, s2send, s2recv, slocal))
    a2a.first()

    own_part = pltpu.make_async_copy(part_ref.at[t], rs_out.at[t], lsem.at[0])
    own_part.start()
    to_r = _remote(part_ref.at[right], rs_out.at[t], rsend.at[0], rrecv.at[0], rdev)
    to_l = _remote(part_ref.at[left], rs_out.at[t], rsend.at[1], rrecv.at[1], ldev)
    via_r = _remote(part_ref.at[across, pl.ds(0, half)], stage_rs.at[0], rsend.at[2], rrecv.at[2],
                    rdev)
    via_l = _remote(part_ref.at[across, pl.ds(half, half)], stage_rs.at[1], rsend.at[3],
                    rrecv.at[3], ldev)
    for c in (to_r, to_l, via_r, via_l):
        c.start()

    a2a.second()

    _remote(part_ref.at[across, pl.ds(0, half)], stage_rs.at[0], rsend.at[2], rrecv.at[2],
            ldev).wait_recv()
    fwd_r = _remote(stage_rs.at[0], rs_out.at[left, pl.ds(0, half)], rsend.at[4], rrecv.at[4],
                    rdev)
    fwd_r.start()
    _remote(part_ref.at[across, pl.ds(half, half)], stage_rs.at[1], rsend.at[3], rrecv.at[3],
            rdev).wait_recv()
    fwd_l = _remote(stage_rs.at[1], rs_out.at[right, pl.ds(half, half)], rsend.at[5],
                    rrecv.at[5], ldev)
    fwd_l.start()

    a2a.arrived()
    _remote(part_ref.at[t], rs_out.at[left], rsend.at[0], rrecv.at[0], ldev).wait_recv()
    _remote(part_ref.at[t], rs_out.at[right], rsend.at[1], rrecv.at[1], rdev).wait_recv()
    _remote(stage_rs.at[0], rs_out.at[across, pl.ds(0, half)], rsend.at[4], rrecv.at[4],
            ldev).wait_recv()
    _remote(stage_rs.at[1], rs_out.at[across, pl.ds(half, half)], rsend.at[5], rrecv.at[5],
            rdev).wait_recv()
    for c in (to_r, to_l, via_r, via_l, fwd_r, fwd_l):
        c.wait_send()
    a2a.finish()
    own_part.wait()


def scatter_outputs(partial, share, na, nb, ntp):
    _, rows, cols = partial.shape
    _, block, width = share.shape
    share4 = share.reshape(na, nb, block, width)
    rs, new = pl.pallas_call(
        functools.partial(_out_kernel, na, nb, ntp),
        out_shape=(
            jax.ShapeDtypeStruct(partial.shape, partial.dtype),
            jax.ShapeDtypeStruct(share4.shape, share.dtype),
        ),
        in_specs=[pl.BlockSpec(memory_space=pl.ANY)] * 2,
        out_specs=(pl.BlockSpec(memory_space=pl.ANY), pl.BlockSpec(memory_space=pl.ANY)),
        scratch_shapes=[
            pltpu.VMEM((2, rows // 2, cols), partial.dtype),
            pltpu.SemaphoreType.DMA((6,)),
            pltpu.SemaphoreType.DMA((6,)),
            pltpu.SemaphoreType.DMA((1,)),
        ] + _seq_scratch(na, nb, block, width, share.dtype),
        compiler_params=pltpu.CompilerParams(collective_id=1, has_side_effects=True),
    )(partial, share4)
    return rs, new.reshape(share.shape)


def _attend_kernel(scale, lens_ref, q_ref, k_ref, v_ref, o_ref):
    chunk = q_ref.shape[0]
    capacity = k_ref.shape[0]
    held = lens_ref[0]
    first = pl.program_id(1) * chunk
    scores = lax.dot_general(
        q_ref[...], k_ref[...], (((1,), (1,)), ((), ())), preferred_element_type=jnp.float32
    ) * scale
    row_pos = first + lax.broadcasted_iota(jnp.int32, (chunk, capacity), 0)
    key_pos = lax.broadcasted_iota(jnp.int32, (chunk, capacity), 1)
    scores = jnp.where(key_pos <= held + row_pos, scores, MASKED)
    top = jnp.max(scores, axis=1, keepdims=True)
    weights = jnp.exp(scores - top)
    probs = (weights / jnp.sum(weights, axis=1, keepdims=True)).astype(jnp.bfloat16)
    o_ref[...] = jnp.dot(probs, v_ref[...], preferred_element_type=jnp.float32).astype(o_ref.dtype)


def attend(query, fresh, held_len, head_size, chunk=128):
    rows, qcols = query.shape
    capacity = fresh.shape[0]
    heads = qcols // head_size
    lens = jnp.reshape(held_len, (1,)).astype(jnp.int32)
    return pl.pallas_call(
        functools.partial(_attend_kernel, head_size ** (-0.5)),
        out_shape=jax.ShapeDtypeStruct((rows, qcols), jnp.bfloat16),
        grid_spec=pltpu.PrefetchScalarGridSpec(
            num_scalar_prefetch=1,
            grid=(heads, rows // chunk),
            in_specs=[
                pl.BlockSpec((chunk, head_size), lambda h, r, lens: (r, h)),
                pl.BlockSpec((capacity, head_size), lambda h, r, lens: (0, 0)),
                pl.BlockSpec((capacity, head_size), lambda h, r, lens: (0, 1)),
            ],
            out_specs=pl.BlockSpec((chunk, head_size), lambda h, r, lens: (r, h)),
        ),
        cost_estimate=pl.CostEstimate(
            flops=4 * rows * capacity * qcols,
            transcendentals=rows * capacity * heads,
            bytes_accessed=2 * (2 * rows * qcols + 2 * capacity * head_size),
        ),
    )(lens, query, fresh, fresh)


def body(
    tokens,
    norm_gain,
    w_query,
    w_keyval,
    w_out,
    span_lens,
    cached_lens,
    old_table,
    new_table,
    old_cache,
):
    groups = lax.axis_size("seq")
    tp_count = lax.axis_size("tp")
    tp_index = lax.axis_index("tp")
    holders = old_table[0]
    held_len = cached_lens[0]
    span_len = span_lens[0]
    tok_rows, tok_cols = tokens.shape
    share = old_cache.shape[1]
    width = old_cache.shape[2]
    block_rows = share * tp_count
    capacity = groups * block_rows

    inner = min(groups, 8)
    outer = groups // inner
    tok_all, cache_all = gather_inputs(tokens, old_cache, outer, inner, tp_count)
    cache_all = cache_all.reshape(groups, tp_count, share, width)
    full_rows = tok_all
    normed = normalize(full_rows, norm_gain)
    query = jnp.dot(normed, w_query, preferred_element_type=jnp.float32).astype(jnp.bfloat16)
    keyval = jnp.dot(normed, w_keyval, preferred_element_type=jnp.float32).astype(jnp.bfloat16)

    cached = jnp.take(cache_all, holders, axis=0).reshape(capacity, width)
    shifted = lax.dynamic_update_slice(
        jnp.zeros((capacity, width), jnp.bfloat16), keyval, (held_len, jnp.int32(0))
    )
    positions = lax.broadcasted_iota(jnp.int32, (capacity, 1), 0)
    fresh = jnp.where(
        positions < held_len,
        cached,
        jnp.where(positions < held_len + span_len, shifted, jnp.zeros_like(shifted)),
    )
    fresh_share = lax.dynamic_slice_in_dim(
        fresh.reshape(groups, block_rows, width), tp_index * share, share, 1
    )
    targets = new_table[0]
    device_ids = lax.broadcasted_iota(jnp.int32, (groups, groups), 0)
    block_ids = lax.broadcasted_iota(jnp.int32, (groups, groups), 1)
    matches = targets[None, :] == device_ids
    sources = jnp.sum(jnp.where(matches, block_ids, 0), axis=1)
    sorted_share = jnp.take(fresh_share, sources, axis=0)
    head_size = width // 2
    context = attend(query, fresh, held_len, head_size)
    row_pos = lax.broadcasted_iota(jnp.int32, (tok_rows, 1), 0)
    out_blocks = w_out.reshape(w_out.shape[0], tp_count, tok_cols)
    partial_out = jnp.einsum(
        "tk,kpn->ptn", context, out_blocks, preferred_element_type=jnp.float32
    ).astype(jnp.bfloat16)
    summed, new_cache = scatter_outputs(partial_out, sorted_share, outer, inner, tp_count)
    summed = summed.astype(jnp.float32)
    total = tokens.astype(jnp.float32) + jnp.sum(summed, axis=0)
    mixed = jnp.where(row_pos < span_len, total, jnp.zeros_like(total)).astype(jnp.bfloat16)
    return (mixed, new_cache)


def solution(mesh):
    in_specs = (
        P("seq", "tp"),
        P(),
        P(None, "tp"),
        P(),
        P("tp", None),
        P("seq"),
        P("seq"),
        P("seq", None),
        P("seq", None),
        P("seq", "tp", None),
    )
    out_specs = (P("seq", "tp"), P("seq", "tp", None))
    return jax.shard_map(body, mesh=mesh, in_specs=in_specs, out_specs=out_specs, check_vma=False)
```

```python
import functools

import jax
import jax.numpy as jnp
from jax import lax
from jax.experimental import pallas as pl
from jax.experimental.pallas import tpu as pltpu
from jax.sharding import PartitionSpec as P

EPSILON = 1e-05
MASKED = -1e30


def normalize(rows, norm_gain):
    values = rows.astype(jnp.float32)
    average = jnp.mean(values, axis=1, keepdims=True)
    centred = values - average
    spread = jnp.mean(centred * centred, axis=1, keepdims=True)
    return (centred * lax.rsqrt(spread + EPSILON) * norm_gain).astype(jnp.bfloat16)


MESH = pl.DeviceIdType.MESH


def _remote(src, dst, send, recv, dev):
    return pltpu.make_async_remote_copy(
        src_ref=src, dst_ref=dst, send_sem=send, recv_sem=recv, device_id=dev, device_id_type=MESH
    )


def _greet(na, nb, s, t, *tp_peers):
    barrier = pltpu.get_barrier_semaphore()
    a = s // nb
    b = s % nb

    def one_b(k, carry):
        pl.semaphore_signal(barrier, inc=1, device_id={"seq": a * nb + lax.rem(b + k, nb), "tp": t},
                            device_id_type=MESH)
        return carry

    def one_a(k, carry):
        pl.semaphore_signal(barrier, inc=1, device_id={"seq": lax.rem(a + k, na) * nb + b, "tp": t},
                            device_id_type=MESH)
        return carry

    lax.fori_loop(1, nb, one_b, 0)
    lax.fori_loop(1, na, one_a, 0)
    for p in tp_peers:
        pl.semaphore_signal(barrier, inc=1, device_id={"seq": s, "tp": p}, device_id_type=MESH)
    pl.semaphore_wait(barrier, na + nb - 2 + len(tp_peers))


class SeqAllToAll:
    def __init__(self, na, nb, s, t, src, stage, dst, sems):
        self.na, self.nb, self.t, self.src, self.stage, self.dst = na, nb, t, src, stage, dst
        self.a = s // nb
        self.b = s % nb
        self.s1send, self.s1recv, self.s2send, self.s2recv, self.local = sems

    def _dev(self, a, b):
        return {"seq": a * self.nb + b, "tp": self.t}

    def _out1(self, k):
        peer = lax.rem(self.b + k, self.nb)
        return _remote(self.src.at[:, peer], self.stage.at[self.b], self.s1send.at[k],
                       self.s1recv.at[k], self._dev(self.a, peer))

    def _in1(self, k):
        sender = lax.rem(self.b + self.nb - k, self.nb)
        return _remote(self.src.at[:, self.b], self.stage.at[sender], self.s1send.at[k],
                       self.s1recv.at[k], self._dev(self.a, sender))

    def _out2(self, k):
        peer = lax.rem(self.a + k, self.na)
        return _remote(self.stage.at[:, peer], self.dst(self.a), self.s2send.at[k],
                       self.s2recv.at[k], self._dev(peer, self.b))

    def _in2(self, k):
        sender = lax.rem(self.a + self.na - k, self.na)
        return _remote(self.stage.at[:, self.a], self.dst(sender), self.s2send.at[k],
                       self.s2recv.at[k], self._dev(sender, self.b))

    def first(self):
        self.own1 = pltpu.make_async_copy(self.src.at[:, self.b], self.stage.at[self.b],
                                          self.local.at[0])
        self.own1.start()
        _loop(self.nb, lambda k: self._out1(k).start())

    def second(self):
        _loop(self.nb, lambda k: self._in1(k).wait_recv())
        self.own1.wait()
        self.own2 = pltpu.make_async_copy(self.stage.at[:, self.a], self.dst(self.a),
                                          self.local.at[1])
        self.own2.start()
        _loop(self.na, lambda k: self._out2(k).start())

    def arrived(self):
        _loop(self.na, lambda k: self._in2(k).wait_recv())
        self.own2.wait()

    def finish(self):
        _loop(self.nb, lambda k: self._out1(k).wait_send())
        _loop(self.na, lambda k: self._out2(k).wait_send())


def _seq_scratch(na, nb, share, width, dtype):
    return [
        pltpu.VMEM((nb, na, share, width), dtype),
        pltpu.SemaphoreType.DMA((nb,)),
        pltpu.SemaphoreType.DMA((nb,)),
        pltpu.SemaphoreType.DMA((na,)),
        pltpu.SemaphoreType.DMA((na,)),
        pltpu.SemaphoreType.DMA((2,)),
    ]


def _loop(n, fn):
    def step(k, carry):
        fn(k)
        return carry

    lax.fori_loop(1, n, step, 0)


def _in_kernel(na, nb, ntp, tok_ref, cache_ref, tok_out, cache_out, tsend, trecv, csend, crecv,
               lsem, stage, s1send, s1recv, s2send, s2recv, slocal):
    s = lax.axis_index("seq")
    t = lax.axis_index("tp")
    right = lax.rem(t + 1, ntp)
    left = lax.rem(t + ntp - 1, ntp)
    across = lax.rem(t + 2, ntp)
    rdev = {"seq": s, "tp": right}
    ldev = {"seq": s, "tp": left}
    rows, cols = tok_ref.shape
    half = rows // 2
    blocks = na * nb // 2
    _greet(na, nb, s, t, left, right)

    def tok_cols(p):
        return pl.ds(p * cols, cols)

    a2a = SeqAllToAll(na, nb, s, t, cache_ref, stage, lambda a_src: cache_out.at[a_src, :, t],
                      (s1send, s1recv, s2send, s2recv, slocal))
    a2a.first()

    own_tok = pltpu.make_async_copy(tok_ref, tok_out.at[:, tok_cols(t)], lsem.at[0])
    own_tok.start()
    tok_r = _remote(tok_ref, tok_out.at[:, tok_cols(t)], tsend.at[0], trecv.at[0], rdev)
    tok_l = _remote(tok_ref, tok_out.at[:, tok_cols(t)], tsend.at[1], trecv.at[1], ldev)
    tok_r.start()
    tok_l.start()

    a2a.second()

    _remote(tok_ref, tok_out.at[:, tok_cols(left)], tsend.at[0], trecv.at[0], ldev).wait_recv()
    fwd_r = _remote(tok_out.at[pl.ds(0, half), tok_cols(left)],
                    tok_out.at[pl.ds(0, half), tok_cols(left)], tsend.at[2], trecv.at[2], rdev)
    fwd_r.start()
    _remote(tok_ref, tok_out.at[:, tok_cols(right)], tsend.at[1], trecv.at[1], rdev).wait_recv()
    fwd_l = _remote(tok_out.at[pl.ds(half, half), tok_cols(right)],
                    tok_out.at[pl.ds(half, half), tok_cols(right)], tsend.at[3], trecv.at[3], ldev)
    fwd_l.start()

    a2a.arrived()
    flat = cache_out.reshape(na * nb, ntp, *cache_out.shape[3:])
    mine = flat.at[:, t]
    cache_r = _remote(mine, mine, csend.at[0], crecv.at[0], rdev)
    cache_l = _remote(mine, mine, csend.at[1], crecv.at[1], ldev)
    cache_r.start()
    cache_l.start()
    _remote(mine, flat.at[:, left], csend.at[0], crecv.at[0], ldev).wait_recv()
    cfwd_r = _remote(flat.at[pl.ds(0, blocks), left], flat.at[pl.ds(0, blocks), left],
                     csend.at[2], crecv.at[2], rdev)
    cfwd_r.start()
    _remote(mine, flat.at[:, right], csend.at[1], crecv.at[1], rdev).wait_recv()
    cfwd_l = _remote(flat.at[pl.ds(blocks, blocks), right], flat.at[pl.ds(blocks, blocks), right],
                     csend.at[3], crecv.at[3], ldev)
    cfwd_l.start()

    _remote(tok_ref.at[pl.ds(0, half)], tok_out.at[pl.ds(0, half), tok_cols(across)],
            tsend.at[2], trecv.at[2], ldev).wait_recv()
    _remote(tok_ref.at[pl.ds(half, half)], tok_out.at[pl.ds(half, half), tok_cols(across)],
            tsend.at[3], trecv.at[3], rdev).wait_recv()
    _remote(flat.at[pl.ds(0, blocks), t], flat.at[pl.ds(0, blocks), across],
            csend.at[2], crecv.at[2], ldev).wait_recv()
    _remote(flat.at[pl.ds(blocks, blocks), t], flat.at[pl.ds(blocks, blocks), across],
            csend.at[3], crecv.at[3], rdev).wait_recv()
    for c in (tok_r, tok_l, fwd_r, fwd_l, cache_r, cache_l, cfwd_r, cfwd_l):
        c.wait_send()
    a2a.finish()
    own_tok.wait()


def gather_inputs(tokens, old_cache, na, nb, ntp):
    rows, cols = tokens.shape
    _, share, width = old_cache.shape
    cache4 = old_cache.reshape(na, nb, share, width)
    return pl.pallas_call(
        functools.partial(_in_kernel, na, nb, ntp),
        out_shape=(
            jax.ShapeDtypeStruct((rows, ntp * cols), tokens.dtype),
            jax.ShapeDtypeStruct((na, nb, ntp, share, width), old_cache.dtype),
        ),
        in_specs=[pl.BlockSpec(memory_space=pl.ANY)] * 2,
        out_specs=(pl.BlockSpec(memory_space=pl.ANY), pl.BlockSpec(memory_space=pl.ANY)),
        scratch_shapes=[
            pltpu.SemaphoreType.DMA((4,)),
            pltpu.SemaphoreType.DMA((4,)),
            pltpu.SemaphoreType.DMA((4,)),
            pltpu.SemaphoreType.DMA((4,)),
            pltpu.SemaphoreType.DMA((2,)),
        ] + _seq_scratch(na, nb, share, width, old_cache.dtype),
        compiler_params=pltpu.CompilerParams(collective_id=0, has_side_effects=True),
    )(tokens, cache4)


def _out_kernel(na, nb, ntp, part_ref, share_ref, rs_out, new_out, stage_rs, rsend, rrecv, lsem,
                stage, s1send, s1recv, s2send, s2recv, slocal):
    s = lax.axis_index("seq")
    t = lax.axis_index("tp")
    right = lax.rem(t + 1, ntp)
    left = lax.rem(t + ntp - 1, ntp)
    across = lax.rem(t + 2, ntp)
    rdev = {"seq": s, "tp": right}
    ldev = {"seq": s, "tp": left}
    half = part_ref.shape[1] // 2
    _greet(na, nb, s, t, left, right)

    a2a = SeqAllToAll(na, nb, s, t, share_ref, stage, lambda a_src: new_out.at[a_src],
                      (s1send, s1recv, s2send, s2recv, slocal))
    a2a.first()

    own_part = pltpu.make_async_copy(part_ref.at[t], rs_out.at[t], lsem.at[0])
    own_part.start()
    to_r = _remote(part_ref.at[right], rs_out.at[t], rsend.at[0], rrecv.at[0], rdev)
    to_l = _remote(part_ref.at[left], rs_out.at[t], rsend.at[1], rrecv.at[1], ldev)
    via_r = _remote(part_ref.at[across, pl.ds(0, half)], stage_rs.at[0], rsend.at[2], rrecv.at[2],
                    rdev)
    via_l = _remote(part_ref.at[across, pl.ds(half, half)], stage_rs.at[1], rsend.at[3],
                    rrecv.at[3], ldev)
    for c in (to_r, to_l, via_r, via_l):
        c.start()

    a2a.second()

    _remote(part_ref.at[across, pl.ds(0, half)], stage_rs.at[0], rsend.at[2], rrecv.at[2],
            ldev).wait_recv()
    fwd_r = _remote(stage_rs.at[0], rs_out.at[left, pl.ds(0, half)], rsend.at[4], rrecv.at[4],
                    rdev)
    fwd_r.start()
    _remote(part_ref.at[across, pl.ds(half, half)], stage_rs.at[1], rsend.at[3], rrecv.at[3],
            rdev).wait_recv()
    fwd_l = _remote(stage_rs.at[1], rs_out.at[right, pl.ds(half, half)], rsend.at[5],
                    rrecv.at[5], ldev)
    fwd_l.start()

    a2a.arrived()
    _remote(part_ref.at[t], rs_out.at[left], rsend.at[0], rrecv.at[0], ldev).wait_recv()
    _remote(part_ref.at[t], rs_out.at[right], rsend.at[1], rrecv.at[1], rdev).wait_recv()
    _remote(stage_rs.at[0], rs_out.at[across, pl.ds(0, half)], rsend.at[4], rrecv.at[4],
            ldev).wait_recv()
    _remote(stage_rs.at[1], rs_out.at[across, pl.ds(half, half)], rsend.at[5], rrecv.at[5],
            rdev).wait_recv()
    for c in (to_r, to_l, via_r, via_l, fwd_r, fwd_l):
        c.wait_send()
    a2a.finish()
    own_part.wait()


def scatter_outputs(partial, share, na, nb, ntp):
    _, rows, cols = partial.shape
    _, block, width = share.shape
    share4 = share.reshape(na, nb, block, width)
    rs, new = pl.pallas_call(
        functools.partial(_out_kernel, na, nb, ntp),
        out_shape=(
            jax.ShapeDtypeStruct(partial.shape, partial.dtype),
            jax.ShapeDtypeStruct(share4.shape, share.dtype),
        ),
        in_specs=[pl.BlockSpec(memory_space=pl.ANY)] * 2,
        out_specs=(pl.BlockSpec(memory_space=pl.ANY), pl.BlockSpec(memory_space=pl.ANY)),
        scratch_shapes=[
            pltpu.VMEM((2, rows // 2, cols), partial.dtype),
            pltpu.SemaphoreType.DMA((6,)),
            pltpu.SemaphoreType.DMA((6,)),
            pltpu.SemaphoreType.DMA((1,)),
        ] + _seq_scratch(na, nb, block, width, share.dtype),
        compiler_params=pltpu.CompilerParams(collective_id=1, has_side_effects=True),
    )(partial, share4)
    return rs, new.reshape(share.shape)


def _attend_kernel(scale, lens_ref, q_ref, k_ref, v_ref, o_ref):
    chunk = q_ref.shape[0]
    capacity = k_ref.shape[0]
    held = lens_ref[0]
    first = pl.program_id(1) * chunk
    scores = lax.dot_general(
        q_ref[...], k_ref[...], (((1,), (1,)), ((), ())), preferred_element_type=jnp.float32
    ) * scale
    row_pos = first + lax.broadcasted_iota(jnp.int32, (chunk, capacity), 0)
    key_pos = lax.broadcasted_iota(jnp.int32, (chunk, capacity), 1)
    scores = jnp.where(key_pos <= held + row_pos, scores, MASKED)
    top = jnp.max(scores, axis=1, keepdims=True)
    weights = jnp.exp(scores - top)
    probs = (weights / jnp.sum(weights, axis=1, keepdims=True)).astype(jnp.bfloat16)
    o_ref[...] = jnp.dot(probs, v_ref[...], preferred_element_type=jnp.float32).astype(o_ref.dtype)


def attend(query, fresh, held_len, head_size, chunk=128):
    rows, qcols = query.shape
    capacity = fresh.shape[0]
    heads = qcols // head_size
    lens = jnp.reshape(held_len, (1,)).astype(jnp.int32)
    return pl.pallas_call(
        functools.partial(_attend_kernel, head_size ** (-0.5)),
        out_shape=jax.ShapeDtypeStruct((rows, qcols), jnp.bfloat16),
        grid_spec=pltpu.PrefetchScalarGridSpec(
            num_scalar_prefetch=1,
            grid=(heads, rows // chunk),
            in_specs=[
                pl.BlockSpec((chunk, head_size), lambda h, r, lens: (r, h)),
                pl.BlockSpec((capacity, head_size), lambda h, r, lens: (0, 0)),
                pl.BlockSpec((capacity, head_size), lambda h, r, lens: (0, 1)),
            ],
            out_specs=pl.BlockSpec((chunk, head_size), lambda h, r, lens: (r, h)),
        ),
        cost_estimate=pl.CostEstimate(
            flops=4 * rows * capacity * qcols,
            transcendentals=rows * capacity * heads,
            bytes_accessed=2 * (2 * rows * qcols + 2 * capacity * head_size),
        ),
    )(lens, query, fresh, fresh)


def _tail_kernel(na, nb, ntp, scale, chunk, lens_ref, q_ref, kt_ref, v_ref, w_ref, share_ref,
                 rs_out, new_out, ctx, part, psend, precv, plocal, stage, s1send, s1recv, s2send,
                 s2recv, slocal):
    s = lax.axis_index("seq")
    t = lax.axis_index("tp")
    rows, qcols = q_ref.shape
    head_size, capacity = kt_ref.shape
    heads = qcols // head_size
    cols = w_ref.shape[1] // ntp
    chunks = rows // chunk
    _greet(na, nb, s, t, *[lax.rem(t + k, ntp) for k in range(1, ntp)])
    a2a = SeqAllToAll(na, nb, s, t, share_ref, stage, lambda a_src: new_out.at[a_src],
                      (s1send, s1recv, s2send, s2recv, slocal))
    a2a.first()
    held = lens_ref[0]

    def slice_out(c, k):
        peer = lax.rem(t + k, ntp)
        return _remote(part.at[c, :, pl.ds(pl.multiple_of(peer * cols, cols), cols)],
                       rs_out.at[t, pl.ds(pl.multiple_of(c * chunk, chunk), chunk)],
                       psend.at[c, k], precv.at[c, k], {"seq": s, "tp": peer})

    def slice_in(c, k):
        sender = lax.rem(t + ntp - k, ntp)
        return _remote(part.at[c, :, pl.ds(0, cols)],
                       rs_out.at[sender, pl.ds(pl.multiple_of(c * chunk, chunk), chunk)],
                       psend.at[c, k], precv.at[c, k], {"seq": s, "tp": sender})

    def slice_own(c):
        return pltpu.make_async_copy(
            part.at[c, :, pl.ds(pl.multiple_of(t * cols, cols), cols)],
            rs_out.at[t, pl.ds(pl.multiple_of(c * chunk, chunk), chunk)], plocal.at[c])

    def do_chunk(c):
        first = pl.multiple_of(c * chunk, chunk)
        row_pos = first + lax.broadcasted_iota(jnp.int32, (chunk, capacity), 0)
        key_pos = lax.broadcasted_iota(jnp.int32, (chunk, capacity), 1)
        allowed = key_pos <= held + row_pos
        for h in range(heads):
            q = q_ref[pl.ds(first, chunk), pl.ds(h * head_size, head_size)]
            scores = jnp.dot(q, kt_ref[...], preferred_element_type=jnp.float32) * scale
            scores = jnp.where(allowed, scores, MASKED)
            top = jnp.max(scores, axis=1, keepdims=True)
            weights = jnp.exp(scores - top)
            inv = 1.0 / jnp.sum(weights, axis=1, keepdims=True)
            probs = (weights * inv).astype(jnp.bfloat16)
            ctx[:, pl.ds(h * head_size, head_size)] = jnp.dot(
                probs, v_ref[...], preferred_element_type=jnp.float32).astype(ctx.dtype)
        part[c] = jnp.dot(ctx[...], w_ref[...], preferred_element_type=jnp.float32).astype(
            part.dtype)
        slice_own(c).start()
        for k in range(1, ntp):
            slice_out(c, k).start()

    do_chunk(0)
    a2a.second()

    def rest(c, carry):
        do_chunk(c)
        return carry

    lax.fori_loop(1, chunks, rest, 0)
    a2a.arrived()

    def drain(c, carry):
        for k in range(1, ntp):
            slice_in(c, k).wait_recv()
            slice_out(c, k).wait_send()
        slice_own(c).wait()
        return carry

    lax.fori_loop(0, chunks, drain, 0)
    a2a.finish()


def attend_and_scatter(query, fresh, held_len, w_out, share, na, nb, ntp, head_size, chunk=128):
    rows, qcols = query.shape
    capacity = fresh.shape[0]
    cols = w_out.shape[1] // ntp
    _, block, width = share.shape
    share4 = share.reshape(na, nb, block, width)
    keys_t = fresh[:, :head_size].T
    values = fresh[:, head_size:]
    lens = jnp.reshape(held_len, (1,)).astype(jnp.int32)
    vmem = pl.BlockSpec(memory_space=pltpu.VMEM)
    rs, new = pl.pallas_call(
        functools.partial(_tail_kernel, na, nb, ntp, head_size ** (-0.5), chunk),
        out_shape=(
            jax.ShapeDtypeStruct((ntp, rows, cols), jnp.bfloat16),
            jax.ShapeDtypeStruct(share4.shape, share.dtype),
        ),
        in_specs=[pl.BlockSpec(memory_space=pltpu.SMEM), vmem, vmem, vmem, vmem,
                  pl.BlockSpec(memory_space=pl.ANY)],
        out_specs=(pl.BlockSpec(memory_space=pl.ANY), pl.BlockSpec(memory_space=pl.ANY)),
        scratch_shapes=[
            pltpu.VMEM((chunk, qcols), jnp.bfloat16),
            pltpu.VMEM((rows // chunk, chunk, w_out.shape[1]), jnp.bfloat16),
            pltpu.SemaphoreType.DMA((rows // chunk, ntp)),
            pltpu.SemaphoreType.DMA((rows // chunk, ntp)),
            pltpu.SemaphoreType.DMA((rows // chunk,)),
        ] + _seq_scratch(na, nb, block, width, share.dtype),
        compiler_params=pltpu.CompilerParams(collective_id=1, has_side_effects=True),
    )(lens, query, keys_t, values, w_out, share4)
    return rs, new.reshape(share.shape)


def body(
    tokens,
    norm_gain,
    w_query,
    w_keyval,
    w_out,
    span_lens,
    cached_lens,
    old_table,
    new_table,
    old_cache,
):
    groups = lax.axis_size("seq")
    tp_count = lax.axis_size("tp")
    tp_index = lax.axis_index("tp")
    holders = old_table[0]
    held_len = cached_lens[0]
    span_len = span_lens[0]
    tok_rows, tok_cols = tokens.shape
    share = old_cache.shape[1]
    width = old_cache.shape[2]
    block_rows = share * tp_count
    capacity = groups * block_rows

    inner = min(groups, 8)
    outer = groups // inner
    tok_all, cache_all = gather_inputs(tokens, old_cache, outer, inner, tp_count)
    cache_all = cache_all.reshape(groups, tp_count, share, width)
    full_rows = tok_all
    normed = normalize(full_rows, norm_gain)
    query = jnp.dot(normed, w_query, preferred_element_type=jnp.float32).astype(jnp.bfloat16)
    keyval = jnp.dot(normed, w_keyval, preferred_element_type=jnp.float32).astype(jnp.bfloat16)

    cached = jnp.take(cache_all, holders, axis=0).reshape(capacity, width)
    shifted = lax.dynamic_update_slice(
        jnp.zeros((capacity, width), jnp.bfloat16), keyval, (held_len, jnp.int32(0))
    )
    positions = lax.broadcasted_iota(jnp.int32, (capacity, 1), 0)
    fresh = jnp.where(
        positions < held_len,
        cached,
        jnp.where(positions < held_len + span_len, shifted, jnp.zeros_like(shifted)),
    )
    fresh_share = lax.dynamic_slice_in_dim(
        fresh.reshape(groups, block_rows, width), tp_index * share, share, 1
    )
    targets = new_table[0]
    device_ids = lax.broadcasted_iota(jnp.int32, (groups, groups), 0)
    block_ids = lax.broadcasted_iota(jnp.int32, (groups, groups), 1)
    matches = targets[None, :] == device_ids
    sources = jnp.sum(jnp.where(matches, block_ids, 0), axis=1)
    sorted_share = jnp.take(fresh_share, sources, axis=0)
    head_size = width // 2
    summed, new_cache = attend_and_scatter(
        query, fresh, held_len, w_out, sorted_share, outer, inner, tp_count, head_size
    )
    row_pos = lax.broadcasted_iota(jnp.int32, (tok_rows, 1), 0)
    summed = summed.astype(jnp.float32)
    total = tokens.astype(jnp.float32) + jnp.sum(summed, axis=0)
    mixed = jnp.where(row_pos < span_len, total, jnp.zeros_like(total)).astype(jnp.bfloat16)
    return (mixed, new_cache)


def solution(mesh):
    in_specs = (
        P("seq", "tp"),
        P(),
        P(None, "tp"),
        P(),
        P("tp", None),
        P("seq"),
        P("seq"),
        P("seq", None),
        P("seq", None),
        P("seq", "tp", None),
    )
    out_specs = (P("seq", "tp"), P("seq", "tp", None))
    return jax.shard_map(body, mesh=mesh, in_specs=in_specs, out_specs=out_specs, check_vma=False)
```

```python
import functools

import jax
import jax.numpy as jnp
from jax import lax
from jax.experimental import pallas as pl
from jax.experimental.pallas import tpu as pltpu
from jax.sharding import PartitionSpec as P

EPSILON = 1e-05
MASKED = -1e30


def normalize(rows, norm_gain):
    values = rows.astype(jnp.float32)
    average = jnp.mean(values, axis=1, keepdims=True)
    centred = values - average
    spread = jnp.mean(centred * centred, axis=1, keepdims=True)
    return (centred * lax.rsqrt(spread + EPSILON) * norm_gain).astype(jnp.bfloat16)


MESH = pl.DeviceIdType.MESH


def _remote(src, dst, send, recv, dev):
    return pltpu.make_async_remote_copy(
        src_ref=src, dst_ref=dst, send_sem=send, recv_sem=recv, device_id=dev, device_id_type=MESH
    )


def _greet(na, nb, s, t, *tp_peers):
    barrier = pltpu.get_barrier_semaphore()
    a = s // nb
    b = s % nb

    def one_b(k, carry):
        pl.semaphore_signal(barrier, inc=1, device_id={"seq": a * nb + lax.rem(b + k, nb), "tp": t},
                            device_id_type=MESH)
        return carry

    def one_a(k, carry):
        pl.semaphore_signal(barrier, inc=1, device_id={"seq": lax.rem(a + k, na) * nb + b, "tp": t},
                            device_id_type=MESH)
        return carry

    lax.fori_loop(1, nb, one_b, 0)
    lax.fori_loop(1, na, one_a, 0)
    for p in tp_peers:
        pl.semaphore_signal(barrier, inc=1, device_id={"seq": s, "tp": p}, device_id_type=MESH)
    pl.semaphore_wait(barrier, na + nb - 2 + len(tp_peers))


class SeqAllToAll:
    def __init__(self, na, nb, s, t, src, stage, dst, sems):
        self.na, self.nb, self.t, self.src, self.stage, self.dst = na, nb, t, src, stage, dst
        self.a = s // nb
        self.b = s % nb
        self.s1send, self.s1recv, self.s2send, self.s2recv, self.local = sems

    def _dev(self, a, b):
        return {"seq": a * self.nb + b, "tp": self.t}

    def _out1(self, k):
        peer = lax.rem(self.b + k, self.nb)
        return _remote(self.src.at[:, peer], self.stage.at[self.b], self.s1send.at[k],
                       self.s1recv.at[k], self._dev(self.a, peer))

    def _in1(self, k):
        sender = lax.rem(self.b + self.nb - k, self.nb)
        return _remote(self.src.at[:, self.b], self.stage.at[sender], self.s1send.at[k],
                       self.s1recv.at[k], self._dev(self.a, sender))

    def _out2(self, k):
        peer = lax.rem(self.a + k, self.na)
        return _remote(self.stage.at[:, peer], self.dst(self.a), self.s2send.at[k],
                       self.s2recv.at[k], self._dev(peer, self.b))

    def _in2(self, k):
        sender = lax.rem(self.a + self.na - k, self.na)
        return _remote(self.stage.at[:, self.a], self.dst(sender), self.s2send.at[k],
                       self.s2recv.at[k], self._dev(sender, self.b))

    def first(self):
        self.own1 = pltpu.make_async_copy(self.src.at[:, self.b], self.stage.at[self.b],
                                          self.local.at[0])
        self.own1.start()
        _loop(self.nb, lambda k: self._out1(k).start())

    def second(self):
        _loop(self.nb, lambda k: self._in1(k).wait_recv())
        self.own1.wait()
        self.own2 = pltpu.make_async_copy(self.stage.at[:, self.a], self.dst(self.a),
                                          self.local.at[1])
        self.own2.start()
        _loop(self.na, lambda k: self._out2(k).start())

    def arrived(self):
        _loop(self.na, lambda k: self._in2(k).wait_recv())
        self.own2.wait()

    def finish(self):
        _loop(self.nb, lambda k: self._out1(k).wait_send())
        _loop(self.na, lambda k: self._out2(k).wait_send())


def _seq_scratch(na, nb, share, width, dtype):
    return [
        pltpu.VMEM((nb, na, share, width), dtype),
        pltpu.SemaphoreType.DMA((nb,)),
        pltpu.SemaphoreType.DMA((nb,)),
        pltpu.SemaphoreType.DMA((na,)),
        pltpu.SemaphoreType.DMA((na,)),
        pltpu.SemaphoreType.DMA((2,)),
    ]


def _loop(n, fn):
    def step(k, carry):
        fn(k)
        return carry

    lax.fori_loop(1, n, step, 0)


def _in_kernel(na, nb, ntp, tok_ref, cache_ref, tok_out, cache_out, tsend, trecv, csend, crecv,
               lsem, stage, s1send, s1recv, s2send, s2recv, slocal):
    s = lax.axis_index("seq")
    t = lax.axis_index("tp")
    right = lax.rem(t + 1, ntp)
    left = lax.rem(t + ntp - 1, ntp)
    across = lax.rem(t + 2, ntp)
    rdev = {"seq": s, "tp": right}
    ldev = {"seq": s, "tp": left}
    rows, cols = tok_ref.shape
    half = rows // 2
    blocks = na * nb // 2
    _greet(na, nb, s, t, left, right)

    def tok_cols(p):
        return pl.ds(p * cols, cols)

    a2a = SeqAllToAll(na, nb, s, t, cache_ref, stage, lambda a_src: cache_out.at[a_src, :, t],
                      (s1send, s1recv, s2send, s2recv, slocal))
    a2a.first()

    own_tok = pltpu.make_async_copy(tok_ref, tok_out.at[:, tok_cols(t)], lsem.at[0])
    own_tok.start()
    tok_r = _remote(tok_ref, tok_out.at[:, tok_cols(t)], tsend.at[0], trecv.at[0], rdev)
    tok_l = _remote(tok_ref, tok_out.at[:, tok_cols(t)], tsend.at[1], trecv.at[1], ldev)
    tok_r.start()
    tok_l.start()

    a2a.second()

    _remote(tok_ref, tok_out.at[:, tok_cols(left)], tsend.at[0], trecv.at[0], ldev).wait_recv()
    fwd_r = _remote(tok_out.at[pl.ds(0, half), tok_cols(left)],
                    tok_out.at[pl.ds(0, half), tok_cols(left)], tsend.at[2], trecv.at[2], rdev)
    fwd_r.start()
    _remote(tok_ref, tok_out.at[:, tok_cols(right)], tsend.at[1], trecv.at[1], rdev).wait_recv()
    fwd_l = _remote(tok_out.at[pl.ds(half, half), tok_cols(right)],
                    tok_out.at[pl.ds(half, half), tok_cols(right)], tsend.at[3], trecv.at[3], ldev)
    fwd_l.start()

    a2a.arrived()
    flat = cache_out.reshape(na * nb, ntp, *cache_out.shape[3:])
    mine = flat.at[:, t]
    cache_r = _remote(mine, mine, csend.at[0], crecv.at[0], rdev)
    cache_l = _remote(mine, mine, csend.at[1], crecv.at[1], ldev)
    cache_r.start()
    cache_l.start()
    _remote(mine, flat.at[:, left], csend.at[0], crecv.at[0], ldev).wait_recv()
    cfwd_r = _remote(flat.at[pl.ds(0, blocks), left], flat.at[pl.ds(0, blocks), left],
                     csend.at[2], crecv.at[2], rdev)
    cfwd_r.start()
    _remote(mine, flat.at[:, right], csend.at[1], crecv.at[1], rdev).wait_recv()
    cfwd_l = _remote(flat.at[pl.ds(blocks, blocks), right], flat.at[pl.ds(blocks, blocks), right],
                     csend.at[3], crecv.at[3], ldev)
    cfwd_l.start()

    _remote(tok_ref.at[pl.ds(0, half)], tok_out.at[pl.ds(0, half), tok_cols(across)],
            tsend.at[2], trecv.at[2], ldev).wait_recv()
    _remote(tok_ref.at[pl.ds(half, half)], tok_out.at[pl.ds(half, half), tok_cols(across)],
            tsend.at[3], trecv.at[3], rdev).wait_recv()
    _remote(flat.at[pl.ds(0, blocks), t], flat.at[pl.ds(0, blocks), across],
            csend.at[2], crecv.at[2], ldev).wait_recv()
    _remote(flat.at[pl.ds(blocks, blocks), t], flat.at[pl.ds(blocks, blocks), across],
            csend.at[3], crecv.at[3], rdev).wait_recv()
    for c in (tok_r, tok_l, fwd_r, fwd_l, cache_r, cache_l, cfwd_r, cfwd_l):
        c.wait_send()
    a2a.finish()
    own_tok.wait()


def gather_inputs(tokens, old_cache, na, nb, ntp):
    rows, cols = tokens.shape
    _, share, width = old_cache.shape
    cache4 = old_cache.reshape(na, nb, share, width)
    return pl.pallas_call(
        functools.partial(_in_kernel, na, nb, ntp),
        out_shape=(
            jax.ShapeDtypeStruct((rows, ntp * cols), tokens.dtype),
            jax.ShapeDtypeStruct((na, nb, ntp, share, width), old_cache.dtype),
        ),
        in_specs=[pl.BlockSpec(memory_space=pl.ANY)] * 2,
        out_specs=(pl.BlockSpec(memory_space=pl.ANY), pl.BlockSpec(memory_space=pl.ANY)),
        scratch_shapes=[
            pltpu.SemaphoreType.DMA((4,)),
            pltpu.SemaphoreType.DMA((4,)),
            pltpu.SemaphoreType.DMA((4,)),
            pltpu.SemaphoreType.DMA((4,)),
            pltpu.SemaphoreType.DMA((2,)),
        ] + _seq_scratch(na, nb, share, width, old_cache.dtype),
        compiler_params=pltpu.CompilerParams(collective_id=0, has_side_effects=True),
    )(tokens, cache4)


def _out_kernel(na, nb, ntp, part_ref, share_ref, rs_out, new_out, stage_rs, rsend, rrecv, lsem,
                stage, s1send, s1recv, s2send, s2recv, slocal):
    s = lax.axis_index("seq")
    t = lax.axis_index("tp")
    right = lax.rem(t + 1, ntp)
    left = lax.rem(t + ntp - 1, ntp)
    across = lax.rem(t + 2, ntp)
    rdev = {"seq": s, "tp": right}
    ldev = {"seq": s, "tp": left}
    half = part_ref.shape[1] // 2
    _greet(na, nb, s, t, left, right)

    a2a = SeqAllToAll(na, nb, s, t, share_ref, stage, lambda a_src: new_out.at[a_src],
                      (s1send, s1recv, s2send, s2recv, slocal))
    a2a.first()

    own_part = pltpu.make_async_copy(part_ref.at[t], rs_out.at[t], lsem.at[0])
    own_part.start()
    to_r = _remote(part_ref.at[right], rs_out.at[t], rsend.at[0], rrecv.at[0], rdev)
    to_l = _remote(part_ref.at[left], rs_out.at[t], rsend.at[1], rrecv.at[1], ldev)
    via_r = _remote(part_ref.at[across, pl.ds(0, half)], stage_rs.at[0], rsend.at[2], rrecv.at[2],
                    rdev)
    via_l = _remote(part_ref.at[across, pl.ds(half, half)], stage_rs.at[1], rsend.at[3],
                    rrecv.at[3], ldev)
    for c in (to_r, to_l, via_r, via_l):
        c.start()

    a2a.second()

    _remote(part_ref.at[across, pl.ds(0, half)], stage_rs.at[0], rsend.at[2], rrecv.at[2],
            ldev).wait_recv()
    fwd_r = _remote(stage_rs.at[0], rs_out.at[left, pl.ds(0, half)], rsend.at[4], rrecv.at[4],
                    rdev)
    fwd_r.start()
    _remote(part_ref.at[across, pl.ds(half, half)], stage_rs.at[1], rsend.at[3], rrecv.at[3],
            rdev).wait_recv()
    fwd_l = _remote(stage_rs.at[1], rs_out.at[right, pl.ds(half, half)], rsend.at[5],
                    rrecv.at[5], ldev)
    fwd_l.start()

    a2a.arrived()
    _remote(part_ref.at[t], rs_out.at[left], rsend.at[0], rrecv.at[0], ldev).wait_recv()
    _remote(part_ref.at[t], rs_out.at[right], rsend.at[1], rrecv.at[1], rdev).wait_recv()
    _remote(stage_rs.at[0], rs_out.at[across, pl.ds(0, half)], rsend.at[4], rrecv.at[4],
            ldev).wait_recv()
    _remote(stage_rs.at[1], rs_out.at[across, pl.ds(half, half)], rsend.at[5], rrecv.at[5],
            rdev).wait_recv()
    for c in (to_r, to_l, via_r, via_l, fwd_r, fwd_l):
        c.wait_send()
    a2a.finish()
    own_part.wait()


def scatter_outputs(partial, share, na, nb, ntp):
    _, rows, cols = partial.shape
    _, block, width = share.shape
    share4 = share.reshape(na, nb, block, width)
    rs, new = pl.pallas_call(
        functools.partial(_out_kernel, na, nb, ntp),
        out_shape=(
            jax.ShapeDtypeStruct(partial.shape, partial.dtype),
            jax.ShapeDtypeStruct(share4.shape, share.dtype),
        ),
        in_specs=[pl.BlockSpec(memory_space=pl.ANY)] * 2,
        out_specs=(pl.BlockSpec(memory_space=pl.ANY), pl.BlockSpec(memory_space=pl.ANY)),
        scratch_shapes=[
            pltpu.VMEM((2, rows // 2, cols), partial.dtype),
            pltpu.SemaphoreType.DMA((6,)),
            pltpu.SemaphoreType.DMA((6,)),
            pltpu.SemaphoreType.DMA((1,)),
        ] + _seq_scratch(na, nb, block, width, share.dtype),
        compiler_params=pltpu.CompilerParams(collective_id=1, has_side_effects=True),
    )(partial, share4)
    return rs, new.reshape(share.shape)


def _attend_kernel(scale, lens_ref, q_ref, k_ref, v_ref, o_ref):
    chunk = q_ref.shape[0]
    capacity = k_ref.shape[0]
    held = lens_ref[0]
    first = pl.program_id(1) * chunk
    scores = lax.dot_general(
        q_ref[...], k_ref[...], (((1,), (1,)), ((), ())), preferred_element_type=jnp.float32
    ) * scale
    row_pos = first + lax.broadcasted_iota(jnp.int32, (chunk, capacity), 0)
    key_pos = lax.broadcasted_iota(jnp.int32, (chunk, capacity), 1)
    scores = jnp.where(key_pos <= held + row_pos, scores, MASKED)
    top = jnp.max(scores, axis=1, keepdims=True)
    weights = jnp.exp(scores - top)
    probs = (weights / jnp.sum(weights, axis=1, keepdims=True)).astype(jnp.bfloat16)
    o_ref[...] = jnp.dot(probs, v_ref[...], preferred_element_type=jnp.float32).astype(o_ref.dtype)


def attend(query, fresh, held_len, head_size, chunk=128):
    rows, qcols = query.shape
    capacity = fresh.shape[0]
    heads = qcols // head_size
    lens = jnp.reshape(held_len, (1,)).astype(jnp.int32)
    return pl.pallas_call(
        functools.partial(_attend_kernel, head_size ** (-0.5)),
        out_shape=jax.ShapeDtypeStruct((rows, qcols), jnp.bfloat16),
        grid_spec=pltpu.PrefetchScalarGridSpec(
            num_scalar_prefetch=1,
            grid=(heads, rows // chunk),
            in_specs=[
                pl.BlockSpec((chunk, head_size), lambda h, r, lens: (r, h)),
                pl.BlockSpec((capacity, head_size), lambda h, r, lens: (0, 0)),
                pl.BlockSpec((capacity, head_size), lambda h, r, lens: (0, 1)),
            ],
            out_specs=pl.BlockSpec((chunk, head_size), lambda h, r, lens: (r, h)),
        ),
        cost_estimate=pl.CostEstimate(
            flops=4 * rows * capacity * qcols,
            transcendentals=rows * capacity * heads,
            bytes_accessed=2 * (2 * rows * qcols + 2 * capacity * head_size),
        ),
    )(lens, query, fresh, fresh)


def _prep_kernel(ntp, lens_ref, holders_ref, sources_ref, cache_ref, kv_ref, fresh, kt, share_buf,
                 fresh32):
    t = lax.axis_index("tp")
    capacity, width = fresh.shape
    head_size = width // 2
    block_rows = cache_ref.shape[1]
    share = block_rows // ntp
    held = lens_ref[0]
    span = lens_ref[1]

    def place(b, carry):
        fresh32[pl.ds(pl.multiple_of(b * block_rows, block_rows), block_rows), :] = (
            cache_ref[holders_ref[b]].astype(jnp.float32))
        return carry

    lax.fori_loop(0, capacity // block_rows, place, 0)
    padded = jnp.concatenate(
        [kv_ref[...].astype(jnp.float32),
         jnp.zeros((capacity - kv_ref.shape[0], width), jnp.float32)], axis=0)
    shifted = pltpu.roll(padded, held, 0)
    positions = lax.broadcasted_iota(jnp.int32, (capacity, width), 0)
    full = jnp.where(positions < held, fresh32[...],
                     jnp.where(positions < held + span, shifted, 0.0))
    fresh32[...] = full
    fresh[...] = full.astype(fresh.dtype)
    kt[...] = fresh[:, pl.ds(0, head_size)].T

    def pick(d, carry):
        start = pl.multiple_of(sources_ref[d] * block_rows + t * share, share)
        share_buf[d] = fresh32[pl.ds(start, share), :].astype(share_buf.dtype)
        return carry

    lax.fori_loop(0, share_buf.shape[0], pick, 0)


def prepare(cache, keyval, lens, holders, sources, ntp):
    blocks, block_rows, width = cache.shape
    capacity = blocks * block_rows
    vmem = pl.BlockSpec(memory_space=pltpu.VMEM)
    smem = pl.BlockSpec(memory_space=pltpu.SMEM)
    return pl.pallas_call(
        functools.partial(_prep_kernel, ntp),
        out_shape=(
            jax.ShapeDtypeStruct((capacity, width), cache.dtype),
            jax.ShapeDtypeStruct((width // 2, capacity), cache.dtype),
            jax.ShapeDtypeStruct((blocks, block_rows // ntp, width), cache.dtype),
        ),
        in_specs=[smem, smem, smem, vmem, vmem],
        out_specs=(vmem, vmem, vmem),
        scratch_shapes=[pltpu.VMEM((capacity, width), jnp.float32)],
    )(lens, holders, sources, cache, keyval)


def _tail_kernel(na, nb, ntp, scale, chunk, lens_ref, q_ref, fresh, kt, share_buf, w_ref,
                 rs_out, new_out, ctx, part, psend, precv, plocal, stage, s1send, s1recv, s2send,
                 s2recv, slocal):
    s = lax.axis_index("seq")
    t = lax.axis_index("tp")
    rows, qcols = q_ref.shape
    capacity, width = fresh.shape
    head_size = width // 2
    share = share_buf.shape[1]
    heads = qcols // head_size
    cols = w_ref.shape[1] // ntp
    chunks = rows // chunk
    held = lens_ref[0]

    _greet(na, nb, s, t, *[lax.rem(t + k, ntp) for k in range(1, ntp)])
    sorted4 = share_buf.reshape(na, nb, share, width)
    a2a = SeqAllToAll(na, nb, s, t, sorted4, stage, lambda a_src: new_out.at[a_src],
                      (s1send, s1recv, s2send, s2recv, slocal))
    a2a.first()

    def slice_out(c, k):
        peer = lax.rem(t + k, ntp)
        return _remote(part.at[c, :, pl.ds(pl.multiple_of(peer * cols, cols), cols)],
                       rs_out.at[t, pl.ds(pl.multiple_of(c * chunk, chunk), chunk)],
                       psend.at[c, k], precv.at[c, k], {"seq": s, "tp": peer})

    def slice_in(c, k):
        sender = lax.rem(t + ntp - k, ntp)
        return _remote(part.at[c, :, pl.ds(0, cols)],
                       rs_out.at[sender, pl.ds(pl.multiple_of(c * chunk, chunk), chunk)],
                       psend.at[c, k], precv.at[c, k], {"seq": s, "tp": sender})

    def slice_own(c):
        return pltpu.make_async_copy(
            part.at[c, :, pl.ds(pl.multiple_of(t * cols, cols), cols)],
            rs_out.at[t, pl.ds(pl.multiple_of(c * chunk, chunk), chunk)], plocal.at[c])

    def do_chunk(c):
        first = pl.multiple_of(c * chunk, chunk)
        row_pos = first + lax.broadcasted_iota(jnp.int32, (chunk, capacity), 0)
        key_pos = lax.broadcasted_iota(jnp.int32, (chunk, capacity), 1)
        allowed = key_pos <= held + row_pos
        for h in range(heads):
            q = q_ref[pl.ds(first, chunk), pl.ds(h * head_size, head_size)]
            scores = jnp.dot(q, kt[...], preferred_element_type=jnp.float32) * scale
            scores = jnp.where(allowed, scores, MASKED)
            top = jnp.max(scores, axis=1, keepdims=True)
            weights = jnp.exp(scores - top)
            inv = 1.0 / jnp.sum(weights, axis=1, keepdims=True)
            probs = (weights * inv).astype(jnp.bfloat16)
            ctx[:, pl.ds(h * head_size, head_size)] = jnp.dot(
                probs, fresh[:, pl.ds(head_size, head_size)],
                preferred_element_type=jnp.float32).astype(ctx.dtype)
        part[c] = jnp.dot(ctx[...], w_ref[...], preferred_element_type=jnp.float32).astype(
            part.dtype)
        slice_own(c).start()
        for k in range(1, ntp):
            slice_out(c, k).start()

    do_chunk(0)
    a2a.second()

    def rest(c, carry):
        do_chunk(c)
        return carry

    lax.fori_loop(1, chunks, rest, 0)
    a2a.arrived()

    def drain(c, carry):
        for k in range(1, ntp):
            slice_in(c, k).wait_recv()
            slice_out(c, k).wait_send()
        slice_own(c).wait()
        return carry

    lax.fori_loop(0, chunks, drain, 0)
    a2a.finish()


def attend_and_scatter(query, cache, keyval, lens, holders, sources, w_out, na, nb, ntp,
                       chunk=128):
    rows, qcols = query.shape
    blocks, block_rows, width = cache.shape
    share = block_rows // ntp
    cols = w_out.shape[1] // ntp
    fresh, keys_t, sorted_share = prepare(cache, keyval, lens, holders, sources, ntp)
    vmem = pl.BlockSpec(memory_space=pltpu.VMEM)
    smem = pl.BlockSpec(memory_space=pltpu.SMEM)
    rs, new = pl.pallas_call(
        functools.partial(_tail_kernel, na, nb, ntp, (width // 2) ** (-0.5), chunk),
        out_shape=(
            jax.ShapeDtypeStruct((ntp, rows, cols), jnp.bfloat16),
            jax.ShapeDtypeStruct((na, nb, share, width), cache.dtype),
        ),
        in_specs=[smem, vmem, vmem, vmem, vmem, vmem],
        out_specs=(pl.BlockSpec(memory_space=pl.ANY), pl.BlockSpec(memory_space=pl.ANY)),
        scratch_shapes=[
            pltpu.VMEM((chunk, qcols), jnp.bfloat16),
            pltpu.VMEM((rows // chunk, chunk, w_out.shape[1]), jnp.bfloat16),
            pltpu.SemaphoreType.DMA((rows // chunk, ntp)),
            pltpu.SemaphoreType.DMA((rows // chunk, ntp)),
            pltpu.SemaphoreType.DMA((rows // chunk,)),
        ] + _seq_scratch(na, nb, share, width, cache.dtype),
        compiler_params=pltpu.CompilerParams(collective_id=1, has_side_effects=True),
    )(lens, query, fresh, keys_t, sorted_share, w_out)
    return rs, new.reshape(blocks, share, width)


def body(
    tokens,
    norm_gain,
    w_query,
    w_keyval,
    w_out,
    span_lens,
    cached_lens,
    old_table,
    new_table,
    old_cache,
):
    groups = lax.axis_size("seq")
    tp_count = lax.axis_size("tp")
    tp_index = lax.axis_index("tp")
    holders = old_table[0]
    held_len = cached_lens[0]
    span_len = span_lens[0]
    tok_rows, tok_cols = tokens.shape
    share = old_cache.shape[1]
    width = old_cache.shape[2]
    block_rows = share * tp_count
    capacity = groups * block_rows

    inner = min(groups, 8)
    outer = groups // inner
    tok_all, cache_all = gather_inputs(tokens, old_cache, outer, inner, tp_count)
    cache_all = cache_all.reshape(groups, tp_count, share, width)
    full_rows = tok_all
    normed = normalize(full_rows, norm_gain)
    query = jnp.dot(normed, w_query, preferred_element_type=jnp.float32).astype(jnp.bfloat16)
    keyval = jnp.dot(normed, w_keyval, preferred_element_type=jnp.float32).astype(jnp.bfloat16)

    targets = new_table[0]
    device_ids = lax.broadcasted_iota(jnp.int32, (groups, groups), 0)
    block_ids = lax.broadcasted_iota(jnp.int32, (groups, groups), 1)
    matches = targets[None, :] == device_ids
    sources = jnp.sum(jnp.where(matches, block_ids, 0), axis=1)
    lens = jnp.stack([held_len, span_len]).astype(jnp.int32)
    summed, new_cache = attend_and_scatter(
        query, cache_all.reshape(groups, block_rows, width), keyval, lens, holders, sources,
        w_out, outer, inner, tp_count
    )
    row_pos = lax.broadcasted_iota(jnp.int32, (tok_rows, 1), 0)
    summed = summed.astype(jnp.float32)
    total = tokens.astype(jnp.float32) + jnp.sum(summed, axis=0)
    mixed = jnp.where(row_pos < span_len, total, jnp.zeros_like(total)).astype(jnp.bfloat16)
    return (mixed, new_cache)


def solution(mesh):
    in_specs = (
        P("seq", "tp"),
        P(),
        P(None, "tp"),
        P(),
        P("tp", None),
        P("seq"),
        P("seq"),
        P("seq", None),
        P("seq", None),
        P("seq", "tp", None),
    )
    out_specs = (P("seq", "tp"), P("seq", "tp", None))
    return jax.shard_map(body, mesh=mesh, in_specs=in_specs, out_specs=out_specs, check_vma=False)
```

```python
import functools

import jax
import jax.numpy as jnp
from jax import lax
from jax.experimental import pallas as pl
from jax.experimental.pallas import tpu as pltpu
from jax.sharding import PartitionSpec as P

EPSILON = 1e-05
MASKED = -1e30


def normalize(rows, norm_gain):
    values = rows.astype(jnp.float32)
    average = jnp.mean(values, axis=1, keepdims=True)
    centred = values - average
    spread = jnp.mean(centred * centred, axis=1, keepdims=True)
    return (centred * lax.rsqrt(spread + EPSILON) * norm_gain).astype(jnp.bfloat16)


MESH = pl.DeviceIdType.MESH


def _remote(src, dst, send, recv, dev):
    return pltpu.make_async_remote_copy(
        src_ref=src, dst_ref=dst, send_sem=send, recv_sem=recv, device_id=dev, device_id_type=MESH
    )


def _greet(na, nb, s, t, *tp_peers):
    barrier = pltpu.get_barrier_semaphore()
    a = s // nb
    b = s % nb

    def one_b(k, carry):
        pl.semaphore_signal(barrier, inc=1, device_id={"seq": a * nb + lax.rem(b + k, nb), "tp": t},
                            device_id_type=MESH)
        return carry

    def one_a(k, carry):
        pl.semaphore_signal(barrier, inc=1, device_id={"seq": lax.rem(a + k, na) * nb + b, "tp": t},
                            device_id_type=MESH)
        return carry

    lax.fori_loop(1, nb, one_b, 0)
    lax.fori_loop(1, na, one_a, 0)
    for p in tp_peers:
        pl.semaphore_signal(barrier, inc=1, device_id={"seq": s, "tp": p}, device_id_type=MESH)
    pl.semaphore_wait(barrier, na + nb - 2 + len(tp_peers))


class SeqAllToAll:
    def __init__(self, na, nb, s, t, src, stage, dst, sems):
        self.na, self.nb, self.t, self.src, self.stage, self.dst = na, nb, t, src, stage, dst
        self.a = s // nb
        self.b = s % nb
        self.s1send, self.s1recv, self.s2send, self.s2recv, self.local = sems

    def _dev(self, a, b):
        return {"seq": a * self.nb + b, "tp": self.t}

    def _out1(self, k):
        peer = lax.rem(self.b + k, self.nb)
        return _remote(self.src.at[:, peer], self.stage.at[self.b], self.s1send.at[k],
                       self.s1recv.at[k], self._dev(self.a, peer))

    def _in1(self, k):
        sender = lax.rem(self.b + self.nb - k, self.nb)
        return _remote(self.src.at[:, self.b], self.stage.at[sender], self.s1send.at[k],
                       self.s1recv.at[k], self._dev(self.a, sender))

    def _out2(self, k):
        peer = lax.rem(self.a + k, self.na)
        return _remote(self.stage.at[:, peer], self.dst(self.a), self.s2send.at[k],
                       self.s2recv.at[k], self._dev(peer, self.b))

    def _in2(self, k):
        sender = lax.rem(self.a + self.na - k, self.na)
        return _remote(self.stage.at[:, self.a], self.dst(sender), self.s2send.at[k],
                       self.s2recv.at[k], self._dev(sender, self.b))

    def first(self):
        self.own1 = pltpu.make_async_copy(self.src.at[:, self.b], self.stage.at[self.b],
                                          self.local.at[0])
        self.own1.start()
        _loop(self.nb, lambda k: self._out1(k).start())

    def second(self):
        _loop(self.nb, lambda k: self._in1(k).wait_recv())
        self.own1.wait()
        self.own2 = pltpu.make_async_copy(self.stage.at[:, self.a], self.dst(self.a),
                                          self.local.at[1])
        self.own2.start()
        _loop(self.na, lambda k: self._out2(k).start())

    def arrived(self):
        _loop(self.na, lambda k: self._in2(k).wait_recv())
        self.own2.wait()

    def finish(self):
        _loop(self.nb, lambda k: self._out1(k).wait_send())
        _loop(self.na, lambda k: self._out2(k).wait_send())


def _seq_scratch(na, nb, share, width, dtype):
    return [
        pltpu.VMEM((nb, na, share, width), dtype),
        pltpu.SemaphoreType.DMA((nb,)),
        pltpu.SemaphoreType.DMA((nb,)),
        pltpu.SemaphoreType.DMA((na,)),
        pltpu.SemaphoreType.DMA((na,)),
        pltpu.SemaphoreType.DMA((2,)),
    ]


def _loop(n, fn):
    def step(k, carry):
        fn(k)
        return carry

    lax.fori_loop(1, n, step, 0)


def _in_kernel(na, nb, ntp, tok_ref, cache_ref, tok_out, cache_out, tsend, trecv, csend, crecv,
               lsem, stage, s1send, s1recv, s2send, s2recv, slocal):
    s = lax.axis_index("seq")
    t = lax.axis_index("tp")
    right = lax.rem(t + 1, ntp)
    left = lax.rem(t + ntp - 1, ntp)
    across = lax.rem(t + 2, ntp)
    rdev = {"seq": s, "tp": right}
    ldev = {"seq": s, "tp": left}
    rows, cols = tok_ref.shape
    half = rows // 2
    blocks = na * nb // 2
    _greet(na, nb, s, t, left, right)

    def tok_cols(p):
        return pl.ds(p * cols, cols)

    a2a = SeqAllToAll(na, nb, s, t, cache_ref, stage, lambda a_src: cache_out.at[a_src, :, t],
                      (s1send, s1recv, s2send, s2recv, slocal))
    a2a.first()

    own_tok = pltpu.make_async_copy(tok_ref, tok_out.at[:, tok_cols(t)], lsem.at[0])
    own_tok.start()
    tok_r = _remote(tok_ref, tok_out.at[:, tok_cols(t)], tsend.at[0], trecv.at[0], rdev)
    tok_l = _remote(tok_ref, tok_out.at[:, tok_cols(t)], tsend.at[1], trecv.at[1], ldev)
    tok_r.start()
    tok_l.start()

    a2a.second()

    _remote(tok_ref, tok_out.at[:, tok_cols(left)], tsend.at[0], trecv.at[0], ldev).wait_recv()
    fwd_r = _remote(tok_out.at[pl.ds(0, half), tok_cols(left)],
                    tok_out.at[pl.ds(0, half), tok_cols(left)], tsend.at[2], trecv.at[2], rdev)
    fwd_r.start()
    _remote(tok_ref, tok_out.at[:, tok_cols(right)], tsend.at[1], trecv.at[1], rdev).wait_recv()
    fwd_l = _remote(tok_out.at[pl.ds(half, half), tok_cols(right)],
                    tok_out.at[pl.ds(half, half), tok_cols(right)], tsend.at[3], trecv.at[3], ldev)
    fwd_l.start()

    a2a.arrived()
    flat = cache_out.reshape(na * nb, ntp, *cache_out.shape[3:])
    mine = flat.at[:, t]
    cache_r = _remote(mine, mine, csend.at[0], crecv.at[0], rdev)
    cache_l = _remote(mine, mine, csend.at[1], crecv.at[1], ldev)
    cache_r.start()
    cache_l.start()
    _remote(mine, flat.at[:, left], csend.at[0], crecv.at[0], ldev).wait_recv()
    cfwd_r = _remote(flat.at[pl.ds(0, blocks), left], flat.at[pl.ds(0, blocks), left],
                     csend.at[2], crecv.at[2], rdev)
    cfwd_r.start()
    _remote(mine, flat.at[:, right], csend.at[1], crecv.at[1], rdev).wait_recv()
    cfwd_l = _remote(flat.at[pl.ds(blocks, blocks), right], flat.at[pl.ds(blocks, blocks), right],
                     csend.at[3], crecv.at[3], ldev)
    cfwd_l.start()

    _remote(tok_ref.at[pl.ds(0, half)], tok_out.at[pl.ds(0, half), tok_cols(across)],
            tsend.at[2], trecv.at[2], ldev).wait_recv()
    _remote(tok_ref.at[pl.ds(half, half)], tok_out.at[pl.ds(half, half), tok_cols(across)],
            tsend.at[3], trecv.at[3], rdev).wait_recv()
    _remote(flat.at[pl.ds(0, blocks), t], flat.at[pl.ds(0, blocks), across],
            csend.at[2], crecv.at[2], ldev).wait_recv()
    _remote(flat.at[pl.ds(blocks, blocks), t], flat.at[pl.ds(blocks, blocks), across],
            csend.at[3], crecv.at[3], rdev).wait_recv()
    for c in (tok_r, tok_l, fwd_r, fwd_l, cache_r, cache_l, cfwd_r, cfwd_l):
        c.wait_send()
    a2a.finish()
    own_tok.wait()


def gather_inputs(tokens, old_cache, na, nb, ntp):
    rows, cols = tokens.shape
    _, share, width = old_cache.shape
    cache4 = old_cache.reshape(na, nb, share, width)
    return pl.pallas_call(
        functools.partial(_in_kernel, na, nb, ntp),
        out_shape=(
            jax.ShapeDtypeStruct((rows, ntp * cols), tokens.dtype),
            jax.ShapeDtypeStruct((na, nb, ntp, share, width), old_cache.dtype),
        ),
        in_specs=[pl.BlockSpec(memory_space=pl.ANY)] * 2,
        out_specs=(pl.BlockSpec(memory_space=pl.ANY), pl.BlockSpec(memory_space=pl.ANY)),
        scratch_shapes=[
            pltpu.SemaphoreType.DMA((4,)),
            pltpu.SemaphoreType.DMA((4,)),
            pltpu.SemaphoreType.DMA((4,)),
            pltpu.SemaphoreType.DMA((4,)),
            pltpu.SemaphoreType.DMA((2,)),
        ] + _seq_scratch(na, nb, share, width, old_cache.dtype),
        compiler_params=pltpu.CompilerParams(collective_id=0, has_side_effects=True),
    )(tokens, cache4)


def _out_kernel(na, nb, ntp, part_ref, share_ref, rs_out, new_out, stage_rs, rsend, rrecv, lsem,
                stage, s1send, s1recv, s2send, s2recv, slocal):
    s = lax.axis_index("seq")
    t = lax.axis_index("tp")
    right = lax.rem(t + 1, ntp)
    left = lax.rem(t + ntp - 1, ntp)
    across = lax.rem(t + 2, ntp)
    rdev = {"seq": s, "tp": right}
    ldev = {"seq": s, "tp": left}
    half = part_ref.shape[1] // 2
    _greet(na, nb, s, t, left, right)

    a2a = SeqAllToAll(na, nb, s, t, share_ref, stage, lambda a_src: new_out.at[a_src],
                      (s1send, s1recv, s2send, s2recv, slocal))
    a2a.first()

    own_part = pltpu.make_async_copy(part_ref.at[t], rs_out.at[t], lsem.at[0])
    own_part.start()
    to_r = _remote(part_ref.at[right], rs_out.at[t], rsend.at[0], rrecv.at[0], rdev)
    to_l = _remote(part_ref.at[left], rs_out.at[t], rsend.at[1], rrecv.at[1], ldev)
    via_r = _remote(part_ref.at[across, pl.ds(0, half)], stage_rs.at[0], rsend.at[2], rrecv.at[2],
                    rdev)
    via_l = _remote(part_ref.at[across, pl.ds(half, half)], stage_rs.at[1], rsend.at[3],
                    rrecv.at[3], ldev)
    for c in (to_r, to_l, via_r, via_l):
        c.start()

    a2a.second()

    _remote(part_ref.at[across, pl.ds(0, half)], stage_rs.at[0], rsend.at[2], rrecv.at[2],
            ldev).wait_recv()
    fwd_r = _remote(stage_rs.at[0], rs_out.at[left, pl.ds(0, half)], rsend.at[4], rrecv.at[4],
                    rdev)
    fwd_r.start()
    _remote(part_ref.at[across, pl.ds(half, half)], stage_rs.at[1], rsend.at[3], rrecv.at[3],
            rdev).wait_recv()
    fwd_l = _remote(stage_rs.at[1], rs_out.at[right, pl.ds(half, half)], rsend.at[5],
                    rrecv.at[5], ldev)
    fwd_l.start()

    a2a.arrived()
    _remote(part_ref.at[t], rs_out.at[left], rsend.at[0], rrecv.at[0], ldev).wait_recv()
    _remote(part_ref.at[t], rs_out.at[right], rsend.at[1], rrecv.at[1], rdev).wait_recv()
    _remote(stage_rs.at[0], rs_out.at[across, pl.ds(0, half)], rsend.at[4], rrecv.at[4],
            ldev).wait_recv()
    _remote(stage_rs.at[1], rs_out.at[across, pl.ds(half, half)], rsend.at[5], rrecv.at[5],
            rdev).wait_recv()
    for c in (to_r, to_l, via_r, via_l, fwd_r, fwd_l):
        c.wait_send()
    a2a.finish()
    own_part.wait()


def scatter_outputs(partial, share, na, nb, ntp):
    _, rows, cols = partial.shape
    _, block, width = share.shape
    share4 = share.reshape(na, nb, block, width)
    rs, new = pl.pallas_call(
        functools.partial(_out_kernel, na, nb, ntp),
        out_shape=(
            jax.ShapeDtypeStruct(partial.shape, partial.dtype),
            jax.ShapeDtypeStruct(share4.shape, share.dtype),
        ),
        in_specs=[pl.BlockSpec(memory_space=pl.ANY)] * 2,
        out_specs=(pl.BlockSpec(memory_space=pl.ANY), pl.BlockSpec(memory_space=pl.ANY)),
        scratch_shapes=[
            pltpu.VMEM((2, rows // 2, cols), partial.dtype),
            pltpu.SemaphoreType.DMA((6,)),
            pltpu.SemaphoreType.DMA((6,)),
            pltpu.SemaphoreType.DMA((1,)),
        ] + _seq_scratch(na, nb, block, width, share.dtype),
        compiler_params=pltpu.CompilerParams(collective_id=1, has_side_effects=True),
    )(partial, share4)
    return rs, new.reshape(share.shape)


def _attend_kernel(scale, lens_ref, q_ref, k_ref, v_ref, o_ref):
    chunk = q_ref.shape[0]
    capacity = k_ref.shape[0]
    held = lens_ref[0]
    first = pl.program_id(1) * chunk
    scores = lax.dot_general(
        q_ref[...], k_ref[...], (((1,), (1,)), ((), ())), preferred_element_type=jnp.float32
    ) * scale
    row_pos = first + lax.broadcasted_iota(jnp.int32, (chunk, capacity), 0)
    key_pos = lax.broadcasted_iota(jnp.int32, (chunk, capacity), 1)
    scores = jnp.where(key_pos <= held + row_pos, scores, MASKED)
    top = jnp.max(scores, axis=1, keepdims=True)
    weights = jnp.exp(scores - top)
    probs = (weights / jnp.sum(weights, axis=1, keepdims=True)).astype(jnp.bfloat16)
    o_ref[...] = jnp.dot(probs, v_ref[...], preferred_element_type=jnp.float32).astype(o_ref.dtype)


def attend(query, fresh, held_len, head_size, chunk=128):
    rows, qcols = query.shape
    capacity = fresh.shape[0]
    heads = qcols // head_size
    lens = jnp.reshape(held_len, (1,)).astype(jnp.int32)
    return pl.pallas_call(
        functools.partial(_attend_kernel, head_size ** (-0.5)),
        out_shape=jax.ShapeDtypeStruct((rows, qcols), jnp.bfloat16),
        grid_spec=pltpu.PrefetchScalarGridSpec(
            num_scalar_prefetch=1,
            grid=(heads, rows // chunk),
            in_specs=[
                pl.BlockSpec((chunk, head_size), lambda h, r, lens: (r, h)),
                pl.BlockSpec((capacity, head_size), lambda h, r, lens: (0, 0)),
                pl.BlockSpec((capacity, head_size), lambda h, r, lens: (0, 1)),
            ],
            out_specs=pl.BlockSpec((chunk, head_size), lambda h, r, lens: (r, h)),
        ),
        cost_estimate=pl.CostEstimate(
            flops=4 * rows * capacity * qcols,
            transcendentals=rows * capacity * heads,
            bytes_accessed=2 * (2 * rows * qcols + 2 * capacity * head_size),
        ),
    )(lens, query, fresh, fresh)


def _prep_kernel(ntp, lens_ref, holders_ref, sources_ref, cache_ref, kv_ref, fresh, kt, share_buf,
                 fresh32):
    t = lax.axis_index("tp")
    capacity, width = fresh.shape
    head_size = width // 2
    block_rows = cache_ref.shape[1]
    share = block_rows // ntp
    held = lens_ref[0]
    span = lens_ref[1]

    def place(b, carry):
        fresh32[pl.ds(pl.multiple_of(b * block_rows, block_rows), block_rows), :] = (
            cache_ref[holders_ref[b]].astype(jnp.float32))
        return carry

    lax.fori_loop(0, capacity // block_rows, place, 0)
    padded = jnp.concatenate(
        [kv_ref[...].astype(jnp.float32),
         jnp.zeros((capacity - kv_ref.shape[0], width), jnp.float32)], axis=0)
    shifted = pltpu.roll(padded, held, 0)
    positions = lax.broadcasted_iota(jnp.int32, (capacity, width), 0)
    full = jnp.where(positions < held, fresh32[...],
                     jnp.where(positions < held + span, shifted, 0.0))
    fresh32[...] = full
    fresh[...] = full.astype(fresh.dtype)
    kt[...] = fresh[:, pl.ds(0, head_size)].T

    def pick(d, carry):
        start = pl.multiple_of(sources_ref[d] * block_rows + t * share, share)
        share_buf[d] = fresh32[pl.ds(start, share), :].astype(share_buf.dtype)
        return carry

    lax.fori_loop(0, share_buf.shape[0], pick, 0)


def prepare(cache, keyval, lens, holders, sources, ntp):
    blocks, block_rows, width = cache.shape
    capacity = blocks * block_rows
    vmem = pl.BlockSpec(memory_space=pltpu.VMEM)
    smem = pl.BlockSpec(memory_space=pltpu.SMEM)
    return pl.pallas_call(
        functools.partial(_prep_kernel, ntp),
        out_shape=(
            jax.ShapeDtypeStruct((capacity, width), cache.dtype),
            jax.ShapeDtypeStruct((width // 2, capacity), cache.dtype),
            jax.ShapeDtypeStruct((blocks, block_rows // ntp, width), cache.dtype),
        ),
        in_specs=[smem, smem, smem, vmem, vmem],
        out_specs=(vmem, vmem, vmem),
        scratch_shapes=[pltpu.VMEM((capacity, width), jnp.float32)],
    )(lens, holders, sources, cache, keyval)


def _tail_kernel(na, nb, ntp, scale, chunk, lens_ref, q_ref, fresh, kt, share_buf, w_ref, tok_ref,
                 mixed_out, new_out, rs_out, ctx, part, psend, precv, plocal, stage, s1send, s1recv,
                 s2send, s2recv, slocal):
    s = lax.axis_index("seq")
    t = lax.axis_index("tp")
    rows, qcols = q_ref.shape
    capacity, width = fresh.shape
    head_size = width // 2
    share = share_buf.shape[1]
    heads = qcols // head_size
    cols = w_ref.shape[1] // ntp
    chunks = rows // chunk
    held = lens_ref[0]

    _greet(na, nb, s, t, *[lax.rem(t + k, ntp) for k in range(1, ntp)])
    sorted4 = share_buf.reshape(na, nb, share, width)
    a2a = SeqAllToAll(na, nb, s, t, sorted4, stage, lambda a_src: new_out.at[a_src],
                      (s1send, s1recv, s2send, s2recv, slocal))
    a2a.first()

    def slice_out(c, k):
        peer = lax.rem(t + k, ntp)
        return _remote(part.at[c, :, pl.ds(pl.multiple_of(peer * cols, cols), cols)],
                       rs_out.at[t, pl.ds(pl.multiple_of(c * chunk, chunk), chunk)],
                       psend.at[c, k], precv.at[c, k], {"seq": s, "tp": peer})

    def slice_in(c, k):
        sender = lax.rem(t + ntp - k, ntp)
        return _remote(part.at[c, :, pl.ds(0, cols)],
                       rs_out.at[sender, pl.ds(pl.multiple_of(c * chunk, chunk), chunk)],
                       psend.at[c, k], precv.at[c, k], {"seq": s, "tp": sender})

    def slice_own(c):
        return pltpu.make_async_copy(
            part.at[c, :, pl.ds(pl.multiple_of(t * cols, cols), cols)],
            rs_out.at[t, pl.ds(pl.multiple_of(c * chunk, chunk), chunk)], plocal.at[c])

    def do_chunk(c):
        first = pl.multiple_of(c * chunk, chunk)
        row_pos = first + lax.broadcasted_iota(jnp.int32, (chunk, capacity), 0)
        key_pos = lax.broadcasted_iota(jnp.int32, (chunk, capacity), 1)
        allowed = key_pos <= held + row_pos
        for h in range(heads):
            q = q_ref[pl.ds(first, chunk), pl.ds(h * head_size, head_size)]
            scores = jnp.dot(q, kt[...], preferred_element_type=jnp.float32) * scale
            scores = jnp.where(allowed, scores, MASKED)
            top = jnp.max(scores, axis=1, keepdims=True)
            weights = jnp.exp(scores - top)
            inv = 1.0 / jnp.sum(weights, axis=1, keepdims=True)
            probs = (weights * inv).astype(jnp.bfloat16)
            ctx[:, pl.ds(h * head_size, head_size)] = jnp.dot(
                probs, fresh[:, pl.ds(head_size, head_size)],
                preferred_element_type=jnp.float32).astype(ctx.dtype)
        part[c] = jnp.dot(ctx[...], w_ref[...], preferred_element_type=jnp.float32).astype(
            part.dtype)
        slice_own(c).start()
        for k in range(1, ntp):
            slice_out(c, k).start()

    do_chunk(0)
    a2a.second()

    def rest(c, carry):
        do_chunk(c)
        return carry

    lax.fori_loop(1, chunks, rest, 0)
    a2a.arrived()

    def drain(c, carry):
        for k in range(1, ntp):
            slice_in(c, k).wait_recv()
            slice_out(c, k).wait_send()
        slice_own(c).wait()
        return carry

    lax.fori_loop(0, chunks, drain, 0)
    span = lens_ref[1]

    def combine(c, carry):
        first = pl.multiple_of(c * chunk, chunk)
        total = tok_ref[pl.ds(first, chunk), :].astype(jnp.float32)
        for p in range(ntp):
            total = total + rs_out[p, pl.ds(first, chunk), :].astype(jnp.float32)
        row_pos = first + lax.broadcasted_iota(jnp.int32, total.shape, 0)
        mixed_out[pl.ds(first, chunk), :] = jnp.where(row_pos < span, total, 0.0).astype(
            mixed_out.dtype)
        return carry

    lax.fori_loop(0, chunks, combine, 0)
    a2a.finish()


def attend_and_scatter(query, cache, keyval, lens, holders, sources, w_out, tokens, na, nb, ntp,
                       chunk=128):
    rows, qcols = query.shape
    blocks, block_rows, width = cache.shape
    share = block_rows // ntp
    cols = w_out.shape[1] // ntp
    fresh, keys_t, sorted_share = prepare(cache, keyval, lens, holders, sources, ntp)
    vmem = pl.BlockSpec(memory_space=pltpu.VMEM)
    smem = pl.BlockSpec(memory_space=pltpu.SMEM)
    mixed, new = pl.pallas_call(
        functools.partial(_tail_kernel, na, nb, ntp, (width // 2) ** (-0.5), chunk),
        out_shape=(
            jax.ShapeDtypeStruct(tokens.shape, tokens.dtype),
            jax.ShapeDtypeStruct((na, nb, share, width), cache.dtype),
        ),
        in_specs=[smem, vmem, vmem, vmem, vmem, vmem, vmem],
        out_specs=(vmem, pl.BlockSpec(memory_space=pl.ANY)),
        scratch_shapes=[
            pltpu.VMEM((ntp, rows, cols), jnp.bfloat16),
            pltpu.VMEM((chunk, qcols), jnp.bfloat16),
            pltpu.VMEM((rows // chunk, chunk, w_out.shape[1]), jnp.bfloat16),
            pltpu.SemaphoreType.DMA((rows // chunk, ntp)),
            pltpu.SemaphoreType.DMA((rows // chunk, ntp)),
            pltpu.SemaphoreType.DMA((rows // chunk,)),
        ] + _seq_scratch(na, nb, share, width, cache.dtype),
        compiler_params=pltpu.CompilerParams(collective_id=1, has_side_effects=True),
    )(lens, query, fresh, keys_t, sorted_share, w_out, tokens)
    return mixed, new.reshape(blocks, share, width)


def body(
    tokens,
    norm_gain,
    w_query,
    w_keyval,
    w_out,
    span_lens,
    cached_lens,
    old_table,
    new_table,
    old_cache,
):
    groups = lax.axis_size("seq")
    tp_count = lax.axis_size("tp")
    tp_index = lax.axis_index("tp")
    holders = old_table[0]
    held_len = cached_lens[0]
    span_len = span_lens[0]
    tok_rows, tok_cols = tokens.shape
    share = old_cache.shape[1]
    width = old_cache.shape[2]
    block_rows = share * tp_count
    capacity = groups * block_rows

    inner = min(groups, 8)
    outer = groups // inner
    tok_all, cache_all = gather_inputs(tokens, old_cache, outer, inner, tp_count)
    cache_all = cache_all.reshape(groups, tp_count, share, width)
    full_rows = tok_all
    normed = normalize(full_rows, norm_gain)
    query = jnp.dot(normed, w_query, preferred_element_type=jnp.float32).astype(jnp.bfloat16)
    keyval = jnp.dot(normed, w_keyval, preferred_element_type=jnp.float32).astype(jnp.bfloat16)

    targets = new_table[0]
    device_ids = lax.broadcasted_iota(jnp.int32, (groups, groups), 0)
    block_ids = lax.broadcasted_iota(jnp.int32, (groups, groups), 1)
    matches = targets[None, :] == device_ids
    sources = jnp.sum(jnp.where(matches, block_ids, 0), axis=1)
    lens = jnp.stack([held_len, span_len]).astype(jnp.int32)
    mixed, new_cache = attend_and_scatter(
        query, cache_all.reshape(groups, block_rows, width), keyval, lens, holders, sources,
        w_out, tokens, outer, inner, tp_count
    )
    return (mixed, new_cache)


def solution(mesh):
    in_specs = (
        P("seq", "tp"),
        P(),
        P(None, "tp"),
        P(),
        P("tp", None),
        P("seq"),
        P("seq"),
        P("seq", None),
        P("seq", None),
        P("seq", "tp", None),
    )
    out_specs = (P("seq", "tp"), P("seq", "tp", None))
    return jax.shard_map(body, mesh=mesh, in_specs=in_specs, out_specs=out_specs, check_vma=False)
```

```python
import functools

import jax
import jax.numpy as jnp
from jax import lax
from jax.experimental import pallas as pl
from jax.experimental.pallas import tpu as pltpu
from jax.sharding import PartitionSpec as P

EPSILON = 1e-05
MASKED = -1e30


def normalize(rows, norm_gain):
    values = rows.astype(jnp.float32)
    average = jnp.mean(values, axis=1, keepdims=True)
    centred = values - average
    spread = jnp.mean(centred * centred, axis=1, keepdims=True)
    return (centred * lax.rsqrt(spread + EPSILON) * norm_gain).astype(jnp.bfloat16)


MESH = pl.DeviceIdType.MESH


def _remote(src, dst, send, recv, dev):
    return pltpu.make_async_remote_copy(
        src_ref=src, dst_ref=dst, send_sem=send, recv_sem=recv, device_id=dev, device_id_type=MESH
    )


def _greet(na, nb, s, t, *tp_peers):
    barrier = pltpu.get_barrier_semaphore()
    a = s // nb
    b = s % nb

    def one_b(k, carry):
        pl.semaphore_signal(barrier, inc=1, device_id={"seq": a * nb + lax.rem(b + k, nb), "tp": t},
                            device_id_type=MESH)
        return carry

    def one_a(k, carry):
        pl.semaphore_signal(barrier, inc=1, device_id={"seq": lax.rem(a + k, na) * nb + b, "tp": t},
                            device_id_type=MESH)
        return carry

    lax.fori_loop(1, nb, one_b, 0)
    lax.fori_loop(1, na, one_a, 0)
    for p in tp_peers:
        pl.semaphore_signal(barrier, inc=1, device_id={"seq": s, "tp": p}, device_id_type=MESH)
    pl.semaphore_wait(barrier, na + nb - 2 + len(tp_peers))


class SeqAllToAll:
    def __init__(self, na, nb, s, t, src, stage, dst, sems):
        self.na, self.nb, self.t, self.src, self.stage, self.dst = na, nb, t, src, stage, dst
        self.a = s // nb
        self.b = s % nb
        self.s1send, self.s1recv, self.s2send, self.s2recv, self.local = sems

    def _dev(self, a, b):
        return {"seq": a * self.nb + b, "tp": self.t}

    def _out1(self, k):
        peer = lax.rem(self.b + k, self.nb)
        return _remote(self.src.at[:, peer], self.stage.at[self.b], self.s1send.at[k],
                       self.s1recv.at[k], self._dev(self.a, peer))

    def _in1(self, k):
        sender = lax.rem(self.b + self.nb - k, self.nb)
        return _remote(self.src.at[:, self.b], self.stage.at[sender], self.s1send.at[k],
                       self.s1recv.at[k], self._dev(self.a, sender))

    def _out2(self, k):
        peer = lax.rem(self.a + k, self.na)
        return _remote(self.stage.at[:, peer], self.dst(self.a), self.s2send.at[k],
                       self.s2recv.at[k], self._dev(peer, self.b))

    def _in2(self, k):
        sender = lax.rem(self.a + self.na - k, self.na)
        return _remote(self.stage.at[:, self.a], self.dst(sender), self.s2send.at[k],
                       self.s2recv.at[k], self._dev(sender, self.b))

    def first(self):
        self.own1 = pltpu.make_async_copy(self.src.at[:, self.b], self.stage.at[self.b],
                                          self.local.at[0])
        self.own1.start()
        _loop(self.nb, lambda k: self._out1(k).start())

    def second(self):
        _loop(self.nb, lambda k: self._in1(k).wait_recv())
        self.own1.wait()
        self.own2 = pltpu.make_async_copy(self.stage.at[:, self.a], self.dst(self.a),
                                          self.local.at[1])
        self.own2.start()
        _loop(self.na, lambda k: self._out2(k).start())

    def arrived(self):
        _loop(self.na, lambda k: self._in2(k).wait_recv())
        self.own2.wait()

    def finish(self):
        _loop(self.nb, lambda k: self._out1(k).wait_send())
        _loop(self.na, lambda k: self._out2(k).wait_send())


def _seq_scratch(na, nb, share, width, dtype):
    return [
        pltpu.VMEM((nb, na, share, width), dtype),
        pltpu.SemaphoreType.DMA((nb,)),
        pltpu.SemaphoreType.DMA((nb,)),
        pltpu.SemaphoreType.DMA((na,)),
        pltpu.SemaphoreType.DMA((na,)),
        pltpu.SemaphoreType.DMA((2,)),
    ]


def _loop(n, fn):
    def step(k, carry):
        fn(k)
        return carry

    lax.fori_loop(1, n, step, 0)


def _in_kernel(na, nb, ntp, tok_ref, cache_ref, gain_ref, wq_ref, wkv_ref, q_out, kv_out,
               cache_out, tok_all, tsend, trecv, csend, crecv, lsem, stage, s1send, s1recv,
               s2send, s2recv, slocal):
    s = lax.axis_index("seq")
    t = lax.axis_index("tp")
    right = lax.rem(t + 1, ntp)
    left = lax.rem(t + ntp - 1, ntp)
    across = lax.rem(t + 2, ntp)
    rdev = {"seq": s, "tp": right}
    ldev = {"seq": s, "tp": left}
    rows, cols = tok_ref.shape
    half = rows // 2
    _greet(na, nb, s, t, left, right, across)

    def tok_cols(p):
        return pl.ds(pl.multiple_of(p * cols, cols), cols)

    a2a = SeqAllToAll(na, nb, s, t, cache_ref, stage, lambda a_src: cache_out.at[a_src, :, t],
                      (s1send, s1recv, s2send, s2recv, slocal))
    a2a.first()

    own_tok = pltpu.make_async_copy(tok_ref, tok_all.at[:, tok_cols(t)], lsem.at[0])
    own_tok.start()
    tok_r = _remote(tok_ref, tok_all.at[:, tok_cols(t)], tsend.at[0], trecv.at[0], rdev)
    tok_l = _remote(tok_ref, tok_all.at[:, tok_cols(t)], tsend.at[1], trecv.at[1], ldev)
    tok_r.start()
    tok_l.start()

    a2a.second()

    _remote(tok_ref, tok_all.at[:, tok_cols(left)], tsend.at[0], trecv.at[0], ldev).wait_recv()
    fwd_r = _remote(tok_all.at[pl.ds(0, half), tok_cols(left)],
                    tok_all.at[pl.ds(0, half), tok_cols(left)], tsend.at[2], trecv.at[2], rdev)
    fwd_r.start()
    _remote(tok_ref, tok_all.at[:, tok_cols(right)], tsend.at[1], trecv.at[1], rdev).wait_recv()
    fwd_l = _remote(tok_all.at[pl.ds(half, half), tok_cols(right)],
                    tok_all.at[pl.ds(half, half), tok_cols(right)], tsend.at[3], trecv.at[3], ldev)
    fwd_l.start()

    a2a.arrived()
    flat = cache_out.reshape(na * nb, ntp, *cache_out.shape[3:])
    mine = flat.at[:, t]

    def cache_to(k):
        peer = lax.rem(t + k, ntp)
        return _remote(mine, mine, csend.at[k], crecv.at[k], {"seq": s, "tp": peer})

    def cache_from(k):
        sender = lax.rem(t + ntp - k, ntp)
        return _remote(mine, flat.at[:, sender], csend.at[k], crecv.at[k],
                       {"seq": s, "tp": sender})

    for k in range(1, ntp):
        cache_to(k).start()

    _remote(tok_ref.at[pl.ds(0, half)], tok_all.at[pl.ds(0, half), tok_cols(across)],
            tsend.at[2], trecv.at[2], ldev).wait_recv()
    _remote(tok_ref.at[pl.ds(half, half)], tok_all.at[pl.ds(half, half), tok_cols(across)],
            tsend.at[3], trecv.at[3], rdev).wait_recv()
    own_tok.wait()

    chunk = 128

    def project(c, carry):
        first = pl.multiple_of(c * chunk, chunk)
        values = tok_all[pl.ds(first, chunk), :].astype(jnp.float32)
        average = jnp.mean(values, axis=1, keepdims=True)
        centred = values - average
        spread = jnp.mean(centred * centred, axis=1, keepdims=True)
        normed = (centred * lax.rsqrt(spread + EPSILON) * gain_ref[...]).astype(jnp.bfloat16)
        q_out[pl.ds(first, chunk), :] = jnp.dot(
            normed, wq_ref[...], preferred_element_type=jnp.float32).astype(q_out.dtype)
        kv_out[pl.ds(first, chunk), :] = jnp.dot(
            normed, wkv_ref[...], preferred_element_type=jnp.float32).astype(kv_out.dtype)
        return carry

    lax.fori_loop(0, rows // chunk, project, 0)

    for k in range(1, ntp):
        cache_from(k).wait_recv()
    for c in (tok_r, tok_l, fwd_r, fwd_l):
        c.wait_send()
    for k in range(1, ntp):
        cache_to(k).wait_send()
    a2a.finish()


def gather_inputs(tokens, old_cache, norm_gain, w_query, w_keyval, na, nb, ntp):
    rows, cols = tokens.shape
    _, share, width = old_cache.shape
    cache4 = old_cache.reshape(na, nb, share, width)
    vmem = pl.BlockSpec(memory_space=pltpu.VMEM)
    anywhere = pl.BlockSpec(memory_space=pl.ANY)
    return pl.pallas_call(
        functools.partial(_in_kernel, na, nb, ntp),
        out_shape=(
            jax.ShapeDtypeStruct((rows, w_query.shape[1]), jnp.bfloat16),
            jax.ShapeDtypeStruct((rows, w_keyval.shape[1]), jnp.bfloat16),
            jax.ShapeDtypeStruct((na, nb, ntp, share, width), old_cache.dtype),
        ),
        in_specs=[anywhere, anywhere, vmem, vmem, vmem],
        out_specs=(vmem, vmem, anywhere),
        scratch_shapes=[
            pltpu.VMEM((rows, ntp * cols), tokens.dtype),
            pltpu.SemaphoreType.DMA((4,)),
            pltpu.SemaphoreType.DMA((4,)),
            pltpu.SemaphoreType.DMA((ntp,)),
            pltpu.SemaphoreType.DMA((ntp,)),
            pltpu.SemaphoreType.DMA((2,)),
        ] + _seq_scratch(na, nb, share, width, old_cache.dtype),
        compiler_params=pltpu.CompilerParams(collective_id=0, has_side_effects=True),
    )(tokens, cache4, norm_gain.reshape(1, -1).astype(jnp.float32), w_query, w_keyval)


def _out_kernel(na, nb, ntp, part_ref, share_ref, rs_out, new_out, stage_rs, rsend, rrecv, lsem,
                stage, s1send, s1recv, s2send, s2recv, slocal):
    s = lax.axis_index("seq")
    t = lax.axis_index("tp")
    right = lax.rem(t + 1, ntp)
    left = lax.rem(t + ntp - 1, ntp)
    across = lax.rem(t + 2, ntp)
    rdev = {"seq": s, "tp": right}
    ldev = {"seq": s, "tp": left}
    half = part_ref.shape[1] // 2
    _greet(na, nb, s, t, left, right)

    a2a = SeqAllToAll(na, nb, s, t, share_ref, stage, lambda a_src: new_out.at[a_src],
                      (s1send, s1recv, s2send, s2recv, slocal))
    a2a.first()

    own_part = pltpu.make_async_copy(part_ref.at[t], rs_out.at[t], lsem.at[0])
    own_part.start()
    to_r = _remote(part_ref.at[right], rs_out.at[t], rsend.at[0], rrecv.at[0], rdev)
    to_l = _remote(part_ref.at[left], rs_out.at[t], rsend.at[1], rrecv.at[1], ldev)
    via_r = _remote(part_ref.at[across, pl.ds(0, half)], stage_rs.at[0], rsend.at[2], rrecv.at[2],
                    rdev)
    via_l = _remote(part_ref.at[across, pl.ds(half, half)], stage_rs.at[1], rsend.at[3],
                    rrecv.at[3], ldev)
    for c in (to_r, to_l, via_r, via_l):
        c.start()

    a2a.second()

    _remote(part_ref.at[across, pl.ds(0, half)], stage_rs.at[0], rsend.at[2], rrecv.at[2],
            ldev).wait_recv()
    fwd_r = _remote(stage_rs.at[0], rs_out.at[left, pl.ds(0, half)], rsend.at[4], rrecv.at[4],
                    rdev)
    fwd_r.start()
    _remote(part_ref.at[across, pl.ds(half, half)], stage_rs.at[1], rsend.at[3], rrecv.at[3],
            rdev).wait_recv()
    fwd_l = _remote(stage_rs.at[1], rs_out.at[right, pl.ds(half, half)], rsend.at[5],
                    rrecv.at[5], ldev)
    fwd_l.start()

    a2a.arrived()
    _remote(part_ref.at[t], rs_out.at[left], rsend.at[0], rrecv.at[0], ldev).wait_recv()
    _remote(part_ref.at[t], rs_out.at[right], rsend.at[1], rrecv.at[1], rdev).wait_recv()
    _remote(stage_rs.at[0], rs_out.at[across, pl.ds(0, half)], rsend.at[4], rrecv.at[4],
            ldev).wait_recv()
    _remote(stage_rs.at[1], rs_out.at[across, pl.ds(half, half)], rsend.at[5], rrecv.at[5],
            rdev).wait_recv()
    for c in (to_r, to_l, via_r, via_l, fwd_r, fwd_l):
        c.wait_send()
    a2a.finish()
    own_part.wait()


def scatter_outputs(partial, share, na, nb, ntp):
    _, rows, cols = partial.shape
    _, block, width = share.shape
    share4 = share.reshape(na, nb, block, width)
    rs, new = pl.pallas_call(
        functools.partial(_out_kernel, na, nb, ntp),
        out_shape=(
            jax.ShapeDtypeStruct(partial.shape, partial.dtype),
            jax.ShapeDtypeStruct(share4.shape, share.dtype),
        ),
        in_specs=[pl.BlockSpec(memory_space=pl.ANY)] * 2,
        out_specs=(pl.BlockSpec(memory_space=pl.ANY), pl.BlockSpec(memory_space=pl.ANY)),
        scratch_shapes=[
            pltpu.VMEM((2, rows // 2, cols), partial.dtype),
            pltpu.SemaphoreType.DMA((6,)),
            pltpu.SemaphoreType.DMA((6,)),
            pltpu.SemaphoreType.DMA((1,)),
        ] + _seq_scratch(na, nb, block, width, share.dtype),
        compiler_params=pltpu.CompilerParams(collective_id=1, has_side_effects=True),
    )(partial, share4)
    return rs, new.reshape(share.shape)


def _attend_kernel(scale, lens_ref, q_ref, k_ref, v_ref, o_ref):
    chunk = q_ref.shape[0]
    capacity = k_ref.shape[0]
    held = lens_ref[0]
    first = pl.program_id(1) * chunk
    scores = lax.dot_general(
        q_ref[...], k_ref[...], (((1,), (1,)), ((), ())), preferred_element_type=jnp.float32
    ) * scale
    row_pos = first + lax.broadcasted_iota(jnp.int32, (chunk, capacity), 0)
    key_pos = lax.broadcasted_iota(jnp.int32, (chunk, capacity), 1)
    scores = jnp.where(key_pos <= held + row_pos, scores, MASKED)
    top = jnp.max(scores, axis=1, keepdims=True)
    weights = jnp.exp(scores - top)
    probs = (weights / jnp.sum(weights, axis=1, keepdims=True)).astype(jnp.bfloat16)
    o_ref[...] = jnp.dot(probs, v_ref[...], preferred_element_type=jnp.float32).astype(o_ref.dtype)


def attend(query, fresh, held_len, head_size, chunk=128):
    rows, qcols = query.shape
    capacity = fresh.shape[0]
    heads = qcols // head_size
    lens = jnp.reshape(held_len, (1,)).astype(jnp.int32)
    return pl.pallas_call(
        functools.partial(_attend_kernel, head_size ** (-0.5)),
        out_shape=jax.ShapeDtypeStruct((rows, qcols), jnp.bfloat16),
        grid_spec=pltpu.PrefetchScalarGridSpec(
            num_scalar_prefetch=1,
            grid=(heads, rows // chunk),
            in_specs=[
                pl.BlockSpec((chunk, head_size), lambda h, r, lens: (r, h)),
                pl.BlockSpec((capacity, head_size), lambda h, r, lens: (0, 0)),
                pl.BlockSpec((capacity, head_size), lambda h, r, lens: (0, 1)),
            ],
            out_specs=pl.BlockSpec((chunk, head_size), lambda h, r, lens: (r, h)),
        ),
        cost_estimate=pl.CostEstimate(
            flops=4 * rows * capacity * qcols,
            transcendentals=rows * capacity * heads,
            bytes_accessed=2 * (2 * rows * qcols + 2 * capacity * head_size),
        ),
    )(lens, query, fresh, fresh)


def _prep_kernel(ntp, lens_ref, holders_ref, sources_ref, cache_ref, kv_ref, fresh, kt, share_buf,
                 fresh32):
    t = lax.axis_index("tp")
    capacity, width = fresh.shape
    head_size = width // 2
    block_rows = cache_ref.shape[1]
    share = block_rows // ntp
    held = lens_ref[0]
    span = lens_ref[1]

    def place(b, carry):
        fresh32[pl.ds(pl.multiple_of(b * block_rows, block_rows), block_rows), :] = (
            cache_ref[holders_ref[b]].astype(jnp.float32))
        return carry

    lax.fori_loop(0, capacity // block_rows, place, 0)
    padded = jnp.concatenate(
        [kv_ref[...].astype(jnp.float32),
         jnp.zeros((capacity - kv_ref.shape[0], width), jnp.float32)], axis=0)
    shifted = pltpu.roll(padded, held, 0)
    positions = lax.broadcasted_iota(jnp.int32, (capacity, width), 0)
    full = jnp.where(positions < held, fresh32[...],
                     jnp.where(positions < held + span, shifted, 0.0))
    fresh32[...] = full
    fresh[...] = full.astype(fresh.dtype)
    kt[...] = fresh[:, pl.ds(0, head_size)].T

    def pick(d, carry):
        start = pl.multiple_of(sources_ref[d] * block_rows + t * share, share)
        share_buf[d] = fresh32[pl.ds(start, share), :].astype(share_buf.dtype)
        return carry

    lax.fori_loop(0, share_buf.shape[0], pick, 0)


def prepare(cache, keyval, lens, holders, sources, ntp):
    blocks, block_rows, width = cache.shape
    capacity = blocks * block_rows
    vmem = pl.BlockSpec(memory_space=pltpu.VMEM)
    smem = pl.BlockSpec(memory_space=pltpu.SMEM)
    return pl.pallas_call(
        functools.partial(_prep_kernel, ntp),
        out_shape=(
            jax.ShapeDtypeStruct((capacity, width), cache.dtype),
            jax.ShapeDtypeStruct((width // 2, capacity), cache.dtype),
            jax.ShapeDtypeStruct((blocks, block_rows // ntp, width), cache.dtype),
        ),
        in_specs=[smem, smem, smem, vmem, vmem],
        out_specs=(vmem, vmem, vmem),
        scratch_shapes=[pltpu.VMEM((capacity, width), jnp.float32)],
    )(lens, holders, sources, cache, keyval)


def _tail_kernel(na, nb, ntp, scale, chunk, lens_ref, q_ref, fresh, kt, share_buf, w_ref,
                 rs_out, new_out, ctx, part, psend, precv, plocal, stage, s1send, s1recv, s2send,
                 s2recv, slocal):
    s = lax.axis_index("seq")
    t = lax.axis_index("tp")
    rows, qcols = q_ref.shape
    capacity, width = fresh.shape
    head_size = width // 2
    share = share_buf.shape[1]
    heads = qcols // head_size
    cols = w_ref.shape[1] // ntp
    chunks = rows // chunk
    held = lens_ref[0]

    _greet(na, nb, s, t, *[lax.rem(t + k, ntp) for k in range(1, ntp)])
    sorted4 = share_buf.reshape(na, nb, share, width)
    a2a = SeqAllToAll(na, nb, s, t, sorted4, stage, lambda a_src: new_out.at[a_src],
                      (s1send, s1recv, s2send, s2recv, slocal))
    a2a.first()

    def slice_out(c, k):
        peer = lax.rem(t + k, ntp)
        return _remote(part.at[c, :, pl.ds(pl.multiple_of(peer * cols, cols), cols)],
                       rs_out.at[t, pl.ds(pl.multiple_of(c * chunk, chunk), chunk)],
                       psend.at[c, k], precv.at[c, k], {"seq": s, "tp": peer})

    def slice_in(c, k):
        sender = lax.rem(t + ntp - k, ntp)
        return _remote(part.at[c, :, pl.ds(0, cols)],
                       rs_out.at[sender, pl.ds(pl.multiple_of(c * chunk, chunk), chunk)],
                       psend.at[c, k], precv.at[c, k], {"seq": s, "tp": sender})

    def slice_own(c):
        return pltpu.make_async_copy(
            part.at[c, :, pl.ds(pl.multiple_of(t * cols, cols), cols)],
            rs_out.at[t, pl.ds(pl.multiple_of(c * chunk, chunk), chunk)], plocal.at[c])

    def do_chunk(c):
        first = pl.multiple_of(c * chunk, chunk)
        row_pos = first + lax.broadcasted_iota(jnp.int32, (chunk, capacity), 0)
        key_pos = lax.broadcasted_iota(jnp.int32, (chunk, capacity), 1)
        allowed = key_pos <= held + row_pos
        for h in range(heads):
            q = q_ref[pl.ds(first, chunk), pl.ds(h * head_size, head_size)]
            scores = jnp.dot(q, kt[...], preferred_element_type=jnp.float32) * scale
            scores = jnp.where(allowed, scores, MASKED)
            top = jnp.max(scores, axis=1, keepdims=True)
            weights = jnp.exp(scores - top)
            inv = 1.0 / jnp.sum(weights, axis=1, keepdims=True)
            probs = (weights * inv).astype(jnp.bfloat16)
            ctx[:, pl.ds(h * head_size, head_size)] = jnp.dot(
                probs, fresh[:, pl.ds(head_size, head_size)],
                preferred_element_type=jnp.float32).astype(ctx.dtype)
        part[c] = jnp.dot(ctx[...], w_ref[...], preferred_element_type=jnp.float32).astype(
            part.dtype)
        slice_own(c).start()
        for k in range(1, ntp):
            slice_out(c, k).start()

    do_chunk(0)
    a2a.second()

    def rest(c, carry):
        do_chunk(c)
        return carry

    lax.fori_loop(1, chunks, rest, 0)
    a2a.arrived()

    def drain(c, carry):
        for k in range(1, ntp):
            slice_in(c, k).wait_recv()
            slice_out(c, k).wait_send()
        slice_own(c).wait()
        return carry

    lax.fori_loop(0, chunks, drain, 0)
    a2a.finish()


def attend_and_scatter(query, cache, keyval, lens, holders, sources, w_out, na, nb, ntp,
                       chunk=128):
    rows, qcols = query.shape
    blocks, block_rows, width = cache.shape
    share = block_rows // ntp
    cols = w_out.shape[1] // ntp
    fresh, keys_t, sorted_share = prepare(cache, keyval, lens, holders, sources, ntp)
    vmem = pl.BlockSpec(memory_space=pltpu.VMEM)
    smem = pl.BlockSpec(memory_space=pltpu.SMEM)
    rs, new = pl.pallas_call(
        functools.partial(_tail_kernel, na, nb, ntp, (width // 2) ** (-0.5), chunk),
        out_shape=(
            jax.ShapeDtypeStruct((ntp, rows, cols), jnp.bfloat16),
            jax.ShapeDtypeStruct((na, nb, share, width), cache.dtype),
        ),
        in_specs=[smem, vmem, vmem, vmem, vmem, vmem],
        out_specs=(pl.BlockSpec(memory_space=pl.ANY), pl.BlockSpec(memory_space=pl.ANY)),
        scratch_shapes=[
            pltpu.VMEM((chunk, qcols), jnp.bfloat16),
            pltpu.VMEM((rows // chunk, chunk, w_out.shape[1]), jnp.bfloat16),
            pltpu.SemaphoreType.DMA((rows // chunk, ntp)),
            pltpu.SemaphoreType.DMA((rows // chunk, ntp)),
            pltpu.SemaphoreType.DMA((rows // chunk,)),
        ] + _seq_scratch(na, nb, share, width, cache.dtype),
        compiler_params=pltpu.CompilerParams(collective_id=1, has_side_effects=True),
    )(lens, query, fresh, keys_t, sorted_share, w_out)
    return rs, new.reshape(blocks, share, width)


def body(
    tokens,
    norm_gain,
    w_query,
    w_keyval,
    w_out,
    span_lens,
    cached_lens,
    old_table,
    new_table,
    old_cache,
):
    groups = lax.axis_size("seq")
    tp_count = lax.axis_size("tp")
    tp_index = lax.axis_index("tp")
    holders = old_table[0]
    held_len = cached_lens[0]
    span_len = span_lens[0]
    tok_rows, tok_cols = tokens.shape
    share = old_cache.shape[1]
    width = old_cache.shape[2]
    block_rows = share * tp_count
    capacity = groups * block_rows

    inner = min(groups, 8)
    outer = groups // inner
    query, keyval, cache_all = gather_inputs(
        tokens, old_cache, norm_gain, w_query, w_keyval, outer, inner, tp_count
    )
    cache_all = cache_all.reshape(groups, tp_count, share, width)

    targets = new_table[0]
    device_ids = lax.broadcasted_iota(jnp.int32, (groups, groups), 0)
    block_ids = lax.broadcasted_iota(jnp.int32, (groups, groups), 1)
    matches = targets[None, :] == device_ids
    sources = jnp.sum(jnp.where(matches, block_ids, 0), axis=1)
    lens = jnp.stack([held_len, span_len]).astype(jnp.int32)
    summed, new_cache = attend_and_scatter(
        query, cache_all.reshape(groups, block_rows, width), keyval, lens, holders, sources,
        w_out, outer, inner, tp_count
    )
    row_pos = lax.broadcasted_iota(jnp.int32, (tok_rows, 1), 0)
    summed = summed.astype(jnp.float32)
    total = tokens.astype(jnp.float32) + jnp.sum(summed, axis=0)
    mixed = jnp.where(row_pos < span_len, total, jnp.zeros_like(total)).astype(jnp.bfloat16)
    return (mixed, new_cache)


def solution(mesh):
    in_specs = (
        P("seq", "tp"),
        P(),
        P(None, "tp"),
        P(),
        P("tp", None),
        P("seq"),
        P("seq"),
        P("seq", None),
        P("seq", None),
        P("seq", "tp", None),
    )
    out_specs = (P("seq", "tp"), P("seq", "tp", None))
    return jax.shard_map(body, mesh=mesh, in_specs=in_specs, out_specs=out_specs, check_vma=False)
```

```python
import functools

import jax
import jax.numpy as jnp
from jax import lax
from jax.experimental import pallas as pl
from jax.experimental.pallas import tpu as pltpu
from jax.sharding import PartitionSpec as P

EPSILON = 1e-05
MASKED = -1e30


def normalize(rows, norm_gain):
    values = rows.astype(jnp.float32)
    average = jnp.mean(values, axis=1, keepdims=True)
    centred = values - average
    spread = jnp.mean(centred * centred, axis=1, keepdims=True)
    return (centred * lax.rsqrt(spread + EPSILON) * norm_gain).astype(jnp.bfloat16)


MESH = pl.DeviceIdType.MESH


def _remote(src, dst, send, recv, dev):
    return pltpu.make_async_remote_copy(
        src_ref=src, dst_ref=dst, send_sem=send, recv_sem=recv, device_id=dev, device_id_type=MESH
    )


def _greet(na, nb, s, t, *tp_peers):
    barrier = pltpu.get_barrier_semaphore()
    a = s // nb
    b = s % nb

    def one_b(k, carry):
        pl.semaphore_signal(barrier, inc=1, device_id={"seq": a * nb + lax.rem(b + k, nb), "tp": t},
                            device_id_type=MESH)
        return carry

    def one_a(k, carry):
        pl.semaphore_signal(barrier, inc=1, device_id={"seq": lax.rem(a + k, na) * nb + b, "tp": t},
                            device_id_type=MESH)
        return carry

    lax.fori_loop(1, nb, one_b, 0)
    lax.fori_loop(1, na, one_a, 0)
    for p in tp_peers:
        pl.semaphore_signal(barrier, inc=1, device_id={"seq": s, "tp": p}, device_id_type=MESH)
    pl.semaphore_wait(barrier, na + nb - 2 + len(tp_peers))


class SeqAllToAll:
    def __init__(self, na, nb, s, t, src, stage, dst, sems):
        self.na, self.nb, self.t, self.src, self.stage, self.dst = na, nb, t, src, stage, dst
        self.a = s // nb
        self.b = s % nb
        self.s1send, self.s1recv, self.s2send, self.s2recv, self.local = sems

    def _dev(self, a, b):
        return {"seq": a * self.nb + b, "tp": self.t}

    def _out1(self, k):
        peer = lax.rem(self.b + k, self.nb)
        return _remote(self.src.at[:, peer], self.stage.at[self.b], self.s1send.at[k],
                       self.s1recv.at[k], self._dev(self.a, peer))

    def _in1(self, k):
        sender = lax.rem(self.b + self.nb - k, self.nb)
        return _remote(self.src.at[:, self.b], self.stage.at[sender], self.s1send.at[k],
                       self.s1recv.at[k], self._dev(self.a, sender))

    def _out2(self, k):
        peer = lax.rem(self.a + k, self.na)
        return _remote(self.stage.at[:, peer], self.dst(self.a), self.s2send.at[k],
                       self.s2recv.at[k], self._dev(peer, self.b))

    def _in2(self, k):
        sender = lax.rem(self.a + self.na - k, self.na)
        return _remote(self.stage.at[:, self.a], self.dst(sender), self.s2send.at[k],
                       self.s2recv.at[k], self._dev(sender, self.b))

    def first(self):
        self.own1 = pltpu.make_async_copy(self.src.at[:, self.b], self.stage.at[self.b],
                                          self.local.at[0])
        self.own1.start()
        _loop(self.nb, lambda k: self._out1(k).start())

    def second(self):
        _loop(self.nb, lambda k: self._in1(k).wait_recv())
        self.own1.wait()
        self.own2 = pltpu.make_async_copy(self.stage.at[:, self.a], self.dst(self.a),
                                          self.local.at[1])
        self.own2.start()
        _loop(self.na, lambda k: self._out2(k).start())

    def arrived(self):
        _loop(self.na, lambda k: self._in2(k).wait_recv())
        self.own2.wait()

    def finish(self):
        _loop(self.nb, lambda k: self._out1(k).wait_send())
        _loop(self.na, lambda k: self._out2(k).wait_send())


def _seq_scratch(na, nb, share, width, dtype):
    return [
        pltpu.VMEM((nb, na, share, width), dtype),
        pltpu.SemaphoreType.DMA((nb,)),
        pltpu.SemaphoreType.DMA((nb,)),
        pltpu.SemaphoreType.DMA((na,)),
        pltpu.SemaphoreType.DMA((na,)),
        pltpu.SemaphoreType.DMA((2,)),
    ]


def _loop(n, fn):
    def step(k, carry):
        fn(k)
        return carry

    lax.fori_loop(1, n, step, 0)


def _in_kernel(na, nb, ntp, tok_ref, cache_ref, gain_ref, wq_ref, wkv_ref, q_out, kv_out,
               cache_out, tok_all, tsend, trecv, csend, crecv, lsem, stage, s1send, s1recv,
               s2send, s2recv, slocal):
    s = lax.axis_index("seq")
    t = lax.axis_index("tp")
    right = lax.rem(t + 1, ntp)
    left = lax.rem(t + ntp - 1, ntp)
    across = lax.rem(t + 2, ntp)
    rdev = {"seq": s, "tp": right}
    ldev = {"seq": s, "tp": left}
    rows, cols = tok_ref.shape
    half = rows // 2
    _greet(na, nb, s, t, left, right, across)

    def tok_cols(p):
        return pl.ds(pl.multiple_of(p * cols, cols), cols)

    a2a = SeqAllToAll(na, nb, s, t, cache_ref, stage, lambda a_src: cache_out.at[a_src, :, t],
                      (s1send, s1recv, s2send, s2recv, slocal))
    a2a.first()

    own_tok = pltpu.make_async_copy(tok_ref, tok_all.at[:, tok_cols(t)], lsem.at[0])
    own_tok.start()
    tok_r = _remote(tok_ref, tok_all.at[:, tok_cols(t)], tsend.at[0], trecv.at[0], rdev)
    tok_l = _remote(tok_ref, tok_all.at[:, tok_cols(t)], tsend.at[1], trecv.at[1], ldev)
    tok_r.start()
    tok_l.start()

    a2a.second()

    _remote(tok_ref, tok_all.at[:, tok_cols(left)], tsend.at[0], trecv.at[0], ldev).wait_recv()
    fwd_r = _remote(tok_all.at[pl.ds(0, half), tok_cols(left)],
                    tok_all.at[pl.ds(0, half), tok_cols(left)], tsend.at[2], trecv.at[2], rdev)
    fwd_r.start()
    _remote(tok_ref, tok_all.at[:, tok_cols(right)], tsend.at[1], trecv.at[1], rdev).wait_recv()
    fwd_l = _remote(tok_all.at[pl.ds(half, half), tok_cols(right)],
                    tok_all.at[pl.ds(half, half), tok_cols(right)], tsend.at[3], trecv.at[3], ldev)
    fwd_l.start()

    _remote(tok_ref.at[pl.ds(0, half)], tok_all.at[pl.ds(0, half), tok_cols(across)],
            tsend.at[2], trecv.at[2], ldev).wait_recv()
    _remote(tok_ref.at[pl.ds(half, half)], tok_all.at[pl.ds(half, half), tok_cols(across)],
            tsend.at[3], trecv.at[3], rdev).wait_recv()
    own_tok.wait()

    a2a.arrived()
    flat = cache_out.reshape(na * nb, ntp, *cache_out.shape[3:])
    mine = flat.at[:, t]

    def cache_to(k):
        peer = lax.rem(t + k, ntp)
        return _remote(mine, mine, csend.at[k], crecv.at[k], {"seq": s, "tp": peer})

    def cache_from(k):
        sender = lax.rem(t + ntp - k, ntp)
        return _remote(mine, flat.at[:, sender], csend.at[k], crecv.at[k],
                       {"seq": s, "tp": sender})

    for k in range(1, ntp):
        cache_to(k).start()

    chunk = 128

    def project(c, carry):
        first = pl.multiple_of(c * chunk, chunk)
        values = tok_all[pl.ds(first, chunk), :].astype(jnp.float32)
        average = jnp.mean(values, axis=1, keepdims=True)
        centred = values - average
        spread = jnp.mean(centred * centred, axis=1, keepdims=True)
        normed = (centred * lax.rsqrt(spread + EPSILON) * gain_ref[...]).astype(jnp.bfloat16)
        q_out[pl.ds(first, chunk), :] = jnp.dot(
            normed, wq_ref[...], preferred_element_type=jnp.float32).astype(q_out.dtype)
        kv_out[pl.ds(first, chunk), :] = jnp.dot(
            normed, wkv_ref[...], preferred_element_type=jnp.float32).astype(kv_out.dtype)
        return carry

    lax.fori_loop(0, rows // chunk, project, 0)

    for k in range(1, ntp):
        cache_from(k).wait_recv()
    for c in (tok_r, tok_l, fwd_r, fwd_l):
        c.wait_send()
    for k in range(1, ntp):
        cache_to(k).wait_send()
    a2a.finish()


def gather_inputs(tokens, old_cache, norm_gain, w_query, w_keyval, na, nb, ntp):
    rows, cols = tokens.shape
    _, share, width = old_cache.shape
    cache4 = old_cache.reshape(na, nb, share, width)
    vmem = pl.BlockSpec(memory_space=pltpu.VMEM)
    anywhere = pl.BlockSpec(memory_space=pl.ANY)
    return pl.pallas_call(
        functools.partial(_in_kernel, na, nb, ntp),
        out_shape=(
            jax.ShapeDtypeStruct((rows, w_query.shape[1]), jnp.bfloat16),
            jax.ShapeDtypeStruct((rows, w_keyval.shape[1]), jnp.bfloat16),
            jax.ShapeDtypeStruct((na, nb, ntp, share, width), old_cache.dtype),
        ),
        in_specs=[anywhere, anywhere, vmem, vmem, vmem],
        out_specs=(vmem, vmem, anywhere),
        scratch_shapes=[
            pltpu.VMEM((rows, ntp * cols), tokens.dtype),
            pltpu.SemaphoreType.DMA((4,)),
            pltpu.SemaphoreType.DMA((4,)),
            pltpu.SemaphoreType.DMA((ntp,)),
            pltpu.SemaphoreType.DMA((ntp,)),
            pltpu.SemaphoreType.DMA((2,)),
        ] + _seq_scratch(na, nb, share, width, old_cache.dtype),
        compiler_params=pltpu.CompilerParams(collective_id=0, has_side_effects=True),
    )(tokens, cache4, norm_gain.reshape(1, -1).astype(jnp.float32), w_query, w_keyval)


def _out_kernel(na, nb, ntp, part_ref, share_ref, rs_out, new_out, stage_rs, rsend, rrecv, lsem,
                stage, s1send, s1recv, s2send, s2recv, slocal):
    s = lax.axis_index("seq")
    t = lax.axis_index("tp")
    right = lax.rem(t + 1, ntp)
    left = lax.rem(t + ntp - 1, ntp)
    across = lax.rem(t + 2, ntp)
    rdev = {"seq": s, "tp": right}
    ldev = {"seq": s, "tp": left}
    half = part_ref.shape[1] // 2
    _greet(na, nb, s, t, left, right)

    a2a = SeqAllToAll(na, nb, s, t, share_ref, stage, lambda a_src: new_out.at[a_src],
                      (s1send, s1recv, s2send, s2recv, slocal))
    a2a.first()

    own_part = pltpu.make_async_copy(part_ref.at[t], rs_out.at[t], lsem.at[0])
    own_part.start()
    to_r = _remote(part_ref.at[right], rs_out.at[t], rsend.at[0], rrecv.at[0], rdev)
    to_l = _remote(part_ref.at[left], rs_out.at[t], rsend.at[1], rrecv.at[1], ldev)
    via_r = _remote(part_ref.at[across, pl.ds(0, half)], stage_rs.at[0], rsend.at[2], rrecv.at[2],
                    rdev)
    via_l = _remote(part_ref.at[across, pl.ds(half, half)], stage_rs.at[1], rsend.at[3],
                    rrecv.at[3], ldev)
    for c in (to_r, to_l, via_r, via_l):
        c.start()

    a2a.second()

    _remote(part_ref.at[across, pl.ds(0, half)], stage_rs.at[0], rsend.at[2], rrecv.at[2],
            ldev).wait_recv()
    fwd_r = _remote(stage_rs.at[0], rs_out.at[left, pl.ds(0, half)], rsend.at[4], rrecv.at[4],
                    rdev)
    fwd_r.start()
    _remote(part_ref.at[across, pl.ds(half, half)], stage_rs.at[1], rsend.at[3], rrecv.at[3],
            rdev).wait_recv()
    fwd_l = _remote(stage_rs.at[1], rs_out.at[right, pl.ds(half, half)], rsend.at[5],
                    rrecv.at[5], ldev)
    fwd_l.start()

    a2a.arrived()
    _remote(part_ref.at[t], rs_out.at[left], rsend.at[0], rrecv.at[0], ldev).wait_recv()
    _remote(part_ref.at[t], rs_out.at[right], rsend.at[1], rrecv.at[1], rdev).wait_recv()
    _remote(stage_rs.at[0], rs_out.at[across, pl.ds(0, half)], rsend.at[4], rrecv.at[4],
            ldev).wait_recv()
    _remote(stage_rs.at[1], rs_out.at[across, pl.ds(half, half)], rsend.at[5], rrecv.at[5],
            rdev).wait_recv()
    for c in (to_r, to_l, via_r, via_l, fwd_r, fwd_l):
        c.wait_send()
    a2a.finish()
    own_part.wait()


def scatter_outputs(partial, share, na, nb, ntp):
    _, rows, cols = partial.shape
    _, block, width = share.shape
    share4 = share.reshape(na, nb, block, width)
    rs, new = pl.pallas_call(
        functools.partial(_out_kernel, na, nb, ntp),
        out_shape=(
            jax.ShapeDtypeStruct(partial.shape, partial.dtype),
            jax.ShapeDtypeStruct(share4.shape, share.dtype),
        ),
        in_specs=[pl.BlockSpec(memory_space=pl.ANY)] * 2,
        out_specs=(pl.BlockSpec(memory_space=pl.ANY), pl.BlockSpec(memory_space=pl.ANY)),
        scratch_shapes=[
            pltpu.VMEM((2, rows // 2, cols), partial.dtype),
            pltpu.SemaphoreType.DMA((6,)),
            pltpu.SemaphoreType.DMA((6,)),
            pltpu.SemaphoreType.DMA((1,)),
        ] + _seq_scratch(na, nb, block, width, share.dtype),
        compiler_params=pltpu.CompilerParams(collective_id=1, has_side_effects=True),
    )(partial, share4)
    return rs, new.reshape(share.shape)


def _attend_kernel(scale, lens_ref, q_ref, k_ref, v_ref, o_ref):
    chunk = q_ref.shape[0]
    capacity = k_ref.shape[0]
    held = lens_ref[0]
    first = pl.program_id(1) * chunk
    scores = lax.dot_general(
        q_ref[...], k_ref[...], (((1,), (1,)), ((), ())), preferred_element_type=jnp.float32
    ) * scale
    row_pos = first + lax.broadcasted_iota(jnp.int32, (chunk, capacity), 0)
    key_pos = lax.broadcasted_iota(jnp.int32, (chunk, capacity), 1)
    scores = jnp.where(key_pos <= held + row_pos, scores, MASKED)
    top = jnp.max(scores, axis=1, keepdims=True)
    weights = jnp.exp(scores - top)
    probs = (weights / jnp.sum(weights, axis=1, keepdims=True)).astype(jnp.bfloat16)
    o_ref[...] = jnp.dot(probs, v_ref[...], preferred_element_type=jnp.float32).astype(o_ref.dtype)


def attend(query, fresh, held_len, head_size, chunk=128):
    rows, qcols = query.shape
    capacity = fresh.shape[0]
    heads = qcols // head_size
    lens = jnp.reshape(held_len, (1,)).astype(jnp.int32)
    return pl.pallas_call(
        functools.partial(_attend_kernel, head_size ** (-0.5)),
        out_shape=jax.ShapeDtypeStruct((rows, qcols), jnp.bfloat16),
        grid_spec=pltpu.PrefetchScalarGridSpec(
            num_scalar_prefetch=1,
            grid=(heads, rows // chunk),
            in_specs=[
                pl.BlockSpec((chunk, head_size), lambda h, r, lens: (r, h)),
                pl.BlockSpec((capacity, head_size), lambda h, r, lens: (0, 0)),
                pl.BlockSpec((capacity, head_size), lambda h, r, lens: (0, 1)),
            ],
            out_specs=pl.BlockSpec((chunk, head_size), lambda h, r, lens: (r, h)),
        ),
        cost_estimate=pl.CostEstimate(
            flops=4 * rows * capacity * qcols,
            transcendentals=rows * capacity * heads,
            bytes_accessed=2 * (2 * rows * qcols + 2 * capacity * head_size),
        ),
    )(lens, query, fresh, fresh)


def _prep_kernel(ntp, lens_ref, holders_ref, sources_ref, cache_ref, kv_ref, fresh, kt, share_buf,
                 fresh32):
    t = lax.axis_index("tp")
    capacity, width = fresh.shape
    head_size = width // 2
    block_rows = cache_ref.shape[1]
    share = block_rows // ntp
    held = lens_ref[0]
    span = lens_ref[1]

    def place(b, carry):
        fresh32[pl.ds(pl.multiple_of(b * block_rows, block_rows), block_rows), :] = (
            cache_ref[holders_ref[b]].astype(jnp.float32))
        return carry

    lax.fori_loop(0, capacity // block_rows, place, 0)
    padded = jnp.concatenate(
        [kv_ref[...].astype(jnp.float32),
         jnp.zeros((capacity - kv_ref.shape[0], width), jnp.float32)], axis=0)
    shifted = pltpu.roll(padded, held, 0)
    positions = lax.broadcasted_iota(jnp.int32, (capacity, width), 0)
    full = jnp.where(positions < held, fresh32[...],
                     jnp.where(positions < held + span, shifted, 0.0))
    fresh32[...] = full
    fresh[...] = full.astype(fresh.dtype)
    kt[...] = fresh[:, pl.ds(0, head_size)].T

    def pick(d, carry):
        start = pl.multiple_of(sources_ref[d] * block_rows + t * share, share)
        share_buf[d] = fresh32[pl.ds(start, share), :].astype(share_buf.dtype)
        return carry

    lax.fori_loop(0, share_buf.shape[0], pick, 0)


def prepare(cache, keyval, lens, holders, sources, ntp):
    blocks, block_rows, width = cache.shape
    capacity = blocks * block_rows
    vmem = pl.BlockSpec(memory_space=pltpu.VMEM)
    smem = pl.BlockSpec(memory_space=pltpu.SMEM)
    return pl.pallas_call(
        functools.partial(_prep_kernel, ntp),
        out_shape=(
            jax.ShapeDtypeStruct((capacity, width), cache.dtype),
            jax.ShapeDtypeStruct((width // 2, capacity), cache.dtype),
            jax.ShapeDtypeStruct((blocks, block_rows // ntp, width), cache.dtype),
        ),
        in_specs=[smem, smem, smem, vmem, vmem],
        out_specs=(vmem, vmem, vmem),
        scratch_shapes=[pltpu.VMEM((capacity, width), jnp.float32)],
    )(lens, holders, sources, cache, keyval)


def _tail_kernel(na, nb, ntp, scale, chunk, lens_ref, q_ref, fresh, kt, share_buf, w_ref,
                 rs_out, new_out, ctx, part, psend, precv, plocal, stage, s1send, s1recv, s2send,
                 s2recv, slocal):
    s = lax.axis_index("seq")
    t = lax.axis_index("tp")
    rows, qcols = q_ref.shape
    capacity, width = fresh.shape
    head_size = width // 2
    share = share_buf.shape[1]
    heads = qcols // head_size
    cols = w_ref.shape[1] // ntp
    chunks = rows // chunk
    held = lens_ref[0]

    _greet(na, nb, s, t, *[lax.rem(t + k, ntp) for k in range(1, ntp)])
    sorted4 = share_buf.reshape(na, nb, share, width)
    a2a = SeqAllToAll(na, nb, s, t, sorted4, stage, lambda a_src: new_out.at[a_src],
                      (s1send, s1recv, s2send, s2recv, slocal))
    a2a.first()

    def slice_out(c, k):
        peer = lax.rem(t + k, ntp)
        return _remote(part.at[c, :, pl.ds(pl.multiple_of(peer * cols, cols), cols)],
                       rs_out.at[t, pl.ds(pl.multiple_of(c * chunk, chunk), chunk)],
                       psend.at[c, k], precv.at[c, k], {"seq": s, "tp": peer})

    def slice_in(c, k):
        sender = lax.rem(t + ntp - k, ntp)
        return _remote(part.at[c, :, pl.ds(0, cols)],
                       rs_out.at[sender, pl.ds(pl.multiple_of(c * chunk, chunk), chunk)],
                       psend.at[c, k], precv.at[c, k], {"seq": s, "tp": sender})

    def slice_own(c):
        return pltpu.make_async_copy(
            part.at[c, :, pl.ds(pl.multiple_of(t * cols, cols), cols)],
            rs_out.at[t, pl.ds(pl.multiple_of(c * chunk, chunk), chunk)], plocal.at[c])

    def do_chunk(c):
        first = pl.multiple_of(c * chunk, chunk)
        row_pos = first + lax.broadcasted_iota(jnp.int32, (chunk, capacity), 0)
        key_pos = lax.broadcasted_iota(jnp.int32, (chunk, capacity), 1)
        allowed = key_pos <= held + row_pos
        for h in range(heads):
            q = q_ref[pl.ds(first, chunk), pl.ds(h * head_size, head_size)]
            scores = jnp.dot(q, kt[...], preferred_element_type=jnp.float32) * scale
            scores = jnp.where(allowed, scores, MASKED)
            top = jnp.max(scores, axis=1, keepdims=True)
            weights = jnp.exp(scores - top)
            inv = 1.0 / jnp.sum(weights, axis=1, keepdims=True)
            probs = (weights * inv).astype(jnp.bfloat16)
            ctx[:, pl.ds(h * head_size, head_size)] = jnp.dot(
                probs, fresh[:, pl.ds(head_size, head_size)],
                preferred_element_type=jnp.float32).astype(ctx.dtype)
        part[c] = jnp.dot(ctx[...], w_ref[...], preferred_element_type=jnp.float32).astype(
            part.dtype)
        slice_own(c).start()
        for k in range(1, ntp):
            slice_out(c, k).start()

    do_chunk(0)
    a2a.second()

    def rest(c, carry):
        do_chunk(c)
        return carry

    lax.fori_loop(1, chunks, rest, 0)
    a2a.arrived()

    def drain(c, carry):
        for k in range(1, ntp):
            slice_in(c, k).wait_recv()
            slice_out(c, k).wait_send()
        slice_own(c).wait()
        return carry

    lax.fori_loop(0, chunks, drain, 0)
    a2a.finish()


def attend_and_scatter(query, cache, keyval, lens, holders, sources, w_out, na, nb, ntp,
                       chunk=128):
    rows, qcols = query.shape
    blocks, block_rows, width = cache.shape
    share = block_rows // ntp
    cols = w_out.shape[1] // ntp
    fresh, keys_t, sorted_share = prepare(cache, keyval, lens, holders, sources, ntp)
    vmem = pl.BlockSpec(memory_space=pltpu.VMEM)
    smem = pl.BlockSpec(memory_space=pltpu.SMEM)
    rs, new = pl.pallas_call(
        functools.partial(_tail_kernel, na, nb, ntp, (width // 2) ** (-0.5), chunk),
        out_shape=(
            jax.ShapeDtypeStruct((ntp, rows, cols), jnp.bfloat16),
            jax.ShapeDtypeStruct((na, nb, share, width), cache.dtype),
        ),
        in_specs=[smem, vmem, vmem, vmem, vmem, vmem],
        out_specs=(pl.BlockSpec(memory_space=pl.ANY), pl.BlockSpec(memory_space=pl.ANY)),
        scratch_shapes=[
            pltpu.VMEM((chunk, qcols), jnp.bfloat16),
            pltpu.VMEM((rows // chunk, chunk, w_out.shape[1]), jnp.bfloat16),
            pltpu.SemaphoreType.DMA((rows // chunk, ntp)),
            pltpu.SemaphoreType.DMA((rows // chunk, ntp)),
            pltpu.SemaphoreType.DMA((rows // chunk,)),
        ] + _seq_scratch(na, nb, share, width, cache.dtype),
        compiler_params=pltpu.CompilerParams(collective_id=1, has_side_effects=True),
    )(lens, query, fresh, keys_t, sorted_share, w_out)
    return rs, new.reshape(blocks, share, width)


def body(
    tokens,
    norm_gain,
    w_query,
    w_keyval,
    w_out,
    span_lens,
    cached_lens,
    old_table,
    new_table,
    old_cache,
):
    groups = lax.axis_size("seq")
    tp_count = lax.axis_size("tp")
    tp_index = lax.axis_index("tp")
    holders = old_table[0]
    held_len = cached_lens[0]
    span_len = span_lens[0]
    tok_rows, tok_cols = tokens.shape
    share = old_cache.shape[1]
    width = old_cache.shape[2]
    block_rows = share * tp_count
    capacity = groups * block_rows

    inner = min(groups, 8)
    outer = groups // inner
    query, keyval, cache_all = gather_inputs(
        tokens, old_cache, norm_gain, w_query, w_keyval, outer, inner, tp_count
    )
    cache_all = cache_all.reshape(groups, tp_count, share, width)

    targets = new_table[0]
    device_ids = lax.broadcasted_iota(jnp.int32, (groups, groups), 0)
    block_ids = lax.broadcasted_iota(jnp.int32, (groups, groups), 1)
    matches = targets[None, :] == device_ids
    sources = jnp.sum(jnp.where(matches, block_ids, 0), axis=1)
    lens = jnp.stack([held_len, span_len]).astype(jnp.int32)
    summed, new_cache = attend_and_scatter(
        query, cache_all.reshape(groups, block_rows, width), keyval, lens, holders, sources,
        w_out, outer, inner, tp_count
    )
    row_pos = lax.broadcasted_iota(jnp.int32, (tok_rows, 1), 0)
    summed = summed.astype(jnp.float32)
    total = tokens.astype(jnp.float32) + jnp.sum(summed, axis=0)
    mixed = jnp.where(row_pos < span_len, total, jnp.zeros_like(total)).astype(jnp.bfloat16)
    return (mixed, new_cache)


def solution(mesh):
    in_specs = (
        P("seq", "tp"),
        P(),
        P(None, "tp"),
        P(),
        P("tp", None),
        P("seq"),
        P("seq"),
        P("seq", None),
        P("seq", None),
        P("seq", "tp", None),
    )
    out_specs = (P("seq", "tp"), P("seq", "tp", None))
    return jax.shard_map(body, mesh=mesh, in_specs=in_specs, out_specs=out_specs, check_vma=False)
```

```python
import functools

import jax
import jax.numpy as jnp
from jax import lax
from jax.experimental import pallas as pl
from jax.experimental.pallas import tpu as pltpu
from jax.sharding import PartitionSpec as P

EPSILON = 1e-05
MASKED = -1e30


def normalize(rows, norm_gain):
    values = rows.astype(jnp.float32)
    average = jnp.mean(values, axis=1, keepdims=True)
    centred = values - average
    spread = jnp.mean(centred * centred, axis=1, keepdims=True)
    return (centred * lax.rsqrt(spread + EPSILON) * norm_gain).astype(jnp.bfloat16)


MESH = pl.DeviceIdType.MESH


def _remote(src, dst, send, recv, dev):
    return pltpu.make_async_remote_copy(
        src_ref=src, dst_ref=dst, send_sem=send, recv_sem=recv, device_id=dev, device_id_type=MESH
    )


def _greet(na, nb, s, t, *tp_peers):
    barrier = pltpu.get_barrier_semaphore()
    a = s // nb
    b = s % nb

    def one_b(k, carry):
        pl.semaphore_signal(barrier, inc=1, device_id={"seq": a * nb + lax.rem(b + k, nb), "tp": t},
                            device_id_type=MESH)
        return carry

    def one_a(k, carry):
        pl.semaphore_signal(barrier, inc=1, device_id={"seq": lax.rem(a + k, na) * nb + b, "tp": t},
                            device_id_type=MESH)
        return carry

    lax.fori_loop(1, nb, one_b, 0)
    lax.fori_loop(1, na, one_a, 0)
    for p in tp_peers:
        pl.semaphore_signal(barrier, inc=1, device_id={"seq": s, "tp": p}, device_id_type=MESH)
    pl.semaphore_wait(barrier, na + nb - 2 + len(tp_peers))


class SeqAllToAll:
    def __init__(self, na, nb, s, t, src, stage, dst, sems):
        self.na, self.nb, self.t, self.src, self.stage, self.dst = na, nb, t, src, stage, dst
        self.a = s // nb
        self.b = s % nb
        self.s1send, self.s1recv, self.s2send, self.s2recv, self.local = sems

    def _dev(self, a, b):
        return {"seq": a * self.nb + b, "tp": self.t}

    def _out1(self, k):
        peer = lax.rem(self.b + k, self.nb)
        return _remote(self.src.at[:, peer], self.stage.at[self.b], self.s1send.at[k],
                       self.s1recv.at[k], self._dev(self.a, peer))

    def _in1(self, k):
        sender = lax.rem(self.b + self.nb - k, self.nb)
        return _remote(self.src.at[:, self.b], self.stage.at[sender], self.s1send.at[k],
                       self.s1recv.at[k], self._dev(self.a, sender))

    def _out2(self, k):
        peer = lax.rem(self.a + k, self.na)
        return _remote(self.stage.at[:, peer], self.dst(self.a), self.s2send.at[k],
                       self.s2recv.at[k], self._dev(peer, self.b))

    def _in2(self, k):
        sender = lax.rem(self.a + self.na - k, self.na)
        return _remote(self.stage.at[:, self.a], self.dst(sender), self.s2send.at[k],
                       self.s2recv.at[k], self._dev(sender, self.b))

    def first(self):
        self.own1 = pltpu.make_async_copy(self.src.at[:, self.b], self.stage.at[self.b],
                                          self.local.at[0])
        self.own1.start()
        _loop(self.nb, lambda k: self._out1(k).start())

    def second(self):
        _loop(self.nb, lambda k: self._in1(k).wait_recv())
        self.own1.wait()
        self.own2 = pltpu.make_async_copy(self.stage.at[:, self.a], self.dst(self.a),
                                          self.local.at[1])
        self.own2.start()
        _loop(self.na, lambda k: self._out2(k).start())

    def arrived(self):
        _loop(self.na, lambda k: self._in2(k).wait_recv())
        self.own2.wait()

    def finish(self):
        _loop(self.nb, lambda k: self._out1(k).wait_send())
        _loop(self.na, lambda k: self._out2(k).wait_send())


def _seq_scratch(na, nb, share, width, dtype):
    return [
        pltpu.VMEM((nb, na, share, width), dtype),
        pltpu.SemaphoreType.DMA((nb,)),
        pltpu.SemaphoreType.DMA((nb,)),
        pltpu.SemaphoreType.DMA((na,)),
        pltpu.SemaphoreType.DMA((na,)),
        pltpu.SemaphoreType.DMA((2,)),
    ]


def _loop(n, fn):
    def step(k, carry):
        fn(k)
        return carry

    lax.fori_loop(1, n, step, 0)


def _in_kernel(na, nb, ntp, tok_ref, cache_ref, gain_ref, wq_ref, wkv_ref, q_out, kv_out,
               cache_out, tok_all, tsend, trecv, csend, crecv, lsem, stage, s1send, s1recv,
               s2send, s2recv, slocal):
    s = lax.axis_index("seq")
    t = lax.axis_index("tp")
    right = lax.rem(t + 1, ntp)
    left = lax.rem(t + ntp - 1, ntp)
    across = lax.rem(t + 2, ntp)
    rdev = {"seq": s, "tp": right}
    ldev = {"seq": s, "tp": left}
    rows, cols = tok_ref.shape
    half = rows // 2
    _greet(na, nb, s, t, left, right, across)

    def tok_cols(p):
        return pl.ds(pl.multiple_of(p * cols, cols), cols)

    a2a = SeqAllToAll(na, nb, s, t, cache_ref, stage, lambda a_src: cache_out.at[a_src, :, t],
                      (s1send, s1recv, s2send, s2recv, slocal))
    a2a.first()

    own_tok = pltpu.make_async_copy(tok_ref, tok_all.at[:, tok_cols(t)], lsem.at[0])
    own_tok.start()
    tok_r = _remote(tok_ref, tok_all.at[:, tok_cols(t)], tsend.at[0], trecv.at[0], rdev)
    tok_l = _remote(tok_ref, tok_all.at[:, tok_cols(t)], tsend.at[1], trecv.at[1], ldev)
    tok_r.start()
    tok_l.start()

    a2a.second()

    _remote(tok_ref, tok_all.at[:, tok_cols(left)], tsend.at[0], trecv.at[0], ldev).wait_recv()
    fwd_r = _remote(tok_all.at[pl.ds(0, half), tok_cols(left)],
                    tok_all.at[pl.ds(0, half), tok_cols(left)], tsend.at[2], trecv.at[2], rdev)
    fwd_r.start()
    _remote(tok_ref, tok_all.at[:, tok_cols(right)], tsend.at[1], trecv.at[1], rdev).wait_recv()
    fwd_l = _remote(tok_all.at[pl.ds(half, half), tok_cols(right)],
                    tok_all.at[pl.ds(half, half), tok_cols(right)], tsend.at[3], trecv.at[3], ldev)
    fwd_l.start()

    a2a.arrived()
    flat = cache_out.reshape(na * nb, ntp, *cache_out.shape[3:])
    mine = flat.at[:, t]

    def cache_to(k):
        peer = lax.rem(t + k, ntp)
        return _remote(mine, mine, csend.at[k], crecv.at[k], {"seq": s, "tp": peer})

    def cache_from(k):
        sender = lax.rem(t + ntp - k, ntp)
        return _remote(mine, flat.at[:, sender], csend.at[k], crecv.at[k],
                       {"seq": s, "tp": sender})

    for k in range(1, ntp):
        cache_to(k).start()

    _remote(tok_ref.at[pl.ds(0, half)], tok_all.at[pl.ds(0, half), tok_cols(across)],
            tsend.at[2], trecv.at[2], ldev).wait_recv()
    _remote(tok_ref.at[pl.ds(half, half)], tok_all.at[pl.ds(half, half), tok_cols(across)],
            tsend.at[3], trecv.at[3], rdev).wait_recv()
    own_tok.wait()

    chunk = 128

    def project(c, carry):
        first = pl.multiple_of(c * chunk, chunk)
        values = tok_all[pl.ds(first, chunk), :].astype(jnp.float32)
        average = jnp.mean(values, axis=1, keepdims=True)
        centred = values - average
        spread = jnp.mean(centred * centred, axis=1, keepdims=True)
        normed = (centred * lax.rsqrt(spread + EPSILON) * gain_ref[...]).astype(jnp.bfloat16)
        q_out[pl.ds(first, chunk), :] = jnp.dot(
            normed, wq_ref[...], preferred_element_type=jnp.float32).astype(q_out.dtype)
        kv_out[pl.ds(first, chunk), :] = jnp.dot(
            normed, wkv_ref[...], preferred_element_type=jnp.float32).astype(kv_out.dtype)
        return carry

    lax.fori_loop(0, rows // chunk, project, 0)

    for k in range(1, ntp):
        cache_from(k).wait_recv()
    for c in (tok_r, tok_l, fwd_r, fwd_l):
        c.wait_send()
    for k in range(1, ntp):
        cache_to(k).wait_send()
    a2a.finish()


def gather_inputs(tokens, old_cache, norm_gain, w_query, w_keyval, na, nb, ntp):
    rows, cols = tokens.shape
    _, share, width = old_cache.shape
    cache4 = old_cache.reshape(na, nb, share, width)
    vmem = pl.BlockSpec(memory_space=pltpu.VMEM)
    anywhere = pl.BlockSpec(memory_space=pl.ANY)
    return pl.pallas_call(
        functools.partial(_in_kernel, na, nb, ntp),
        out_shape=(
            jax.ShapeDtypeStruct((rows, w_query.shape[1]), jnp.bfloat16),
            jax.ShapeDtypeStruct((rows, w_keyval.shape[1]), jnp.bfloat16),
            jax.ShapeDtypeStruct((na, nb, ntp, share, width), old_cache.dtype),
        ),
        in_specs=[anywhere, anywhere, vmem, vmem, vmem],
        out_specs=(vmem, vmem, anywhere),
        scratch_shapes=[
            pltpu.VMEM((rows, ntp * cols), tokens.dtype),
            pltpu.SemaphoreType.DMA((4,)),
            pltpu.SemaphoreType.DMA((4,)),
            pltpu.SemaphoreType.DMA((ntp,)),
            pltpu.SemaphoreType.DMA((ntp,)),
            pltpu.SemaphoreType.DMA((2,)),
        ] + _seq_scratch(na, nb, share, width, old_cache.dtype),
        compiler_params=pltpu.CompilerParams(collective_id=0, has_side_effects=True),
    )(tokens, cache4, norm_gain.reshape(1, -1).astype(jnp.float32), w_query, w_keyval)


def _out_kernel(na, nb, ntp, part_ref, share_ref, rs_out, new_out, stage_rs, rsend, rrecv, lsem,
                stage, s1send, s1recv, s2send, s2recv, slocal):
    s = lax.axis_index("seq")
    t = lax.axis_index("tp")
    right = lax.rem(t + 1, ntp)
    left = lax.rem(t + ntp - 1, ntp)
    across = lax.rem(t + 2, ntp)
    rdev = {"seq": s, "tp": right}
    ldev = {"seq": s, "tp": left}
    half = part_ref.shape[1] // 2
    _greet(na, nb, s, t, left, right)

    a2a = SeqAllToAll(na, nb, s, t, share_ref, stage, lambda a_src: new_out.at[a_src],
                      (s1send, s1recv, s2send, s2recv, slocal))
    a2a.first()

    own_part = pltpu.make_async_copy(part_ref.at[t], rs_out.at[t], lsem.at[0])
    own_part.start()
    to_r = _remote(part_ref.at[right], rs_out.at[t], rsend.at[0], rrecv.at[0], rdev)
    to_l = _remote(part_ref.at[left], rs_out.at[t], rsend.at[1], rrecv.at[1], ldev)
    via_r = _remote(part_ref.at[across, pl.ds(0, half)], stage_rs.at[0], rsend.at[2], rrecv.at[2],
                    rdev)
    via_l = _remote(part_ref.at[across, pl.ds(half, half)], stage_rs.at[1], rsend.at[3],
                    rrecv.at[3], ldev)
    for c in (to_r, to_l, via_r, via_l):
        c.start()

    a2a.second()

    _remote(part_ref.at[across, pl.ds(0, half)], stage_rs.at[0], rsend.at[2], rrecv.at[2],
            ldev).wait_recv()
    fwd_r = _remote(stage_rs.at[0], rs_out.at[left, pl.ds(0, half)], rsend.at[4], rrecv.at[4],
                    rdev)
    fwd_r.start()
    _remote(part_ref.at[across, pl.ds(half, half)], stage_rs.at[1], rsend.at[3], rrecv.at[3],
            rdev).wait_recv()
    fwd_l = _remote(stage_rs.at[1], rs_out.at[right, pl.ds(half, half)], rsend.at[5],
                    rrecv.at[5], ldev)
    fwd_l.start()

    a2a.arrived()
    _remote(part_ref.at[t], rs_out.at[left], rsend.at[0], rrecv.at[0], ldev).wait_recv()
    _remote(part_ref.at[t], rs_out.at[right], rsend.at[1], rrecv.at[1], rdev).wait_recv()
    _remote(stage_rs.at[0], rs_out.at[across, pl.ds(0, half)], rsend.at[4], rrecv.at[4],
            ldev).wait_recv()
    _remote(stage_rs.at[1], rs_out.at[across, pl.ds(half, half)], rsend.at[5], rrecv.at[5],
            rdev).wait_recv()
    for c in (to_r, to_l, via_r, via_l, fwd_r, fwd_l):
        c.wait_send()
    a2a.finish()
    own_part.wait()


def scatter_outputs(partial, share, na, nb, ntp):
    _, rows, cols = partial.shape
    _, block, width = share.shape
    share4 = share.reshape(na, nb, block, width)
    rs, new = pl.pallas_call(
        functools.partial(_out_kernel, na, nb, ntp),
        out_shape=(
            jax.ShapeDtypeStruct(partial.shape, partial.dtype),
            jax.ShapeDtypeStruct(share4.shape, share.dtype),
        ),
        in_specs=[pl.BlockSpec(memory_space=pl.ANY)] * 2,
        out_specs=(pl.BlockSpec(memory_space=pl.ANY), pl.BlockSpec(memory_space=pl.ANY)),
        scratch_shapes=[
            pltpu.VMEM((2, rows // 2, cols), partial.dtype),
            pltpu.SemaphoreType.DMA((6,)),
            pltpu.SemaphoreType.DMA((6,)),
            pltpu.SemaphoreType.DMA((1,)),
        ] + _seq_scratch(na, nb, block, width, share.dtype),
        compiler_params=pltpu.CompilerParams(collective_id=1, has_side_effects=True),
    )(partial, share4)
    return rs, new.reshape(share.shape)


def _attend_kernel(scale, lens_ref, q_ref, k_ref, v_ref, o_ref):
    chunk = q_ref.shape[0]
    capacity = k_ref.shape[0]
    held = lens_ref[0]
    first = pl.program_id(1) * chunk
    scores = lax.dot_general(
        q_ref[...], k_ref[...], (((1,), (1,)), ((), ())), preferred_element_type=jnp.float32
    ) * scale
    row_pos = first + lax.broadcasted_iota(jnp.int32, (chunk, capacity), 0)
    key_pos = lax.broadcasted_iota(jnp.int32, (chunk, capacity), 1)
    scores = jnp.where(key_pos <= held + row_pos, scores, MASKED)
    top = jnp.max(scores, axis=1, keepdims=True)
    weights = jnp.exp(scores - top)
    probs = (weights / jnp.sum(weights, axis=1, keepdims=True)).astype(jnp.bfloat16)
    o_ref[...] = jnp.dot(probs, v_ref[...], preferred_element_type=jnp.float32).astype(o_ref.dtype)


def attend(query, fresh, held_len, head_size, chunk=128):
    rows, qcols = query.shape
    capacity = fresh.shape[0]
    heads = qcols // head_size
    lens = jnp.reshape(held_len, (1,)).astype(jnp.int32)
    return pl.pallas_call(
        functools.partial(_attend_kernel, head_size ** (-0.5)),
        out_shape=jax.ShapeDtypeStruct((rows, qcols), jnp.bfloat16),
        grid_spec=pltpu.PrefetchScalarGridSpec(
            num_scalar_prefetch=1,
            grid=(heads, rows // chunk),
            in_specs=[
                pl.BlockSpec((chunk, head_size), lambda h, r, lens: (r, h)),
                pl.BlockSpec((capacity, head_size), lambda h, r, lens: (0, 0)),
                pl.BlockSpec((capacity, head_size), lambda h, r, lens: (0, 1)),
            ],
            out_specs=pl.BlockSpec((chunk, head_size), lambda h, r, lens: (r, h)),
        ),
        cost_estimate=pl.CostEstimate(
            flops=4 * rows * capacity * qcols,
            transcendentals=rows * capacity * heads,
            bytes_accessed=2 * (2 * rows * qcols + 2 * capacity * head_size),
        ),
    )(lens, query, fresh, fresh)


def _prep_kernel(ntp, lens_ref, holders_ref, sources_ref, cache_ref, kv_ref, fresh, kt, share_buf,
                 fresh32):
    t = lax.axis_index("tp")
    capacity, width = fresh.shape
    head_size = width // 2
    block_rows = cache_ref.shape[1]
    share = block_rows // ntp
    held = lens_ref[0]
    span = lens_ref[1]

    def place(b, carry):
        fresh32[pl.ds(pl.multiple_of(b * block_rows, block_rows), block_rows), :] = (
            cache_ref[holders_ref[b]].astype(jnp.float32))
        return carry

    lax.fori_loop(0, capacity // block_rows, place, 0)
    padded = jnp.concatenate(
        [kv_ref[...].astype(jnp.float32),
         jnp.zeros((capacity - kv_ref.shape[0], width), jnp.float32)], axis=0)
    shifted = pltpu.roll(padded, held, 0)
    positions = lax.broadcasted_iota(jnp.int32, (capacity, width), 0)
    full = jnp.where(positions < held, fresh32[...],
                     jnp.where(positions < held + span, shifted, 0.0))
    fresh32[...] = full
    fresh[...] = full.astype(fresh.dtype)
    kt[...] = fresh[:, pl.ds(0, head_size)].T

    def pick(d, carry):
        start = pl.multiple_of(sources_ref[d] * block_rows + t * share, share)
        share_buf[d] = fresh32[pl.ds(start, share), :].astype(share_buf.dtype)
        return carry

    lax.fori_loop(0, share_buf.shape[0], pick, 0)


def prepare(cache, keyval, lens, holders, sources, ntp):
    blocks, block_rows, width = cache.shape
    capacity = blocks * block_rows
    vmem = pl.BlockSpec(memory_space=pltpu.VMEM)
    smem = pl.BlockSpec(memory_space=pltpu.SMEM)
    return pl.pallas_call(
        functools.partial(_prep_kernel, ntp),
        out_shape=(
            jax.ShapeDtypeStruct((capacity, width), cache.dtype),
            jax.ShapeDtypeStruct((width // 2, capacity), cache.dtype),
            jax.ShapeDtypeStruct((blocks, block_rows // ntp, width), cache.dtype),
        ),
        in_specs=[smem, smem, smem, vmem, vmem],
        out_specs=(vmem, vmem, vmem),
        scratch_shapes=[pltpu.VMEM((capacity, width), jnp.float32)],
    )(lens, holders, sources, cache, keyval)


def _tail_kernel(na, nb, ntp, scale, chunk, lens_ref, q_ref, fresh, kt, share_buf, w_ref,
                 rs_out, new_out, ctx, part, psend, precv, plocal, stage, s1send, s1recv, s2send,
                 s2recv, slocal):
    s = lax.axis_index("seq")
    t = lax.axis_index("tp")
    rows, qcols = q_ref.shape
    capacity, width = fresh.shape
    head_size = width // 2
    share = share_buf.shape[1]
    heads = qcols // head_size
    cols = w_ref.shape[1] // ntp
    chunks = rows // chunk
    held = lens_ref[0]

    _greet(na, nb, s, t, *[lax.rem(t + k, ntp) for k in range(1, ntp)])
    sorted4 = share_buf.reshape(na, nb, share, width)
    a2a = SeqAllToAll(na, nb, s, t, sorted4, stage, lambda a_src: new_out.at[a_src],
                      (s1send, s1recv, s2send, s2recv, slocal))
    a2a.first()

    def slice_out(c, k):
        peer = lax.rem(t + k, ntp)
        return _remote(part.at[c, :, pl.ds(pl.multiple_of(peer * cols, cols), cols)],
                       rs_out.at[t, pl.ds(pl.multiple_of(c * chunk, chunk), chunk)],
                       psend.at[c, k], precv.at[c, k], {"seq": s, "tp": peer})

    def slice_in(c, k):
        sender = lax.rem(t + ntp - k, ntp)
        return _remote(part.at[c, :, pl.ds(0, cols)],
                       rs_out.at[sender, pl.ds(pl.multiple_of(c * chunk, chunk), chunk)],
                       psend.at[c, k], precv.at[c, k], {"seq": s, "tp": sender})

    def slice_own(c):
        return pltpu.make_async_copy(
            part.at[c, :, pl.ds(pl.multiple_of(t * cols, cols), cols)],
            rs_out.at[t, pl.ds(pl.multiple_of(c * chunk, chunk), chunk)], plocal.at[c])

    def do_chunk(c):
        first = pl.multiple_of(c * chunk, chunk)
        row_pos = first + lax.broadcasted_iota(jnp.int32, (chunk, capacity), 0)
        key_pos = lax.broadcasted_iota(jnp.int32, (chunk, capacity), 1)
        allowed = key_pos <= held + row_pos
        for h in range(heads):
            q = q_ref[pl.ds(first, chunk), pl.ds(h * head_size, head_size)]
            scores = jnp.dot(q, kt[...], preferred_element_type=jnp.float32) * scale
            scores = jnp.where(allowed, scores, MASKED)
            top = jnp.max(scores, axis=1, keepdims=True)
            weights = jnp.exp(scores - top)
            inv = 1.0 / jnp.sum(weights, axis=1, keepdims=True)
            probs = (weights * inv).astype(jnp.bfloat16)
            ctx[:, pl.ds(h * head_size, head_size)] = jnp.dot(
                probs, fresh[:, pl.ds(head_size, head_size)],
                preferred_element_type=jnp.float32).astype(ctx.dtype)
        part[c] = jnp.dot(ctx[...], w_ref[...], preferred_element_type=jnp.float32).astype(
            part.dtype)
        slice_own(c).start()
        for k in range(1, ntp):
            slice_out(c, k).start()

    do_chunk(0)
    a2a.second()

    def rest(c, carry):
        do_chunk(c)
        return carry

    lax.fori_loop(1, chunks, rest, 0)
    a2a.arrived()

    def drain(c, carry):
        for k in range(1, ntp):
            slice_in(c, k).wait_recv()
            slice_out(c, k).wait_send()
        slice_own(c).wait()
        return carry

    lax.fori_loop(0, chunks, drain, 0)
    a2a.finish()


def attend_and_scatter(query, cache, keyval, lens, holders, sources, w_out, na, nb, ntp,
                       chunk=64):
    rows, qcols = query.shape
    blocks, block_rows, width = cache.shape
    share = block_rows // ntp
    cols = w_out.shape[1] // ntp
    fresh, keys_t, sorted_share = prepare(cache, keyval, lens, holders, sources, ntp)
    vmem = pl.BlockSpec(memory_space=pltpu.VMEM)
    smem = pl.BlockSpec(memory_space=pltpu.SMEM)
    rs, new = pl.pallas_call(
        functools.partial(_tail_kernel, na, nb, ntp, (width // 2) ** (-0.5), chunk),
        out_shape=(
            jax.ShapeDtypeStruct((ntp, rows, cols), jnp.bfloat16),
            jax.ShapeDtypeStruct((na, nb, share, width), cache.dtype),
        ),
        in_specs=[smem, vmem, vmem, vmem, vmem, vmem],
        out_specs=(pl.BlockSpec(memory_space=pl.ANY), pl.BlockSpec(memory_space=pl.ANY)),
        scratch_shapes=[
            pltpu.VMEM((chunk, qcols), jnp.bfloat16),
            pltpu.VMEM((rows // chunk, chunk, w_out.shape[1]), jnp.bfloat16),
            pltpu.SemaphoreType.DMA((rows // chunk, ntp)),
            pltpu.SemaphoreType.DMA((rows // chunk, ntp)),
            pltpu.SemaphoreType.DMA((rows // chunk,)),
        ] + _seq_scratch(na, nb, share, width, cache.dtype),
        compiler_params=pltpu.CompilerParams(collective_id=1, has_side_effects=True),
    )(lens, query, fresh, keys_t, sorted_share, w_out)
    return rs, new.reshape(blocks, share, width)


def body(
    tokens,
    norm_gain,
    w_query,
    w_keyval,
    w_out,
    span_lens,
    cached_lens,
    old_table,
    new_table,
    old_cache,
):
    groups = lax.axis_size("seq")
    tp_count = lax.axis_size("tp")
    tp_index = lax.axis_index("tp")
    holders = old_table[0]
    held_len = cached_lens[0]
    span_len = span_lens[0]
    tok_rows, tok_cols = tokens.shape
    share = old_cache.shape[1]
    width = old_cache.shape[2]
    block_rows = share * tp_count
    capacity = groups * block_rows

    inner = min(groups, 8)
    outer = groups // inner
    query, keyval, cache_all = gather_inputs(
        tokens, old_cache, norm_gain, w_query, w_keyval, outer, inner, tp_count
    )
    cache_all = cache_all.reshape(groups, tp_count, share, width)

    targets = new_table[0]
    device_ids = lax.broadcasted_iota(jnp.int32, (groups, groups), 0)
    block_ids = lax.broadcasted_iota(jnp.int32, (groups, groups), 1)
    matches = targets[None, :] == device_ids
    sources = jnp.sum(jnp.where(matches, block_ids, 0), axis=1)
    lens = jnp.stack([held_len, span_len]).astype(jnp.int32)
    summed, new_cache = attend_and_scatter(
        query, cache_all.reshape(groups, block_rows, width), keyval, lens, holders, sources,
        w_out, outer, inner, tp_count
    )
    row_pos = lax.broadcasted_iota(jnp.int32, (tok_rows, 1), 0)
    total = tokens.astype(jnp.float32)
    for p in range(tp_count):
        total = total + summed[p].astype(jnp.float32)
    mixed = jnp.where(row_pos < span_len, total, jnp.zeros_like(total)).astype(jnp.bfloat16)
    return (mixed, new_cache)


def solution(mesh):
    in_specs = (
        P("seq", "tp"),
        P(),
        P(None, "tp"),
        P(),
        P("tp", None),
        P("seq"),
        P("seq"),
        P("seq", None),
        P("seq", None),
        P("seq", "tp", None),
    )
    out_specs = (P("seq", "tp"), P("seq", "tp", None))
    return jax.shard_map(body, mesh=mesh, in_specs=in_specs, out_specs=out_specs, check_vma=False)
```

```python
import functools

import jax
import jax.numpy as jnp
from jax import lax
from jax.experimental import pallas as pl
from jax.experimental.pallas import tpu as pltpu
from jax.sharding import PartitionSpec as P

EPSILON = 1e-05
MASKED = -1e30


def normalize(rows, norm_gain):
    values = rows.astype(jnp.float32)
    average = jnp.mean(values, axis=1, keepdims=True)
    centred = values - average
    spread = jnp.mean(centred * centred, axis=1, keepdims=True)
    return (centred * lax.rsqrt(spread + EPSILON) * norm_gain).astype(jnp.bfloat16)


MESH = pl.DeviceIdType.MESH


def _remote(src, dst, send, recv, dev):
    return pltpu.make_async_remote_copy(
        src_ref=src, dst_ref=dst, send_sem=send, recv_sem=recv, device_id=dev, device_id_type=MESH
    )


def _greet(na, nb, s, t, *tp_peers):
    barrier = pltpu.get_barrier_semaphore()
    a = s // nb
    b = s % nb

    def one_b(k, carry):
        pl.semaphore_signal(barrier, inc=1, device_id={"seq": a * nb + lax.rem(b + k, nb), "tp": t},
                            device_id_type=MESH)
        return carry

    def one_a(k, carry):
        pl.semaphore_signal(barrier, inc=1, device_id={"seq": lax.rem(a + k, na) * nb + b, "tp": t},
                            device_id_type=MESH)
        return carry

    lax.fori_loop(1, nb, one_b, 0)
    lax.fori_loop(1, na, one_a, 0)
    for p in tp_peers:
        pl.semaphore_signal(barrier, inc=1, device_id={"seq": s, "tp": p}, device_id_type=MESH)
    pl.semaphore_wait(barrier, na + nb - 2 + len(tp_peers))


class SeqAllToAll:
    def __init__(self, na, nb, s, t, src, stage, dst, sems):
        self.na, self.nb, self.t, self.src, self.stage, self.dst = na, nb, t, src, stage, dst
        self.a = s // nb
        self.b = s % nb
        self.s1send, self.s1recv, self.s2send, self.s2recv, self.local = sems

    def _dev(self, a, b):
        return {"seq": a * self.nb + b, "tp": self.t}

    def _out1(self, k):
        peer = lax.rem(self.b + k, self.nb)
        return _remote(self.src.at[:, peer], self.stage.at[self.b], self.s1send.at[k],
                       self.s1recv.at[k], self._dev(self.a, peer))

    def _in1(self, k):
        sender = lax.rem(self.b + self.nb - k, self.nb)
        return _remote(self.src.at[:, self.b], self.stage.at[sender], self.s1send.at[k],
                       self.s1recv.at[k], self._dev(self.a, sender))

    def _out2(self, k):
        peer = lax.rem(self.a + k, self.na)
        return _remote(self.stage.at[:, peer], self.dst(self.a), self.s2send.at[k],
                       self.s2recv.at[k], self._dev(peer, self.b))

    def _in2(self, k):
        sender = lax.rem(self.a + self.na - k, self.na)
        return _remote(self.stage.at[:, self.a], self.dst(sender), self.s2send.at[k],
                       self.s2recv.at[k], self._dev(sender, self.b))

    def first(self):
        self.own1 = pltpu.make_async_copy(self.src.at[:, self.b], self.stage.at[self.b],
                                          self.local.at[0])
        self.own1.start()
        _loop(self.nb, lambda k: self._out1(k).start())

    def second(self):
        _loop(self.nb, lambda k: self._in1(k).wait_recv())
        self.own1.wait()
        self.own2 = pltpu.make_async_copy(self.stage.at[:, self.a], self.dst(self.a),
                                          self.local.at[1])
        self.own2.start()
        _loop(self.na, lambda k: self._out2(k).start())

    def arrived(self):
        _loop(self.na, lambda k: self._in2(k).wait_recv())
        self.own2.wait()

    def finish(self):
        _loop(self.nb, lambda k: self._out1(k).wait_send())
        _loop(self.na, lambda k: self._out2(k).wait_send())


def _seq_scratch(na, nb, share, width, dtype):
    return [
        pltpu.VMEM((nb, na, share, width), dtype),
        pltpu.SemaphoreType.DMA((nb,)),
        pltpu.SemaphoreType.DMA((nb,)),
        pltpu.SemaphoreType.DMA((na,)),
        pltpu.SemaphoreType.DMA((na,)),
        pltpu.SemaphoreType.DMA((2,)),
    ]


def _loop(n, fn):
    def step(k, carry):
        fn(k)
        return carry

    lax.fori_loop(1, n, step, 0)


def _in_kernel(na, nb, ntp, tok_ref, cache_ref, gain_ref, wq_ref, wkv_ref, q_out, kv_out,
               cache_out, tok_all, tsend, trecv, csend, crecv, lsem, stage, s1send, s1recv,
               s2send, s2recv, slocal):
    s = lax.axis_index("seq")
    t = lax.axis_index("tp")
    right = lax.rem(t + 1, ntp)
    left = lax.rem(t + ntp - 1, ntp)
    across = lax.rem(t + 2, ntp)
    rdev = {"seq": s, "tp": right}
    ldev = {"seq": s, "tp": left}
    rows, cols = tok_ref.shape
    half = rows // 2
    _greet(na, nb, s, t, left, right, across)

    def tok_cols(p):
        return pl.ds(pl.multiple_of(p * cols, cols), cols)

    a2a = SeqAllToAll(na, nb, s, t, cache_ref, stage, lambda a_src: cache_out.at[a_src, :, t],
                      (s1send, s1recv, s2send, s2recv, slocal))
    a2a.first()

    own_tok = pltpu.make_async_copy(tok_ref, tok_all.at[:, tok_cols(t)], lsem.at[0])
    own_tok.start()
    tok_r = _remote(tok_ref, tok_all.at[:, tok_cols(t)], tsend.at[0], trecv.at[0], rdev)
    tok_l = _remote(tok_ref, tok_all.at[:, tok_cols(t)], tsend.at[1], trecv.at[1], ldev)
    tok_r.start()
    tok_l.start()

    a2a.second()

    _remote(tok_ref, tok_all.at[:, tok_cols(left)], tsend.at[0], trecv.at[0], ldev).wait_recv()
    fwd_r = _remote(tok_all.at[pl.ds(0, half), tok_cols(left)],
                    tok_all.at[pl.ds(0, half), tok_cols(left)], tsend.at[2], trecv.at[2], rdev)
    fwd_r.start()
    _remote(tok_ref, tok_all.at[:, tok_cols(right)], tsend.at[1], trecv.at[1], rdev).wait_recv()
    fwd_l = _remote(tok_all.at[pl.ds(half, half), tok_cols(right)],
                    tok_all.at[pl.ds(half, half), tok_cols(right)], tsend.at[3], trecv.at[3], ldev)
    fwd_l.start()

    a2a.arrived()
    flat = cache_out.reshape(na * nb, ntp, *cache_out.shape[3:])
    mine = flat.at[:, t]

    def cache_to(k):
        peer = lax.rem(t + k, ntp)
        return _remote(mine, mine, csend.at[k], crecv.at[k], {"seq": s, "tp": peer})

    def cache_from(k):
        sender = lax.rem(t + ntp - k, ntp)
        return _remote(mine, flat.at[:, sender], csend.at[k], crecv.at[k],
                       {"seq": s, "tp": sender})

    for k in range(1, ntp):
        cache_to(k).start()

    _remote(tok_ref.at[pl.ds(0, half)], tok_all.at[pl.ds(0, half), tok_cols(across)],
            tsend.at[2], trecv.at[2], ldev).wait_recv()
    _remote(tok_ref.at[pl.ds(half, half)], tok_all.at[pl.ds(half, half), tok_cols(across)],
            tsend.at[3], trecv.at[3], rdev).wait_recv()
    own_tok.wait()

    chunk = 128

    def project(c, carry):
        first = pl.multiple_of(c * chunk, chunk)
        values = tok_all[pl.ds(first, chunk), :].astype(jnp.float32)
        average = jnp.mean(values, axis=1, keepdims=True)
        centred = values - average
        spread = jnp.mean(centred * centred, axis=1, keepdims=True)
        normed = (centred * lax.rsqrt(spread + EPSILON) * gain_ref[...]).astype(jnp.bfloat16)
        q_out[pl.ds(first, chunk), :] = jnp.dot(
            normed, wq_ref[...], preferred_element_type=jnp.float32).astype(q_out.dtype)
        kv_out[pl.ds(first, chunk), :] = jnp.dot(
            normed, wkv_ref[...], preferred_element_type=jnp.float32).astype(kv_out.dtype)
        return carry

    lax.fori_loop(0, rows // chunk, project, 0)

    for k in range(1, ntp):
        cache_from(k).wait_recv()
    for c in (tok_r, tok_l, fwd_r, fwd_l):
        c.wait_send()
    for k in range(1, ntp):
        cache_to(k).wait_send()
    a2a.finish()


def gather_inputs(tokens, old_cache, norm_gain, w_query, w_keyval, na, nb, ntp):
    rows, cols = tokens.shape
    _, share, width = old_cache.shape
    cache4 = old_cache.reshape(na, nb, share, width)
    vmem = pl.BlockSpec(memory_space=pltpu.VMEM)
    anywhere = pl.BlockSpec(memory_space=pl.ANY)
    return pl.pallas_call(
        functools.partial(_in_kernel, na, nb, ntp),
        out_shape=(
            jax.ShapeDtypeStruct((rows, w_query.shape[1]), jnp.bfloat16),
            jax.ShapeDtypeStruct((rows, w_keyval.shape[1]), jnp.bfloat16),
            jax.ShapeDtypeStruct((na, nb, ntp, share, width), old_cache.dtype),
        ),
        in_specs=[anywhere, anywhere, vmem, vmem, vmem],
        out_specs=(vmem, vmem, anywhere),
        scratch_shapes=[
            pltpu.VMEM((rows, ntp * cols), tokens.dtype),
            pltpu.SemaphoreType.DMA((4,)),
            pltpu.SemaphoreType.DMA((4,)),
            pltpu.SemaphoreType.DMA((ntp,)),
            pltpu.SemaphoreType.DMA((ntp,)),
            pltpu.SemaphoreType.DMA((2,)),
        ] + _seq_scratch(na, nb, share, width, old_cache.dtype),
        compiler_params=pltpu.CompilerParams(collective_id=0, has_side_effects=True),
    )(tokens, cache4, norm_gain.reshape(1, -1).astype(jnp.float32), w_query, w_keyval)


def _out_kernel(na, nb, ntp, part_ref, share_ref, rs_out, new_out, stage_rs, rsend, rrecv, lsem,
                stage, s1send, s1recv, s2send, s2recv, slocal):
    s = lax.axis_index("seq")
    t = lax.axis_index("tp")
    right = lax.rem(t + 1, ntp)
    left = lax.rem(t + ntp - 1, ntp)
    across = lax.rem(t + 2, ntp)
    rdev = {"seq": s, "tp": right}
    ldev = {"seq": s, "tp": left}
    half = part_ref.shape[1] // 2
    _greet(na, nb, s, t, left, right)

    a2a = SeqAllToAll(na, nb, s, t, share_ref, stage, lambda a_src: new_out.at[a_src],
                      (s1send, s1recv, s2send, s2recv, slocal))
    a2a.first()

    own_part = pltpu.make_async_copy(part_ref.at[t], rs_out.at[t], lsem.at[0])
    own_part.start()
    to_r = _remote(part_ref.at[right], rs_out.at[t], rsend.at[0], rrecv.at[0], rdev)
    to_l = _remote(part_ref.at[left], rs_out.at[t], rsend.at[1], rrecv.at[1], ldev)
    via_r = _remote(part_ref.at[across, pl.ds(0, half)], stage_rs.at[0], rsend.at[2], rrecv.at[2],
                    rdev)
    via_l = _remote(part_ref.at[across, pl.ds(half, half)], stage_rs.at[1], rsend.at[3],
                    rrecv.at[3], ldev)
    for c in (to_r, to_l, via_r, via_l):
        c.start()

    a2a.second()

    _remote(part_ref.at[across, pl.ds(0, half)], stage_rs.at[0], rsend.at[2], rrecv.at[2],
            ldev).wait_recv()
    fwd_r = _remote(stage_rs.at[0], rs_out.at[left, pl.ds(0, half)], rsend.at[4], rrecv.at[4],
                    rdev)
    fwd_r.start()
    _remote(part_ref.at[across, pl.ds(half, half)], stage_rs.at[1], rsend.at[3], rrecv.at[3],
            rdev).wait_recv()
    fwd_l = _remote(stage_rs.at[1], rs_out.at[right, pl.ds(half, half)], rsend.at[5],
                    rrecv.at[5], ldev)
    fwd_l.start()

    a2a.arrived()
    _remote(part_ref.at[t], rs_out.at[left], rsend.at[0], rrecv.at[0], ldev).wait_recv()
    _remote(part_ref.at[t], rs_out.at[right], rsend.at[1], rrecv.at[1], rdev).wait_recv()
    _remote(stage_rs.at[0], rs_out.at[across, pl.ds(0, half)], rsend.at[4], rrecv.at[4],
            ldev).wait_recv()
    _remote(stage_rs.at[1], rs_out.at[across, pl.ds(half, half)], rsend.at[5], rrecv.at[5],
            rdev).wait_recv()
    for c in (to_r, to_l, via_r, via_l, fwd_r, fwd_l):
        c.wait_send()
    a2a.finish()
    own_part.wait()


def scatter_outputs(partial, share, na, nb, ntp):
    _, rows, cols = partial.shape
    _, block, width = share.shape
    share4 = share.reshape(na, nb, block, width)
    rs, new = pl.pallas_call(
        functools.partial(_out_kernel, na, nb, ntp),
        out_shape=(
            jax.ShapeDtypeStruct(partial.shape, partial.dtype),
            jax.ShapeDtypeStruct(share4.shape, share.dtype),
        ),
        in_specs=[pl.BlockSpec(memory_space=pl.ANY)] * 2,
        out_specs=(pl.BlockSpec(memory_space=pl.ANY), pl.BlockSpec(memory_space=pl.ANY)),
        scratch_shapes=[
            pltpu.VMEM((2, rows // 2, cols), partial.dtype),
            pltpu.SemaphoreType.DMA((6,)),
            pltpu.SemaphoreType.DMA((6,)),
            pltpu.SemaphoreType.DMA((1,)),
        ] + _seq_scratch(na, nb, block, width, share.dtype),
        compiler_params=pltpu.CompilerParams(collective_id=1, has_side_effects=True),
    )(partial, share4)
    return rs, new.reshape(share.shape)


def _attend_kernel(scale, lens_ref, q_ref, k_ref, v_ref, o_ref):
    chunk = q_ref.shape[0]
    capacity = k_ref.shape[0]
    held = lens_ref[0]
    first = pl.program_id(1) * chunk
    scores = lax.dot_general(
        q_ref[...], k_ref[...], (((1,), (1,)), ((), ())), preferred_element_type=jnp.float32
    ) * scale
    row_pos = first + lax.broadcasted_iota(jnp.int32, (chunk, capacity), 0)
    key_pos = lax.broadcasted_iota(jnp.int32, (chunk, capacity), 1)
    scores = jnp.where(key_pos <= held + row_pos, scores, MASKED)
    top = jnp.max(scores, axis=1, keepdims=True)
    weights = jnp.exp(scores - top)
    probs = (weights / jnp.sum(weights, axis=1, keepdims=True)).astype(jnp.bfloat16)
    o_ref[...] = jnp.dot(probs, v_ref[...], preferred_element_type=jnp.float32).astype(o_ref.dtype)


def attend(query, fresh, held_len, head_size, chunk=128):
    rows, qcols = query.shape
    capacity = fresh.shape[0]
    heads = qcols // head_size
    lens = jnp.reshape(held_len, (1,)).astype(jnp.int32)
    return pl.pallas_call(
        functools.partial(_attend_kernel, head_size ** (-0.5)),
        out_shape=jax.ShapeDtypeStruct((rows, qcols), jnp.bfloat16),
        grid_spec=pltpu.PrefetchScalarGridSpec(
            num_scalar_prefetch=1,
            grid=(heads, rows // chunk),
            in_specs=[
                pl.BlockSpec((chunk, head_size), lambda h, r, lens: (r, h)),
                pl.BlockSpec((capacity, head_size), lambda h, r, lens: (0, 0)),
                pl.BlockSpec((capacity, head_size), lambda h, r, lens: (0, 1)),
            ],
            out_specs=pl.BlockSpec((chunk, head_size), lambda h, r, lens: (r, h)),
        ),
        cost_estimate=pl.CostEstimate(
            flops=4 * rows * capacity * qcols,
            transcendentals=rows * capacity * heads,
            bytes_accessed=2 * (2 * rows * qcols + 2 * capacity * head_size),
        ),
    )(lens, query, fresh, fresh)


def _prep_kernel(ntp, held_ref, span_ref, holders_ref, targets_ref, cache_ref, kv_ref, fresh, kt,
                 share_buf, fresh32, sources_ref):
    t = lax.axis_index("tp")
    capacity, width = fresh.shape
    head_size = width // 2
    block_rows = cache_ref.shape[1]
    share = block_rows // ntp
    held = held_ref[0]
    span = span_ref[0]

    def invert(b, carry):
        sources_ref[targets_ref[b]] = b
        return carry

    lax.fori_loop(0, targets_ref.shape[0], invert, 0)

    def place(b, carry):
        fresh32[pl.ds(pl.multiple_of(b * block_rows, block_rows), block_rows), :] = (
            cache_ref[holders_ref[b]].astype(jnp.float32))
        return carry

    lax.fori_loop(0, capacity // block_rows, place, 0)
    padded = jnp.concatenate(
        [kv_ref[...].astype(jnp.float32),
         jnp.zeros((capacity - kv_ref.shape[0], width), jnp.float32)], axis=0)
    shifted = pltpu.roll(padded, held, 0)
    positions = lax.broadcasted_iota(jnp.int32, (capacity, width), 0)
    full = jnp.where(positions < held, fresh32[...],
                     jnp.where(positions < held + span, shifted, 0.0))
    fresh32[...] = full
    fresh[...] = full.astype(fresh.dtype)
    kt[...] = fresh[:, pl.ds(0, head_size)].T

    def pick(d, carry):
        start = pl.multiple_of(sources_ref[d] * block_rows + t * share, share)
        share_buf[d] = fresh32[pl.ds(start, share), :].astype(share_buf.dtype)
        return carry

    lax.fori_loop(0, share_buf.shape[0], pick, 0)


def prepare(cache, keyval, held, span, holders, targets, ntp):
    blocks, block_rows, width = cache.shape
    capacity = blocks * block_rows
    vmem = pl.BlockSpec(memory_space=pltpu.VMEM)
    smem = pl.BlockSpec(memory_space=pltpu.SMEM)
    return pl.pallas_call(
        functools.partial(_prep_kernel, ntp),
        out_shape=(
            jax.ShapeDtypeStruct((capacity, width), cache.dtype),
            jax.ShapeDtypeStruct((width // 2, capacity), cache.dtype),
            jax.ShapeDtypeStruct((blocks, block_rows // ntp, width), cache.dtype),
        ),
        in_specs=[smem, smem, smem, smem, vmem, vmem],
        out_specs=(vmem, vmem, vmem),
        scratch_shapes=[pltpu.VMEM((capacity, width), jnp.float32),
                        pltpu.SMEM((targets.shape[0],), jnp.int32)],
    )(held, span, holders, targets, cache, keyval)


def _tail_kernel(na, nb, ntp, scale, chunk, lens_ref, q_ref, fresh, kt, share_buf, w_ref,
                 rs_out, new_out, ctx, part, psend, precv, plocal, stage, s1send, s1recv, s2send,
                 s2recv, slocal):
    s = lax.axis_index("seq")
    t = lax.axis_index("tp")
    rows, qcols = q_ref.shape
    capacity, width = fresh.shape
    head_size = width // 2
    share = share_buf.shape[1]
    heads = qcols // head_size
    cols = w_ref.shape[1] // ntp
    chunks = rows // chunk
    held = lens_ref[0]

    _greet(na, nb, s, t, *[lax.rem(t + k, ntp) for k in range(1, ntp)])
    sorted4 = share_buf.reshape(na, nb, share, width)
    a2a = SeqAllToAll(na, nb, s, t, sorted4, stage, lambda a_src: new_out.at[a_src],
                      (s1send, s1recv, s2send, s2recv, slocal))
    a2a.first()

    def slice_out(c, k):
        peer = lax.rem(t + k, ntp)
        return _remote(part.at[c, :, pl.ds(pl.multiple_of(peer * cols, cols), cols)],
                       rs_out.at[t, pl.ds(pl.multiple_of(c * chunk, chunk), chunk)],
                       psend.at[c, k], precv.at[c, k], {"seq": s, "tp": peer})

    def slice_in(c, k):
        sender = lax.rem(t + ntp - k, ntp)
        return _remote(part.at[c, :, pl.ds(0, cols)],
                       rs_out.at[sender, pl.ds(pl.multiple_of(c * chunk, chunk), chunk)],
                       psend.at[c, k], precv.at[c, k], {"seq": s, "tp": sender})

    def slice_own(c):
        return pltpu.make_async_copy(
            part.at[c, :, pl.ds(pl.multiple_of(t * cols, cols), cols)],
            rs_out.at[t, pl.ds(pl.multiple_of(c * chunk, chunk), chunk)], plocal.at[c])

    def do_chunk(c):
        first = pl.multiple_of(c * chunk, chunk)
        row_pos = first + lax.broadcasted_iota(jnp.int32, (chunk, capacity), 0)
        key_pos = lax.broadcasted_iota(jnp.int32, (chunk, capacity), 1)
        allowed = key_pos <= held + row_pos
        for h in range(heads):
            q = q_ref[pl.ds(first, chunk), pl.ds(h * head_size, head_size)]
            scores = jnp.dot(q, kt[...], preferred_element_type=jnp.float32) * scale
            scores = jnp.where(allowed, scores, MASKED)
            top = jnp.max(scores, axis=1, keepdims=True)
            weights = jnp.exp(scores - top)
            inv = 1.0 / jnp.sum(weights, axis=1, keepdims=True)
            probs = (weights * inv).astype(jnp.bfloat16)
            ctx[:, pl.ds(h * head_size, head_size)] = jnp.dot(
                probs, fresh[:, pl.ds(head_size, head_size)],
                preferred_element_type=jnp.float32).astype(ctx.dtype)
        part[c] = jnp.dot(ctx[...], w_ref[...], preferred_element_type=jnp.float32).astype(
            part.dtype)
        slice_own(c).start()
        for k in range(1, ntp):
            slice_out(c, k).start()

    do_chunk(0)
    a2a.second()

    def rest(c, carry):
        do_chunk(c)
        return carry

    lax.fori_loop(1, chunks, rest, 0)
    a2a.arrived()

    def drain(c, carry):
        for k in range(1, ntp):
            slice_in(c, k).wait_recv()
            slice_out(c, k).wait_send()
        slice_own(c).wait()
        return carry

    lax.fori_loop(0, chunks, drain, 0)
    a2a.finish()


def attend_and_scatter(query, cache, keyval, held, span, holders, targets, w_out, na, nb, ntp,
                       chunk=128):
    rows, qcols = query.shape
    blocks, block_rows, width = cache.shape
    share = block_rows // ntp
    cols = w_out.shape[1] // ntp
    fresh, keys_t, sorted_share = prepare(cache, keyval, held, span, holders, targets, ntp)
    vmem = pl.BlockSpec(memory_space=pltpu.VMEM)
    smem = pl.BlockSpec(memory_space=pltpu.SMEM)
    rs, new = pl.pallas_call(
        functools.partial(_tail_kernel, na, nb, ntp, (width // 2) ** (-0.5), chunk),
        out_shape=(
            jax.ShapeDtypeStruct((ntp, rows, cols), jnp.bfloat16),
            jax.ShapeDtypeStruct((na, nb, share, width), cache.dtype),
        ),
        in_specs=[smem, vmem, vmem, vmem, vmem, vmem],
        out_specs=(pl.BlockSpec(memory_space=pl.ANY), pl.BlockSpec(memory_space=pl.ANY)),
        scratch_shapes=[
            pltpu.VMEM((chunk, qcols), jnp.bfloat16),
            pltpu.VMEM((rows // chunk, chunk, w_out.shape[1]), jnp.bfloat16),
            pltpu.SemaphoreType.DMA((rows // chunk, ntp)),
            pltpu.SemaphoreType.DMA((rows // chunk, ntp)),
            pltpu.SemaphoreType.DMA((rows // chunk,)),
        ] + _seq_scratch(na, nb, share, width, cache.dtype),
        compiler_params=pltpu.CompilerParams(collective_id=1, has_side_effects=True),
    )(held, query, fresh, keys_t, sorted_share, w_out)
    return rs, new.reshape(blocks, share, width)


def body(
    tokens,
    norm_gain,
    w_query,
    w_keyval,
    w_out,
    span_lens,
    cached_lens,
    old_table,
    new_table,
    old_cache,
):
    groups = lax.axis_size("seq")
    tp_count = lax.axis_size("tp")
    tp_index = lax.axis_index("tp")
    holders = old_table[0]
    held_len = cached_lens[0]
    span_len = span_lens[0]
    tok_rows, tok_cols = tokens.shape
    share = old_cache.shape[1]
    width = old_cache.shape[2]
    block_rows = share * tp_count
    capacity = groups * block_rows

    inner = min(groups, 8)
    outer = groups // inner
    query, keyval, cache_all = gather_inputs(
        tokens, old_cache, norm_gain, w_query, w_keyval, outer, inner, tp_count
    )
    cache_all = cache_all.reshape(groups, tp_count, share, width)

    summed, new_cache = attend_and_scatter(
        query, cache_all.reshape(groups, block_rows, width), keyval, cached_lens, span_lens,
        holders, new_table[0], w_out, outer, inner, tp_count
    )
    row_pos = lax.broadcasted_iota(jnp.int32, (tok_rows, 1), 0)
    total = tokens.astype(jnp.float32)
    for p in range(tp_count):
        total = total + summed[p].astype(jnp.float32)
    mixed = jnp.where(row_pos < span_len, total, jnp.zeros_like(total)).astype(jnp.bfloat16)
    return (mixed, new_cache)


def solution(mesh):
    in_specs = (
        P("seq", "tp"),
        P(),
        P(None, "tp"),
        P(),
        P("tp", None),
        P("seq"),
        P("seq"),
        P("seq", None),
        P("seq", None),
        P("seq", "tp", None),
    )
    out_specs = (P("seq", "tp"), P("seq", "tp", None))
    return jax.shard_map(body, mesh=mesh, in_specs=in_specs, out_specs=out_specs, check_vma=False)
```

```python
import functools

import jax
import jax.numpy as jnp
from jax import lax
from jax.experimental import pallas as pl
from jax.experimental.pallas import tpu as pltpu
from jax.sharding import PartitionSpec as P

EPSILON = 1e-05
MASKED = -1e30


def normalize(rows, norm_gain):
    values = rows.astype(jnp.float32)
    average = jnp.mean(values, axis=1, keepdims=True)
    centred = values - average
    spread = jnp.mean(centred * centred, axis=1, keepdims=True)
    return (centred * lax.rsqrt(spread + EPSILON) * norm_gain).astype(jnp.bfloat16)


MESH = pl.DeviceIdType.MESH


def _remote(src, dst, send, recv, dev):
    return pltpu.make_async_remote_copy(
        src_ref=src, dst_ref=dst, send_sem=send, recv_sem=recv, device_id=dev, device_id_type=MESH
    )


def _greet(na, nb, s, t, *tp_peers):
    barrier = pltpu.get_barrier_semaphore()
    a = s // nb
    b = s % nb

    def one_b(k, carry):
        pl.semaphore_signal(barrier, inc=1, device_id={"seq": a * nb + lax.rem(b + k, nb), "tp": t},
                            device_id_type=MESH)
        return carry

    def one_a(k, carry):
        pl.semaphore_signal(barrier, inc=1, device_id={"seq": lax.rem(a + k, na) * nb + b, "tp": t},
                            device_id_type=MESH)
        return carry

    lax.fori_loop(1, nb, one_b, 0)
    lax.fori_loop(1, na, one_a, 0)
    for p in tp_peers:
        pl.semaphore_signal(barrier, inc=1, device_id={"seq": s, "tp": p}, device_id_type=MESH)
    pl.semaphore_wait(barrier, na + nb - 2 + len(tp_peers))


class SeqAllToAll:
    def __init__(self, na, nb, s, t, src, stage, dst, sems):
        self.na, self.nb, self.t, self.src, self.stage, self.dst = na, nb, t, src, stage, dst
        self.a = s // nb
        self.b = s % nb
        self.s1send, self.s1recv, self.s2send, self.s2recv, self.local = sems

    def _dev(self, a, b):
        return {"seq": a * self.nb + b, "tp": self.t}

    def _out1(self, k):
        peer = lax.rem(self.b + k, self.nb)
        return _remote(self.src.at[:, peer], self.stage.at[self.b], self.s1send.at[k],
                       self.s1recv.at[k], self._dev(self.a, peer))

    def _in1(self, k):
        sender = lax.rem(self.b + self.nb - k, self.nb)
        return _remote(self.src.at[:, self.b], self.stage.at[sender], self.s1send.at[k],
                       self.s1recv.at[k], self._dev(self.a, sender))

    def _out2(self, k):
        peer = lax.rem(self.a + k, self.na)
        return _remote(self.stage.at[:, peer], self.dst(self.a), self.s2send.at[k],
                       self.s2recv.at[k], self._dev(peer, self.b))

    def _in2(self, k):
        sender = lax.rem(self.a + self.na - k, self.na)
        return _remote(self.stage.at[:, self.a], self.dst(sender), self.s2send.at[k],
                       self.s2recv.at[k], self._dev(sender, self.b))

    def first(self):
        self.own1 = pltpu.make_async_copy(self.src.at[:, self.b], self.stage.at[self.b],
                                          self.local.at[0])
        self.own1.start()
        _loop(self.nb, lambda k: self._out1(k).start())

    def second(self):
        _loop(self.nb, lambda k: self._in1(k).wait_recv())
        self.own1.wait()
        self.own2 = pltpu.make_async_copy(self.stage.at[:, self.a], self.dst(self.a),
                                          self.local.at[1])
        self.own2.start()
        _loop(self.na, lambda k: self._out2(k).start())

    def arrived(self):
        _loop(self.na, lambda k: self._in2(k).wait_recv())
        self.own2.wait()

    def finish(self):
        _loop(self.nb, lambda k: self._out1(k).wait_send())
        _loop(self.na, lambda k: self._out2(k).wait_send())


def _seq_scratch(na, nb, share, width, dtype):
    return [
        pltpu.VMEM((nb, na, share, width), dtype),
        pltpu.SemaphoreType.DMA((nb,)),
        pltpu.SemaphoreType.DMA((nb,)),
        pltpu.SemaphoreType.DMA((na,)),
        pltpu.SemaphoreType.DMA((na,)),
        pltpu.SemaphoreType.DMA((2,)),
    ]


def _loop(n, fn):
    def step(k, carry):
        fn(k)
        return carry

    lax.fori_loop(1, n, step, 0)


def _in_kernel(na, nb, ntp, tok_ref, cache_ref, gain_ref, wq_ref, wkv_ref, q_out, kv_out,
               cache_out, tok_all, tsend, trecv, csend, crecv, lsem, stage, s1send, s1recv,
               s2send, s2recv, slocal):
    s = lax.axis_index("seq")
    t = lax.axis_index("tp")
    right = lax.rem(t + 1, ntp)
    left = lax.rem(t + ntp - 1, ntp)
    across = lax.rem(t + 2, ntp)
    rdev = {"seq": s, "tp": right}
    ldev = {"seq": s, "tp": left}
    rows, cols = tok_ref.shape
    half = rows // 2
    _greet(na, nb, s, t, left, right, across)

    def tok_cols(p):
        return pl.ds(pl.multiple_of(p * cols, cols), cols)

    a2a = SeqAllToAll(na, nb, s, t, cache_ref, stage, lambda a_src: cache_out.at[a_src, :, t],
                      (s1send, s1recv, s2send, s2recv, slocal))
    a2a.first()

    own_tok = pltpu.make_async_copy(tok_ref, tok_all.at[:, tok_cols(t)], lsem.at[0])
    own_tok.start()
    tok_r = _remote(tok_ref, tok_all.at[:, tok_cols(t)], tsend.at[0], trecv.at[0], rdev)
    tok_l = _remote(tok_ref, tok_all.at[:, tok_cols(t)], tsend.at[1], trecv.at[1], ldev)
    tok_r.start()
    tok_l.start()

    a2a.second()

    _remote(tok_ref, tok_all.at[:, tok_cols(left)], tsend.at[0], trecv.at[0], ldev).wait_recv()
    fwd_r = _remote(tok_all.at[pl.ds(0, half), tok_cols(left)],
                    tok_all.at[pl.ds(0, half), tok_cols(left)], tsend.at[2], trecv.at[2], rdev)
    fwd_r.start()
    _remote(tok_ref, tok_all.at[:, tok_cols(right)], tsend.at[1], trecv.at[1], rdev).wait_recv()
    fwd_l = _remote(tok_all.at[pl.ds(half, half), tok_cols(right)],
                    tok_all.at[pl.ds(half, half), tok_cols(right)], tsend.at[3], trecv.at[3], ldev)
    fwd_l.start()

    a2a.arrived()
    flat = cache_out.reshape(na * nb, ntp, *cache_out.shape[3:])
    mine = flat.at[:, t]

    def cache_to(k):
        peer = lax.rem(t + k, ntp)
        return _remote(mine, mine, csend.at[k], crecv.at[k], {"seq": s, "tp": peer})

    def cache_from(k):
        sender = lax.rem(t + ntp - k, ntp)
        return _remote(mine, flat.at[:, sender], csend.at[k], crecv.at[k],
                       {"seq": s, "tp": sender})

    for k in range(1, ntp):
        cache_to(k).start()

    _remote(tok_ref.at[pl.ds(0, half)], tok_all.at[pl.ds(0, half), tok_cols(across)],
            tsend.at[2], trecv.at[2], ldev).wait_recv()
    _remote(tok_ref.at[pl.ds(half, half)], tok_all.at[pl.ds(half, half), tok_cols(across)],
            tsend.at[3], trecv.at[3], rdev).wait_recv()
    own_tok.wait()

    chunk = 128

    def project(c, carry):
        first = pl.multiple_of(c * chunk, chunk)
        values = tok_all[pl.ds(first, chunk), :].astype(jnp.float32)
        average = jnp.mean(values, axis=1, keepdims=True)
        centred = values - average
        spread = jnp.mean(centred * centred, axis=1, keepdims=True)
        normed = (centred * lax.rsqrt(spread + EPSILON) * gain_ref[...]).astype(jnp.bfloat16)
        q_out[pl.ds(first, chunk), :] = jnp.dot(
            normed, wq_ref[...], preferred_element_type=jnp.float32).astype(q_out.dtype)
        kv_out[pl.ds(first, chunk), :] = jnp.dot(
            normed, wkv_ref[...], preferred_element_type=jnp.float32).astype(kv_out.dtype)
        return carry

    lax.fori_loop(0, rows // chunk, project, 0)

    for k in range(1, ntp):
        cache_from(k).wait_recv()
    for c in (tok_r, tok_l, fwd_r, fwd_l):
        c.wait_send()
    for k in range(1, ntp):
        cache_to(k).wait_send()
    a2a.finish()


def gather_inputs(tokens, old_cache, norm_gain, w_query, w_keyval, na, nb, ntp):
    rows, cols = tokens.shape
    _, share, width = old_cache.shape
    cache4 = old_cache.reshape(na, nb, share, width)
    vmem = pl.BlockSpec(memory_space=pltpu.VMEM)
    anywhere = pl.BlockSpec(memory_space=pl.ANY)
    return pl.pallas_call(
        functools.partial(_in_kernel, na, nb, ntp),
        out_shape=(
            jax.ShapeDtypeStruct((rows, w_query.shape[1]), jnp.bfloat16),
            jax.ShapeDtypeStruct((rows, w_keyval.shape[1]), jnp.bfloat16),
            jax.ShapeDtypeStruct((na, nb, ntp, share, width), old_cache.dtype),
        ),
        in_specs=[anywhere, anywhere, vmem, vmem, vmem],
        out_specs=(vmem, vmem, anywhere),
        scratch_shapes=[
            pltpu.VMEM((rows, ntp * cols), tokens.dtype),
            pltpu.SemaphoreType.DMA((4,)),
            pltpu.SemaphoreType.DMA((4,)),
            pltpu.SemaphoreType.DMA((ntp,)),
            pltpu.SemaphoreType.DMA((ntp,)),
            pltpu.SemaphoreType.DMA((2,)),
        ] + _seq_scratch(na, nb, share, width, old_cache.dtype),
        compiler_params=pltpu.CompilerParams(collective_id=0, has_side_effects=True),
    )(tokens, cache4, norm_gain.reshape(1, -1).astype(jnp.float32), w_query, w_keyval)


def _out_kernel(na, nb, ntp, part_ref, share_ref, rs_out, new_out, stage_rs, rsend, rrecv, lsem,
                stage, s1send, s1recv, s2send, s2recv, slocal):
    s = lax.axis_index("seq")
    t = lax.axis_index("tp")
    right = lax.rem(t + 1, ntp)
    left = lax.rem(t + ntp - 1, ntp)
    across = lax.rem(t + 2, ntp)
    rdev = {"seq": s, "tp": right}
    ldev = {"seq": s, "tp": left}
    half = part_ref.shape[1] // 2
    _greet(na, nb, s, t, left, right)

    a2a = SeqAllToAll(na, nb, s, t, share_ref, stage, lambda a_src: new_out.at[a_src],
                      (s1send, s1recv, s2send, s2recv, slocal))
    a2a.first()

    own_part = pltpu.make_async_copy(part_ref.at[t], rs_out.at[t], lsem.at[0])
    own_part.start()
    to_r = _remote(part_ref.at[right], rs_out.at[t], rsend.at[0], rrecv.at[0], rdev)
    to_l = _remote(part_ref.at[left], rs_out.at[t], rsend.at[1], rrecv.at[1], ldev)
    via_r = _remote(part_ref.at[across, pl.ds(0, half)], stage_rs.at[0], rsend.at[2], rrecv.at[2],
                    rdev)
    via_l = _remote(part_ref.at[across, pl.ds(half, half)], stage_rs.at[1], rsend.at[3],
                    rrecv.at[3], ldev)
    for c in (to_r, to_l, via_r, via_l):
        c.start()

    a2a.second()

    _remote(part_ref.at[across, pl.ds(0, half)], stage_rs.at[0], rsend.at[2], rrecv.at[2],
            ldev).wait_recv()
    fwd_r = _remote(stage_rs.at[0], rs_out.at[left, pl.ds(0, half)], rsend.at[4], rrecv.at[4],
                    rdev)
    fwd_r.start()
    _remote(part_ref.at[across, pl.ds(half, half)], stage_rs.at[1], rsend.at[3], rrecv.at[3],
            rdev).wait_recv()
    fwd_l = _remote(stage_rs.at[1], rs_out.at[right, pl.ds(half, half)], rsend.at[5],
                    rrecv.at[5], ldev)
    fwd_l.start()

    a2a.arrived()
    _remote(part_ref.at[t], rs_out.at[left], rsend.at[0], rrecv.at[0], ldev).wait_recv()
    _remote(part_ref.at[t], rs_out.at[right], rsend.at[1], rrecv.at[1], rdev).wait_recv()
    _remote(stage_rs.at[0], rs_out.at[across, pl.ds(0, half)], rsend.at[4], rrecv.at[4],
            ldev).wait_recv()
    _remote(stage_rs.at[1], rs_out.at[across, pl.ds(half, half)], rsend.at[5], rrecv.at[5],
            rdev).wait_recv()
    for c in (to_r, to_l, via_r, via_l, fwd_r, fwd_l):
        c.wait_send()
    a2a.finish()
    own_part.wait()


def scatter_outputs(partial, share, na, nb, ntp):
    _, rows, cols = partial.shape
    _, block, width = share.shape
    share4 = share.reshape(na, nb, block, width)
    rs, new = pl.pallas_call(
        functools.partial(_out_kernel, na, nb, ntp),
        out_shape=(
            jax.ShapeDtypeStruct(partial.shape, partial.dtype),
            jax.ShapeDtypeStruct(share4.shape, share.dtype),
        ),
        in_specs=[pl.BlockSpec(memory_space=pl.ANY)] * 2,
        out_specs=(pl.BlockSpec(memory_space=pl.ANY), pl.BlockSpec(memory_space=pl.ANY)),
        scratch_shapes=[
            pltpu.VMEM((2, rows // 2, cols), partial.dtype),
            pltpu.SemaphoreType.DMA((6,)),
            pltpu.SemaphoreType.DMA((6,)),
            pltpu.SemaphoreType.DMA((1,)),
        ] + _seq_scratch(na, nb, block, width, share.dtype),
        compiler_params=pltpu.CompilerParams(collective_id=1, has_side_effects=True),
    )(partial, share4)
    return rs, new.reshape(share.shape)


def _attend_kernel(scale, lens_ref, q_ref, k_ref, v_ref, o_ref):
    chunk = q_ref.shape[0]
    capacity = k_ref.shape[0]
    held = lens_ref[0]
    first = pl.program_id(1) * chunk
    scores = lax.dot_general(
        q_ref[...], k_ref[...], (((1,), (1,)), ((), ())), preferred_element_type=jnp.float32
    ) * scale
    row_pos = first + lax.broadcasted_iota(jnp.int32, (chunk, capacity), 0)
    key_pos = lax.broadcasted_iota(jnp.int32, (chunk, capacity), 1)
    scores = jnp.where(key_pos <= held + row_pos, scores, MASKED)
    top = jnp.max(scores, axis=1, keepdims=True)
    weights = jnp.exp(scores - top)
    probs = (weights / jnp.sum(weights, axis=1, keepdims=True)).astype(jnp.bfloat16)
    o_ref[...] = jnp.dot(probs, v_ref[...], preferred_element_type=jnp.float32).astype(o_ref.dtype)


def attend(query, fresh, held_len, head_size, chunk=128):
    rows, qcols = query.shape
    capacity = fresh.shape[0]
    heads = qcols // head_size
    lens = jnp.reshape(held_len, (1,)).astype(jnp.int32)
    return pl.pallas_call(
        functools.partial(_attend_kernel, head_size ** (-0.5)),
        out_shape=jax.ShapeDtypeStruct((rows, qcols), jnp.bfloat16),
        grid_spec=pltpu.PrefetchScalarGridSpec(
            num_scalar_prefetch=1,
            grid=(heads, rows // chunk),
            in_specs=[
                pl.BlockSpec((chunk, head_size), lambda h, r, lens: (r, h)),
                pl.BlockSpec((capacity, head_size), lambda h, r, lens: (0, 0)),
                pl.BlockSpec((capacity, head_size), lambda h, r, lens: (0, 1)),
            ],
            out_specs=pl.BlockSpec((chunk, head_size), lambda h, r, lens: (r, h)),
        ),
        cost_estimate=pl.CostEstimate(
            flops=4 * rows * capacity * qcols,
            transcendentals=rows * capacity * heads,
            bytes_accessed=2 * (2 * rows * qcols + 2 * capacity * head_size),
        ),
    )(lens, query, fresh, fresh)


def _prep_kernel(ntp, held_ref, span_ref, holders_ref, targets_ref, cache_ref, kv_ref, fresh, kt,
                 share_buf, fresh32, sources_ref):
    t = lax.axis_index("tp")
    capacity, width = fresh.shape
    head_size = width // 2
    block_rows = cache_ref.shape[1]
    share = block_rows // ntp
    held = held_ref[0]
    span = span_ref[0]

    def invert(b, carry):
        sources_ref[targets_ref[b]] = b
        return carry

    lax.fori_loop(0, targets_ref.shape[0], invert, 0)

    def place(b, carry):
        fresh32[pl.ds(pl.multiple_of(b * block_rows, block_rows), block_rows), :] = (
            cache_ref[holders_ref[b]].astype(jnp.float32))
        return carry

    lax.fori_loop(0, capacity // block_rows, place, 0)
    padded = jnp.concatenate(
        [kv_ref[...].astype(jnp.float32),
         jnp.zeros((capacity - kv_ref.shape[0], width), jnp.float32)], axis=0)
    shifted = pltpu.roll(padded, held, 0)
    positions = lax.broadcasted_iota(jnp.int32, (capacity, width), 0)
    full = jnp.where(positions < held, fresh32[...],
                     jnp.where(positions < held + span, shifted, 0.0))
    fresh32[...] = full
    fresh[...] = full.astype(fresh.dtype)
    kt[...] = fresh[:, pl.ds(0, head_size)].T

    def pick(d, carry):
        start = pl.multiple_of(sources_ref[d] * block_rows + t * share, share)
        share_buf[d] = fresh32[pl.ds(start, share), :].astype(share_buf.dtype)
        return carry

    lax.fori_loop(0, share_buf.shape[0], pick, 0)


def prepare(cache, keyval, held, span, holders, targets, ntp):
    blocks, block_rows, width = cache.shape
    capacity = blocks * block_rows
    vmem = pl.BlockSpec(memory_space=pltpu.VMEM)
    smem = pl.BlockSpec(memory_space=pltpu.SMEM)
    return pl.pallas_call(
        functools.partial(_prep_kernel, ntp),
        out_shape=(
            jax.ShapeDtypeStruct((capacity, width), cache.dtype),
            jax.ShapeDtypeStruct((width // 2, capacity), cache.dtype),
            jax.ShapeDtypeStruct((blocks, block_rows // ntp, width), cache.dtype),
        ),
        in_specs=[smem, smem, smem, smem, vmem, vmem],
        out_specs=(vmem, vmem, vmem),
        scratch_shapes=[pltpu.VMEM((capacity, width), jnp.float32),
                        pltpu.SMEM((targets.shape[0],), jnp.int32)],
    )(held, span, holders, targets, cache, keyval)


def _tail_kernel(na, nb, ntp, scale, chunk, lens_ref, q_ref, fresh, kt, share_buf, w_ref,
                 rs_out, new_out, ctx, part, psend, precv, plocal, stage, s1send, s1recv, s2send,
                 s2recv, slocal):
    s = lax.axis_index("seq")
    t = lax.axis_index("tp")
    rows, qcols = q_ref.shape
    capacity, width = fresh.shape
    head_size = width // 2
    share = share_buf.shape[1]
    heads = qcols // head_size
    cols = w_ref.shape[1] // ntp
    chunks = rows // chunk
    held = lens_ref[0]

    _greet(na, nb, s, t, *[lax.rem(t + k, ntp) for k in range(1, ntp)])
    sorted4 = share_buf.reshape(na, nb, share, width)
    a2a = SeqAllToAll(na, nb, s, t, sorted4, stage, lambda a_src: new_out.at[a_src],
                      (s1send, s1recv, s2send, s2recv, slocal))
    a2a.first()

    def slice_out(c, k):
        peer = lax.rem(t + k, ntp)
        return _remote(part.at[c, :, pl.ds(pl.multiple_of(peer * cols, cols), cols)],
                       rs_out.at[t, pl.ds(pl.multiple_of(c * chunk, chunk), chunk)],
                       psend.at[c, k], precv.at[c, k], {"seq": s, "tp": peer})

    def slice_in(c, k):
        sender = lax.rem(t + ntp - k, ntp)
        return _remote(part.at[c, :, pl.ds(0, cols)],
                       rs_out.at[sender, pl.ds(pl.multiple_of(c * chunk, chunk), chunk)],
                       psend.at[c, k], precv.at[c, k], {"seq": s, "tp": sender})

    def slice_own(c):
        return pltpu.make_async_copy(
            part.at[c, :, pl.ds(pl.multiple_of(t * cols, cols), cols)],
            rs_out.at[t, pl.ds(pl.multiple_of(c * chunk, chunk), chunk)], plocal.at[c])

    def do_chunk(c):
        first = pl.multiple_of(c * chunk, chunk)
        row_pos = first + lax.broadcasted_iota(jnp.int32, (chunk, capacity), 0)
        key_pos = lax.broadcasted_iota(jnp.int32, (chunk, capacity), 1)
        allowed = key_pos <= held + row_pos
        for h in range(heads):
            q = q_ref[pl.ds(first, chunk), pl.ds(h * head_size, head_size)]
            scores = jnp.dot(q, kt[...], preferred_element_type=jnp.float32) * scale
            scores = jnp.where(allowed, scores, MASKED)
            top = jnp.max(scores, axis=1, keepdims=True)
            weights = jnp.exp(scores - top)
            inv = 1.0 / jnp.sum(weights, axis=1, keepdims=True)
            probs = (weights * inv).astype(jnp.bfloat16)
            ctx[:, pl.ds(h * head_size, head_size)] = jnp.dot(
                probs, fresh[:, pl.ds(head_size, head_size)],
                preferred_element_type=jnp.float32).astype(ctx.dtype)
        part[c] = jnp.dot(ctx[...], w_ref[...], preferred_element_type=jnp.float32).astype(
            part.dtype)
        slice_own(c).start()
        for k in range(1, ntp):
            slice_out(c, k).start()

    do_chunk(0)
    a2a.second()

    def rest(c, carry):
        do_chunk(c)
        return carry

    lax.fori_loop(1, chunks, rest, 0)
    a2a.arrived()

    def drain(c, carry):
        for k in range(1, ntp):
            slice_in(c, k).wait_recv()
            slice_out(c, k).wait_send()
        slice_own(c).wait()
        return carry

    lax.fori_loop(0, chunks, drain, 0)
    a2a.finish()


def attend_and_scatter(query, cache, keyval, held, span, holders, targets, w_out, na, nb, ntp,
                       chunk=128):
    rows, qcols = query.shape
    blocks, block_rows, width = cache.shape
    share = block_rows // ntp
    cols = w_out.shape[1] // ntp
    fresh, keys_t, sorted_share = prepare(cache, keyval, held, span, holders, targets, ntp)
    vmem = pl.BlockSpec(memory_space=pltpu.VMEM)
    smem = pl.BlockSpec(memory_space=pltpu.SMEM)
    rs, new = pl.pallas_call(
        functools.partial(_tail_kernel, na, nb, ntp, (width // 2) ** (-0.5), chunk),
        out_shape=(
            jax.ShapeDtypeStruct((ntp, rows, cols), jnp.bfloat16),
            jax.ShapeDtypeStruct((na, nb, share, width), cache.dtype),
        ),
        in_specs=[smem, vmem, vmem, vmem, vmem, vmem],
        out_specs=(vmem, pl.BlockSpec(memory_space=pl.ANY)),
        scratch_shapes=[
            pltpu.VMEM((chunk, qcols), jnp.bfloat16),
            pltpu.VMEM((rows // chunk, chunk, w_out.shape[1]), jnp.bfloat16),
            pltpu.SemaphoreType.DMA((rows // chunk, ntp)),
            pltpu.SemaphoreType.DMA((rows // chunk, ntp)),
            pltpu.SemaphoreType.DMA((rows // chunk,)),
        ] + _seq_scratch(na, nb, share, width, cache.dtype),
        compiler_params=pltpu.CompilerParams(collective_id=1, has_side_effects=True),
    )(held, query, fresh, keys_t, sorted_share, w_out)
    return rs, new.reshape(blocks, share, width)


def body(
    tokens,
    norm_gain,
    w_query,
    w_keyval,
    w_out,
    span_lens,
    cached_lens,
    old_table,
    new_table,
    old_cache,
):
    groups = lax.axis_size("seq")
    tp_count = lax.axis_size("tp")
    tp_index = lax.axis_index("tp")
    holders = old_table[0]
    held_len = cached_lens[0]
    span_len = span_lens[0]
    tok_rows, tok_cols = tokens.shape
    share = old_cache.shape[1]
    width = old_cache.shape[2]
    block_rows = share * tp_count
    capacity = groups * block_rows

    inner = min(groups, 8)
    outer = groups // inner
    query, keyval, cache_all = gather_inputs(
        tokens, old_cache, norm_gain, w_query, w_keyval, outer, inner, tp_count
    )
    cache_all = cache_all.reshape(groups, tp_count, share, width)

    summed, new_cache = attend_and_scatter(
        query, cache_all.reshape(groups, block_rows, width), keyval, cached_lens, span_lens,
        holders, new_table[0], w_out, outer, inner, tp_count
    )
    row_pos = lax.broadcasted_iota(jnp.int32, (tok_rows, 1), 0)
    total = tokens.astype(jnp.float32)
    for p in range(tp_count):
        total = total + summed[p].astype(jnp.float32)
    mixed = jnp.where(row_pos < span_len, total, jnp.zeros_like(total)).astype(jnp.bfloat16)
    return (mixed, new_cache)


def solution(mesh):
    in_specs = (
        P("seq", "tp"),
        P(),
        P(None, "tp"),
        P(),
        P("tp", None),
        P("seq"),
        P("seq"),
        P("seq", None),
        P("seq", None),
        P("seq", "tp", None),
    )
    out_specs = (P("seq", "tp"), P("seq", "tp", None))
    return jax.shard_map(body, mesh=mesh, in_specs=in_specs, out_specs=out_specs, check_vma=False)
```

```python
import functools

import jax
import jax.numpy as jnp
from jax import lax
from jax.experimental import pallas as pl
from jax.experimental.pallas import tpu as pltpu
from jax.sharding import PartitionSpec as P

EPSILON = 1e-05
MASKED = -1e30


def normalize(rows, norm_gain):
    values = rows.astype(jnp.float32)
    average = jnp.mean(values, axis=1, keepdims=True)
    centred = values - average
    spread = jnp.mean(centred * centred, axis=1, keepdims=True)
    return (centred * lax.rsqrt(spread + EPSILON) * norm_gain).astype(jnp.bfloat16)


MESH = pl.DeviceIdType.MESH


def _remote(src, dst, send, recv, dev):
    return pltpu.make_async_remote_copy(
        src_ref=src, dst_ref=dst, send_sem=send, recv_sem=recv, device_id=dev, device_id_type=MESH
    )


def _greet(na, nb, s, t, *tp_peers):
    barrier = pltpu.get_barrier_semaphore()
    a = s // nb
    b = s % nb

    def one_b(k, carry):
        pl.semaphore_signal(barrier, inc=1, device_id={"seq": a * nb + lax.rem(b + k, nb), "tp": t},
                            device_id_type=MESH)
        return carry

    def one_a(k, carry):
        pl.semaphore_signal(barrier, inc=1, device_id={"seq": lax.rem(a + k, na) * nb + b, "tp": t},
                            device_id_type=MESH)
        return carry

    lax.fori_loop(1, nb, one_b, 0)
    lax.fori_loop(1, na, one_a, 0)
    for p in tp_peers:
        pl.semaphore_signal(barrier, inc=1, device_id={"seq": s, "tp": p}, device_id_type=MESH)
    pl.semaphore_wait(barrier, na + nb - 2 + len(tp_peers))


class SeqAllToAll:
    def __init__(self, na, nb, s, t, src, stage, dst, sems):
        self.na, self.nb, self.t, self.src, self.stage, self.dst = na, nb, t, src, stage, dst
        self.a = s // nb
        self.b = s % nb
        self.s1send, self.s1recv, self.s2send, self.s2recv, self.local = sems

    def _dev(self, a, b):
        return {"seq": a * self.nb + b, "tp": self.t}

    def _out1(self, k):
        peer = lax.rem(self.b + k, self.nb)
        return _remote(self.src.at[:, peer], self.stage.at[self.b], self.s1send.at[k],
                       self.s1recv.at[k], self._dev(self.a, peer))

    def _in1(self, k):
        sender = lax.rem(self.b + self.nb - k, self.nb)
        return _remote(self.src.at[:, self.b], self.stage.at[sender], self.s1send.at[k],
                       self.s1recv.at[k], self._dev(self.a, sender))

    def _out2(self, k):
        peer = lax.rem(self.a + k, self.na)
        return _remote(self.stage.at[:, peer], self.dst(self.a), self.s2send.at[k],
                       self.s2recv.at[k], self._dev(peer, self.b))

    def _in2(self, k):
        sender = lax.rem(self.a + self.na - k, self.na)
        return _remote(self.stage.at[:, self.a], self.dst(sender), self.s2send.at[k],
                       self.s2recv.at[k], self._dev(sender, self.b))

    def first(self):
        self.own1 = pltpu.make_async_copy(self.src.at[:, self.b], self.stage.at[self.b],
                                          self.local.at[0])
        self.own1.start()
        _loop(self.nb, lambda k: self._out1(k).start())

    def second(self):
        _loop(self.nb, lambda k: self._in1(k).wait_recv())
        self.own1.wait()
        self.own2 = pltpu.make_async_copy(self.stage.at[:, self.a], self.dst(self.a),
                                          self.local.at[1])
        self.own2.start()
        _loop(self.na, lambda k: self._out2(k).start())

    def arrived(self):
        _loop(self.na, lambda k: self._in2(k).wait_recv())
        self.own2.wait()

    def finish(self):
        _loop(self.nb, lambda k: self._out1(k).wait_send())
        _loop(self.na, lambda k: self._out2(k).wait_send())


def _seq_scratch(na, nb, share, width, dtype):
    return [
        pltpu.VMEM((nb, na, share, width), dtype),
        pltpu.SemaphoreType.DMA((nb,)),
        pltpu.SemaphoreType.DMA((nb,)),
        pltpu.SemaphoreType.DMA((na,)),
        pltpu.SemaphoreType.DMA((na,)),
        pltpu.SemaphoreType.DMA((2,)),
    ]


def _loop(n, fn):
    def step(k, carry):
        fn(k)
        return carry

    lax.fori_loop(1, n, step, 0)


def _in_kernel(na, nb, ntp, tok_ref, cache_ref, gain_ref, wq_ref, wkv_ref, q_out, kv_out,
               cache_out, tok_all, tsend, trecv, csend, crecv, lsem, stage, s1send, s1recv,
               s2send, s2recv, slocal):
    s = lax.axis_index("seq")
    t = lax.axis_index("tp")
    right = lax.rem(t + 1, ntp)
    left = lax.rem(t + ntp - 1, ntp)
    across = lax.rem(t + 2, ntp)
    rdev = {"seq": s, "tp": right}
    ldev = {"seq": s, "tp": left}
    rows, cols = tok_ref.shape
    half = rows // 2
    _greet(na, nb, s, t, left, right, across)

    def tok_cols(p):
        return pl.ds(pl.multiple_of(p * cols, cols), cols)

    a2a = SeqAllToAll(na, nb, s, t, cache_ref, stage, lambda a_src: cache_out.at[a_src, :, t],
                      (s1send, s1recv, s2send, s2recv, slocal))
    a2a.first()

    own_tok = pltpu.make_async_copy(tok_ref, tok_all.at[:, tok_cols(t)], lsem.at[0])
    own_tok.start()
    tok_r = _remote(tok_ref, tok_all.at[:, tok_cols(t)], tsend.at[0], trecv.at[0], rdev)
    tok_l = _remote(tok_ref, tok_all.at[:, tok_cols(t)], tsend.at[1], trecv.at[1], ldev)
    tok_r.start()
    tok_l.start()

    a2a.second()
    a2a.arrived()
    flat = cache_out.reshape(na * nb, ntp, *cache_out.shape[3:])
    mine = flat.at[:, t]

    def cache_to(k):
        peer = lax.rem(t + k, ntp)
        return _remote(mine, mine, csend.at[k], crecv.at[k], {"seq": s, "tp": peer})

    def cache_from(k):
        sender = lax.rem(t + ntp - k, ntp)
        return _remote(mine, flat.at[:, sender], csend.at[k], crecv.at[k],
                       {"seq": s, "tp": sender})

    for k in range(1, ntp):
        cache_to(k).start()

    _remote(tok_ref, tok_all.at[:, tok_cols(left)], tsend.at[0], trecv.at[0], ldev).wait_recv()
    fwd_r = _remote(tok_all.at[pl.ds(0, half), tok_cols(left)],
                    tok_all.at[pl.ds(0, half), tok_cols(left)], tsend.at[2], trecv.at[2], rdev)
    fwd_r.start()
    _remote(tok_ref, tok_all.at[:, tok_cols(right)], tsend.at[1], trecv.at[1], rdev).wait_recv()
    fwd_l = _remote(tok_all.at[pl.ds(half, half), tok_cols(right)],
                    tok_all.at[pl.ds(half, half), tok_cols(right)], tsend.at[3], trecv.at[3], ldev)
    fwd_l.start()

    _remote(tok_ref.at[pl.ds(0, half)], tok_all.at[pl.ds(0, half), tok_cols(across)],
            tsend.at[2], trecv.at[2], ldev).wait_recv()
    _remote(tok_ref.at[pl.ds(half, half)], tok_all.at[pl.ds(half, half), tok_cols(across)],
            tsend.at[3], trecv.at[3], rdev).wait_recv()
    own_tok.wait()

    chunk = 128

    def project(c, carry):
        first = pl.multiple_of(c * chunk, chunk)
        values = tok_all[pl.ds(first, chunk), :].astype(jnp.float32)
        average = jnp.mean(values, axis=1, keepdims=True)
        centred = values - average
        spread = jnp.mean(centred * centred, axis=1, keepdims=True)
        normed = (centred * lax.rsqrt(spread + EPSILON) * gain_ref[...]).astype(jnp.bfloat16)
        q_out[pl.ds(first, chunk), :] = jnp.dot(
            normed, wq_ref[...], preferred_element_type=jnp.float32).astype(q_out.dtype)
        kv_out[pl.ds(first, chunk), :] = jnp.dot(
            normed, wkv_ref[...], preferred_element_type=jnp.float32).astype(kv_out.dtype)
        return carry

    lax.fori_loop(0, rows // chunk, project, 0)

    for k in range(1, ntp):
        cache_from(k).wait_recv()
    for c in (tok_r, tok_l, fwd_r, fwd_l):
        c.wait_send()
    for k in range(1, ntp):
        cache_to(k).wait_send()
    a2a.finish()


def gather_inputs(tokens, old_cache, norm_gain, w_query, w_keyval, na, nb, ntp):
    rows, cols = tokens.shape
    _, share, width = old_cache.shape
    cache4 = old_cache.reshape(na, nb, share, width)
    vmem = pl.BlockSpec(memory_space=pltpu.VMEM)
    anywhere = pl.BlockSpec(memory_space=pl.ANY)
    return pl.pallas_call(
        functools.partial(_in_kernel, na, nb, ntp),
        out_shape=(
            jax.ShapeDtypeStruct((rows, w_query.shape[1]), jnp.bfloat16),
            jax.ShapeDtypeStruct((rows, w_keyval.shape[1]), jnp.bfloat16),
            jax.ShapeDtypeStruct((na, nb, ntp, share, width), old_cache.dtype),
        ),
        in_specs=[anywhere, anywhere, vmem, vmem, vmem],
        out_specs=(vmem, vmem, anywhere),
        scratch_shapes=[
            pltpu.VMEM((rows, ntp * cols), tokens.dtype),
            pltpu.SemaphoreType.DMA((4,)),
            pltpu.SemaphoreType.DMA((4,)),
            pltpu.SemaphoreType.DMA((ntp,)),
            pltpu.SemaphoreType.DMA((ntp,)),
            pltpu.SemaphoreType.DMA((2,)),
        ] + _seq_scratch(na, nb, share, width, old_cache.dtype),
        compiler_params=pltpu.CompilerParams(collective_id=0, has_side_effects=True),
    )(tokens, cache4, norm_gain.reshape(1, -1).astype(jnp.float32), w_query, w_keyval)


def _out_kernel(na, nb, ntp, part_ref, share_ref, rs_out, new_out, stage_rs, rsend, rrecv, lsem,
                stage, s1send, s1recv, s2send, s2recv, slocal):
    s = lax.axis_index("seq")
    t = lax.axis_index("tp")
    right = lax.rem(t + 1, ntp)
    left = lax.rem(t + ntp - 1, ntp)
    across = lax.rem(t + 2, ntp)
    rdev = {"seq": s, "tp": right}
    ldev = {"seq": s, "tp": left}
    half = part_ref.shape[1] // 2
    _greet(na, nb, s, t, left, right)

    a2a = SeqAllToAll(na, nb, s, t, share_ref, stage, lambda a_src: new_out.at[a_src],
                      (s1send, s1recv, s2send, s2recv, slocal))
    a2a.first()

    own_part = pltpu.make_async_copy(part_ref.at[t], rs_out.at[t], lsem.at[0])
    own_part.start()
    to_r = _remote(part_ref.at[right], rs_out.at[t], rsend.at[0], rrecv.at[0], rdev)
    to_l = _remote(part_ref.at[left], rs_out.at[t], rsend.at[1], rrecv.at[1], ldev)
    via_r = _remote(part_ref.at[across, pl.ds(0, half)], stage_rs.at[0], rsend.at[2], rrecv.at[2],
                    rdev)
    via_l = _remote(part_ref.at[across, pl.ds(half, half)], stage_rs.at[1], rsend.at[3],
                    rrecv.at[3], ldev)
    for c in (to_r, to_l, via_r, via_l):
        c.start()

    a2a.second()

    _remote(part_ref.at[across, pl.ds(0, half)], stage_rs.at[0], rsend.at[2], rrecv.at[2],
            ldev).wait_recv()
    fwd_r = _remote(stage_rs.at[0], rs_out.at[left, pl.ds(0, half)], rsend.at[4], rrecv.at[4],
                    rdev)
    fwd_r.start()
    _remote(part_ref.at[across, pl.ds(half, half)], stage_rs.at[1], rsend.at[3], rrecv.at[3],
            rdev).wait_recv()
    fwd_l = _remote(stage_rs.at[1], rs_out.at[right, pl.ds(half, half)], rsend.at[5],
                    rrecv.at[5], ldev)
    fwd_l.start()

    a2a.arrived()
    _remote(part_ref.at[t], rs_out.at[left], rsend.at[0], rrecv.at[0], ldev).wait_recv()
    _remote(part_ref.at[t], rs_out.at[right], rsend.at[1], rrecv.at[1], rdev).wait_recv()
    _remote(stage_rs.at[0], rs_out.at[across, pl.ds(0, half)], rsend.at[4], rrecv.at[4],
            ldev).wait_recv()
    _remote(stage_rs.at[1], rs_out.at[across, pl.ds(half, half)], rsend.at[5], rrecv.at[5],
            rdev).wait_recv()
    for c in (to_r, to_l, via_r, via_l, fwd_r, fwd_l):
        c.wait_send()
    a2a.finish()
    own_part.wait()


def scatter_outputs(partial, share, na, nb, ntp):
    _, rows, cols = partial.shape
    _, block, width = share.shape
    share4 = share.reshape(na, nb, block, width)
    rs, new = pl.pallas_call(
        functools.partial(_out_kernel, na, nb, ntp),
        out_shape=(
            jax.ShapeDtypeStruct(partial.shape, partial.dtype),
            jax.ShapeDtypeStruct(share4.shape, share.dtype),
        ),
        in_specs=[pl.BlockSpec(memory_space=pl.ANY)] * 2,
        out_specs=(pl.BlockSpec(memory_space=pl.ANY), pl.BlockSpec(memory_space=pl.ANY)),
        scratch_shapes=[
            pltpu.VMEM((2, rows // 2, cols), partial.dtype),
            pltpu.SemaphoreType.DMA((6,)),
            pltpu.SemaphoreType.DMA((6,)),
            pltpu.SemaphoreType.DMA((1,)),
        ] + _seq_scratch(na, nb, block, width, share.dtype),
        compiler_params=pltpu.CompilerParams(collective_id=1, has_side_effects=True),
    )(partial, share4)
    return rs, new.reshape(share.shape)


def _attend_kernel(scale, lens_ref, q_ref, k_ref, v_ref, o_ref):
    chunk = q_ref.shape[0]
    capacity = k_ref.shape[0]
    held = lens_ref[0]
    first = pl.program_id(1) * chunk
    scores = lax.dot_general(
        q_ref[...], k_ref[...], (((1,), (1,)), ((), ())), preferred_element_type=jnp.float32
    ) * scale
    row_pos = first + lax.broadcasted_iota(jnp.int32, (chunk, capacity), 0)
    key_pos = lax.broadcasted_iota(jnp.int32, (chunk, capacity), 1)
    scores = jnp.where(key_pos <= held + row_pos, scores, MASKED)
    top = jnp.max(scores, axis=1, keepdims=True)
    weights = jnp.exp(scores - top)
    probs = (weights / jnp.sum(weights, axis=1, keepdims=True)).astype(jnp.bfloat16)
    o_ref[...] = jnp.dot(probs, v_ref[...], preferred_element_type=jnp.float32).astype(o_ref.dtype)


def attend(query, fresh, held_len, head_size, chunk=128):
    rows, qcols = query.shape
    capacity = fresh.shape[0]
    heads = qcols // head_size
    lens = jnp.reshape(held_len, (1,)).astype(jnp.int32)
    return pl.pallas_call(
        functools.partial(_attend_kernel, head_size ** (-0.5)),
        out_shape=jax.ShapeDtypeStruct((rows, qcols), jnp.bfloat16),
        grid_spec=pltpu.PrefetchScalarGridSpec(
            num_scalar_prefetch=1,
            grid=(heads, rows // chunk),
            in_specs=[
                pl.BlockSpec((chunk, head_size), lambda h, r, lens: (r, h)),
                pl.BlockSpec((capacity, head_size), lambda h, r, lens: (0, 0)),
                pl.BlockSpec((capacity, head_size), lambda h, r, lens: (0, 1)),
            ],
            out_specs=pl.BlockSpec((chunk, head_size), lambda h, r, lens: (r, h)),
        ),
        cost_estimate=pl.CostEstimate(
            flops=4 * rows * capacity * qcols,
            transcendentals=rows * capacity * heads,
            bytes_accessed=2 * (2 * rows * qcols + 2 * capacity * head_size),
        ),
    )(lens, query, fresh, fresh)


def _prep_kernel(ntp, held_ref, span_ref, holders_ref, targets_ref, cache_ref, kv_ref, fresh, kt,
                 share_buf, fresh32, sources_ref):
    t = lax.axis_index("tp")
    capacity, width = fresh.shape
    head_size = width // 2
    block_rows = cache_ref.shape[1]
    share = block_rows // ntp
    held = held_ref[0]
    span = span_ref[0]

    def invert(b, carry):
        sources_ref[targets_ref[b]] = b
        return carry

    lax.fori_loop(0, targets_ref.shape[0], invert, 0)

    def place(b, carry):
        fresh32[pl.ds(pl.multiple_of(b * block_rows, block_rows), block_rows), :] = (
            cache_ref[holders_ref[b]].astype(jnp.float32))
        return carry

    lax.fori_loop(0, capacity // block_rows, place, 0)
    padded = jnp.concatenate(
        [kv_ref[...].astype(jnp.float32),
         jnp.zeros((capacity - kv_ref.shape[0], width), jnp.float32)], axis=0)
    shifted = pltpu.roll(padded, held, 0)
    positions = lax.broadcasted_iota(jnp.int32, (capacity, width), 0)
    full = jnp.where(positions < held, fresh32[...],
                     jnp.where(positions < held + span, shifted, 0.0))
    fresh32[...] = full
    fresh[...] = full.astype(fresh.dtype)
    kt[...] = fresh[:, pl.ds(0, head_size)].T

    def pick(d, carry):
        start = pl.multiple_of(sources_ref[d] * block_rows + t * share, share)
        share_buf[d] = fresh32[pl.ds(start, share), :].astype(share_buf.dtype)
        return carry

    lax.fori_loop(0, share_buf.shape[0], pick, 0)


def prepare(cache, keyval, held, span, holders, targets, ntp):
    blocks, block_rows, width = cache.shape
    capacity = blocks * block_rows
    vmem = pl.BlockSpec(memory_space=pltpu.VMEM)
    smem = pl.BlockSpec(memory_space=pltpu.SMEM)
    return pl.pallas_call(
        functools.partial(_prep_kernel, ntp),
        out_shape=(
            jax.ShapeDtypeStruct((capacity, width), cache.dtype),
            jax.ShapeDtypeStruct((width // 2, capacity), cache.dtype),
            jax.ShapeDtypeStruct((blocks, block_rows // ntp, width), cache.dtype),
        ),
        in_specs=[smem, smem, smem, smem, vmem, vmem],
        out_specs=(vmem, vmem, vmem),
        scratch_shapes=[pltpu.VMEM((capacity, width), jnp.float32),
                        pltpu.SMEM((targets.shape[0],), jnp.int32)],
    )(held, span, holders, targets, cache, keyval)


def _tail_kernel(na, nb, ntp, scale, chunk, lens_ref, q_ref, fresh, kt, share_buf, w_ref,
                 rs_out, new_out, ctx, part, psend, precv, plocal, stage, s1send, s1recv, s2send,
                 s2recv, slocal):
    s = lax.axis_index("seq")
    t = lax.axis_index("tp")
    rows, qcols = q_ref.shape
    capacity, width = fresh.shape
    head_size = width // 2
    share = share_buf.shape[1]
    heads = qcols // head_size
    cols = w_ref.shape[1] // ntp
    chunks = rows // chunk
    held = lens_ref[0]

    _greet(na, nb, s, t, *[lax.rem(t + k, ntp) for k in range(1, ntp)])
    sorted4 = share_buf.reshape(na, nb, share, width)
    a2a = SeqAllToAll(na, nb, s, t, sorted4, stage, lambda a_src: new_out.at[a_src],
                      (s1send, s1recv, s2send, s2recv, slocal))
    a2a.first()

    def slice_out(c, k):
        peer = lax.rem(t + k, ntp)
        return _remote(part.at[c, :, pl.ds(pl.multiple_of(peer * cols, cols), cols)],
                       rs_out.at[t, pl.ds(pl.multiple_of(c * chunk, chunk), chunk)],
                       psend.at[c, k], precv.at[c, k], {"seq": s, "tp": peer})

    def slice_in(c, k):
        sender = lax.rem(t + ntp - k, ntp)
        return _remote(part.at[c, :, pl.ds(0, cols)],
                       rs_out.at[sender, pl.ds(pl.multiple_of(c * chunk, chunk), chunk)],
                       psend.at[c, k], precv.at[c, k], {"seq": s, "tp": sender})

    def slice_own(c):
        return pltpu.make_async_copy(
            part.at[c, :, pl.ds(pl.multiple_of(t * cols, cols), cols)],
            rs_out.at[t, pl.ds(pl.multiple_of(c * chunk, chunk), chunk)], plocal.at[c])

    def do_chunk(c):
        first = pl.multiple_of(c * chunk, chunk)
        row_pos = first + lax.broadcasted_iota(jnp.int32, (chunk, capacity), 0)
        key_pos = lax.broadcasted_iota(jnp.int32, (chunk, capacity), 1)
        allowed = key_pos <= held + row_pos
        for h in range(heads):
            q = q_ref[pl.ds(first, chunk), pl.ds(h * head_size, head_size)]
            scores = jnp.dot(q, kt[...], preferred_element_type=jnp.float32) * scale
            scores = jnp.where(allowed, scores, MASKED)
            top = jnp.max(scores, axis=1, keepdims=True)
            weights = jnp.exp(scores - top)
            inv = 1.0 / jnp.sum(weights, axis=1, keepdims=True)
            probs = (weights * inv).astype(jnp.bfloat16)
            ctx[:, pl.ds(h * head_size, head_size)] = jnp.dot(
                probs, fresh[:, pl.ds(head_size, head_size)],
                preferred_element_type=jnp.float32).astype(ctx.dtype)
        part[c] = jnp.dot(ctx[...], w_ref[...], preferred_element_type=jnp.float32).astype(
            part.dtype)
        slice_own(c).start()
        for k in range(1, ntp):
            slice_out(c, k).start()

    do_chunk(0)
    a2a.second()

    def rest(c, carry):
        do_chunk(c)
        return carry

    lax.fori_loop(1, chunks, rest, 0)
    a2a.arrived()

    def drain(c, carry):
        for k in range(1, ntp):
            slice_in(c, k).wait_recv()
            slice_out(c, k).wait_send()
        slice_own(c).wait()
        return carry

    lax.fori_loop(0, chunks, drain, 0)
    a2a.finish()


def attend_and_scatter(query, cache, keyval, held, span, holders, targets, w_out, na, nb, ntp,
                       chunk=128):
    rows, qcols = query.shape
    blocks, block_rows, width = cache.shape
    share = block_rows // ntp
    cols = w_out.shape[1] // ntp
    fresh, keys_t, sorted_share = prepare(cache, keyval, held, span, holders, targets, ntp)
    vmem = pl.BlockSpec(memory_space=pltpu.VMEM)
    smem = pl.BlockSpec(memory_space=pltpu.SMEM)
    rs, new = pl.pallas_call(
        functools.partial(_tail_kernel, na, nb, ntp, (width // 2) ** (-0.5), chunk),
        out_shape=(
            jax.ShapeDtypeStruct((ntp, rows, cols), jnp.bfloat16),
            jax.ShapeDtypeStruct((na, nb, share, width), cache.dtype),
        ),
        in_specs=[smem, vmem, vmem, vmem, vmem, vmem],
        out_specs=(pl.BlockSpec(memory_space=pl.ANY), pl.BlockSpec(memory_space=pl.ANY)),
        scratch_shapes=[
            pltpu.VMEM((chunk, qcols), jnp.bfloat16),
            pltpu.VMEM((rows // chunk, chunk, w_out.shape[1]), jnp.bfloat16),
            pltpu.SemaphoreType.DMA((rows // chunk, ntp)),
            pltpu.SemaphoreType.DMA((rows // chunk, ntp)),
            pltpu.SemaphoreType.DMA((rows // chunk,)),
        ] + _seq_scratch(na, nb, share, width, cache.dtype),
        compiler_params=pltpu.CompilerParams(collective_id=1, has_side_effects=True),
    )(held, query, fresh, keys_t, sorted_share, w_out)
    return rs, new.reshape(blocks, share, width)


def body(
    tokens,
    norm_gain,
    w_query,
    w_keyval,
    w_out,
    span_lens,
    cached_lens,
    old_table,
    new_table,
    old_cache,
):
    groups = lax.axis_size("seq")
    tp_count = lax.axis_size("tp")
    tp_index = lax.axis_index("tp")
    holders = old_table[0]
    held_len = cached_lens[0]
    span_len = span_lens[0]
    tok_rows, tok_cols = tokens.shape
    share = old_cache.shape[1]
    width = old_cache.shape[2]
    block_rows = share * tp_count
    capacity = groups * block_rows

    inner = min(groups, 8)
    outer = groups // inner
    query, keyval, cache_all = gather_inputs(
        tokens, old_cache, norm_gain, w_query, w_keyval, outer, inner, tp_count
    )
    cache_all = cache_all.reshape(groups, tp_count, share, width)

    summed, new_cache = attend_and_scatter(
        query, cache_all.reshape(groups, block_rows, width), keyval, cached_lens, span_lens,
        holders, new_table[0], w_out, outer, inner, tp_count
    )
    row_pos = lax.broadcasted_iota(jnp.int32, (tok_rows, 1), 0)
    total = tokens.astype(jnp.float32)
    for p in range(tp_count):
        total = total + summed[p].astype(jnp.float32)
    mixed = jnp.where(row_pos < span_len, total, jnp.zeros_like(total)).astype(jnp.bfloat16)
    return (mixed, new_cache)


def solution(mesh):
    in_specs = (
        P("seq", "tp"),
        P(),
        P(None, "tp"),
        P(),
        P("tp", None),
        P("seq"),
        P("seq"),
        P("seq", None),
        P("seq", None),
        P("seq", "tp", None),
    )
    out_specs = (P("seq", "tp"), P("seq", "tp", None))
    return jax.shard_map(body, mesh=mesh, in_specs=in_specs, out_specs=out_specs, check_vma=False)
```

```python
import functools

import jax
import jax.numpy as jnp
from jax import lax
from jax.experimental import pallas as pl
from jax.experimental.pallas import tpu as pltpu
from jax.sharding import PartitionSpec as P

EPSILON = 1e-05
MASKED = -1e30


def normalize(rows, norm_gain):
    values = rows.astype(jnp.float32)
    average = jnp.mean(values, axis=1, keepdims=True)
    centred = values - average
    spread = jnp.mean(centred * centred, axis=1, keepdims=True)
    return (centred * lax.rsqrt(spread + EPSILON) * norm_gain).astype(jnp.bfloat16)


MESH = pl.DeviceIdType.MESH


def _remote(src, dst, send, recv, dev):
    return pltpu.make_async_remote_copy(
        src_ref=src, dst_ref=dst, send_sem=send, recv_sem=recv, device_id=dev, device_id_type=MESH
    )


def _greet(na, nb, s, t, *tp_peers):
    barrier = pltpu.get_barrier_semaphore()
    a = s // nb
    b = s % nb

    def one_b(k, carry):
        pl.semaphore_signal(barrier, inc=1, device_id={"seq": a * nb + lax.rem(b + k, nb), "tp": t},
                            device_id_type=MESH)
        return carry

    def one_a(k, carry):
        pl.semaphore_signal(barrier, inc=1, device_id={"seq": lax.rem(a + k, na) * nb + b, "tp": t},
                            device_id_type=MESH)
        return carry

    lax.fori_loop(1, nb, one_b, 0)
    lax.fori_loop(1, na, one_a, 0)
    for p in tp_peers:
        pl.semaphore_signal(barrier, inc=1, device_id={"seq": s, "tp": p}, device_id_type=MESH)
    pl.semaphore_wait(barrier, na + nb - 2 + len(tp_peers))


class SeqAllToAll:
    def __init__(self, na, nb, s, t, src, stage, dst, sems):
        self.na, self.nb, self.t, self.src, self.stage, self.dst = na, nb, t, src, stage, dst
        self.a = s // nb
        self.b = s % nb
        self.s1send, self.s1recv, self.s2send, self.s2recv, self.local = sems

    def _dev(self, a, b):
        return {"seq": a * self.nb + b, "tp": self.t}

    def _out1(self, k):
        peer = lax.rem(self.b + k, self.nb)
        return _remote(self.src.at[:, peer], self.stage.at[self.b], self.s1send.at[k],
                       self.s1recv.at[k], self._dev(self.a, peer))

    def _in1(self, k):
        sender = lax.rem(self.b + self.nb - k, self.nb)
        return _remote(self.src.at[:, self.b], self.stage.at[sender], self.s1send.at[k],
                       self.s1recv.at[k], self._dev(self.a, sender))

    def _out2(self, k):
        peer = lax.rem(self.a + k, self.na)
        return _remote(self.stage.at[:, peer], self.dst(self.a), self.s2send.at[k],
                       self.s2recv.at[k], self._dev(peer, self.b))

    def _in2(self, k):
        sender = lax.rem(self.a + self.na - k, self.na)
        return _remote(self.stage.at[:, self.a], self.dst(sender), self.s2send.at[k],
                       self.s2recv.at[k], self._dev(sender, self.b))

    def first(self):
        self.own1 = pltpu.make_async_copy(self.src.at[:, self.b], self.stage.at[self.b],
                                          self.local.at[0])
        self.own1.start()
        _loop(self.nb, lambda k: self._out1(k).start())

    def second(self):
        _loop(self.nb, lambda k: self._in1(k).wait_recv())
        self.own1.wait()
        self.own2 = pltpu.make_async_copy(self.stage.at[:, self.a], self.dst(self.a),
                                          self.local.at[1])
        self.own2.start()
        _loop(self.na, lambda k: self._out2(k).start())

    def arrived(self):
        _loop(self.na, lambda k: self._in2(k).wait_recv())
        self.own2.wait()

    def finish(self):
        _loop(self.nb, lambda k: self._out1(k).wait_send())
        _loop(self.na, lambda k: self._out2(k).wait_send())


def _seq_scratch(na, nb, share, width, dtype):
    return [
        pltpu.VMEM((nb, na, share, width), dtype),
        pltpu.SemaphoreType.DMA((nb,)),
        pltpu.SemaphoreType.DMA((nb,)),
        pltpu.SemaphoreType.DMA((na,)),
        pltpu.SemaphoreType.DMA((na,)),
        pltpu.SemaphoreType.DMA((2,)),
    ]


def _loop(n, fn):
    def step(k, carry):
        fn(k)
        return carry

    lax.fori_loop(1, n, step, 0)


def _in_kernel(na, nb, ntp, tok_ref, cache_ref, gain_ref, wq_ref, wkv_ref, q_out, kv_out,
               cache_out, tok_all, tsend, trecv, csend, crecv, lsem, stage, s1send, s1recv,
               s2send, s2recv, slocal):
    s = lax.axis_index("seq")
    t = lax.axis_index("tp")
    right = lax.rem(t + 1, ntp)
    left = lax.rem(t + ntp - 1, ntp)
    across = lax.rem(t + 2, ntp)
    rdev = {"seq": s, "tp": right}
    ldev = {"seq": s, "tp": left}
    rows, cols = tok_ref.shape
    half = rows // 2
    _greet(na, nb, s, t, left, right, across)

    def tok_cols(p):
        return pl.ds(pl.multiple_of(p * cols, cols), cols)

    a2a = SeqAllToAll(na, nb, s, t, cache_ref, stage, lambda a_src: cache_out.at[a_src, :, t],
                      (s1send, s1recv, s2send, s2recv, slocal))
    a2a.first()

    own_tok = pltpu.make_async_copy(tok_ref, tok_all.at[:, tok_cols(t)], lsem.at[0])
    own_tok.start()
    tok_r = _remote(tok_ref, tok_all.at[:, tok_cols(t)], tsend.at[0], trecv.at[0], rdev)
    tok_l = _remote(tok_ref, tok_all.at[:, tok_cols(t)], tsend.at[1], trecv.at[1], ldev)
    tok_r.start()
    tok_l.start()

    a2a.second()

    _remote(tok_ref, tok_all.at[:, tok_cols(left)], tsend.at[0], trecv.at[0], ldev).wait_recv()
    fwd_r = _remote(tok_all.at[pl.ds(0, half), tok_cols(left)],
                    tok_all.at[pl.ds(0, half), tok_cols(left)], tsend.at[2], trecv.at[2], rdev)
    fwd_r.start()
    _remote(tok_ref, tok_all.at[:, tok_cols(right)], tsend.at[1], trecv.at[1], rdev).wait_recv()
    fwd_l = _remote(tok_all.at[pl.ds(half, half), tok_cols(right)],
                    tok_all.at[pl.ds(half, half), tok_cols(right)], tsend.at[3], trecv.at[3], ldev)
    fwd_l.start()

    a2a.arrived()
    flat = cache_out.reshape(na * nb, ntp, *cache_out.shape[3:])
    mine = flat.at[:, t]

    def cache_to(k):
        peer = lax.rem(t + k, ntp)
        return _remote(mine, mine, csend.at[k], crecv.at[k], {"seq": s, "tp": peer})

    def cache_from(k):
        sender = lax.rem(t + ntp - k, ntp)
        return _remote(mine, flat.at[:, sender], csend.at[k], crecv.at[k],
                       {"seq": s, "tp": sender})

    for k in range(1, ntp):
        cache_to(k).start()

    _remote(tok_ref.at[pl.ds(0, half)], tok_all.at[pl.ds(0, half), tok_cols(across)],
            tsend.at[2], trecv.at[2], ldev).wait_recv()
    _remote(tok_ref.at[pl.ds(half, half)], tok_all.at[pl.ds(half, half), tok_cols(across)],
            tsend.at[3], trecv.at[3], rdev).wait_recv()
    own_tok.wait()

    chunk = min(rows, 256)

    def project(c, carry):
        first = pl.multiple_of(c * chunk, chunk)
        values = tok_all[pl.ds(first, chunk), :].astype(jnp.float32)
        average = jnp.mean(values, axis=1, keepdims=True)
        centred = values - average
        spread = jnp.mean(centred * centred, axis=1, keepdims=True)
        normed = (centred * lax.rsqrt(spread + EPSILON) * gain_ref[...]).astype(jnp.bfloat16)
        q_out[pl.ds(first, chunk), :] = jnp.dot(
            normed, wq_ref[...], preferred_element_type=jnp.float32).astype(q_out.dtype)
        kv_out[pl.ds(first, chunk), :] = jnp.dot(
            normed, wkv_ref[...], preferred_element_type=jnp.float32).astype(kv_out.dtype)
        return carry

    lax.fori_loop(0, rows // chunk, project, 0)

    for k in range(1, ntp):
        cache_from(k).wait_recv()
    for c in (tok_r, tok_l, fwd_r, fwd_l):
        c.wait_send()
    for k in range(1, ntp):
        cache_to(k).wait_send()
    a2a.finish()


def gather_inputs(tokens, old_cache, norm_gain, w_query, w_keyval, na, nb, ntp):
    rows, cols = tokens.shape
    _, share, width = old_cache.shape
    cache4 = old_cache.reshape(na, nb, share, width)
    vmem = pl.BlockSpec(memory_space=pltpu.VMEM)
    anywhere = pl.BlockSpec(memory_space=pl.ANY)
    return pl.pallas_call(
        functools.partial(_in_kernel, na, nb, ntp),
        out_shape=(
            jax.ShapeDtypeStruct((rows, w_query.shape[1]), jnp.bfloat16),
            jax.ShapeDtypeStruct((rows, w_keyval.shape[1]), jnp.bfloat16),
            jax.ShapeDtypeStruct((na, nb, ntp, share, width), old_cache.dtype),
        ),
        in_specs=[anywhere, anywhere, vmem, vmem, vmem],
        out_specs=(vmem, vmem, anywhere),
        scratch_shapes=[
            pltpu.VMEM((rows, ntp * cols), tokens.dtype),
            pltpu.SemaphoreType.DMA((4,)),
            pltpu.SemaphoreType.DMA((4,)),
            pltpu.SemaphoreType.DMA((ntp,)),
            pltpu.SemaphoreType.DMA((ntp,)),
            pltpu.SemaphoreType.DMA((2,)),
        ] + _seq_scratch(na, nb, share, width, old_cache.dtype),
        compiler_params=pltpu.CompilerParams(collective_id=0, has_side_effects=True),
    )(tokens, cache4, norm_gain.reshape(1, -1).astype(jnp.float32), w_query, w_keyval)


def _out_kernel(na, nb, ntp, part_ref, share_ref, rs_out, new_out, stage_rs, rsend, rrecv, lsem,
                stage, s1send, s1recv, s2send, s2recv, slocal):
    s = lax.axis_index("seq")
    t = lax.axis_index("tp")
    right = lax.rem(t + 1, ntp)
    left = lax.rem(t + ntp - 1, ntp)
    across = lax.rem(t + 2, ntp)
    rdev = {"seq": s, "tp": right}
    ldev = {"seq": s, "tp": left}
    half = part_ref.shape[1] // 2
    _greet(na, nb, s, t, left, right)

    a2a = SeqAllToAll(na, nb, s, t, share_ref, stage, lambda a_src: new_out.at[a_src],
                      (s1send, s1recv, s2send, s2recv, slocal))
    a2a.first()

    own_part = pltpu.make_async_copy(part_ref.at[t], rs_out.at[t], lsem.at[0])
    own_part.start()
    to_r = _remote(part_ref.at[right], rs_out.at[t], rsend.at[0], rrecv.at[0], rdev)
    to_l = _remote(part_ref.at[left], rs_out.at[t], rsend.at[1], rrecv.at[1], ldev)
    via_r = _remote(part_ref.at[across, pl.ds(0, half)], stage_rs.at[0], rsend.at[2], rrecv.at[2],
                    rdev)
    via_l = _remote(part_ref.at[across, pl.ds(half, half)], stage_rs.at[1], rsend.at[3],
                    rrecv.at[3], ldev)
    for c in (to_r, to_l, via_r, via_l):
        c.start()

    a2a.second()

    _remote(part_ref.at[across, pl.ds(0, half)], stage_rs.at[0], rsend.at[2], rrecv.at[2],
            ldev).wait_recv()
    fwd_r = _remote(stage_rs.at[0], rs_out.at[left, pl.ds(0, half)], rsend.at[4], rrecv.at[4],
                    rdev)
    fwd_r.start()
    _remote(part_ref.at[across, pl.ds(half, half)], stage_rs.at[1], rsend.at[3], rrecv.at[3],
            rdev).wait_recv()
    fwd_l = _remote(stage_rs.at[1], rs_out.at[right, pl.ds(half, half)], rsend.at[5],
                    rrecv.at[5], ldev)
    fwd_l.start()

    a2a.arrived()
    _remote(part_ref.at[t], rs_out.at[left], rsend.at[0], rrecv.at[0], ldev).wait_recv()
    _remote(part_ref.at[t], rs_out.at[right], rsend.at[1], rrecv.at[1], rdev).wait_recv()
    _remote(stage_rs.at[0], rs_out.at[across, pl.ds(0, half)], rsend.at[4], rrecv.at[4],
            ldev).wait_recv()
    _remote(stage_rs.at[1], rs_out.at[across, pl.ds(half, half)], rsend.at[5], rrecv.at[5],
            rdev).wait_recv()
    for c in (to_r, to_l, via_r, via_l, fwd_r, fwd_l):
        c.wait_send()
    a2a.finish()
    own_part.wait()


def scatter_outputs(partial, share, na, nb, ntp):
    _, rows, cols = partial.shape
    _, block, width = share.shape
    share4 = share.reshape(na, nb, block, width)
    rs, new = pl.pallas_call(
        functools.partial(_out_kernel, na, nb, ntp),
        out_shape=(
            jax.ShapeDtypeStruct(partial.shape, partial.dtype),
            jax.ShapeDtypeStruct(share4.shape, share.dtype),
        ),
        in_specs=[pl.BlockSpec(memory_space=pl.ANY)] * 2,
        out_specs=(pl.BlockSpec(memory_space=pl.ANY), pl.BlockSpec(memory_space=pl.ANY)),
        scratch_shapes=[
            pltpu.VMEM((2, rows // 2, cols), partial.dtype),
            pltpu.SemaphoreType.DMA((6,)),
            pltpu.SemaphoreType.DMA((6,)),
            pltpu.SemaphoreType.DMA((1,)),
        ] + _seq_scratch(na, nb, block, width, share.dtype),
        compiler_params=pltpu.CompilerParams(collective_id=1, has_side_effects=True),
    )(partial, share4)
    return rs, new.reshape(share.shape)


def _attend_kernel(scale, lens_ref, q_ref, k_ref, v_ref, o_ref):
    chunk = q_ref.shape[0]
    capacity = k_ref.shape[0]
    held = lens_ref[0]
    first = pl.program_id(1) * chunk
    scores = lax.dot_general(
        q_ref[...], k_ref[...], (((1,), (1,)), ((), ())), preferred_element_type=jnp.float32
    ) * scale
    row_pos = first + lax.broadcasted_iota(jnp.int32, (chunk, capacity), 0)
    key_pos = lax.broadcasted_iota(jnp.int32, (chunk, capacity), 1)
    scores = jnp.where(key_pos <= held + row_pos, scores, MASKED)
    top = jnp.max(scores, axis=1, keepdims=True)
    weights = jnp.exp(scores - top)
    probs = (weights / jnp.sum(weights, axis=1, keepdims=True)).astype(jnp.bfloat16)
    o_ref[...] = jnp.dot(probs, v_ref[...], preferred_element_type=jnp.float32).astype(o_ref.dtype)


def attend(query, fresh, held_len, head_size, chunk=128):
    rows, qcols = query.shape
    capacity = fresh.shape[0]
    heads = qcols // head_size
    lens = jnp.reshape(held_len, (1,)).astype(jnp.int32)
    return pl.pallas_call(
        functools.partial(_attend_kernel, head_size ** (-0.5)),
        out_shape=jax.ShapeDtypeStruct((rows, qcols), jnp.bfloat16),
        grid_spec=pltpu.PrefetchScalarGridSpec(
            num_scalar_prefetch=1,
            grid=(heads, rows // chunk),
            in_specs=[
                pl.BlockSpec((chunk, head_size), lambda h, r, lens: (r, h)),
                pl.BlockSpec((capacity, head_size), lambda h, r, lens: (0, 0)),
                pl.BlockSpec((capacity, head_size), lambda h, r, lens: (0, 1)),
            ],
            out_specs=pl.BlockSpec((chunk, head_size), lambda h, r, lens: (r, h)),
        ),
        cost_estimate=pl.CostEstimate(
            flops=4 * rows * capacity * qcols,
            transcendentals=rows * capacity * heads,
            bytes_accessed=2 * (2 * rows * qcols + 2 * capacity * head_size),
        ),
    )(lens, query, fresh, fresh)


def _prep_kernel(ntp, held_ref, span_ref, holders_ref, targets_ref, cache_ref, kv_ref, fresh, kt,
                 share_buf, fresh32, sources_ref):
    t = lax.axis_index("tp")
    capacity, width = fresh.shape
    head_size = width // 2
    block_rows = cache_ref.shape[1]
    share = block_rows // ntp
    held = held_ref[0]
    span = span_ref[0]

    def invert(b, carry):
        sources_ref[targets_ref[b]] = b
        return carry

    lax.fori_loop(0, targets_ref.shape[0], invert, 0)

    def place(b, carry):
        fresh32[pl.ds(pl.multiple_of(b * block_rows, block_rows), block_rows), :] = (
            cache_ref[holders_ref[b]].astype(jnp.float32))
        return carry

    lax.fori_loop(0, capacity // block_rows, place, 0)
    padded = jnp.concatenate(
        [kv_ref[...].astype(jnp.float32),
         jnp.zeros((capacity - kv_ref.shape[0], width), jnp.float32)], axis=0)
    shifted = pltpu.roll(padded, held, 0)
    positions = lax.broadcasted_iota(jnp.int32, (capacity, width), 0)
    full = jnp.where(positions < held, fresh32[...],
                     jnp.where(positions < held + span, shifted, 0.0))
    fresh32[...] = full
    fresh[...] = full.astype(fresh.dtype)
    kt[...] = fresh[:, pl.ds(0, head_size)].T

    def pick(d, carry):
        start = pl.multiple_of(sources_ref[d] * block_rows + t * share, share)
        share_buf[d] = fresh32[pl.ds(start, share), :].astype(share_buf.dtype)
        return carry

    lax.fori_loop(0, share_buf.shape[0], pick, 0)


def prepare(cache, keyval, held, span, holders, targets, ntp):
    blocks, block_rows, width = cache.shape
    capacity = blocks * block_rows
    vmem = pl.BlockSpec(memory_space=pltpu.VMEM)
    smem = pl.BlockSpec(memory_space=pltpu.SMEM)
    return pl.pallas_call(
        functools.partial(_prep_kernel, ntp),
        out_shape=(
            jax.ShapeDtypeStruct((capacity, width), cache.dtype),
            jax.ShapeDtypeStruct((width // 2, capacity), cache.dtype),
            jax.ShapeDtypeStruct((blocks, block_rows // ntp, width), cache.dtype),
        ),
        in_specs=[smem, smem, smem, smem, vmem, vmem],
        out_specs=(vmem, vmem, vmem),
        scratch_shapes=[pltpu.VMEM((capacity, width), jnp.float32),
                        pltpu.SMEM((targets.shape[0],), jnp.int32)],
    )(held, span, holders, targets, cache, keyval)


def _tail_kernel(na, nb, ntp, scale, chunk, lens_ref, q_ref, fresh, kt, share_buf, w_ref,
                 rs_out, new_out, ctx, part, psend, precv, plocal, stage, s1send, s1recv, s2send,
                 s2recv, slocal):
    s = lax.axis_index("seq")
    t = lax.axis_index("tp")
    rows, qcols = q_ref.shape
    capacity, width = fresh.shape
    head_size = width // 2
    share = share_buf.shape[1]
    heads = qcols // head_size
    cols = w_ref.shape[1] // ntp
    chunks = rows // chunk
    held = lens_ref[0]

    _greet(na, nb, s, t, *[lax.rem(t + k, ntp) for k in range(1, ntp)])
    sorted4 = share_buf.reshape(na, nb, share, width)
    a2a = SeqAllToAll(na, nb, s, t, sorted4, stage, lambda a_src: new_out.at[a_src],
                      (s1send, s1recv, s2send, s2recv, slocal))
    a2a.first()

    def slice_out(c, k):
        peer = lax.rem(t + k, ntp)
        return _remote(part.at[c, :, pl.ds(pl.multiple_of(peer * cols, cols), cols)],
                       rs_out.at[t, pl.ds(pl.multiple_of(c * chunk, chunk), chunk)],
                       psend.at[c, k], precv.at[c, k], {"seq": s, "tp": peer})

    def slice_in(c, k):
        sender = lax.rem(t + ntp - k, ntp)
        return _remote(part.at[c, :, pl.ds(0, cols)],
                       rs_out.at[sender, pl.ds(pl.multiple_of(c * chunk, chunk), chunk)],
                       psend.at[c, k], precv.at[c, k], {"seq": s, "tp": sender})

    def slice_own(c):
        return pltpu.make_async_copy(
            part.at[c, :, pl.ds(pl.multiple_of(t * cols, cols), cols)],
            rs_out.at[t, pl.ds(pl.multiple_of(c * chunk, chunk), chunk)], plocal.at[c])

    def do_chunk(c):
        first = pl.multiple_of(c * chunk, chunk)
        row_pos = first + lax.broadcasted_iota(jnp.int32, (chunk, capacity), 0)
        key_pos = lax.broadcasted_iota(jnp.int32, (chunk, capacity), 1)
        allowed = key_pos <= held + row_pos
        for h in range(heads):
            q = q_ref[pl.ds(first, chunk), pl.ds(h * head_size, head_size)]
            scores = jnp.dot(q, kt[...], preferred_element_type=jnp.float32) * scale
            scores = jnp.where(allowed, scores, MASKED)
            top = jnp.max(scores, axis=1, keepdims=True)
            weights = jnp.exp(scores - top)
            inv = 1.0 / jnp.sum(weights, axis=1, keepdims=True)
            probs = (weights * inv).astype(jnp.bfloat16)
            ctx[:, pl.ds(h * head_size, head_size)] = jnp.dot(
                probs, fresh[:, pl.ds(head_size, head_size)],
                preferred_element_type=jnp.float32).astype(ctx.dtype)
        part[c] = jnp.dot(ctx[...], w_ref[...], preferred_element_type=jnp.float32).astype(
            part.dtype)
        slice_own(c).start()
        for k in range(1, ntp):
            slice_out(c, k).start()

    do_chunk(0)
    a2a.second()

    def rest(c, carry):
        do_chunk(c)
        return carry

    lax.fori_loop(1, chunks, rest, 0)
    a2a.arrived()

    def drain(c, carry):
        for k in range(1, ntp):
            slice_in(c, k).wait_recv()
            slice_out(c, k).wait_send()
        slice_own(c).wait()
        return carry

    lax.fori_loop(0, chunks, drain, 0)
    a2a.finish()


def attend_and_scatter(query, cache, keyval, held, span, holders, targets, w_out, na, nb, ntp,
                       chunk=128):
    rows, qcols = query.shape
    blocks, block_rows, width = cache.shape
    share = block_rows // ntp
    cols = w_out.shape[1] // ntp
    fresh, keys_t, sorted_share = prepare(cache, keyval, held, span, holders, targets, ntp)
    vmem = pl.BlockSpec(memory_space=pltpu.VMEM)
    smem = pl.BlockSpec(memory_space=pltpu.SMEM)
    rs, new = pl.pallas_call(
        functools.partial(_tail_kernel, na, nb, ntp, (width // 2) ** (-0.5), chunk),
        out_shape=(
            jax.ShapeDtypeStruct((ntp, rows, cols), jnp.bfloat16),
            jax.ShapeDtypeStruct((na, nb, share, width), cache.dtype),
        ),
        in_specs=[smem, vmem, vmem, vmem, vmem, vmem],
        out_specs=(pl.BlockSpec(memory_space=pl.ANY), pl.BlockSpec(memory_space=pl.ANY)),
        scratch_shapes=[
            pltpu.VMEM((chunk, qcols), jnp.bfloat16),
            pltpu.VMEM((rows // chunk, chunk, w_out.shape[1]), jnp.bfloat16),
            pltpu.SemaphoreType.DMA((rows // chunk, ntp)),
            pltpu.SemaphoreType.DMA((rows // chunk, ntp)),
            pltpu.SemaphoreType.DMA((rows // chunk,)),
        ] + _seq_scratch(na, nb, share, width, cache.dtype),
        compiler_params=pltpu.CompilerParams(collective_id=1, has_side_effects=True),
    )(held, query, fresh, keys_t, sorted_share, w_out)
    return rs, new.reshape(blocks, share, width)


def body(
    tokens,
    norm_gain,
    w_query,
    w_keyval,
    w_out,
    span_lens,
    cached_lens,
    old_table,
    new_table,
    old_cache,
):
    groups = lax.axis_size("seq")
    tp_count = lax.axis_size("tp")
    tp_index = lax.axis_index("tp")
    holders = old_table[0]
    held_len = cached_lens[0]
    span_len = span_lens[0]
    tok_rows, tok_cols = tokens.shape
    share = old_cache.shape[1]
    width = old_cache.shape[2]
    block_rows = share * tp_count
    capacity = groups * block_rows

    inner = min(groups, 8)
    outer = groups // inner
    query, keyval, cache_all = gather_inputs(
        tokens, old_cache, norm_gain, w_query, w_keyval, outer, inner, tp_count
    )
    cache_all = cache_all.reshape(groups, tp_count, share, width)

    summed, new_cache = attend_and_scatter(
        query, cache_all.reshape(groups, block_rows, width), keyval, cached_lens, span_lens,
        holders, new_table[0], w_out, outer, inner, tp_count
    )
    row_pos = lax.broadcasted_iota(jnp.int32, (tok_rows, 1), 0)
    total = tokens.astype(jnp.float32)
    for p in range(tp_count):
        total = total + summed[p].astype(jnp.float32)
    mixed = jnp.where(row_pos < span_len, total, jnp.zeros_like(total)).astype(jnp.bfloat16)
    return (mixed, new_cache)


def solution(mesh):
    in_specs = (
        P("seq", "tp"),
        P(),
        P(None, "tp"),
        P(),
        P("tp", None),
        P("seq"),
        P("seq"),
        P("seq", None),
        P("seq", None),
        P("seq", "tp", None),
    )
    out_specs = (P("seq", "tp"), P("seq", "tp", None))
    return jax.shard_map(body, mesh=mesh, in_specs=in_specs, out_specs=out_specs, check_vma=False)
```

```python
import functools

import jax
import jax.numpy as jnp
from jax import lax
from jax.experimental import pallas as pl
from jax.experimental.pallas import tpu as pltpu
from jax.sharding import PartitionSpec as P

EPSILON = 1e-05
MASKED = -1e30


def normalize(rows, norm_gain):
    values = rows.astype(jnp.float32)
    average = jnp.mean(values, axis=1, keepdims=True)
    centred = values - average
    spread = jnp.mean(centred * centred, axis=1, keepdims=True)
    return (centred * lax.rsqrt(spread + EPSILON) * norm_gain).astype(jnp.bfloat16)


MESH = pl.DeviceIdType.MESH


def _remote(src, dst, send, recv, dev):
    return pltpu.make_async_remote_copy(
        src_ref=src, dst_ref=dst, send_sem=send, recv_sem=recv, device_id=dev, device_id_type=MESH
    )


def _greet(na, nb, s, t, *tp_peers):
    barrier = pltpu.get_barrier_semaphore()
    a = s // nb
    b = s % nb

    def one_b(k, carry):
        pl.semaphore_signal(barrier, inc=1, device_id={"seq": a * nb + lax.rem(b + k, nb), "tp": t},
                            device_id_type=MESH)
        return carry

    def one_a(k, carry):
        pl.semaphore_signal(barrier, inc=1, device_id={"seq": lax.rem(a + k, na) * nb + b, "tp": t},
                            device_id_type=MESH)
        return carry

    lax.fori_loop(1, nb, one_b, 0)
    lax.fori_loop(1, na, one_a, 0)
    for p in tp_peers:
        pl.semaphore_signal(barrier, inc=1, device_id={"seq": s, "tp": p}, device_id_type=MESH)
    pl.semaphore_wait(barrier, na + nb - 2 + len(tp_peers))


class SeqAllToAll:
    def __init__(self, na, nb, s, t, src, stage, dst, sems):
        self.na, self.nb, self.t, self.src, self.stage, self.dst = na, nb, t, src, stage, dst
        self.a = s // nb
        self.b = s % nb
        self.s1send, self.s1recv, self.s2send, self.s2recv, self.local = sems

    def _dev(self, a, b):
        return {"seq": a * self.nb + b, "tp": self.t}

    def _out1(self, k):
        peer = lax.rem(self.b + k, self.nb)
        return _remote(self.src.at[:, peer], self.stage.at[self.b], self.s1send.at[k],
                       self.s1recv.at[k], self._dev(self.a, peer))

    def _in1(self, k):
        sender = lax.rem(self.b + self.nb - k, self.nb)
        return _remote(self.src.at[:, self.b], self.stage.at[sender], self.s1send.at[k],
                       self.s1recv.at[k], self._dev(self.a, sender))

    def _out2(self, k):
        peer = lax.rem(self.a + k, self.na)
        return _remote(self.stage.at[:, peer], self.dst(self.a), self.s2send.at[k],
                       self.s2recv.at[k], self._dev(peer, self.b))

    def _in2(self, k):
        sender = lax.rem(self.a + self.na - k, self.na)
        return _remote(self.stage.at[:, self.a], self.dst(sender), self.s2send.at[k],
                       self.s2recv.at[k], self._dev(sender, self.b))

    def first(self):
        self.own1 = pltpu.make_async_copy(self.src.at[:, self.b], self.stage.at[self.b],
                                          self.local.at[0])
        self.own1.start()
        _loop(self.nb, lambda k: self._out1(k).start())

    def second(self):
        _loop(self.nb, lambda k: self._in1(k).wait_recv())
        self.own1.wait()
        self.own2 = pltpu.make_async_copy(self.stage.at[:, self.a], self.dst(self.a),
                                          self.local.at[1])
        self.own2.start()
        _loop(self.na, lambda k: self._out2(k).start())

    def arrived(self):
        _loop(self.na, lambda k: self._in2(k).wait_recv())
        self.own2.wait()

    def finish(self):
        _loop(self.nb, lambda k: self._out1(k).wait_send())
        _loop(self.na, lambda k: self._out2(k).wait_send())


def _seq_scratch(na, nb, share, width, dtype):
    return [
        pltpu.VMEM((nb, na, share, width), dtype),
        pltpu.SemaphoreType.DMA((nb,)),
        pltpu.SemaphoreType.DMA((nb,)),
        pltpu.SemaphoreType.DMA((na,)),
        pltpu.SemaphoreType.DMA((na,)),
        pltpu.SemaphoreType.DMA((2,)),
    ]


def _loop(n, fn):
    def step(k, carry):
        fn(k)
        return carry

    lax.fori_loop(1, n, step, 0)


def _in_kernel(na, nb, ntp, tok_ref, cache_ref, gain_ref, wq_ref, wkv_ref, q_out, kv_out,
               cache_out, tok_all, tsend, trecv, csend, crecv, lsem, stage, s1send, s1recv,
               s2send, s2recv, slocal):
    s = lax.axis_index("seq")
    t = lax.axis_index("tp")
    right = lax.rem(t + 1, ntp)
    left = lax.rem(t + ntp - 1, ntp)
    across = lax.rem(t + 2, ntp)
    rdev = {"seq": s, "tp": right}
    ldev = {"seq": s, "tp": left}
    rows, cols = tok_ref.shape
    half = rows // 2
    _greet(na, nb, s, t, left, right, across)

    def tok_cols(p):
        return pl.ds(pl.multiple_of(p * cols, cols), cols)

    a2a = SeqAllToAll(na, nb, s, t, cache_ref, stage, lambda a_src: cache_out.at[a_src, :, t],
                      (s1send, s1recv, s2send, s2recv, slocal))
    a2a.first()

    own_tok = pltpu.make_async_copy(tok_ref, tok_all.at[:, tok_cols(t)], lsem.at[0])
    own_tok.start()
    tok_r = _remote(tok_ref, tok_all.at[:, tok_cols(t)], tsend.at[0], trecv.at[0], rdev)
    tok_l = _remote(tok_ref, tok_all.at[:, tok_cols(t)], tsend.at[1], trecv.at[1], ldev)
    tok_r.start()
    tok_l.start()

    a2a.second()

    _remote(tok_ref, tok_all.at[:, tok_cols(left)], tsend.at[0], trecv.at[0], ldev).wait_recv()
    fwd_r = _remote(tok_all.at[pl.ds(0, half), tok_cols(left)],
                    tok_all.at[pl.ds(0, half), tok_cols(left)], tsend.at[2], trecv.at[2], rdev)
    fwd_r.start()
    _remote(tok_ref, tok_all.at[:, tok_cols(right)], tsend.at[1], trecv.at[1], rdev).wait_recv()
    fwd_l = _remote(tok_all.at[pl.ds(half, half), tok_cols(right)],
                    tok_all.at[pl.ds(half, half), tok_cols(right)], tsend.at[3], trecv.at[3], ldev)
    fwd_l.start()

    a2a.arrived()
    flat = cache_out.reshape(na * nb, ntp, *cache_out.shape[3:])
    mine = flat.at[:, t]

    def cache_to(k):
        peer = lax.rem(t + k, ntp)
        return _remote(mine, mine, csend.at[k], crecv.at[k], {"seq": s, "tp": peer})

    def cache_from(k):
        sender = lax.rem(t + ntp - k, ntp)
        return _remote(mine, flat.at[:, sender], csend.at[k], crecv.at[k],
                       {"seq": s, "tp": sender})

    for k in range(1, ntp):
        cache_to(k).start()

    _remote(tok_ref.at[pl.ds(0, half)], tok_all.at[pl.ds(0, half), tok_cols(across)],
            tsend.at[2], trecv.at[2], ldev).wait_recv()
    _remote(tok_ref.at[pl.ds(half, half)], tok_all.at[pl.ds(half, half), tok_cols(across)],
            tsend.at[3], trecv.at[3], rdev).wait_recv()
    own_tok.wait()

    chunk = min(rows, 256)

    def project(c, carry):
        first = pl.multiple_of(c * chunk, chunk)
        values = tok_all[pl.ds(first, chunk), :].astype(jnp.float32)
        average = jnp.mean(values, axis=1, keepdims=True)
        centred = values - average
        spread = jnp.mean(centred * centred, axis=1, keepdims=True)
        normed = (centred * lax.rsqrt(spread + EPSILON) * gain_ref[...]).astype(jnp.bfloat16)
        q_out[pl.ds(first, chunk), :] = jnp.dot(
            normed, wq_ref[...], preferred_element_type=jnp.float32).astype(q_out.dtype)
        kv_out[pl.ds(first, chunk), :] = jnp.dot(
            normed, wkv_ref[...], preferred_element_type=jnp.float32).astype(kv_out.dtype)
        return carry

    lax.fori_loop(0, rows // chunk, project, 0)

    for k in range(1, ntp):
        cache_from(k).wait_recv()
    for c in (tok_r, tok_l, fwd_r, fwd_l):
        c.wait_send()
    for k in range(1, ntp):
        cache_to(k).wait_send()
    a2a.finish()


def gather_inputs(tokens, old_cache, norm_gain, w_query, w_keyval, na, nb, ntp):
    rows, cols = tokens.shape
    _, share, width = old_cache.shape
    cache4 = old_cache.reshape(na, nb, share, width)
    vmem = pl.BlockSpec(memory_space=pltpu.VMEM)
    anywhere = pl.BlockSpec(memory_space=pl.ANY)
    return pl.pallas_call(
        functools.partial(_in_kernel, na, nb, ntp),
        out_shape=(
            jax.ShapeDtypeStruct((rows, w_query.shape[1]), jnp.bfloat16),
            jax.ShapeDtypeStruct((rows, w_keyval.shape[1]), jnp.bfloat16),
            jax.ShapeDtypeStruct((na, nb, ntp, share, width), old_cache.dtype),
        ),
        in_specs=[anywhere, anywhere, vmem, vmem, vmem],
        out_specs=(vmem, vmem, anywhere),
        scratch_shapes=[
            pltpu.VMEM((rows, ntp * cols), tokens.dtype),
            pltpu.SemaphoreType.DMA((4,)),
            pltpu.SemaphoreType.DMA((4,)),
            pltpu.SemaphoreType.DMA((ntp,)),
            pltpu.SemaphoreType.DMA((ntp,)),
            pltpu.SemaphoreType.DMA((2,)),
        ] + _seq_scratch(na, nb, share, width, old_cache.dtype),
        compiler_params=pltpu.CompilerParams(collective_id=0, has_side_effects=True),
    )(tokens, cache4, norm_gain.reshape(1, -1).astype(jnp.float32), w_query, w_keyval)


def _out_kernel(na, nb, ntp, part_ref, share_ref, rs_out, new_out, stage_rs, rsend, rrecv, lsem,
                stage, s1send, s1recv, s2send, s2recv, slocal):
    s = lax.axis_index("seq")
    t = lax.axis_index("tp")
    right = lax.rem(t + 1, ntp)
    left = lax.rem(t + ntp - 1, ntp)
    across = lax.rem(t + 2, ntp)
    rdev = {"seq": s, "tp": right}
    ldev = {"seq": s, "tp": left}
    half = part_ref.shape[1] // 2
    _greet(na, nb, s, t, left, right)

    a2a = SeqAllToAll(na, nb, s, t, share_ref, stage, lambda a_src: new_out.at[a_src],
                      (s1send, s1recv, s2send, s2recv, slocal))
    a2a.first()

    own_part = pltpu.make_async_copy(part_ref.at[t], rs_out.at[t], lsem.at[0])
    own_part.start()
    to_r = _remote(part_ref.at[right], rs_out.at[t], rsend.at[0], rrecv.at[0], rdev)
    to_l = _remote(part_ref.at[left], rs_out.at[t], rsend.at[1], rrecv.at[1], ldev)
    via_r = _remote(part_ref.at[across, pl.ds(0, half)], stage_rs.at[0], rsend.at[2], rrecv.at[2],
                    rdev)
    via_l = _remote(part_ref.at[across, pl.ds(half, half)], stage_rs.at[1], rsend.at[3],
                    rrecv.at[3], ldev)
    for c in (to_r, to_l, via_r, via_l):
        c.start()

    a2a.second()

    _remote(part_ref.at[across, pl.ds(0, half)], stage_rs.at[0], rsend.at[2], rrecv.at[2],
            ldev).wait_recv()
    fwd_r = _remote(stage_rs.at[0], rs_out.at[left, pl.ds(0, half)], rsend.at[4], rrecv.at[4],
                    rdev)
    fwd_r.start()
    _remote(part_ref.at[across, pl.ds(half, half)], stage_rs.at[1], rsend.at[3], rrecv.at[3],
            rdev).wait_recv()
    fwd_l = _remote(stage_rs.at[1], rs_out.at[right, pl.ds(half, half)], rsend.at[5],
                    rrecv.at[5], ldev)
    fwd_l.start()

    a2a.arrived()
    _remote(part_ref.at[t], rs_out.at[left], rsend.at[0], rrecv.at[0], ldev).wait_recv()
    _remote(part_ref.at[t], rs_out.at[right], rsend.at[1], rrecv.at[1], rdev).wait_recv()
    _remote(stage_rs.at[0], rs_out.at[across, pl.ds(0, half)], rsend.at[4], rrecv.at[4],
            ldev).wait_recv()
    _remote(stage_rs.at[1], rs_out.at[across, pl.ds(half, half)], rsend.at[5], rrecv.at[5],
            rdev).wait_recv()
    for c in (to_r, to_l, via_r, via_l, fwd_r, fwd_l):
        c.wait_send()
    a2a.finish()
    own_part.wait()


def scatter_outputs(partial, share, na, nb, ntp):
    _, rows, cols = partial.shape
    _, block, width = share.shape
    share4 = share.reshape(na, nb, block, width)
    rs, new = pl.pallas_call(
        functools.partial(_out_kernel, na, nb, ntp),
        out_shape=(
            jax.ShapeDtypeStruct(partial.shape, partial.dtype),
            jax.ShapeDtypeStruct(share4.shape, share.dtype),
        ),
        in_specs=[pl.BlockSpec(memory_space=pl.ANY)] * 2,
        out_specs=(pl.BlockSpec(memory_space=pl.ANY), pl.BlockSpec(memory_space=pl.ANY)),
        scratch_shapes=[
            pltpu.VMEM((2, rows // 2, cols), partial.dtype),
            pltpu.SemaphoreType.DMA((6,)),
            pltpu.SemaphoreType.DMA((6,)),
            pltpu.SemaphoreType.DMA((1,)),
        ] + _seq_scratch(na, nb, block, width, share.dtype),
        compiler_params=pltpu.CompilerParams(collective_id=1, has_side_effects=True),
    )(partial, share4)
    return rs, new.reshape(share.shape)


def _attend_kernel(scale, lens_ref, q_ref, k_ref, v_ref, o_ref):
    chunk = q_ref.shape[0]
    capacity = k_ref.shape[0]
    held = lens_ref[0]
    first = pl.program_id(1) * chunk
    scores = lax.dot_general(
        q_ref[...], k_ref[...], (((1,), (1,)), ((), ())), preferred_element_type=jnp.float32
    ) * scale
    row_pos = first + lax.broadcasted_iota(jnp.int32, (chunk, capacity), 0)
    key_pos = lax.broadcasted_iota(jnp.int32, (chunk, capacity), 1)
    scores = jnp.where(key_pos <= held + row_pos, scores, MASKED)
    top = jnp.max(scores, axis=1, keepdims=True)
    weights = jnp.exp(scores - top)
    probs = (weights / jnp.sum(weights, axis=1, keepdims=True)).astype(jnp.bfloat16)
    o_ref[...] = jnp.dot(probs, v_ref[...], preferred_element_type=jnp.float32).astype(o_ref.dtype)


def attend(query, fresh, held_len, head_size, chunk=128):
    rows, qcols = query.shape
    capacity = fresh.shape[0]
    heads = qcols // head_size
    lens = jnp.reshape(held_len, (1,)).astype(jnp.int32)
    return pl.pallas_call(
        functools.partial(_attend_kernel, head_size ** (-0.5)),
        out_shape=jax.ShapeDtypeStruct((rows, qcols), jnp.bfloat16),
        grid_spec=pltpu.PrefetchScalarGridSpec(
            num_scalar_prefetch=1,
            grid=(heads, rows // chunk),
            in_specs=[
                pl.BlockSpec((chunk, head_size), lambda h, r, lens: (r, h)),
                pl.BlockSpec((capacity, head_size), lambda h, r, lens: (0, 0)),
                pl.BlockSpec((capacity, head_size), lambda h, r, lens: (0, 1)),
            ],
            out_specs=pl.BlockSpec((chunk, head_size), lambda h, r, lens: (r, h)),
        ),
        cost_estimate=pl.CostEstimate(
            flops=4 * rows * capacity * qcols,
            transcendentals=rows * capacity * heads,
            bytes_accessed=2 * (2 * rows * qcols + 2 * capacity * head_size),
        ),
    )(lens, query, fresh, fresh)


def _prep_kernel(ntp, held_ref, span_ref, holders_ref, targets_ref, cache_ref, kv_ref, fresh, kt,
                 share_buf, fresh32, sources_ref):
    t = lax.axis_index("tp")
    capacity, width = fresh.shape
    head_size = width // 2
    block_rows = cache_ref.shape[1]
    share = block_rows // ntp
    held = held_ref[0]
    span = span_ref[0]

    def invert(b, carry):
        sources_ref[targets_ref[b]] = b
        return carry

    lax.fori_loop(0, targets_ref.shape[0], invert, 0)

    def place(b, carry):
        fresh32[pl.ds(pl.multiple_of(b * block_rows, block_rows), block_rows), :] = (
            cache_ref[holders_ref[b]].astype(jnp.float32))
        return carry

    lax.fori_loop(0, capacity // block_rows, place, 0)
    padded = jnp.concatenate(
        [kv_ref[...].astype(jnp.float32),
         jnp.zeros((capacity - kv_ref.shape[0], width), jnp.float32)], axis=0)
    shifted = pltpu.roll(padded, held, 0)
    positions = lax.broadcasted_iota(jnp.int32, (capacity, width), 0)
    full = jnp.where(positions < held, fresh32[...],
                     jnp.where(positions < held + span, shifted, 0.0))
    fresh32[...] = full
    fresh[...] = full.astype(fresh.dtype)
    kt[...] = fresh[:, pl.ds(0, head_size)].T

    def pick(d, carry):
        start = pl.multiple_of(sources_ref[d] * block_rows + t * share, share)
        share_buf[d] = fresh32[pl.ds(start, share), :].astype(share_buf.dtype)
        return carry

    lax.fori_loop(0, share_buf.shape[0], pick, 0)


def prepare(cache, keyval, held, span, holders, targets, ntp):
    blocks, block_rows, width = cache.shape
    capacity = blocks * block_rows
    vmem = pl.BlockSpec(memory_space=pltpu.VMEM)
    smem = pl.BlockSpec(memory_space=pltpu.SMEM)
    return pl.pallas_call(
        functools.partial(_prep_kernel, ntp),
        out_shape=(
            jax.ShapeDtypeStruct((capacity, width), cache.dtype),
            jax.ShapeDtypeStruct((width // 2, capacity), cache.dtype),
            jax.ShapeDtypeStruct((blocks, block_rows // ntp, width), cache.dtype),
        ),
        in_specs=[smem, smem, smem, smem, vmem, vmem],
        out_specs=(vmem, vmem, vmem),
        scratch_shapes=[pltpu.VMEM((capacity, width), jnp.float32),
                        pltpu.SMEM((targets.shape[0],), jnp.int32)],
    )(held, span, holders, targets, cache, keyval)


def _tail_kernel(na, nb, ntp, scale, chunk, lens_ref, q_ref, fresh, kt, share_buf, w_ref,
                 rs_out, new_out, ctx, part, psend, precv, plocal, stage, s1send, s1recv, s2send,
                 s2recv, slocal):
    s = lax.axis_index("seq")
    t = lax.axis_index("tp")
    rows, qcols = q_ref.shape
    capacity, width = fresh.shape
    head_size = width // 2
    share = share_buf.shape[1]
    heads = qcols // head_size
    cols = w_ref.shape[1] // ntp
    chunks = rows // chunk
    held = lens_ref[0]

    _greet(na, nb, s, t, *[lax.rem(t + k, ntp) for k in range(1, ntp)])
    sorted4 = share_buf.reshape(na, nb, share, width)
    a2a = SeqAllToAll(na, nb, s, t, sorted4, stage, lambda a_src: new_out.at[a_src],
                      (s1send, s1recv, s2send, s2recv, slocal))
    a2a.first()

    def slice_out(c, k):
        peer = lax.rem(t + k, ntp)
        return _remote(part.at[c, :, pl.ds(pl.multiple_of(peer * cols, cols), cols)],
                       rs_out.at[t, pl.ds(pl.multiple_of(c * chunk, chunk), chunk)],
                       psend.at[c, k], precv.at[c, k], {"seq": s, "tp": peer})

    def slice_in(c, k):
        sender = lax.rem(t + ntp - k, ntp)
        return _remote(part.at[c, :, pl.ds(0, cols)],
                       rs_out.at[sender, pl.ds(pl.multiple_of(c * chunk, chunk), chunk)],
                       psend.at[c, k], precv.at[c, k], {"seq": s, "tp": sender})

    def slice_own(c):
        return pltpu.make_async_copy(
            part.at[c, :, pl.ds(pl.multiple_of(t * cols, cols), cols)],
            rs_out.at[t, pl.ds(pl.multiple_of(c * chunk, chunk), chunk)], plocal.at[c])

    def do_chunk(c):
        first = pl.multiple_of(c * chunk, chunk)
        row_pos = first + lax.broadcasted_iota(jnp.int32, (chunk, capacity), 0)
        key_pos = lax.broadcasted_iota(jnp.int32, (chunk, capacity), 1)
        allowed = key_pos <= held + row_pos
        for h in range(heads):
            q = q_ref[pl.ds(first, chunk), pl.ds(h * head_size, head_size)]
            scores = jnp.dot(q, kt[...], preferred_element_type=jnp.float32) * scale
            scores = jnp.where(allowed, scores, MASKED)
            top = jnp.max(scores, axis=1, keepdims=True)
            weights = jnp.exp(scores - top)
            inv = 1.0 / jnp.sum(weights, axis=1, keepdims=True)
            probs = (weights * inv).astype(jnp.bfloat16)
            ctx[:, pl.ds(h * head_size, head_size)] = jnp.dot(
                probs, fresh[:, pl.ds(head_size, head_size)],
                preferred_element_type=jnp.float32).astype(ctx.dtype)
        part[c] = jnp.dot(ctx[...], w_ref[...], preferred_element_type=jnp.float32).astype(
            part.dtype)
        slice_own(c).start()
        for k in range(1, ntp):
            slice_out(c, k).start()

    do_chunk(0)
    a2a.second()

    def rest(c, carry):
        do_chunk(c)
        return carry

    lax.fori_loop(1, chunks, rest, 0)
    a2a.arrived()

    def drain(c, carry):
        for k in range(1, ntp):
            slice_in(c, k).wait_recv()
            slice_out(c, k).wait_send()
        slice_own(c).wait()
        return carry

    lax.fori_loop(0, chunks, drain, 0)
    a2a.finish()


def attend_and_scatter(query, cache, keyval, held, span, holders, targets, w_out, na, nb, ntp,
                       chunk=256):
    rows, qcols = query.shape
    blocks, block_rows, width = cache.shape
    share = block_rows // ntp
    cols = w_out.shape[1] // ntp
    fresh, keys_t, sorted_share = prepare(cache, keyval, held, span, holders, targets, ntp)
    vmem = pl.BlockSpec(memory_space=pltpu.VMEM)
    smem = pl.BlockSpec(memory_space=pltpu.SMEM)
    rs, new = pl.pallas_call(
        functools.partial(_tail_kernel, na, nb, ntp, (width // 2) ** (-0.5), chunk),
        out_shape=(
            jax.ShapeDtypeStruct((ntp, rows, cols), jnp.bfloat16),
            jax.ShapeDtypeStruct((na, nb, share, width), cache.dtype),
        ),
        in_specs=[smem, vmem, vmem, vmem, vmem, vmem],
        out_specs=(pl.BlockSpec(memory_space=pl.ANY), pl.BlockSpec(memory_space=pl.ANY)),
        scratch_shapes=[
            pltpu.VMEM((chunk, qcols), jnp.bfloat16),
            pltpu.VMEM((rows // chunk, chunk, w_out.shape[1]), jnp.bfloat16),
            pltpu.SemaphoreType.DMA((rows // chunk, ntp)),
            pltpu.SemaphoreType.DMA((rows // chunk, ntp)),
            pltpu.SemaphoreType.DMA((rows // chunk,)),
        ] + _seq_scratch(na, nb, share, width, cache.dtype),
        compiler_params=pltpu.CompilerParams(collective_id=1, has_side_effects=True),
    )(held, query, fresh, keys_t, sorted_share, w_out)
    return rs, new.reshape(blocks, share, width)


def body(
    tokens,
    norm_gain,
    w_query,
    w_keyval,
    w_out,
    span_lens,
    cached_lens,
    old_table,
    new_table,
    old_cache,
):
    groups = lax.axis_size("seq")
    tp_count = lax.axis_size("tp")
    tp_index = lax.axis_index("tp")
    holders = old_table[0]
    held_len = cached_lens[0]
    span_len = span_lens[0]
    tok_rows, tok_cols = tokens.shape
    share = old_cache.shape[1]
    width = old_cache.shape[2]
    block_rows = share * tp_count
    capacity = groups * block_rows

    inner = min(groups, 8)
    outer = groups // inner
    query, keyval, cache_all = gather_inputs(
        tokens, old_cache, norm_gain, w_query, w_keyval, outer, inner, tp_count
    )
    cache_all = cache_all.reshape(groups, tp_count, share, width)

    summed, new_cache = attend_and_scatter(
        query, cache_all.reshape(groups, block_rows, width), keyval, cached_lens, span_lens,
        holders, new_table[0], w_out, outer, inner, tp_count
    )
    row_pos = lax.broadcasted_iota(jnp.int32, (tok_rows, 1), 0)
    total = tokens.astype(jnp.float32)
    for p in range(tp_count):
        total = total + summed[p].astype(jnp.float32)
    mixed = jnp.where(row_pos < span_len, total, jnp.zeros_like(total)).astype(jnp.bfloat16)
    return (mixed, new_cache)


def solution(mesh):
    in_specs = (
        P("seq", "tp"),
        P(),
        P(None, "tp"),
        P(),
        P("tp", None),
        P("seq"),
        P("seq"),
        P("seq", None),
        P("seq", None),
        P("seq", "tp", None),
    )
    out_specs = (P("seq", "tp"), P("seq", "tp", None))
    return jax.shard_map(body, mesh=mesh, in_specs=in_specs, out_specs=out_specs, check_vma=False)
```

```python
import functools

import jax
import jax.numpy as jnp
from jax import lax
from jax.experimental import pallas as pl
from jax.experimental.pallas import tpu as pltpu
from jax.sharding import PartitionSpec as P

EPSILON = 1e-05
MASKED = -1e30


def normalize(rows, norm_gain):
    values = rows.astype(jnp.float32)
    average = jnp.mean(values, axis=1, keepdims=True)
    centred = values - average
    spread = jnp.mean(centred * centred, axis=1, keepdims=True)
    return (centred * lax.rsqrt(spread + EPSILON) * norm_gain).astype(jnp.bfloat16)


MESH = pl.DeviceIdType.MESH


def _remote(src, dst, send, recv, dev):
    return pltpu.make_async_remote_copy(
        src_ref=src, dst_ref=dst, send_sem=send, recv_sem=recv, device_id=dev, device_id_type=MESH
    )


def _greet(na, nb, s, t, *tp_peers):
    barrier = pltpu.get_barrier_semaphore()
    a = s // nb
    b = s % nb

    def one_b(k, carry):
        pl.semaphore_signal(barrier, inc=1, device_id={"seq": a * nb + lax.rem(b + k, nb), "tp": t},
                            device_id_type=MESH)
        return carry

    def one_a(k, carry):
        pl.semaphore_signal(barrier, inc=1, device_id={"seq": lax.rem(a + k, na) * nb + b, "tp": t},
                            device_id_type=MESH)
        return carry

    lax.fori_loop(1, nb, one_b, 0)
    lax.fori_loop(1, na, one_a, 0)
    for p in tp_peers:
        pl.semaphore_signal(barrier, inc=1, device_id={"seq": s, "tp": p}, device_id_type=MESH)
    pl.semaphore_wait(barrier, na + nb - 2 + len(tp_peers))


class SeqAllToAll:
    def __init__(self, na, nb, s, t, src, stage, dst, sems):
        self.na, self.nb, self.t, self.src, self.stage, self.dst = na, nb, t, src, stage, dst
        self.a = s // nb
        self.b = s % nb
        self.s1send, self.s1recv, self.s2send, self.s2recv, self.local = sems

    def _dev(self, a, b):
        return {"seq": a * self.nb + b, "tp": self.t}

    def _out1(self, k):
        peer = lax.rem(self.b + k, self.nb)
        return _remote(self.src.at[:, peer], self.stage.at[self.b], self.s1send.at[k],
                       self.s1recv.at[k], self._dev(self.a, peer))

    def _in1(self, k):
        sender = lax.rem(self.b + self.nb - k, self.nb)
        return _remote(self.src.at[:, self.b], self.stage.at[sender], self.s1send.at[k],
                       self.s1recv.at[k], self._dev(self.a, sender))

    def _out2(self, k):
        peer = lax.rem(self.a + k, self.na)
        return _remote(self.stage.at[:, peer], self.dst(self.a), self.s2send.at[k],
                       self.s2recv.at[k], self._dev(peer, self.b))

    def _in2(self, k):
        sender = lax.rem(self.a + self.na - k, self.na)
        return _remote(self.stage.at[:, self.a], self.dst(sender), self.s2send.at[k],
                       self.s2recv.at[k], self._dev(sender, self.b))

    def first(self):
        self.own1 = pltpu.make_async_copy(self.src.at[:, self.b], self.stage.at[self.b],
                                          self.local.at[0])
        self.own1.start()
        _loop(self.nb, lambda k: self._out1(k).start())

    def second(self):
        _loop(self.nb, lambda k: self._in1(k).wait_recv())
        self.own1.wait()
        self.own2 = pltpu.make_async_copy(self.stage.at[:, self.a], self.dst(self.a),
                                          self.local.at[1])
        self.own2.start()
        _loop(self.na, lambda k: self._out2(k).start())

    def arrived(self):
        _loop(self.na, lambda k: self._in2(k).wait_recv())
        self.own2.wait()

    def finish(self):
        _loop(self.nb, lambda k: self._out1(k).wait_send())
        _loop(self.na, lambda k: self._out2(k).wait_send())


def _seq_scratch(na, nb, share, width, dtype):
    return [
        pltpu.VMEM((nb, na, share, width), dtype),
        pltpu.SemaphoreType.DMA((nb,)),
        pltpu.SemaphoreType.DMA((nb,)),
        pltpu.SemaphoreType.DMA((na,)),
        pltpu.SemaphoreType.DMA((na,)),
        pltpu.SemaphoreType.DMA((2,)),
    ]


def _loop(n, fn):
    def step(k, carry):
        fn(k)
        return carry

    lax.fori_loop(1, n, step, 0)


def _in_kernel(na, nb, ntp, tok_ref, cache_ref, gain_ref, wq_ref, wkv_ref, q_out, kv_out,
               cache_out, tok_all, tsend, trecv, csend, crecv, lsem, stage, s1send, s1recv,
               s2send, s2recv, slocal):
    s = lax.axis_index("seq")
    t = lax.axis_index("tp")
    right = lax.rem(t + 1, ntp)
    left = lax.rem(t + ntp - 1, ntp)
    across = lax.rem(t + 2, ntp)
    rdev = {"seq": s, "tp": right}
    ldev = {"seq": s, "tp": left}
    rows, cols = tok_ref.shape
    half = rows // 2
    _greet(na, nb, s, t, left, right, across)

    def tok_cols(p):
        return pl.ds(pl.multiple_of(p * cols, cols), cols)

    a2a = SeqAllToAll(na, nb, s, t, cache_ref, stage, lambda a_src: cache_out.at[a_src, :, t],
                      (s1send, s1recv, s2send, s2recv, slocal))
    a2a.first()

    own_tok = pltpu.make_async_copy(tok_ref, tok_all.at[:, tok_cols(t)], lsem.at[0])
    own_tok.start()
    tok_r = _remote(tok_ref, tok_all.at[:, tok_cols(t)], tsend.at[0], trecv.at[0], rdev)
    tok_l = _remote(tok_ref, tok_all.at[:, tok_cols(t)], tsend.at[1], trecv.at[1], ldev)
    tok_r.start()
    tok_l.start()

    a2a.second()

    _remote(tok_ref, tok_all.at[:, tok_cols(left)], tsend.at[0], trecv.at[0], ldev).wait_recv()
    fwd_r = _remote(tok_all.at[pl.ds(0, half), tok_cols(left)],
                    tok_all.at[pl.ds(0, half), tok_cols(left)], tsend.at[2], trecv.at[2], rdev)
    fwd_r.start()
    _remote(tok_ref, tok_all.at[:, tok_cols(right)], tsend.at[1], trecv.at[1], rdev).wait_recv()
    fwd_l = _remote(tok_all.at[pl.ds(half, half), tok_cols(right)],
                    tok_all.at[pl.ds(half, half), tok_cols(right)], tsend.at[3], trecv.at[3], ldev)
    fwd_l.start()

    a2a.arrived()
    flat = cache_out.reshape(na * nb, ntp, *cache_out.shape[3:])
    mine = flat.at[:, t]

    def cache_to(k):
        peer = lax.rem(t + k, ntp)
        return _remote(mine, mine, csend.at[k], crecv.at[k], {"seq": s, "tp": peer})

    def cache_from(k):
        sender = lax.rem(t + ntp - k, ntp)
        return _remote(mine, flat.at[:, sender], csend.at[k], crecv.at[k],
                       {"seq": s, "tp": sender})

    for k in range(1, ntp):
        cache_to(k).start()

    _remote(tok_ref.at[pl.ds(0, half)], tok_all.at[pl.ds(0, half), tok_cols(across)],
            tsend.at[2], trecv.at[2], ldev).wait_recv()
    _remote(tok_ref.at[pl.ds(half, half)], tok_all.at[pl.ds(half, half), tok_cols(across)],
            tsend.at[3], trecv.at[3], rdev).wait_recv()
    own_tok.wait()

    chunk = min(rows, 256)

    def project(c, carry):
        first = pl.multiple_of(c * chunk, chunk)
        values = tok_all[pl.ds(first, chunk), :].astype(jnp.float32)
        average = jnp.mean(values, axis=1, keepdims=True)
        centred = values - average
        spread = jnp.mean(centred * centred, axis=1, keepdims=True)
        normed = (centred * lax.rsqrt(spread + EPSILON) * gain_ref[...]).astype(jnp.bfloat16)
        q_out[pl.ds(first, chunk), :] = jnp.dot(
            normed, wq_ref[...], preferred_element_type=jnp.float32).astype(q_out.dtype)
        kv_out[pl.ds(first, chunk), :] = jnp.dot(
            normed, wkv_ref[...], preferred_element_type=jnp.float32).astype(kv_out.dtype)
        return carry

    lax.fori_loop(0, rows // chunk, project, 0)

    for k in range(1, ntp):
        cache_from(k).wait_recv()
    for c in (tok_r, tok_l, fwd_r, fwd_l):
        c.wait_send()
    for k in range(1, ntp):
        cache_to(k).wait_send()
    a2a.finish()


def gather_inputs(tokens, old_cache, norm_gain, w_query, w_keyval, na, nb, ntp):
    rows, cols = tokens.shape
    _, share, width = old_cache.shape
    cache4 = old_cache.reshape(na, nb, share, width)
    vmem = pl.BlockSpec(memory_space=pltpu.VMEM)
    anywhere = pl.BlockSpec(memory_space=pl.ANY)
    return pl.pallas_call(
        functools.partial(_in_kernel, na, nb, ntp),
        out_shape=(
            jax.ShapeDtypeStruct((rows, w_query.shape[1]), jnp.bfloat16),
            jax.ShapeDtypeStruct((rows, w_keyval.shape[1]), jnp.bfloat16),
            jax.ShapeDtypeStruct((na, nb, ntp, share, width), old_cache.dtype),
        ),
        in_specs=[anywhere, anywhere, vmem, vmem, vmem],
        out_specs=(vmem, vmem, anywhere),
        scratch_shapes=[
            pltpu.VMEM((rows, ntp * cols), tokens.dtype),
            pltpu.SemaphoreType.DMA((4,)),
            pltpu.SemaphoreType.DMA((4,)),
            pltpu.SemaphoreType.DMA((ntp,)),
            pltpu.SemaphoreType.DMA((ntp,)),
            pltpu.SemaphoreType.DMA((2,)),
        ] + _seq_scratch(na, nb, share, width, old_cache.dtype),
        compiler_params=pltpu.CompilerParams(collective_id=0, has_side_effects=True),
    )(tokens, cache4, norm_gain.reshape(1, -1).astype(jnp.float32), w_query, w_keyval)


def _out_kernel(na, nb, ntp, part_ref, share_ref, rs_out, new_out, stage_rs, rsend, rrecv, lsem,
                stage, s1send, s1recv, s2send, s2recv, slocal):
    s = lax.axis_index("seq")
    t = lax.axis_index("tp")
    right = lax.rem(t + 1, ntp)
    left = lax.rem(t + ntp - 1, ntp)
    across = lax.rem(t + 2, ntp)
    rdev = {"seq": s, "tp": right}
    ldev = {"seq": s, "tp": left}
    half = part_ref.shape[1] // 2
    _greet(na, nb, s, t, left, right)

    a2a = SeqAllToAll(na, nb, s, t, share_ref, stage, lambda a_src: new_out.at[a_src],
                      (s1send, s1recv, s2send, s2recv, slocal))
    a2a.first()

    own_part = pltpu.make_async_copy(part_ref.at[t], rs_out.at[t], lsem.at[0])
    own_part.start()
    to_r = _remote(part_ref.at[right], rs_out.at[t], rsend.at[0], rrecv.at[0], rdev)
    to_l = _remote(part_ref.at[left], rs_out.at[t], rsend.at[1], rrecv.at[1], ldev)
    via_r = _remote(part_ref.at[across, pl.ds(0, half)], stage_rs.at[0], rsend.at[2], rrecv.at[2],
                    rdev)
    via_l = _remote(part_ref.at[across, pl.ds(half, half)], stage_rs.at[1], rsend.at[3],
                    rrecv.at[3], ldev)
    for c in (to_r, to_l, via_r, via_l):
        c.start()

    a2a.second()

    _remote(part_ref.at[across, pl.ds(0, half)], stage_rs.at[0], rsend.at[2], rrecv.at[2],
            ldev).wait_recv()
    fwd_r = _remote(stage_rs.at[0], rs_out.at[left, pl.ds(0, half)], rsend.at[4], rrecv.at[4],
                    rdev)
    fwd_r.start()
    _remote(part_ref.at[across, pl.ds(half, half)], stage_rs.at[1], rsend.at[3], rrecv.at[3],
            rdev).wait_recv()
    fwd_l = _remote(stage_rs.at[1], rs_out.at[right, pl.ds(half, half)], rsend.at[5],
                    rrecv.at[5], ldev)
    fwd_l.start()

    a2a.arrived()
    _remote(part_ref.at[t], rs_out.at[left], rsend.at[0], rrecv.at[0], ldev).wait_recv()
    _remote(part_ref.at[t], rs_out.at[right], rsend.at[1], rrecv.at[1], rdev).wait_recv()
    _remote(stage_rs.at[0], rs_out.at[across, pl.ds(0, half)], rsend.at[4], rrecv.at[4],
            ldev).wait_recv()
    _remote(stage_rs.at[1], rs_out.at[across, pl.ds(half, half)], rsend.at[5], rrecv.at[5],
            rdev).wait_recv()
    for c in (to_r, to_l, via_r, via_l, fwd_r, fwd_l):
        c.wait_send()
    a2a.finish()
    own_part.wait()


def scatter_outputs(partial, share, na, nb, ntp):
    _, rows, cols = partial.shape
    _, block, width = share.shape
    share4 = share.reshape(na, nb, block, width)
    rs, new = pl.pallas_call(
        functools.partial(_out_kernel, na, nb, ntp),
        out_shape=(
            jax.ShapeDtypeStruct(partial.shape, partial.dtype),
            jax.ShapeDtypeStruct(share4.shape, share.dtype),
        ),
        in_specs=[pl.BlockSpec(memory_space=pl.ANY)] * 2,
        out_specs=(pl.BlockSpec(memory_space=pl.ANY), pl.BlockSpec(memory_space=pl.ANY)),
        scratch_shapes=[
            pltpu.VMEM((2, rows // 2, cols), partial.dtype),
            pltpu.SemaphoreType.DMA((6,)),
            pltpu.SemaphoreType.DMA((6,)),
            pltpu.SemaphoreType.DMA((1,)),
        ] + _seq_scratch(na, nb, block, width, share.dtype),
        compiler_params=pltpu.CompilerParams(collective_id=1, has_side_effects=True),
    )(partial, share4)
    return rs, new.reshape(share.shape)


def _attend_kernel(scale, lens_ref, q_ref, k_ref, v_ref, o_ref):
    chunk = q_ref.shape[0]
    capacity = k_ref.shape[0]
    held = lens_ref[0]
    first = pl.program_id(1) * chunk
    scores = lax.dot_general(
        q_ref[...], k_ref[...], (((1,), (1,)), ((), ())), preferred_element_type=jnp.float32
    ) * scale
    row_pos = first + lax.broadcasted_iota(jnp.int32, (chunk, capacity), 0)
    key_pos = lax.broadcasted_iota(jnp.int32, (chunk, capacity), 1)
    scores = jnp.where(key_pos <= held + row_pos, scores, MASKED)
    top = jnp.max(scores, axis=1, keepdims=True)
    weights = jnp.exp(scores - top)
    probs = (weights / jnp.sum(weights, axis=1, keepdims=True)).astype(jnp.bfloat16)
    o_ref[...] = jnp.dot(probs, v_ref[...], preferred_element_type=jnp.float32).astype(o_ref.dtype)


def attend(query, fresh, held_len, head_size, chunk=128):
    rows, qcols = query.shape
    capacity = fresh.shape[0]
    heads = qcols // head_size
    lens = jnp.reshape(held_len, (1,)).astype(jnp.int32)
    return pl.pallas_call(
        functools.partial(_attend_kernel, head_size ** (-0.5)),
        out_shape=jax.ShapeDtypeStruct((rows, qcols), jnp.bfloat16),
        grid_spec=pltpu.PrefetchScalarGridSpec(
            num_scalar_prefetch=1,
            grid=(heads, rows // chunk),
            in_specs=[
                pl.BlockSpec((chunk, head_size), lambda h, r, lens: (r, h)),
                pl.BlockSpec((capacity, head_size), lambda h, r, lens: (0, 0)),
                pl.BlockSpec((capacity, head_size), lambda h, r, lens: (0, 1)),
            ],
            out_specs=pl.BlockSpec((chunk, head_size), lambda h, r, lens: (r, h)),
        ),
        cost_estimate=pl.CostEstimate(
            flops=4 * rows * capacity * qcols,
            transcendentals=rows * capacity * heads,
            bytes_accessed=2 * (2 * rows * qcols + 2 * capacity * head_size),
        ),
    )(lens, query, fresh, fresh)


def _prep_kernel(ntp, held_ref, span_ref, holders_ref, targets_ref, cache_ref, kv_ref, fresh, kt,
                 share_buf, fresh32, sources_ref):
    t = lax.axis_index("tp")
    capacity, width = fresh.shape
    head_size = width // 2
    block_rows = cache_ref.shape[1]
    share = block_rows // ntp
    held = held_ref[0]
    span = span_ref[0]

    def invert(b, carry):
        sources_ref[targets_ref[b]] = b
        return carry

    lax.fori_loop(0, targets_ref.shape[0], invert, 0, unroll=8)

    def place(b, carry):
        fresh32[pl.ds(pl.multiple_of(b * block_rows, block_rows), block_rows), :] = (
            cache_ref[holders_ref[b]].astype(jnp.float32))
        return carry

    lax.fori_loop(0, capacity // block_rows, place, 0, unroll=8)
    padded = jnp.concatenate(
        [kv_ref[...].astype(jnp.float32),
         jnp.zeros((capacity - kv_ref.shape[0], width), jnp.float32)], axis=0)
    shifted = pltpu.roll(padded, held, 0)
    positions = lax.broadcasted_iota(jnp.int32, (capacity, width), 0)
    full = jnp.where(positions < held, fresh32[...],
                     jnp.where(positions < held + span, shifted, 0.0))
    fresh32[...] = full
    fresh[...] = full.astype(fresh.dtype)
    kt[...] = fresh[:, pl.ds(0, head_size)].T

    def pick(d, carry):
        start = pl.multiple_of(sources_ref[d] * block_rows + t * share, share)
        share_buf[d] = fresh32[pl.ds(start, share), :].astype(share_buf.dtype)
        return carry

    lax.fori_loop(0, share_buf.shape[0], pick, 0, unroll=8)


def prepare(cache, keyval, held, span, holders, targets, ntp):
    blocks, block_rows, width = cache.shape
    capacity = blocks * block_rows
    vmem = pl.BlockSpec(memory_space=pltpu.VMEM)
    smem = pl.BlockSpec(memory_space=pltpu.SMEM)
    return pl.pallas_call(
        functools.partial(_prep_kernel, ntp),
        out_shape=(
            jax.ShapeDtypeStruct((capacity, width), cache.dtype),
            jax.ShapeDtypeStruct((width // 2, capacity), cache.dtype),
            jax.ShapeDtypeStruct((blocks, block_rows // ntp, width), cache.dtype),
        ),
        in_specs=[smem, smem, smem, smem, vmem, vmem],
        out_specs=(vmem, vmem, vmem),
        scratch_shapes=[pltpu.VMEM((capacity, width), jnp.float32),
                        pltpu.SMEM((targets.shape[0],), jnp.int32)],
    )(held, span, holders, targets, cache, keyval)


def _tail_kernel(na, nb, ntp, scale, chunk, lens_ref, q_ref, fresh, kt, share_buf, w_ref,
                 rs_out, new_out, ctx, part, psend, precv, plocal, stage, s1send, s1recv, s2send,
                 s2recv, slocal):
    s = lax.axis_index("seq")
    t = lax.axis_index("tp")
    rows, qcols = q_ref.shape
    capacity, width = fresh.shape
    head_size = width // 2
    share = share_buf.shape[1]
    heads = qcols // head_size
    cols = w_ref.shape[1] // ntp
    chunks = rows // chunk
    held = lens_ref[0]

    _greet(na, nb, s, t, *[lax.rem(t + k, ntp) for k in range(1, ntp)])
    sorted4 = share_buf.reshape(na, nb, share, width)
    a2a = SeqAllToAll(na, nb, s, t, sorted4, stage, lambda a_src: new_out.at[a_src],
                      (s1send, s1recv, s2send, s2recv, slocal))
    a2a.first()

    def slice_out(c, k):
        peer = lax.rem(t + k, ntp)
        return _remote(part.at[c, :, pl.ds(pl.multiple_of(peer * cols, cols), cols)],
                       rs_out.at[t, pl.ds(pl.multiple_of(c * chunk, chunk), chunk)],
                       psend.at[c, k], precv.at[c, k], {"seq": s, "tp": peer})

    def slice_in(c, k):
        sender = lax.rem(t + ntp - k, ntp)
        return _remote(part.at[c, :, pl.ds(0, cols)],
                       rs_out.at[sender, pl.ds(pl.multiple_of(c * chunk, chunk), chunk)],
                       psend.at[c, k], precv.at[c, k], {"seq": s, "tp": sender})

    def slice_own(c):
        return pltpu.make_async_copy(
            part.at[c, :, pl.ds(pl.multiple_of(t * cols, cols), cols)],
            rs_out.at[t, pl.ds(pl.multiple_of(c * chunk, chunk), chunk)], plocal.at[c])

    def do_chunk(c):
        first = pl.multiple_of(c * chunk, chunk)
        row_pos = first + lax.broadcasted_iota(jnp.int32, (chunk, capacity), 0)
        key_pos = lax.broadcasted_iota(jnp.int32, (chunk, capacity), 1)
        allowed = key_pos <= held + row_pos
        for h in range(heads):
            q = q_ref[pl.ds(first, chunk), pl.ds(h * head_size, head_size)]
            scores = jnp.dot(q, kt[...], preferred_element_type=jnp.float32) * scale
            scores = jnp.where(allowed, scores, MASKED)
            top = jnp.max(scores, axis=1, keepdims=True)
            weights = jnp.exp(scores - top)
            inv = 1.0 / jnp.sum(weights, axis=1, keepdims=True)
            probs = (weights * inv).astype(jnp.bfloat16)
            ctx[:, pl.ds(h * head_size, head_size)] = jnp.dot(
                probs, fresh[:, pl.ds(head_size, head_size)],
                preferred_element_type=jnp.float32).astype(ctx.dtype)
        part[c] = jnp.dot(ctx[...], w_ref[...], preferred_element_type=jnp.float32).astype(
            part.dtype)
        slice_own(c).start()
        for k in range(1, ntp):
            slice_out(c, k).start()

    do_chunk(0)
    a2a.second()

    def rest(c, carry):
        do_chunk(c)
        return carry

    lax.fori_loop(1, chunks, rest, 0)
    a2a.arrived()

    def drain(c, carry):
        for k in range(1, ntp):
            slice_in(c, k).wait_recv()
            slice_out(c, k).wait_send()
        slice_own(c).wait()
        return carry

    lax.fori_loop(0, chunks, drain, 0)
    a2a.finish()


def attend_and_scatter(query, cache, keyval, held, span, holders, targets, w_out, na, nb, ntp,
                       chunk=128):
    rows, qcols = query.shape
    blocks, block_rows, width = cache.shape
    share = block_rows // ntp
    cols = w_out.shape[1] // ntp
    fresh, keys_t, sorted_share = prepare(cache, keyval, held, span, holders, targets, ntp)
    vmem = pl.BlockSpec(memory_space=pltpu.VMEM)
    smem = pl.BlockSpec(memory_space=pltpu.SMEM)
    rs, new = pl.pallas_call(
        functools.partial(_tail_kernel, na, nb, ntp, (width // 2) ** (-0.5), chunk),
        out_shape=(
            jax.ShapeDtypeStruct((ntp, rows, cols), jnp.bfloat16),
            jax.ShapeDtypeStruct((na, nb, share, width), cache.dtype),
        ),
        in_specs=[smem, vmem, vmem, vmem, vmem, vmem],
        out_specs=(pl.BlockSpec(memory_space=pl.ANY), pl.BlockSpec(memory_space=pl.ANY)),
        scratch_shapes=[
            pltpu.VMEM((chunk, qcols), jnp.bfloat16),
            pltpu.VMEM((rows // chunk, chunk, w_out.shape[1]), jnp.bfloat16),
            pltpu.SemaphoreType.DMA((rows // chunk, ntp)),
            pltpu.SemaphoreType.DMA((rows // chunk, ntp)),
            pltpu.SemaphoreType.DMA((rows // chunk,)),
        ] + _seq_scratch(na, nb, share, width, cache.dtype),
        compiler_params=pltpu.CompilerParams(collective_id=1, has_side_effects=True),
    )(held, query, fresh, keys_t, sorted_share, w_out)
    return rs, new.reshape(blocks, share, width)


def body(
    tokens,
    norm_gain,
    w_query,
    w_keyval,
    w_out,
    span_lens,
    cached_lens,
    old_table,
    new_table,
    old_cache,
):
    groups = lax.axis_size("seq")
    tp_count = lax.axis_size("tp")
    tp_index = lax.axis_index("tp")
    holders = old_table[0]
    held_len = cached_lens[0]
    span_len = span_lens[0]
    tok_rows, tok_cols = tokens.shape
    share = old_cache.shape[1]
    width = old_cache.shape[2]
    block_rows = share * tp_count
    capacity = groups * block_rows

    inner = min(groups, 8)
    outer = groups // inner
    query, keyval, cache_all = gather_inputs(
        tokens, old_cache, norm_gain, w_query, w_keyval, outer, inner, tp_count
    )
    cache_all = cache_all.reshape(groups, tp_count, share, width)

    summed, new_cache = attend_and_scatter(
        query, cache_all.reshape(groups, block_rows, width), keyval, cached_lens, span_lens,
        holders, new_table[0], w_out, outer, inner, tp_count
    )
    row_pos = lax.broadcasted_iota(jnp.int32, (tok_rows, 1), 0)
    total = tokens.astype(jnp.float32)
    for p in range(tp_count):
        total = total + summed[p].astype(jnp.float32)
    mixed = jnp.where(row_pos < span_len, total, jnp.zeros_like(total)).astype(jnp.bfloat16)
    return (mixed, new_cache)


def solution(mesh):
    in_specs = (
        P("seq", "tp"),
        P(),
        P(None, "tp"),
        P(),
        P("tp", None),
        P("seq"),
        P("seq"),
        P("seq", None),
        P("seq", None),
        P("seq", "tp", None),
    )
    out_specs = (P("seq", "tp"), P("seq", "tp", None))
    return jax.shard_map(body, mesh=mesh, in_specs=in_specs, out_specs=out_specs, check_vma=False)
```

```python
import functools

import jax
import jax.numpy as jnp
from jax import lax
from jax.experimental import pallas as pl
from jax.experimental.pallas import tpu as pltpu
from jax.sharding import PartitionSpec as P

EPSILON = 1e-05
MASKED = -1e30


def normalize(rows, norm_gain):
    values = rows.astype(jnp.float32)
    average = jnp.mean(values, axis=1, keepdims=True)
    centred = values - average
    spread = jnp.mean(centred * centred, axis=1, keepdims=True)
    return (centred * lax.rsqrt(spread + EPSILON) * norm_gain).astype(jnp.bfloat16)


MESH = pl.DeviceIdType.MESH


def _remote(src, dst, send, recv, dev):
    return pltpu.make_async_remote_copy(
        src_ref=src, dst_ref=dst, send_sem=send, recv_sem=recv, device_id=dev, device_id_type=MESH
    )


def _greet(na, nb, s, t, *tp_peers):
    barrier = pltpu.get_barrier_semaphore()
    a = s // nb
    b = s % nb

    def one_b(k, carry):
        pl.semaphore_signal(barrier, inc=1, device_id={"seq": a * nb + lax.rem(b + k, nb), "tp": t},
                            device_id_type=MESH)
        return carry

    def one_a(k, carry):
        pl.semaphore_signal(barrier, inc=1, device_id={"seq": lax.rem(a + k, na) * nb + b, "tp": t},
                            device_id_type=MESH)
        return carry

    lax.fori_loop(1, nb, one_b, 0)
    lax.fori_loop(1, na, one_a, 0)
    for p in tp_peers:
        pl.semaphore_signal(barrier, inc=1, device_id={"seq": s, "tp": p}, device_id_type=MESH)
    pl.semaphore_wait(barrier, na + nb - 2 + len(tp_peers))


class SeqAllToAll:
    def __init__(self, na, nb, s, t, src, stage, dst, sems):
        self.na, self.nb, self.t, self.src, self.stage, self.dst = na, nb, t, src, stage, dst
        self.a = s // nb
        self.b = s % nb
        self.s1send, self.s1recv, self.s2send, self.s2recv, self.local = sems

    def _dev(self, a, b):
        return {"seq": a * self.nb + b, "tp": self.t}

    def _out1(self, k):
        peer = lax.rem(self.b + k, self.nb)
        return _remote(self.src.at[:, peer], self.stage.at[self.b], self.s1send.at[k],
                       self.s1recv.at[k], self._dev(self.a, peer))

    def _in1(self, k):
        sender = lax.rem(self.b + self.nb - k, self.nb)
        return _remote(self.src.at[:, self.b], self.stage.at[sender], self.s1send.at[k],
                       self.s1recv.at[k], self._dev(self.a, sender))

    def _out2(self, k):
        peer = lax.rem(self.a + k, self.na)
        return _remote(self.stage.at[:, peer], self.dst(self.a), self.s2send.at[k],
                       self.s2recv.at[k], self._dev(peer, self.b))

    def _in2(self, k):
        sender = lax.rem(self.a + self.na - k, self.na)
        return _remote(self.stage.at[:, self.a], self.dst(sender), self.s2send.at[k],
                       self.s2recv.at[k], self._dev(sender, self.b))

    def first(self):
        self.own1 = pltpu.make_async_copy(self.src.at[:, self.b], self.stage.at[self.b],
                                          self.local.at[0])
        self.own1.start()
        _loop(self.nb, lambda k: self._out1(k).start())

    def second(self):
        _loop(self.nb, lambda k: self._in1(k).wait_recv())
        self.own1.wait()
        self.own2 = pltpu.make_async_copy(self.stage.at[:, self.a], self.dst(self.a),
                                          self.local.at[1])
        self.own2.start()
        _loop(self.na, lambda k: self._out2(k).start())

    def arrived(self):
        _loop(self.na, lambda k: self._in2(k).wait_recv())
        self.own2.wait()

    def finish(self):
        _loop(self.nb, lambda k: self._out1(k).wait_send())
        _loop(self.na, lambda k: self._out2(k).wait_send())


def _seq_scratch(na, nb, share, width, dtype):
    return [
        pltpu.VMEM((nb, na, share, width), dtype),
        pltpu.SemaphoreType.DMA((nb,)),
        pltpu.SemaphoreType.DMA((nb,)),
        pltpu.SemaphoreType.DMA((na,)),
        pltpu.SemaphoreType.DMA((na,)),
        pltpu.SemaphoreType.DMA((2,)),
    ]


def _loop(n, fn):
    def step(k, carry):
        fn(k)
        return carry

    lax.fori_loop(1, n, step, 0)


def _in_kernel(na, nb, ntp, tok_ref, cache_ref, gain_ref, wq_ref, wkv_ref, q_out, kv_out,
               cache_out, tok_all, tsend, trecv, csend, crecv, lsem, stage, s1send, s1recv,
               s2send, s2recv, slocal):
    s = lax.axis_index("seq")
    t = lax.axis_index("tp")
    right = lax.rem(t + 1, ntp)
    left = lax.rem(t + ntp - 1, ntp)
    across = lax.rem(t + 2, ntp)
    rdev = {"seq": s, "tp": right}
    ldev = {"seq": s, "tp": left}
    rows, cols = tok_ref.shape
    half = rows // 2
    _greet(na, nb, s, t, left, right, across)

    def tok_cols(p):
        return pl.ds(pl.multiple_of(p * cols, cols), cols)

    a2a = SeqAllToAll(na, nb, s, t, cache_ref, stage, lambda a_src: cache_out.at[a_src, :, t],
                      (s1send, s1recv, s2send, s2recv, slocal))
    a2a.first()

    own_tok = pltpu.make_async_copy(tok_ref, tok_all.at[:, tok_cols(t)], lsem.at[0])
    own_tok.start()
    tok_r = _remote(tok_ref, tok_all.at[:, tok_cols(t)], tsend.at[0], trecv.at[0], rdev)
    tok_l = _remote(tok_ref, tok_all.at[:, tok_cols(t)], tsend.at[1], trecv.at[1], ldev)
    tok_r.start()
    tok_l.start()

    a2a.second()

    _remote(tok_ref, tok_all.at[:, tok_cols(left)], tsend.at[0], trecv.at[0], ldev).wait_recv()
    fwd_r = _remote(tok_all.at[pl.ds(0, half), tok_cols(left)],
                    tok_all.at[pl.ds(0, half), tok_cols(left)], tsend.at[2], trecv.at[2], rdev)
    fwd_r.start()
    _remote(tok_ref, tok_all.at[:, tok_cols(right)], tsend.at[1], trecv.at[1], rdev).wait_recv()
    fwd_l = _remote(tok_all.at[pl.ds(half, half), tok_cols(right)],
                    tok_all.at[pl.ds(half, half), tok_cols(right)], tsend.at[3], trecv.at[3], ldev)
    fwd_l.start()

    a2a.arrived()
    flat = cache_out.reshape(na * nb, ntp, *cache_out.shape[3:])
    mine = flat.at[:, t]

    def cache_to(k):
        peer = lax.rem(t + k, ntp)
        return _remote(mine, mine, csend.at[k], crecv.at[k], {"seq": s, "tp": peer})

    def cache_from(k):
        sender = lax.rem(t + ntp - k, ntp)
        return _remote(mine, flat.at[:, sender], csend.at[k], crecv.at[k],
                       {"seq": s, "tp": sender})

    for k in range(1, ntp):
        cache_to(k).start()

    _remote(tok_ref.at[pl.ds(0, half)], tok_all.at[pl.ds(0, half), tok_cols(across)],
            tsend.at[2], trecv.at[2], ldev).wait_recv()
    _remote(tok_ref.at[pl.ds(half, half)], tok_all.at[pl.ds(half, half), tok_cols(across)],
            tsend.at[3], trecv.at[3], rdev).wait_recv()
    own_tok.wait()

    chunk = min(rows, 256)

    def project(c, carry):
        first = pl.multiple_of(c * chunk, chunk)
        values = tok_all[pl.ds(first, chunk), :].astype(jnp.float32)
        average = jnp.mean(values, axis=1, keepdims=True)
        centred = values - average
        spread = jnp.mean(centred * centred, axis=1, keepdims=True)
        normed = (centred * lax.rsqrt(spread + EPSILON) * gain_ref[...]).astype(jnp.bfloat16)
        q_out[pl.ds(first, chunk), :] = jnp.dot(
            normed, wq_ref[...], preferred_element_type=jnp.float32).astype(q_out.dtype)
        kv_out[pl.ds(first, chunk), :] = jnp.dot(
            normed, wkv_ref[...], preferred_element_type=jnp.float32).astype(kv_out.dtype)
        return carry

    lax.fori_loop(0, rows // chunk, project, 0)

    for k in range(1, ntp):
        cache_from(k).wait_recv()
    for c in (tok_r, tok_l, fwd_r, fwd_l):
        c.wait_send()
    for k in range(1, ntp):
        cache_to(k).wait_send()
    a2a.finish()


def gather_inputs(tokens, old_cache, norm_gain, w_query, w_keyval, na, nb, ntp):
    rows, cols = tokens.shape
    _, share, width = old_cache.shape
    cache4 = old_cache.reshape(na, nb, share, width)
    vmem = pl.BlockSpec(memory_space=pltpu.VMEM)
    anywhere = pl.BlockSpec(memory_space=pl.ANY)
    return pl.pallas_call(
        functools.partial(_in_kernel, na, nb, ntp),
        out_shape=(
            jax.ShapeDtypeStruct((rows, w_query.shape[1]), jnp.bfloat16),
            jax.ShapeDtypeStruct((rows, w_keyval.shape[1]), jnp.bfloat16),
            jax.ShapeDtypeStruct((na, nb, ntp, share, width), old_cache.dtype),
        ),
        in_specs=[anywhere, anywhere, vmem, vmem, vmem],
        out_specs=(vmem, vmem, anywhere),
        scratch_shapes=[
            pltpu.VMEM((rows, ntp * cols), tokens.dtype),
            pltpu.SemaphoreType.DMA((4,)),
            pltpu.SemaphoreType.DMA((4,)),
            pltpu.SemaphoreType.DMA((ntp,)),
            pltpu.SemaphoreType.DMA((ntp,)),
            pltpu.SemaphoreType.DMA((2,)),
        ] + _seq_scratch(na, nb, share, width, old_cache.dtype),
        compiler_params=pltpu.CompilerParams(collective_id=0, has_side_effects=True),
    )(tokens, cache4, norm_gain.reshape(1, -1).astype(jnp.float32), w_query, w_keyval)


def _out_kernel(na, nb, ntp, part_ref, share_ref, rs_out, new_out, stage_rs, rsend, rrecv, lsem,
                stage, s1send, s1recv, s2send, s2recv, slocal):
    s = lax.axis_index("seq")
    t = lax.axis_index("tp")
    right = lax.rem(t + 1, ntp)
    left = lax.rem(t + ntp - 1, ntp)
    across = lax.rem(t + 2, ntp)
    rdev = {"seq": s, "tp": right}
    ldev = {"seq": s, "tp": left}
    half = part_ref.shape[1] // 2
    _greet(na, nb, s, t, left, right)

    a2a = SeqAllToAll(na, nb, s, t, share_ref, stage, lambda a_src: new_out.at[a_src],
                      (s1send, s1recv, s2send, s2recv, slocal))
    a2a.first()

    own_part = pltpu.make_async_copy(part_ref.at[t], rs_out.at[t], lsem.at[0])
    own_part.start()
    to_r = _remote(part_ref.at[right], rs_out.at[t], rsend.at[0], rrecv.at[0], rdev)
    to_l = _remote(part_ref.at[left], rs_out.at[t], rsend.at[1], rrecv.at[1], ldev)
    via_r = _remote(part_ref.at[across, pl.ds(0, half)], stage_rs.at[0], rsend.at[2], rrecv.at[2],
                    rdev)
    via_l = _remote(part_ref.at[across, pl.ds(half, half)], stage_rs.at[1], rsend.at[3],
                    rrecv.at[3], ldev)
    for c in (to_r, to_l, via_r, via_l):
        c.start()

    a2a.second()

    _remote(part_ref.at[across, pl.ds(0, half)], stage_rs.at[0], rsend.at[2], rrecv.at[2],
            ldev).wait_recv()
    fwd_r = _remote(stage_rs.at[0], rs_out.at[left, pl.ds(0, half)], rsend.at[4], rrecv.at[4],
                    rdev)
    fwd_r.start()
    _remote(part_ref.at[across, pl.ds(half, half)], stage_rs.at[1], rsend.at[3], rrecv.at[3],
            rdev).wait_recv()
    fwd_l = _remote(stage_rs.at[1], rs_out.at[right, pl.ds(half, half)], rsend.at[5],
                    rrecv.at[5], ldev)
    fwd_l.start()

    a2a.arrived()
    _remote(part_ref.at[t], rs_out.at[left], rsend.at[0], rrecv.at[0], ldev).wait_recv()
    _remote(part_ref.at[t], rs_out.at[right], rsend.at[1], rrecv.at[1], rdev).wait_recv()
    _remote(stage_rs.at[0], rs_out.at[across, pl.ds(0, half)], rsend.at[4], rrecv.at[4],
            ldev).wait_recv()
    _remote(stage_rs.at[1], rs_out.at[across, pl.ds(half, half)], rsend.at[5], rrecv.at[5],
            rdev).wait_recv()
    for c in (to_r, to_l, via_r, via_l, fwd_r, fwd_l):
        c.wait_send()
    a2a.finish()
    own_part.wait()


def scatter_outputs(partial, share, na, nb, ntp):
    _, rows, cols = partial.shape
    _, block, width = share.shape
    share4 = share.reshape(na, nb, block, width)
    rs, new = pl.pallas_call(
        functools.partial(_out_kernel, na, nb, ntp),
        out_shape=(
            jax.ShapeDtypeStruct(partial.shape, partial.dtype),
            jax.ShapeDtypeStruct(share4.shape, share.dtype),
        ),
        in_specs=[pl.BlockSpec(memory_space=pl.ANY)] * 2,
        out_specs=(pl.BlockSpec(memory_space=pl.ANY), pl.BlockSpec(memory_space=pl.ANY)),
        scratch_shapes=[
            pltpu.VMEM((2, rows // 2, cols), partial.dtype),
            pltpu.SemaphoreType.DMA((6,)),
            pltpu.SemaphoreType.DMA((6,)),
            pltpu.SemaphoreType.DMA((1,)),
        ] + _seq_scratch(na, nb, block, width, share.dtype),
        compiler_params=pltpu.CompilerParams(collective_id=1, has_side_effects=True),
    )(partial, share4)
    return rs, new.reshape(share.shape)


def _attend_kernel(scale, lens_ref, q_ref, k_ref, v_ref, o_ref):
    chunk = q_ref.shape[0]
    capacity = k_ref.shape[0]
    held = lens_ref[0]
    first = pl.program_id(1) * chunk
    scores = lax.dot_general(
        q_ref[...], k_ref[...], (((1,), (1,)), ((), ())), preferred_element_type=jnp.float32
    ) * scale
    row_pos = first + lax.broadcasted_iota(jnp.int32, (chunk, capacity), 0)
    key_pos = lax.broadcasted_iota(jnp.int32, (chunk, capacity), 1)
    scores = jnp.where(key_pos <= held + row_pos, scores, MASKED)
    top = jnp.max(scores, axis=1, keepdims=True)
    weights = jnp.exp(scores - top)
    probs = (weights / jnp.sum(weights, axis=1, keepdims=True)).astype(jnp.bfloat16)
    o_ref[...] = jnp.dot(probs, v_ref[...], preferred_element_type=jnp.float32).astype(o_ref.dtype)


def attend(query, fresh, held_len, head_size, chunk=128):
    rows, qcols = query.shape
    capacity = fresh.shape[0]
    heads = qcols // head_size
    lens = jnp.reshape(held_len, (1,)).astype(jnp.int32)
    return pl.pallas_call(
        functools.partial(_attend_kernel, head_size ** (-0.5)),
        out_shape=jax.ShapeDtypeStruct((rows, qcols), jnp.bfloat16),
        grid_spec=pltpu.PrefetchScalarGridSpec(
            num_scalar_prefetch=1,
            grid=(heads, rows // chunk),
            in_specs=[
                pl.BlockSpec((chunk, head_size), lambda h, r, lens: (r, h)),
                pl.BlockSpec((capacity, head_size), lambda h, r, lens: (0, 0)),
                pl.BlockSpec((capacity, head_size), lambda h, r, lens: (0, 1)),
            ],
            out_specs=pl.BlockSpec((chunk, head_size), lambda h, r, lens: (r, h)),
        ),
        cost_estimate=pl.CostEstimate(
            flops=4 * rows * capacity * qcols,
            transcendentals=rows * capacity * heads,
            bytes_accessed=2 * (2 * rows * qcols + 2 * capacity * head_size),
        ),
    )(lens, query, fresh, fresh)


def _prep_kernel(ntp, held_ref, span_ref, holders_ref, targets_ref, cache_ref, kv_ref, fresh, kt,
                 share_buf, fresh32, sources_ref):
    t = lax.axis_index("tp")
    capacity, width = fresh.shape
    head_size = width // 2
    block_rows = cache_ref.shape[1]
    share = block_rows // ntp
    held = held_ref[0]
    span = span_ref[0]

    def invert(b, carry):
        sources_ref[targets_ref[b]] = b
        return carry

    lax.fori_loop(0, targets_ref.shape[0], invert, 0, unroll=True)

    def place(b, carry):
        fresh32[pl.ds(pl.multiple_of(b * block_rows, block_rows), block_rows), :] = (
            cache_ref[holders_ref[b]].astype(jnp.float32))
        return carry

    lax.fori_loop(0, capacity // block_rows, place, 0, unroll=True)
    padded = jnp.concatenate(
        [kv_ref[...].astype(jnp.float32),
         jnp.zeros((capacity - kv_ref.shape[0], width), jnp.float32)], axis=0)
    shifted = pltpu.roll(padded, held, 0)
    positions = lax.broadcasted_iota(jnp.int32, (capacity, width), 0)
    full = jnp.where(positions < held, fresh32[...],
                     jnp.where(positions < held + span, shifted, 0.0))
    fresh32[...] = full
    fresh[...] = full.astype(fresh.dtype)
    kt[...] = fresh[:, pl.ds(0, head_size)].T

    def pick(d, carry):
        start = pl.multiple_of(sources_ref[d] * block_rows + t * share, share)
        share_buf[d] = fresh32[pl.ds(start, share), :].astype(share_buf.dtype)
        return carry

    lax.fori_loop(0, share_buf.shape[0], pick, 0, unroll=True)


def prepare(cache, keyval, held, span, holders, targets, ntp):
    blocks, block_rows, width = cache.shape
    capacity = blocks * block_rows
    vmem = pl.BlockSpec(memory_space=pltpu.VMEM)
    smem = pl.BlockSpec(memory_space=pltpu.SMEM)
    return pl.pallas_call(
        functools.partial(_prep_kernel, ntp),
        out_shape=(
            jax.ShapeDtypeStruct((capacity, width), cache.dtype),
            jax.ShapeDtypeStruct((width // 2, capacity), cache.dtype),
            jax.ShapeDtypeStruct((blocks, block_rows // ntp, width), cache.dtype),
        ),
        in_specs=[smem, smem, smem, smem, vmem, vmem],
        out_specs=(vmem, vmem, vmem),
        scratch_shapes=[pltpu.VMEM((capacity, width), jnp.float32),
                        pltpu.SMEM((targets.shape[0],), jnp.int32)],
    )(held, span, holders, targets, cache, keyval)


def _tail_kernel(na, nb, ntp, scale, chunk, lens_ref, q_ref, fresh, kt, share_buf, w_ref,
                 rs_out, new_out, ctx, part, psend, precv, plocal, stage, s1send, s1recv, s2send,
                 s2recv, slocal):
    s = lax.axis_index("seq")
    t = lax.axis_index("tp")
    rows, qcols = q_ref.shape
    capacity, width = fresh.shape
    head_size = width // 2
    share = share_buf.shape[1]
    heads = qcols // head_size
    cols = w_ref.shape[1] // ntp
    chunks = rows // chunk
    held = lens_ref[0]

    _greet(na, nb, s, t, *[lax.rem(t + k, ntp) for k in range(1, ntp)])
    sorted4 = share_buf.reshape(na, nb, share, width)
    a2a = SeqAllToAll(na, nb, s, t, sorted4, stage, lambda a_src: new_out.at[a_src],
                      (s1send, s1recv, s2send, s2recv, slocal))
    a2a.first()

    def slice_out(c, k):
        peer = lax.rem(t + k, ntp)
        return _remote(part.at[c, :, pl.ds(pl.multiple_of(peer * cols, cols), cols)],
                       rs_out.at[t, pl.ds(pl.multiple_of(c * chunk, chunk), chunk)],
                       psend.at[c, k], precv.at[c, k], {"seq": s, "tp": peer})

    def slice_in(c, k):
        sender = lax.rem(t + ntp - k, ntp)
        return _remote(part.at[c, :, pl.ds(0, cols)],
                       rs_out.at[sender, pl.ds(pl.multiple_of(c * chunk, chunk), chunk)],
                       psend.at[c, k], precv.at[c, k], {"seq": s, "tp": sender})

    def slice_own(c):
        return pltpu.make_async_copy(
            part.at[c, :, pl.ds(pl.multiple_of(t * cols, cols), cols)],
            rs_out.at[t, pl.ds(pl.multiple_of(c * chunk, chunk), chunk)], plocal.at[c])

    def do_chunk(c):
        first = pl.multiple_of(c * chunk, chunk)
        row_pos = first + lax.broadcasted_iota(jnp.int32, (chunk, capacity), 0)
        key_pos = lax.broadcasted_iota(jnp.int32, (chunk, capacity), 1)
        allowed = key_pos <= held + row_pos
        for h in range(heads):
            q = q_ref[pl.ds(first, chunk), pl.ds(h * head_size, head_size)]
            scores = jnp.dot(q, kt[...], preferred_element_type=jnp.float32) * scale
            scores = jnp.where(allowed, scores, MASKED)
            top = jnp.max(scores, axis=1, keepdims=True)
            weights = jnp.exp(scores - top)
            inv = 1.0 / jnp.sum(weights, axis=1, keepdims=True)
            probs = (weights * inv).astype(jnp.bfloat16)
            ctx[:, pl.ds(h * head_size, head_size)] = jnp.dot(
                probs, fresh[:, pl.ds(head_size, head_size)],
                preferred_element_type=jnp.float32).astype(ctx.dtype)
        part[c] = jnp.dot(ctx[...], w_ref[...], preferred_element_type=jnp.float32).astype(
            part.dtype)
        slice_own(c).start()
        for k in range(1, ntp):
            slice_out(c, k).start()

    do_chunk(0)
    a2a.second()

    def rest(c, carry):
        do_chunk(c)
        return carry

    lax.fori_loop(1, chunks, rest, 0)
    a2a.arrived()

    def drain(c, carry):
        for k in range(1, ntp):
            slice_in(c, k).wait_recv()
            slice_out(c, k).wait_send()
        slice_own(c).wait()
        return carry

    lax.fori_loop(0, chunks, drain, 0)
    a2a.finish()


def attend_and_scatter(query, cache, keyval, held, span, holders, targets, w_out, na, nb, ntp,
                       chunk=128):
    rows, qcols = query.shape
    blocks, block_rows, width = cache.shape
    share = block_rows // ntp
    cols = w_out.shape[1] // ntp
    fresh, keys_t, sorted_share = prepare(cache, keyval, held, span, holders, targets, ntp)
    vmem = pl.BlockSpec(memory_space=pltpu.VMEM)
    smem = pl.BlockSpec(memory_space=pltpu.SMEM)
    rs, new = pl.pallas_call(
        functools.partial(_tail_kernel, na, nb, ntp, (width // 2) ** (-0.5), chunk),
        out_shape=(
            jax.ShapeDtypeStruct((ntp, rows, cols), jnp.bfloat16),
            jax.ShapeDtypeStruct((na, nb, share, width), cache.dtype),
        ),
        in_specs=[smem, vmem, vmem, vmem, vmem, vmem],
        out_specs=(pl.BlockSpec(memory_space=pl.ANY), pl.BlockSpec(memory_space=pl.ANY)),
        scratch_shapes=[
            pltpu.VMEM((chunk, qcols), jnp.bfloat16),
            pltpu.VMEM((rows // chunk, chunk, w_out.shape[1]), jnp.bfloat16),
            pltpu.SemaphoreType.DMA((rows // chunk, ntp)),
            pltpu.SemaphoreType.DMA((rows // chunk, ntp)),
            pltpu.SemaphoreType.DMA((rows // chunk,)),
        ] + _seq_scratch(na, nb, share, width, cache.dtype),
        compiler_params=pltpu.CompilerParams(collective_id=1, has_side_effects=True),
    )(held, query, fresh, keys_t, sorted_share, w_out)
    return rs, new.reshape(blocks, share, width)


def body(
    tokens,
    norm_gain,
    w_query,
    w_keyval,
    w_out,
    span_lens,
    cached_lens,
    old_table,
    new_table,
    old_cache,
):
    groups = lax.axis_size("seq")
    tp_count = lax.axis_size("tp")
    tp_index = lax.axis_index("tp")
    holders = old_table[0]
    held_len = cached_lens[0]
    span_len = span_lens[0]
    tok_rows, tok_cols = tokens.shape
    share = old_cache.shape[1]
    width = old_cache.shape[2]
    block_rows = share * tp_count
    capacity = groups * block_rows

    inner = min(groups, 8)
    outer = groups // inner
    query, keyval, cache_all = gather_inputs(
        tokens, old_cache, norm_gain, w_query, w_keyval, outer, inner, tp_count
    )
    cache_all = cache_all.reshape(groups, tp_count, share, width)

    summed, new_cache = attend_and_scatter(
        query, cache_all.reshape(groups, block_rows, width), keyval, cached_lens, span_lens,
        holders, new_table[0], w_out, outer, inner, tp_count
    )
    row_pos = lax.broadcasted_iota(jnp.int32, (tok_rows, 1), 0)
    total = tokens.astype(jnp.float32)
    for p in range(tp_count):
        total = total + summed[p].astype(jnp.float32)
    mixed = jnp.where(row_pos < span_len, total, jnp.zeros_like(total)).astype(jnp.bfloat16)
    return (mixed, new_cache)


def solution(mesh):
    in_specs = (
        P("seq", "tp"),
        P(),
        P(None, "tp"),
        P(),
        P("tp", None),
        P("seq"),
        P("seq"),
        P("seq", None),
        P("seq", None),
        P("seq", "tp", None),
    )
    out_specs = (P("seq", "tp"), P("seq", "tp", None))
    return jax.shard_map(body, mesh=mesh, in_specs=in_specs, out_specs=out_specs, check_vma=False)
```

```python
import functools

import jax
import jax.numpy as jnp
from jax import lax
from jax.experimental import pallas as pl
from jax.experimental.pallas import tpu as pltpu
from jax.sharding import PartitionSpec as P

EPSILON = 1e-05
MASKED = -1e30


def normalize(rows, norm_gain):
    values = rows.astype(jnp.float32)
    average = jnp.mean(values, axis=1, keepdims=True)
    centred = values - average
    spread = jnp.mean(centred * centred, axis=1, keepdims=True)
    return (centred * lax.rsqrt(spread + EPSILON) * norm_gain).astype(jnp.bfloat16)


MESH = pl.DeviceIdType.MESH


def _remote(src, dst, send, recv, dev):
    return pltpu.make_async_remote_copy(
        src_ref=src, dst_ref=dst, send_sem=send, recv_sem=recv, device_id=dev, device_id_type=MESH
    )


def _greet(na, nb, s, t, *tp_peers):
    barrier = pltpu.get_barrier_semaphore()
    a = s // nb
    b = s % nb

    def one_b(k, carry):
        pl.semaphore_signal(barrier, inc=1, device_id={"seq": a * nb + lax.rem(b + k, nb), "tp": t},
                            device_id_type=MESH)
        return carry

    def one_a(k, carry):
        pl.semaphore_signal(barrier, inc=1, device_id={"seq": lax.rem(a + k, na) * nb + b, "tp": t},
                            device_id_type=MESH)
        return carry

    lax.fori_loop(1, nb, one_b, 0, unroll=True)
    lax.fori_loop(1, na, one_a, 0, unroll=True)
    for p in tp_peers:
        pl.semaphore_signal(barrier, inc=1, device_id={"seq": s, "tp": p}, device_id_type=MESH)
    pl.semaphore_wait(barrier, na + nb - 2 + len(tp_peers))


class SeqAllToAll:
    def __init__(self, na, nb, s, t, src, stage, dst, sems):
        self.na, self.nb, self.t, self.src, self.stage, self.dst = na, nb, t, src, stage, dst
        self.a = s // nb
        self.b = s % nb
        self.s1send, self.s1recv, self.s2send, self.s2recv, self.local = sems

    def _dev(self, a, b):
        return {"seq": a * self.nb + b, "tp": self.t}

    def _out1(self, k):
        peer = lax.rem(self.b + k, self.nb)
        return _remote(self.src.at[:, peer], self.stage.at[self.b], self.s1send.at[k],
                       self.s1recv.at[k], self._dev(self.a, peer))

    def _in1(self, k):
        sender = lax.rem(self.b + self.nb - k, self.nb)
        return _remote(self.src.at[:, self.b], self.stage.at[sender], self.s1send.at[k],
                       self.s1recv.at[k], self._dev(self.a, sender))

    def _out2(self, k):
        peer = lax.rem(self.a + k, self.na)
        return _remote(self.stage.at[:, peer], self.dst(self.a), self.s2send.at[k],
                       self.s2recv.at[k], self._dev(peer, self.b))

    def _in2(self, k):
        sender = lax.rem(self.a + self.na - k, self.na)
        return _remote(self.stage.at[:, self.a], self.dst(sender), self.s2send.at[k],
                       self.s2recv.at[k], self._dev(sender, self.b))

    def first(self):
        self.own1 = pltpu.make_async_copy(self.src.at[:, self.b], self.stage.at[self.b],
                                          self.local.at[0])
        self.own1.start()
        _loop(self.nb, lambda k: self._out1(k).start())

    def second(self):
        _loop(self.nb, lambda k: self._in1(k).wait_recv())
        self.own1.wait()
        self.own2 = pltpu.make_async_copy(self.stage.at[:, self.a], self.dst(self.a),
                                          self.local.at[1])
        self.own2.start()
        _loop(self.na, lambda k: self._out2(k).start())

    def arrived(self):
        _loop(self.na, lambda k: self._in2(k).wait_recv())
        self.own2.wait()

    def finish(self):
        _loop(self.nb, lambda k: self._out1(k).wait_send())
        _loop(self.na, lambda k: self._out2(k).wait_send())


def _seq_scratch(na, nb, share, width, dtype):
    return [
        pltpu.VMEM((nb, na, share, width), dtype),
        pltpu.SemaphoreType.DMA((nb,)),
        pltpu.SemaphoreType.DMA((nb,)),
        pltpu.SemaphoreType.DMA((na,)),
        pltpu.SemaphoreType.DMA((na,)),
        pltpu.SemaphoreType.DMA((2,)),
    ]


def _loop(n, fn):
    def step(k, carry):
        fn(k)
        return carry

    lax.fori_loop(1, n, step, 0, unroll=True)


def _in_kernel(na, nb, ntp, tok_ref, cache_ref, gain_ref, wq_ref, wkv_ref, q_out, kv_out,
               cache_out, tok_all, tsend, trecv, csend, crecv, lsem, stage, s1send, s1recv,
               s2send, s2recv, slocal):
    s = lax.axis_index("seq")
    t = lax.axis_index("tp")
    right = lax.rem(t + 1, ntp)
    left = lax.rem(t + ntp - 1, ntp)
    across = lax.rem(t + 2, ntp)
    rdev = {"seq": s, "tp": right}
    ldev = {"seq": s, "tp": left}
    rows, cols = tok_ref.shape
    half = rows // 2
    _greet(na, nb, s, t, left, right, across)

    def tok_cols(p):
        return pl.ds(pl.multiple_of(p * cols, cols), cols)

    a2a = SeqAllToAll(na, nb, s, t, cache_ref, stage, lambda a_src: cache_out.at[a_src, :, t],
                      (s1send, s1recv, s2send, s2recv, slocal))
    a2a.first()

    own_tok = pltpu.make_async_copy(tok_ref, tok_all.at[:, tok_cols(t)], lsem.at[0])
    own_tok.start()
    tok_r = _remote(tok_ref, tok_all.at[:, tok_cols(t)], tsend.at[0], trecv.at[0], rdev)
    tok_l = _remote(tok_ref, tok_all.at[:, tok_cols(t)], tsend.at[1], trecv.at[1], ldev)
    tok_r.start()
    tok_l.start()

    a2a.second()

    _remote(tok_ref, tok_all.at[:, tok_cols(left)], tsend.at[0], trecv.at[0], ldev).wait_recv()
    fwd_r = _remote(tok_all.at[pl.ds(0, half), tok_cols(left)],
                    tok_all.at[pl.ds(0, half), tok_cols(left)], tsend.at[2], trecv.at[2], rdev)
    fwd_r.start()
    _remote(tok_ref, tok_all.at[:, tok_cols(right)], tsend.at[1], trecv.at[1], rdev).wait_recv()
    fwd_l = _remote(tok_all.at[pl.ds(half, half), tok_cols(right)],
                    tok_all.at[pl.ds(half, half), tok_cols(right)], tsend.at[3], trecv.at[3], ldev)
    fwd_l.start()

    a2a.arrived()
    flat = cache_out.reshape(na * nb, ntp, *cache_out.shape[3:])
    mine = flat.at[:, t]

    def cache_to(k):
        peer = lax.rem(t + k, ntp)
        return _remote(mine, mine, csend.at[k], crecv.at[k], {"seq": s, "tp": peer})

    def cache_from(k):
        sender = lax.rem(t + ntp - k, ntp)
        return _remote(mine, flat.at[:, sender], csend.at[k], crecv.at[k],
                       {"seq": s, "tp": sender})

    for k in range(1, ntp):
        cache_to(k).start()

    _remote(tok_ref.at[pl.ds(0, half)], tok_all.at[pl.ds(0, half), tok_cols(across)],
            tsend.at[2], trecv.at[2], ldev).wait_recv()
    _remote(tok_ref.at[pl.ds(half, half)], tok_all.at[pl.ds(half, half), tok_cols(across)],
            tsend.at[3], trecv.at[3], rdev).wait_recv()
    own_tok.wait()

    chunk = min(rows, 256)

    def project(c, carry):
        first = pl.multiple_of(c * chunk, chunk)
        values = tok_all[pl.ds(first, chunk), :].astype(jnp.float32)
        average = jnp.mean(values, axis=1, keepdims=True)
        centred = values - average
        spread = jnp.mean(centred * centred, axis=1, keepdims=True)
        normed = (centred * lax.rsqrt(spread + EPSILON) * gain_ref[...]).astype(jnp.bfloat16)
        q_out[pl.ds(first, chunk), :] = jnp.dot(
            normed, wq_ref[...], preferred_element_type=jnp.float32).astype(q_out.dtype)
        kv_out[pl.ds(first, chunk), :] = jnp.dot(
            normed, wkv_ref[...], preferred_element_type=jnp.float32).astype(kv_out.dtype)
        return carry

    lax.fori_loop(0, rows // chunk, project, 0)

    for k in range(1, ntp):
        cache_from(k).wait_recv()
    for c in (tok_r, tok_l, fwd_r, fwd_l):
        c.wait_send()
    for k in range(1, ntp):
        cache_to(k).wait_send()
    a2a.finish()


def gather_inputs(tokens, old_cache, norm_gain, w_query, w_keyval, na, nb, ntp):
    rows, cols = tokens.shape
    _, share, width = old_cache.shape
    cache4 = old_cache.reshape(na, nb, share, width)
    vmem = pl.BlockSpec(memory_space=pltpu.VMEM)
    anywhere = pl.BlockSpec(memory_space=pl.ANY)
    return pl.pallas_call(
        functools.partial(_in_kernel, na, nb, ntp),
        out_shape=(
            jax.ShapeDtypeStruct((rows, w_query.shape[1]), jnp.bfloat16),
            jax.ShapeDtypeStruct((rows, w_keyval.shape[1]), jnp.bfloat16),
            jax.ShapeDtypeStruct((na, nb, ntp, share, width), old_cache.dtype),
        ),
        in_specs=[anywhere, anywhere, vmem, vmem, vmem],
        out_specs=(vmem, vmem, anywhere),
        scratch_shapes=[
            pltpu.VMEM((rows, ntp * cols), tokens.dtype),
            pltpu.SemaphoreType.DMA((4,)),
            pltpu.SemaphoreType.DMA((4,)),
            pltpu.SemaphoreType.DMA((ntp,)),
            pltpu.SemaphoreType.DMA((ntp,)),
            pltpu.SemaphoreType.DMA((2,)),
        ] + _seq_scratch(na, nb, share, width, old_cache.dtype),
        compiler_params=pltpu.CompilerParams(collective_id=0, has_side_effects=True),
    )(tokens, cache4, norm_gain.reshape(1, -1).astype(jnp.float32), w_query, w_keyval)


def _out_kernel(na, nb, ntp, part_ref, share_ref, rs_out, new_out, stage_rs, rsend, rrecv, lsem,
                stage, s1send, s1recv, s2send, s2recv, slocal):
    s = lax.axis_index("seq")
    t = lax.axis_index("tp")
    right = lax.rem(t + 1, ntp)
    left = lax.rem(t + ntp - 1, ntp)
    across = lax.rem(t + 2, ntp)
    rdev = {"seq": s, "tp": right}
    ldev = {"seq": s, "tp": left}
    half = part_ref.shape[1] // 2
    _greet(na, nb, s, t, left, right)

    a2a = SeqAllToAll(na, nb, s, t, share_ref, stage, lambda a_src: new_out.at[a_src],
                      (s1send, s1recv, s2send, s2recv, slocal))
    a2a.first()

    own_part = pltpu.make_async_copy(part_ref.at[t], rs_out.at[t], lsem.at[0])
    own_part.start()
    to_r = _remote(part_ref.at[right], rs_out.at[t], rsend.at[0], rrecv.at[0], rdev)
    to_l = _remote(part_ref.at[left], rs_out.at[t], rsend.at[1], rrecv.at[1], ldev)
    via_r = _remote(part_ref.at[across, pl.ds(0, half)], stage_rs.at[0], rsend.at[2], rrecv.at[2],
                    rdev)
    via_l = _remote(part_ref.at[across, pl.ds(half, half)], stage_rs.at[1], rsend.at[3],
                    rrecv.at[3], ldev)
    for c in (to_r, to_l, via_r, via_l):
        c.start()

    a2a.second()

    _remote(part_ref.at[across, pl.ds(0, half)], stage_rs.at[0], rsend.at[2], rrecv.at[2],
            ldev).wait_recv()
    fwd_r = _remote(stage_rs.at[0], rs_out.at[left, pl.ds(0, half)], rsend.at[4], rrecv.at[4],
                    rdev)
    fwd_r.start()
    _remote(part_ref.at[across, pl.ds(half, half)], stage_rs.at[1], rsend.at[3], rrecv.at[3],
            rdev).wait_recv()
    fwd_l = _remote(stage_rs.at[1], rs_out.at[right, pl.ds(half, half)], rsend.at[5],
                    rrecv.at[5], ldev)
    fwd_l.start()

    a2a.arrived()
    _remote(part_ref.at[t], rs_out.at[left], rsend.at[0], rrecv.at[0], ldev).wait_recv()
    _remote(part_ref.at[t], rs_out.at[right], rsend.at[1], rrecv.at[1], rdev).wait_recv()
    _remote(stage_rs.at[0], rs_out.at[across, pl.ds(0, half)], rsend.at[4], rrecv.at[4],
            ldev).wait_recv()
    _remote(stage_rs.at[1], rs_out.at[across, pl.ds(half, half)], rsend.at[5], rrecv.at[5],
            rdev).wait_recv()
    for c in (to_r, to_l, via_r, via_l, fwd_r, fwd_l):
        c.wait_send()
    a2a.finish()
    own_part.wait()


def scatter_outputs(partial, share, na, nb, ntp):
    _, rows, cols = partial.shape
    _, block, width = share.shape
    share4 = share.reshape(na, nb, block, width)
    rs, new = pl.pallas_call(
        functools.partial(_out_kernel, na, nb, ntp),
        out_shape=(
            jax.ShapeDtypeStruct(partial.shape, partial.dtype),
            jax.ShapeDtypeStruct(share4.shape, share.dtype),
        ),
        in_specs=[pl.BlockSpec(memory_space=pl.ANY)] * 2,
        out_specs=(pl.BlockSpec(memory_space=pl.ANY), pl.BlockSpec(memory_space=pl.ANY)),
        scratch_shapes=[
            pltpu.VMEM((2, rows // 2, cols), partial.dtype),
            pltpu.SemaphoreType.DMA((6,)),
            pltpu.SemaphoreType.DMA((6,)),
            pltpu.SemaphoreType.DMA((1,)),
        ] + _seq_scratch(na, nb, block, width, share.dtype),
        compiler_params=pltpu.CompilerParams(collective_id=1, has_side_effects=True),
    )(partial, share4)
    return rs, new.reshape(share.shape)


def _attend_kernel(scale, lens_ref, q_ref, k_ref, v_ref, o_ref):
    chunk = q_ref.shape[0]
    capacity = k_ref.shape[0]
    held = lens_ref[0]
    first = pl.program_id(1) * chunk
    scores = lax.dot_general(
        q_ref[...], k_ref[...], (((1,), (1,)), ((), ())), preferred_element_type=jnp.float32
    ) * scale
    row_pos = first + lax.broadcasted_iota(jnp.int32, (chunk, capacity), 0)
    key_pos = lax.broadcasted_iota(jnp.int32, (chunk, capacity), 1)
    scores = jnp.where(key_pos <= held + row_pos, scores, MASKED)
    top = jnp.max(scores, axis=1, keepdims=True)
    weights = jnp.exp(scores - top)
    probs = (weights / jnp.sum(weights, axis=1, keepdims=True)).astype(jnp.bfloat16)
    o_ref[...] = jnp.dot(probs, v_ref[...], preferred_element_type=jnp.float32).astype(o_ref.dtype)


def attend(query, fresh, held_len, head_size, chunk=128):
    rows, qcols = query.shape
    capacity = fresh.shape[0]
    heads = qcols // head_size
    lens = jnp.reshape(held_len, (1,)).astype(jnp.int32)
    return pl.pallas_call(
        functools.partial(_attend_kernel, head_size ** (-0.5)),
        out_shape=jax.ShapeDtypeStruct((rows, qcols), jnp.bfloat16),
        grid_spec=pltpu.PrefetchScalarGridSpec(
            num_scalar_prefetch=1,
            grid=(heads, rows // chunk),
            in_specs=[
                pl.BlockSpec((chunk, head_size), lambda h, r, lens: (r, h)),
                pl.BlockSpec((capacity, head_size), lambda h, r, lens: (0, 0)),
                pl.BlockSpec((capacity, head_size), lambda h, r, lens: (0, 1)),
            ],
            out_specs=pl.BlockSpec((chunk, head_size), lambda h, r, lens: (r, h)),
        ),
        cost_estimate=pl.CostEstimate(
            flops=4 * rows * capacity * qcols,
            transcendentals=rows * capacity * heads,
            bytes_accessed=2 * (2 * rows * qcols + 2 * capacity * head_size),
        ),
    )(lens, query, fresh, fresh)


def _prep_kernel(ntp, held_ref, span_ref, holders_ref, targets_ref, cache_ref, kv_ref, fresh, kt,
                 share_buf, fresh32, sources_ref):
    t = lax.axis_index("tp")
    capacity, width = fresh.shape
    head_size = width // 2
    block_rows = cache_ref.shape[1]
    share = block_rows // ntp
    held = held_ref[0]
    span = span_ref[0]

    def invert(b, carry):
        sources_ref[targets_ref[b]] = b
        return carry

    lax.fori_loop(0, targets_ref.shape[0], invert, 0, unroll=True)

    def place(b, carry):
        fresh32[pl.ds(pl.multiple_of(b * block_rows, block_rows), block_rows), :] = (
            cache_ref[holders_ref[b]].astype(jnp.float32))
        return carry

    lax.fori_loop(0, capacity // block_rows, place, 0, unroll=True)
    padded = jnp.concatenate(
        [kv_ref[...].astype(jnp.float32),
         jnp.zeros((capacity - kv_ref.shape[0], width), jnp.float32)], axis=0)
    shifted = pltpu.roll(padded, held, 0)
    positions = lax.broadcasted_iota(jnp.int32, (capacity, width), 0)
    full = jnp.where(positions < held, fresh32[...],
                     jnp.where(positions < held + span, shifted, 0.0))
    fresh32[...] = full
    fresh[...] = full.astype(fresh.dtype)
    kt[...] = fresh[:, pl.ds(0, head_size)].T

    def pick(d, carry):
        start = pl.multiple_of(sources_ref[d] * block_rows + t * share, share)
        share_buf[d] = fresh32[pl.ds(start, share), :].astype(share_buf.dtype)
        return carry

    lax.fori_loop(0, share_buf.shape[0], pick, 0, unroll=True)


def prepare(cache, keyval, held, span, holders, targets, ntp):
    blocks, block_rows, width = cache.shape
    capacity = blocks * block_rows
    vmem = pl.BlockSpec(memory_space=pltpu.VMEM)
    smem = pl.BlockSpec(memory_space=pltpu.SMEM)
    return pl.pallas_call(
        functools.partial(_prep_kernel, ntp),
        out_shape=(
            jax.ShapeDtypeStruct((capacity, width), cache.dtype),
            jax.ShapeDtypeStruct((width // 2, capacity), cache.dtype),
            jax.ShapeDtypeStruct((blocks, block_rows // ntp, width), cache.dtype),
        ),
        in_specs=[smem, smem, smem, smem, vmem, vmem],
        out_specs=(vmem, vmem, vmem),
        scratch_shapes=[pltpu.VMEM((capacity, width), jnp.float32),
                        pltpu.SMEM((targets.shape[0],), jnp.int32)],
    )(held, span, holders, targets, cache, keyval)


def _tail_kernel(na, nb, ntp, scale, chunk, lens_ref, q_ref, fresh, kt, share_buf, w_ref,
                 rs_out, new_out, ctx, part, psend, precv, plocal, stage, s1send, s1recv, s2send,
                 s2recv, slocal):
    s = lax.axis_index("seq")
    t = lax.axis_index("tp")
    rows, qcols = q_ref.shape
    capacity, width = fresh.shape
    head_size = width // 2
    share = share_buf.shape[1]
    heads = qcols // head_size
    cols = w_ref.shape[1] // ntp
    chunks = rows // chunk
    held = lens_ref[0]

    _greet(na, nb, s, t, *[lax.rem(t + k, ntp) for k in range(1, ntp)])
    sorted4 = share_buf.reshape(na, nb, share, width)
    a2a = SeqAllToAll(na, nb, s, t, sorted4, stage, lambda a_src: new_out.at[a_src],
                      (s1send, s1recv, s2send, s2recv, slocal))
    a2a.first()

    def slice_out(c, k):
        peer = lax.rem(t + k, ntp)
        return _remote(part.at[c, :, pl.ds(pl.multiple_of(peer * cols, cols), cols)],
                       rs_out.at[t, pl.ds(pl.multiple_of(c * chunk, chunk), chunk)],
                       psend.at[c, k], precv.at[c, k], {"seq": s, "tp": peer})

    def slice_in(c, k):
        sender = lax.rem(t + ntp - k, ntp)
        return _remote(part.at[c, :, pl.ds(0, cols)],
                       rs_out.at[sender, pl.ds(pl.multiple_of(c * chunk, chunk), chunk)],
                       psend.at[c, k], precv.at[c, k], {"seq": s, "tp": sender})

    def slice_own(c):
        return pltpu.make_async_copy(
            part.at[c, :, pl.ds(pl.multiple_of(t * cols, cols), cols)],
            rs_out.at[t, pl.ds(pl.multiple_of(c * chunk, chunk), chunk)], plocal.at[c])

    def do_chunk(c):
        first = pl.multiple_of(c * chunk, chunk)
        row_pos = first + lax.broadcasted_iota(jnp.int32, (chunk, capacity), 0)
        key_pos = lax.broadcasted_iota(jnp.int32, (chunk, capacity), 1)
        allowed = key_pos <= held + row_pos
        for h in range(heads):
            q = q_ref[pl.ds(first, chunk), pl.ds(h * head_size, head_size)]
            scores = jnp.dot(q, kt[...], preferred_element_type=jnp.float32) * scale
            scores = jnp.where(allowed, scores, MASKED)
            top = jnp.max(scores, axis=1, keepdims=True)
            weights = jnp.exp(scores - top)
            inv = 1.0 / jnp.sum(weights, axis=1, keepdims=True)
            probs = (weights * inv).astype(jnp.bfloat16)
            ctx[:, pl.ds(h * head_size, head_size)] = jnp.dot(
                probs, fresh[:, pl.ds(head_size, head_size)],
                preferred_element_type=jnp.float32).astype(ctx.dtype)
        part[c] = jnp.dot(ctx[...], w_ref[...], preferred_element_type=jnp.float32).astype(
            part.dtype)
        slice_own(c).start()
        for k in range(1, ntp):
            slice_out(c, k).start()

    do_chunk(0)
    a2a.second()

    def rest(c, carry):
        do_chunk(c)
        return carry

    lax.fori_loop(1, chunks, rest, 0)
    a2a.arrived()

    def drain(c, carry):
        for k in range(1, ntp):
            slice_in(c, k).wait_recv()
            slice_out(c, k).wait_send()
        slice_own(c).wait()
        return carry

    lax.fori_loop(0, chunks, drain, 0)
    a2a.finish()


def attend_and_scatter(query, cache, keyval, held, span, holders, targets, w_out, na, nb, ntp,
                       chunk=128):
    rows, qcols = query.shape
    blocks, block_rows, width = cache.shape
    share = block_rows // ntp
    cols = w_out.shape[1] // ntp
    fresh, keys_t, sorted_share = prepare(cache, keyval, held, span, holders, targets, ntp)
    vmem = pl.BlockSpec(memory_space=pltpu.VMEM)
    smem = pl.BlockSpec(memory_space=pltpu.SMEM)
    rs, new = pl.pallas_call(
        functools.partial(_tail_kernel, na, nb, ntp, (width // 2) ** (-0.5), chunk),
        out_shape=(
            jax.ShapeDtypeStruct((ntp, rows, cols), jnp.bfloat16),
            jax.ShapeDtypeStruct((na, nb, share, width), cache.dtype),
        ),
        in_specs=[smem, vmem, vmem, vmem, vmem, vmem],
        out_specs=(pl.BlockSpec(memory_space=pl.ANY), pl.BlockSpec(memory_space=pl.ANY)),
        scratch_shapes=[
            pltpu.VMEM((chunk, qcols), jnp.bfloat16),
            pltpu.VMEM((rows // chunk, chunk, w_out.shape[1]), jnp.bfloat16),
            pltpu.SemaphoreType.DMA((rows // chunk, ntp)),
            pltpu.SemaphoreType.DMA((rows // chunk, ntp)),
            pltpu.SemaphoreType.DMA((rows // chunk,)),
        ] + _seq_scratch(na, nb, share, width, cache.dtype),
        compiler_params=pltpu.CompilerParams(collective_id=1, has_side_effects=True),
    )(held, query, fresh, keys_t, sorted_share, w_out)
    return rs, new.reshape(blocks, share, width)


def body(
    tokens,
    norm_gain,
    w_query,
    w_keyval,
    w_out,
    span_lens,
    cached_lens,
    old_table,
    new_table,
    old_cache,
):
    groups = lax.axis_size("seq")
    tp_count = lax.axis_size("tp")
    tp_index = lax.axis_index("tp")
    holders = old_table[0]
    held_len = cached_lens[0]
    span_len = span_lens[0]
    tok_rows, tok_cols = tokens.shape
    share = old_cache.shape[1]
    width = old_cache.shape[2]
    block_rows = share * tp_count
    capacity = groups * block_rows

    inner = min(groups, 8)
    outer = groups // inner
    query, keyval, cache_all = gather_inputs(
        tokens, old_cache, norm_gain, w_query, w_keyval, outer, inner, tp_count
    )
    cache_all = cache_all.reshape(groups, tp_count, share, width)

    summed, new_cache = attend_and_scatter(
        query, cache_all.reshape(groups, block_rows, width), keyval, cached_lens, span_lens,
        holders, new_table[0], w_out, outer, inner, tp_count
    )
    row_pos = lax.broadcasted_iota(jnp.int32, (tok_rows, 1), 0)
    total = tokens.astype(jnp.float32)
    for p in range(tp_count):
        total = total + summed[p].astype(jnp.float32)
    mixed = jnp.where(row_pos < span_len, total, jnp.zeros_like(total)).astype(jnp.bfloat16)
    return (mixed, new_cache)


def solution(mesh):
    in_specs = (
        P("seq", "tp"),
        P(),
        P(None, "tp"),
        P(),
        P("tp", None),
        P("seq"),
        P("seq"),
        P("seq", None),
        P("seq", None),
        P("seq", "tp", None),
    )
    out_specs = (P("seq", "tp"), P("seq", "tp", None))
    return jax.shard_map(body, mesh=mesh, in_specs=in_specs, out_specs=out_specs, check_vma=False)
```

```python
import functools

import jax
import jax.numpy as jnp
from jax import lax
from jax.experimental import pallas as pl
from jax.experimental.pallas import tpu as pltpu
from jax.sharding import PartitionSpec as P

EPSILON = 1e-05
MASKED = -1e30


def normalize(rows, norm_gain):
    values = rows.astype(jnp.float32)
    average = jnp.mean(values, axis=1, keepdims=True)
    centred = values - average
    spread = jnp.mean(centred * centred, axis=1, keepdims=True)
    return (centred * lax.rsqrt(spread + EPSILON) * norm_gain).astype(jnp.bfloat16)


MESH = pl.DeviceIdType.MESH


def _remote(src, dst, send, recv, dev):
    return pltpu.make_async_remote_copy(
        src_ref=src, dst_ref=dst, send_sem=send, recv_sem=recv, device_id=dev, device_id_type=MESH
    )


def _greet(na, nb, s, t, *tp_peers):
    barrier = pltpu.get_barrier_semaphore()
    a = s // nb
    b = s % nb

    def one_b(k, carry):
        pl.semaphore_signal(barrier, inc=1, device_id={"seq": a * nb + lax.rem(b + k, nb), "tp": t},
                            device_id_type=MESH)
        return carry

    def one_a(k, carry):
        pl.semaphore_signal(barrier, inc=1, device_id={"seq": lax.rem(a + k, na) * nb + b, "tp": t},
                            device_id_type=MESH)
        return carry

    lax.fori_loop(1, nb, one_b, 0)
    lax.fori_loop(1, na, one_a, 0)
    for p in tp_peers:
        pl.semaphore_signal(barrier, inc=1, device_id={"seq": s, "tp": p}, device_id_type=MESH)
    pl.semaphore_wait(barrier, na + nb - 2 + len(tp_peers))


class SeqAllToAll:
    def __init__(self, na, nb, s, t, src, stage, dst, sems):
        self.na, self.nb, self.t, self.src, self.stage, self.dst = na, nb, t, src, stage, dst
        self.a = s // nb
        self.b = s % nb
        self.s1send, self.s1recv, self.s2send, self.s2recv, self.local = sems

    def _dev(self, a, b):
        return {"seq": a * self.nb + b, "tp": self.t}

    def _out1(self, k):
        peer = lax.rem(self.b + k, self.nb)
        return _remote(self.src.at[:, peer], self.stage.at[self.b], self.s1send.at[k],
                       self.s1recv.at[k], self._dev(self.a, peer))

    def _in1(self, k):
        sender = lax.rem(self.b + self.nb - k, self.nb)
        return _remote(self.src.at[:, self.b], self.stage.at[sender], self.s1send.at[k],
                       self.s1recv.at[k], self._dev(self.a, sender))

    def _out2(self, k):
        peer = lax.rem(self.a + k, self.na)
        return _remote(self.stage.at[:, peer], self.dst(self.a), self.s2send.at[k],
                       self.s2recv.at[k], self._dev(peer, self.b))

    def _in2(self, k):
        sender = lax.rem(self.a + self.na - k, self.na)
        return _remote(self.stage.at[:, self.a], self.dst(sender), self.s2send.at[k],
                       self.s2recv.at[k], self._dev(sender, self.b))

    def first(self):
        self.own1 = pltpu.make_async_copy(self.src.at[:, self.b], self.stage.at[self.b],
                                          self.local.at[0])
        self.own1.start()
        _loop(self.nb, lambda k: self._out1(k).start())

    def second(self):
        _loop(self.nb, lambda k: self._in1(k).wait_recv())
        self.own1.wait()
        self.own2 = pltpu.make_async_copy(self.stage.at[:, self.a], self.dst(self.a),
                                          self.local.at[1])
        self.own2.start()
        _loop(self.na, lambda k: self._out2(k).start())

    def arrived(self):
        _loop(self.na, lambda k: self._in2(k).wait_recv())
        self.own2.wait()

    def finish(self):
        _loop(self.nb, lambda k: self._out1(k).wait_send())
        _loop(self.na, lambda k: self._out2(k).wait_send())


def _seq_scratch(na, nb, share, width, dtype):
    return [
        pltpu.VMEM((nb, na, share, width), dtype),
        pltpu.SemaphoreType.DMA((nb,)),
        pltpu.SemaphoreType.DMA((nb,)),
        pltpu.SemaphoreType.DMA((na,)),
        pltpu.SemaphoreType.DMA((na,)),
        pltpu.SemaphoreType.DMA((2,)),
    ]


def _loop(n, fn):
    def step(k, carry):
        fn(k)
        return carry

    lax.fori_loop(1, n, step, 0)


def _in_kernel(na, nb, ntp, tok_ref, cache_ref, gain_ref, wq_ref, wkv_ref, q_out, kv_out,
               cache_out, tok_all, tsend, trecv, csend, crecv, lsem, stage, s1send, s1recv,
               s2send, s2recv, slocal):
    s = lax.axis_index("seq")
    t = lax.axis_index("tp")
    right = lax.rem(t + 1, ntp)
    left = lax.rem(t + ntp - 1, ntp)
    across = lax.rem(t + 2, ntp)
    rdev = {"seq": s, "tp": right}
    ldev = {"seq": s, "tp": left}
    rows, cols = tok_ref.shape
    half = rows // 2
    _greet(na, nb, s, t, left, right, across)

    def tok_cols(p):
        return pl.ds(pl.multiple_of(p * cols, cols), cols)

    a2a = SeqAllToAll(na, nb, s, t, cache_ref, stage, lambda a_src: cache_out.at[a_src, :, t],
                      (s1send, s1recv, s2send, s2recv, slocal))
    a2a.first()

    own_tok = pltpu.make_async_copy(tok_ref, tok_all.at[:, tok_cols(t)], lsem.at[0])
    own_tok.start()
    tok_r = _remote(tok_ref, tok_all.at[:, tok_cols(t)], tsend.at[0], trecv.at[0], rdev)
    tok_l = _remote(tok_ref, tok_all.at[:, tok_cols(t)], tsend.at[1], trecv.at[1], ldev)
    tok_r.start()
    tok_l.start()

    a2a.second()

    _remote(tok_ref, tok_all.at[:, tok_cols(left)], tsend.at[0], trecv.at[0], ldev).wait_recv()
    fwd_r = _remote(tok_all.at[pl.ds(0, half), tok_cols(left)],
                    tok_all.at[pl.ds(0, half), tok_cols(left)], tsend.at[2], trecv.at[2], rdev)
    fwd_r.start()
    _remote(tok_ref, tok_all.at[:, tok_cols(right)], tsend.at[1], trecv.at[1], rdev).wait_recv()
    fwd_l = _remote(tok_all.at[pl.ds(half, half), tok_cols(right)],
                    tok_all.at[pl.ds(half, half), tok_cols(right)], tsend.at[3], trecv.at[3], ldev)
    fwd_l.start()

    a2a.arrived()
    flat = cache_out.reshape(na * nb, ntp, *cache_out.shape[3:])
    mine = flat.at[:, t]

    def cache_to(k):
        peer = lax.rem(t + k, ntp)
        return _remote(mine, mine, csend.at[k], crecv.at[k], {"seq": s, "tp": peer})

    def cache_from(k):
        sender = lax.rem(t + ntp - k, ntp)
        return _remote(mine, flat.at[:, sender], csend.at[k], crecv.at[k],
                       {"seq": s, "tp": sender})

    for k in range(1, ntp):
        cache_to(k).start()

    _remote(tok_ref.at[pl.ds(0, half)], tok_all.at[pl.ds(0, half), tok_cols(across)],
            tsend.at[2], trecv.at[2], ldev).wait_recv()
    _remote(tok_ref.at[pl.ds(half, half)], tok_all.at[pl.ds(half, half), tok_cols(across)],
            tsend.at[3], trecv.at[3], rdev).wait_recv()
    own_tok.wait()

    chunk = rows

    def project(c, carry):
        first = pl.multiple_of(c * chunk, chunk)
        values = tok_all[pl.ds(first, chunk), :].astype(jnp.float32)
        average = jnp.mean(values, axis=1, keepdims=True)
        centred = values - average
        spread = jnp.mean(centred * centred, axis=1, keepdims=True)
        normed = (centred * lax.rsqrt(spread + EPSILON) * gain_ref[...]).astype(jnp.bfloat16)
        q_out[pl.ds(first, chunk), :] = jnp.dot(
            normed, wq_ref[...], preferred_element_type=jnp.float32).astype(q_out.dtype)
        kv_out[pl.ds(first, chunk), :] = jnp.dot(
            normed, wkv_ref[...], preferred_element_type=jnp.float32).astype(kv_out.dtype)
        return carry

    lax.fori_loop(0, rows // chunk, project, 0)

    for k in range(1, ntp):
        cache_from(k).wait_recv()
    for c in (tok_r, tok_l, fwd_r, fwd_l):
        c.wait_send()
    for k in range(1, ntp):
        cache_to(k).wait_send()
    a2a.finish()


def gather_inputs(tokens, old_cache, norm_gain, w_query, w_keyval, na, nb, ntp):
    rows, cols = tokens.shape
    _, share, width = old_cache.shape
    cache4 = old_cache.reshape(na, nb, share, width)
    vmem = pl.BlockSpec(memory_space=pltpu.VMEM)
    anywhere = pl.BlockSpec(memory_space=pl.ANY)
    return pl.pallas_call(
        functools.partial(_in_kernel, na, nb, ntp),
        out_shape=(
            jax.ShapeDtypeStruct((rows, w_query.shape[1]), jnp.bfloat16),
            jax.ShapeDtypeStruct((rows, w_keyval.shape[1]), jnp.bfloat16),
            jax.ShapeDtypeStruct((na, nb, ntp, share, width), old_cache.dtype),
        ),
        in_specs=[anywhere, anywhere, vmem, vmem, vmem],
        out_specs=(vmem, vmem, anywhere),
        scratch_shapes=[
            pltpu.VMEM((rows, ntp * cols), tokens.dtype),
            pltpu.SemaphoreType.DMA((4,)),
            pltpu.SemaphoreType.DMA((4,)),
            pltpu.SemaphoreType.DMA((ntp,)),
            pltpu.SemaphoreType.DMA((ntp,)),
            pltpu.SemaphoreType.DMA((2,)),
        ] + _seq_scratch(na, nb, share, width, old_cache.dtype),
        compiler_params=pltpu.CompilerParams(collective_id=0, has_side_effects=True),
    )(tokens, cache4, norm_gain.reshape(1, -1).astype(jnp.float32), w_query, w_keyval)


def _out_kernel(na, nb, ntp, part_ref, share_ref, rs_out, new_out, stage_rs, rsend, rrecv, lsem,
                stage, s1send, s1recv, s2send, s2recv, slocal):
    s = lax.axis_index("seq")
    t = lax.axis_index("tp")
    right = lax.rem(t + 1, ntp)
    left = lax.rem(t + ntp - 1, ntp)
    across = lax.rem(t + 2, ntp)
    rdev = {"seq": s, "tp": right}
    ldev = {"seq": s, "tp": left}
    half = part_ref.shape[1] // 2
    _greet(na, nb, s, t, left, right)

    a2a = SeqAllToAll(na, nb, s, t, share_ref, stage, lambda a_src: new_out.at[a_src],
                      (s1send, s1recv, s2send, s2recv, slocal))
    a2a.first()

    own_part = pltpu.make_async_copy(part_ref.at[t], rs_out.at[t], lsem.at[0])
    own_part.start()
    to_r = _remote(part_ref.at[right], rs_out.at[t], rsend.at[0], rrecv.at[0], rdev)
    to_l = _remote(part_ref.at[left], rs_out.at[t], rsend.at[1], rrecv.at[1], ldev)
    via_r = _remote(part_ref.at[across, pl.ds(0, half)], stage_rs.at[0], rsend.at[2], rrecv.at[2],
                    rdev)
    via_l = _remote(part_ref.at[across, pl.ds(half, half)], stage_rs.at[1], rsend.at[3],
                    rrecv.at[3], ldev)
    for c in (to_r, to_l, via_r, via_l):
        c.start()

    a2a.second()

    _remote(part_ref.at[across, pl.ds(0, half)], stage_rs.at[0], rsend.at[2], rrecv.at[2],
            ldev).wait_recv()
    fwd_r = _remote(stage_rs.at[0], rs_out.at[left, pl.ds(0, half)], rsend.at[4], rrecv.at[4],
                    rdev)
    fwd_r.start()
    _remote(part_ref.at[across, pl.ds(half, half)], stage_rs.at[1], rsend.at[3], rrecv.at[3],
            rdev).wait_recv()
    fwd_l = _remote(stage_rs.at[1], rs_out.at[right, pl.ds(half, half)], rsend.at[5],
                    rrecv.at[5], ldev)
    fwd_l.start()

    a2a.arrived()
    _remote(part_ref.at[t], rs_out.at[left], rsend.at[0], rrecv.at[0], ldev).wait_recv()
    _remote(part_ref.at[t], rs_out.at[right], rsend.at[1], rrecv.at[1], rdev).wait_recv()
    _remote(stage_rs.at[0], rs_out.at[across, pl.ds(0, half)], rsend.at[4], rrecv.at[4],
            ldev).wait_recv()
    _remote(stage_rs.at[1], rs_out.at[across, pl.ds(half, half)], rsend.at[5], rrecv.at[5],
            rdev).wait_recv()
    for c in (to_r, to_l, via_r, via_l, fwd_r, fwd_l):
        c.wait_send()
    a2a.finish()
    own_part.wait()


def scatter_outputs(partial, share, na, nb, ntp):
    _, rows, cols = partial.shape
    _, block, width = share.shape
    share4 = share.reshape(na, nb, block, width)
    rs, new = pl.pallas_call(
        functools.partial(_out_kernel, na, nb, ntp),
        out_shape=(
            jax.ShapeDtypeStruct(partial.shape, partial.dtype),
            jax.ShapeDtypeStruct(share4.shape, share.dtype),
        ),
        in_specs=[pl.BlockSpec(memory_space=pl.ANY)] * 2,
        out_specs=(pl.BlockSpec(memory_space=pl.ANY), pl.BlockSpec(memory_space=pl.ANY)),
        scratch_shapes=[
            pltpu.VMEM((2, rows // 2, cols), partial.dtype),
            pltpu.SemaphoreType.DMA((6,)),
            pltpu.SemaphoreType.DMA((6,)),
            pltpu.SemaphoreType.DMA((1,)),
        ] + _seq_scratch(na, nb, block, width, share.dtype),
        compiler_params=pltpu.CompilerParams(collective_id=1, has_side_effects=True),
    )(partial, share4)
    return rs, new.reshape(share.shape)


def _attend_kernel(scale, lens_ref, q_ref, k_ref, v_ref, o_ref):
    chunk = q_ref.shape[0]
    capacity = k_ref.shape[0]
    held = lens_ref[0]
    first = pl.program_id(1) * chunk
    scores = lax.dot_general(
        q_ref[...], k_ref[...], (((1,), (1,)), ((), ())), preferred_element_type=jnp.float32
    ) * scale
    row_pos = first + lax.broadcasted_iota(jnp.int32, (chunk, capacity), 0)
    key_pos = lax.broadcasted_iota(jnp.int32, (chunk, capacity), 1)
    scores = jnp.where(key_pos <= held + row_pos, scores, MASKED)
    top = jnp.max(scores, axis=1, keepdims=True)
    weights = jnp.exp(scores - top)
    probs = (weights / jnp.sum(weights, axis=1, keepdims=True)).astype(jnp.bfloat16)
    o_ref[...] = jnp.dot(probs, v_ref[...], preferred_element_type=jnp.float32).astype(o_ref.dtype)


def attend(query, fresh, held_len, head_size, chunk=128):
    rows, qcols = query.shape
    capacity = fresh.shape[0]
    heads = qcols // head_size
    lens = jnp.reshape(held_len, (1,)).astype(jnp.int32)
    return pl.pallas_call(
        functools.partial(_attend_kernel, head_size ** (-0.5)),
        out_shape=jax.ShapeDtypeStruct((rows, qcols), jnp.bfloat16),
        grid_spec=pltpu.PrefetchScalarGridSpec(
            num_scalar_prefetch=1,
            grid=(heads, rows // chunk),
            in_specs=[
                pl.BlockSpec((chunk, head_size), lambda h, r, lens: (r, h)),
                pl.BlockSpec((capacity, head_size), lambda h, r, lens: (0, 0)),
                pl.BlockSpec((capacity, head_size), lambda h, r, lens: (0, 1)),
            ],
            out_specs=pl.BlockSpec((chunk, head_size), lambda h, r, lens: (r, h)),
        ),
        cost_estimate=pl.CostEstimate(
            flops=4 * rows * capacity * qcols,
            transcendentals=rows * capacity * heads,
            bytes_accessed=2 * (2 * rows * qcols + 2 * capacity * head_size),
        ),
    )(lens, query, fresh, fresh)


def _prep_kernel(ntp, held_ref, span_ref, holders_ref, targets_ref, cache_ref, kv_ref, fresh, kt,
                 share_buf, fresh32, sources_ref):
    t = lax.axis_index("tp")
    capacity, width = fresh.shape
    head_size = width // 2
    block_rows = cache_ref.shape[1]
    share = block_rows // ntp
    held = held_ref[0]
    span = span_ref[0]

    def invert(b, carry):
        sources_ref[targets_ref[b]] = b
        return carry

    lax.fori_loop(0, targets_ref.shape[0], invert, 0, unroll=True)

    def place(b, carry):
        fresh32[pl.ds(pl.multiple_of(b * block_rows, block_rows), block_rows), :] = (
            cache_ref[holders_ref[b]].astype(jnp.float32))
        return carry

    lax.fori_loop(0, capacity // block_rows, place, 0, unroll=True)
    padded = jnp.concatenate(
        [kv_ref[...].astype(jnp.float32),
         jnp.zeros((capacity - kv_ref.shape[0], width), jnp.float32)], axis=0)
    shifted = pltpu.roll(padded, held, 0)
    positions = lax.broadcasted_iota(jnp.int32, (capacity, width), 0)
    full = jnp.where(positions < held, fresh32[...],
                     jnp.where(positions < held + span, shifted, 0.0))
    fresh32[...] = full
    fresh[...] = full.astype(fresh.dtype)
    kt[...] = fresh[:, pl.ds(0, head_size)].T

    def pick(d, carry):
        start = pl.multiple_of(sources_ref[d] * block_rows + t * share, share)
        share_buf[d] = fresh32[pl.ds(start, share), :].astype(share_buf.dtype)
        return carry

    lax.fori_loop(0, share_buf.shape[0], pick, 0, unroll=True)


def prepare(cache, keyval, held, span, holders, targets, ntp):
    blocks, block_rows, width = cache.shape
    capacity = blocks * block_rows
    vmem = pl.BlockSpec(memory_space=pltpu.VMEM)
    smem = pl.BlockSpec(memory_space=pltpu.SMEM)
    return pl.pallas_call(
        functools.partial(_prep_kernel, ntp),
        out_shape=(
            jax.ShapeDtypeStruct((capacity, width), cache.dtype),
            jax.ShapeDtypeStruct((width // 2, capacity), cache.dtype),
            jax.ShapeDtypeStruct((blocks, block_rows // ntp, width), cache.dtype),
        ),
        in_specs=[smem, smem, smem, smem, vmem, vmem],
        out_specs=(vmem, vmem, vmem),
        scratch_shapes=[pltpu.VMEM((capacity, width), jnp.float32),
                        pltpu.SMEM((targets.shape[0],), jnp.int32)],
    )(held, span, holders, targets, cache, keyval)


def _tail_kernel(na, nb, ntp, scale, chunk, lens_ref, q_ref, fresh, kt, share_buf, w_ref,
                 rs_out, new_out, ctx, part, psend, precv, plocal, stage, s1send, s1recv, s2send,
                 s2recv, slocal):
    s = lax.axis_index("seq")
    t = lax.axis_index("tp")
    rows, qcols = q_ref.shape
    capacity, width = fresh.shape
    head_size = width // 2
    share = share_buf.shape[1]
    heads = qcols // head_size
    cols = w_ref.shape[1] // ntp
    chunks = rows // chunk
    held = lens_ref[0]

    _greet(na, nb, s, t, *[lax.rem(t + k, ntp) for k in range(1, ntp)])
    sorted4 = share_buf.reshape(na, nb, share, width)
    a2a = SeqAllToAll(na, nb, s, t, sorted4, stage, lambda a_src: new_out.at[a_src],
                      (s1send, s1recv, s2send, s2recv, slocal))
    a2a.first()

    def slice_out(c, k):
        peer = lax.rem(t + k, ntp)
        return _remote(part.at[c, :, pl.ds(pl.multiple_of(peer * cols, cols), cols)],
                       rs_out.at[t, pl.ds(pl.multiple_of(c * chunk, chunk), chunk)],
                       psend.at[c, k], precv.at[c, k], {"seq": s, "tp": peer})

    def slice_in(c, k):
        sender = lax.rem(t + ntp - k, ntp)
        return _remote(part.at[c, :, pl.ds(0, cols)],
                       rs_out.at[sender, pl.ds(pl.multiple_of(c * chunk, chunk), chunk)],
                       psend.at[c, k], precv.at[c, k], {"seq": s, "tp": sender})

    def slice_own(c):
        return pltpu.make_async_copy(
            part.at[c, :, pl.ds(pl.multiple_of(t * cols, cols), cols)],
            rs_out.at[t, pl.ds(pl.multiple_of(c * chunk, chunk), chunk)], plocal.at[c])

    def do_chunk(c):
        first = pl.multiple_of(c * chunk, chunk)
        row_pos = first + lax.broadcasted_iota(jnp.int32, (chunk, capacity), 0)
        key_pos = lax.broadcasted_iota(jnp.int32, (chunk, capacity), 1)
        allowed = key_pos <= held + row_pos
        for h in range(heads):
            q = q_ref[pl.ds(first, chunk), pl.ds(h * head_size, head_size)]
            scores = jnp.dot(q, kt[...], preferred_element_type=jnp.float32) * scale
            scores = jnp.where(allowed, scores, MASKED)
            top = jnp.max(scores, axis=1, keepdims=True)
            weights = jnp.exp(scores - top)
            inv = 1.0 / jnp.sum(weights, axis=1, keepdims=True)
            probs = (weights * inv).astype(jnp.bfloat16)
            ctx[:, pl.ds(h * head_size, head_size)] = jnp.dot(
                probs, fresh[:, pl.ds(head_size, head_size)],
                preferred_element_type=jnp.float32).astype(ctx.dtype)
        part[c] = jnp.dot(ctx[...], w_ref[...], preferred_element_type=jnp.float32).astype(
            part.dtype)
        slice_own(c).start()
        for k in range(1, ntp):
            slice_out(c, k).start()

    do_chunk(0)
    a2a.second()

    def rest(c, carry):
        do_chunk(c)
        return carry

    lax.fori_loop(1, chunks, rest, 0)
    a2a.arrived()

    def drain(c, carry):
        for k in range(1, ntp):
            slice_in(c, k).wait_recv()
            slice_out(c, k).wait_send()
        slice_own(c).wait()
        return carry

    lax.fori_loop(0, chunks, drain, 0)
    a2a.finish()


def attend_and_scatter(query, cache, keyval, held, span, holders, targets, w_out, na, nb, ntp,
                       chunk=128):
    rows, qcols = query.shape
    blocks, block_rows, width = cache.shape
    share = block_rows // ntp
    cols = w_out.shape[1] // ntp
    fresh, keys_t, sorted_share = prepare(cache, keyval, held, span, holders, targets, ntp)
    vmem = pl.BlockSpec(memory_space=pltpu.VMEM)
    smem = pl.BlockSpec(memory_space=pltpu.SMEM)
    rs, new = pl.pallas_call(
        functools.partial(_tail_kernel, na, nb, ntp, (width // 2) ** (-0.5), chunk),
        out_shape=(
            jax.ShapeDtypeStruct((ntp, rows, cols), jnp.bfloat16),
            jax.ShapeDtypeStruct((na, nb, share, width), cache.dtype),
        ),
        in_specs=[smem, vmem, vmem, vmem, vmem, vmem],
        out_specs=(pl.BlockSpec(memory_space=pl.ANY), pl.BlockSpec(memory_space=pl.ANY)),
        scratch_shapes=[
            pltpu.VMEM((chunk, qcols), jnp.bfloat16),
            pltpu.VMEM((rows // chunk, chunk, w_out.shape[1]), jnp.bfloat16),
            pltpu.SemaphoreType.DMA((rows // chunk, ntp)),
            pltpu.SemaphoreType.DMA((rows // chunk, ntp)),
            pltpu.SemaphoreType.DMA((rows // chunk,)),
        ] + _seq_scratch(na, nb, share, width, cache.dtype),
        compiler_params=pltpu.CompilerParams(collective_id=1, has_side_effects=True),
    )(held, query, fresh, keys_t, sorted_share, w_out)
    return rs, new.reshape(blocks, share, width)


def body(
    tokens,
    norm_gain,
    w_query,
    w_keyval,
    w_out,
    span_lens,
    cached_lens,
    old_table,
    new_table,
    old_cache,
):
    groups = lax.axis_size("seq")
    tp_count = lax.axis_size("tp")
    tp_index = lax.axis_index("tp")
    holders = old_table[0]
    held_len = cached_lens[0]
    span_len = span_lens[0]
    tok_rows, tok_cols = tokens.shape
    share = old_cache.shape[1]
    width = old_cache.shape[2]
    block_rows = share * tp_count
    capacity = groups * block_rows

    inner = min(groups, 8)
    outer = groups // inner
    query, keyval, cache_all = gather_inputs(
        tokens, old_cache, norm_gain, w_query, w_keyval, outer, inner, tp_count
    )
    cache_all = cache_all.reshape(groups, tp_count, share, width)

    summed, new_cache = attend_and_scatter(
        query, cache_all.reshape(groups, block_rows, width), keyval, cached_lens, span_lens,
        holders, new_table[0], w_out, outer, inner, tp_count
    )
    row_pos = lax.broadcasted_iota(jnp.int32, (tok_rows, 1), 0)
    total = tokens.astype(jnp.float32)
    for p in range(tp_count):
        total = total + summed[p].astype(jnp.float32)
    mixed = jnp.where(row_pos < span_len, total, jnp.zeros_like(total)).astype(jnp.bfloat16)
    return (mixed, new_cache)


def solution(mesh):
    in_specs = (
        P("seq", "tp"),
        P(),
        P(None, "tp"),
        P(),
        P("tp", None),
        P("seq"),
        P("seq"),
        P("seq", None),
        P("seq", None),
        P("seq", "tp", None),
    )
    out_specs = (P("seq", "tp"), P("seq", "tp", None))
    return jax.shard_map(body, mesh=mesh, in_specs=in_specs, out_specs=out_specs, check_vma=False)
```

```python
import functools

import jax
import jax.numpy as jnp
from jax import lax
from jax.experimental import pallas as pl
from jax.experimental.pallas import tpu as pltpu
from jax.sharding import PartitionSpec as P

EPSILON = 1e-05
MASKED = -1e30


def normalize(rows, norm_gain):
    values = rows.astype(jnp.float32)
    average = jnp.mean(values, axis=1, keepdims=True)
    centred = values - average
    spread = jnp.mean(centred * centred, axis=1, keepdims=True)
    return (centred * lax.rsqrt(spread + EPSILON) * norm_gain).astype(jnp.bfloat16)


MESH = pl.DeviceIdType.MESH


def _remote(src, dst, send, recv, dev):
    return pltpu.make_async_remote_copy(
        src_ref=src, dst_ref=dst, send_sem=send, recv_sem=recv, device_id=dev, device_id_type=MESH
    )


def _greet(na, nb, s, t, *tp_peers):
    barrier = pltpu.get_barrier_semaphore()
    a = s // nb
    b = s % nb

    def one_b(k, carry):
        pl.semaphore_signal(barrier, inc=1, device_id={"seq": a * nb + lax.rem(b + k, nb), "tp": t},
                            device_id_type=MESH)
        return carry

    def one_a(k, carry):
        pl.semaphore_signal(barrier, inc=1, device_id={"seq": lax.rem(a + k, na) * nb + b, "tp": t},
                            device_id_type=MESH)
        return carry

    lax.fori_loop(1, nb, one_b, 0)
    lax.fori_loop(1, na, one_a, 0)
    for p in tp_peers:
        pl.semaphore_signal(barrier, inc=1, device_id={"seq": s, "tp": p}, device_id_type=MESH)
    pl.semaphore_wait(barrier, na + nb - 2 + len(tp_peers))


class SeqAllToAll:
    def __init__(self, na, nb, s, t, src, stage, dst, sems):
        self.na, self.nb, self.t, self.src, self.stage, self.dst = na, nb, t, src, stage, dst
        self.a = s // nb
        self.b = s % nb
        self.s1send, self.s1recv, self.s2send, self.s2recv, self.local = sems

    def _dev(self, a, b):
        return {"seq": a * self.nb + b, "tp": self.t}

    def _out1(self, k):
        peer = lax.rem(self.b + k, self.nb)
        return _remote(self.src.at[:, peer], self.stage.at[self.b], self.s1send.at[k],
                       self.s1recv.at[k], self._dev(self.a, peer))

    def _in1(self, k):
        sender = lax.rem(self.b + self.nb - k, self.nb)
        return _remote(self.src.at[:, self.b], self.stage.at[sender], self.s1send.at[k],
                       self.s1recv.at[k], self._dev(self.a, sender))

    def _out2(self, k):
        peer = lax.rem(self.a + k, self.na)
        return _remote(self.stage.at[:, peer], self.dst(self.a), self.s2send.at[k],
                       self.s2recv.at[k], self._dev(peer, self.b))

    def _in2(self, k):
        sender = lax.rem(self.a + self.na - k, self.na)
        return _remote(self.stage.at[:, self.a], self.dst(sender), self.s2send.at[k],
                       self.s2recv.at[k], self._dev(sender, self.b))

    def first(self):
        self.own1 = pltpu.make_async_copy(self.src.at[:, self.b], self.stage.at[self.b],
                                          self.local.at[0])
        self.own1.start()
        _loop(self.nb, lambda k: self._out1(k).start())

    def second(self):
        _loop(self.nb, lambda k: self._in1(k).wait_recv())
        self.own1.wait()
        self.own2 = pltpu.make_async_copy(self.stage.at[:, self.a], self.dst(self.a),
                                          self.local.at[1])
        self.own2.start()
        _loop(self.na, lambda k: self._out2(k).start())

    def arrived(self):
        _loop(self.na, lambda k: self._in2(k).wait_recv())
        self.own2.wait()

    def finish(self):
        _loop(self.nb, lambda k: self._out1(k).wait_send())
        _loop(self.na, lambda k: self._out2(k).wait_send())


def _seq_scratch(na, nb, share, width, dtype):
    return [
        pltpu.VMEM((nb, na, share, width), dtype),
        pltpu.SemaphoreType.DMA((nb,)),
        pltpu.SemaphoreType.DMA((nb,)),
        pltpu.SemaphoreType.DMA((na,)),
        pltpu.SemaphoreType.DMA((na,)),
        pltpu.SemaphoreType.DMA((2,)),
    ]


def _loop(n, fn):
    def step(k, carry):
        fn(k)
        return carry

    lax.fori_loop(1, n, step, 0)


def _in_kernel(na, nb, ntp, tok_ref, cache_ref, gain_ref, wq_ref, wkv_ref, q_out, kv_out,
               cache_out, tok_all, tsend, trecv, csend, crecv, lsem, stage, s1send, s1recv,
               s2send, s2recv, slocal):
    s = lax.axis_index("seq")
    t = lax.axis_index("tp")
    right = lax.rem(t + 1, ntp)
    left = lax.rem(t + ntp - 1, ntp)
    across = lax.rem(t + 2, ntp)
    rdev = {"seq": s, "tp": right}
    ldev = {"seq": s, "tp": left}
    rows, cols = tok_ref.shape
    half = rows // 2
    _greet(na, nb, s, t, left, right, across)

    def tok_cols(p):
        return pl.ds(pl.multiple_of(p * cols, cols), cols)

    a2a = SeqAllToAll(na, nb, s, t, cache_ref, stage, lambda a_src: cache_out.at[a_src, :, t],
                      (s1send, s1recv, s2send, s2recv, slocal))
    a2a.first()

    own_tok = pltpu.make_async_copy(tok_ref, tok_all.at[:, tok_cols(t)], lsem.at[0])
    own_tok.start()
    tok_r = _remote(tok_ref, tok_all.at[:, tok_cols(t)], tsend.at[0], trecv.at[0], rdev)
    tok_l = _remote(tok_ref, tok_all.at[:, tok_cols(t)], tsend.at[1], trecv.at[1], ldev)
    tok_r.start()
    tok_l.start()

    a2a.second()

    _remote(tok_ref, tok_all.at[:, tok_cols(left)], tsend.at[0], trecv.at[0], ldev).wait_recv()
    fwd_r = _remote(tok_all.at[pl.ds(0, half), tok_cols(left)],
                    tok_all.at[pl.ds(0, half), tok_cols(left)], tsend.at[2], trecv.at[2], rdev)
    fwd_r.start()
    _remote(tok_ref, tok_all.at[:, tok_cols(right)], tsend.at[1], trecv.at[1], rdev).wait_recv()
    fwd_l = _remote(tok_all.at[pl.ds(half, half), tok_cols(right)],
                    tok_all.at[pl.ds(half, half), tok_cols(right)], tsend.at[3], trecv.at[3], ldev)
    fwd_l.start()

    a2a.arrived()
    flat = cache_out.reshape(na * nb, ntp, *cache_out.shape[3:])
    mine = flat.at[:, t]

    def cache_to(k):
        peer = lax.rem(t + k, ntp)
        return _remote(mine, mine, csend.at[k], crecv.at[k], {"seq": s, "tp": peer})

    def cache_from(k):
        sender = lax.rem(t + ntp - k, ntp)
        return _remote(mine, flat.at[:, sender], csend.at[k], crecv.at[k],
                       {"seq": s, "tp": sender})

    for k in range(1, ntp):
        cache_to(k).start()

    _remote(tok_ref.at[pl.ds(0, half)], tok_all.at[pl.ds(0, half), tok_cols(across)],
            tsend.at[2], trecv.at[2], ldev).wait_recv()
    _remote(tok_ref.at[pl.ds(half, half)], tok_all.at[pl.ds(half, half), tok_cols(across)],
            tsend.at[3], trecv.at[3], rdev).wait_recv()
    own_tok.wait()

    chunk = min(rows, 256)

    def project(c, carry):
        first = pl.multiple_of(c * chunk, chunk)
        values = tok_all[pl.ds(first, chunk), :].astype(jnp.float32)
        average = jnp.mean(values, axis=1, keepdims=True)
        centred = values - average
        spread = jnp.mean(centred * centred, axis=1, keepdims=True)
        normed = (centred * lax.rsqrt(spread + EPSILON) * gain_ref[...]).astype(jnp.bfloat16)
        q_out[pl.ds(first, chunk), :] = jnp.dot(
            normed, wq_ref[...], preferred_element_type=jnp.float32).astype(q_out.dtype)
        kv_out[pl.ds(first, chunk), :] = jnp.dot(
            normed, wkv_ref[...], preferred_element_type=jnp.float32).astype(kv_out.dtype)
        return carry

    lax.fori_loop(0, rows // chunk, project, 0)

    for k in range(1, ntp):
        cache_from(k).wait_recv()
    for c in (tok_r, tok_l, fwd_r, fwd_l):
        c.wait_send()
    for k in range(1, ntp):
        cache_to(k).wait_send()
    a2a.finish()


def gather_inputs(tokens, old_cache, norm_gain, w_query, w_keyval, na, nb, ntp):
    rows, cols = tokens.shape
    _, share, width = old_cache.shape
    cache4 = old_cache.reshape(na, nb, share, width)
    vmem = pl.BlockSpec(memory_space=pltpu.VMEM)
    anywhere = pl.BlockSpec(memory_space=pl.ANY)
    return pl.pallas_call(
        functools.partial(_in_kernel, na, nb, ntp),
        out_shape=(
            jax.ShapeDtypeStruct((rows, w_query.shape[1]), jnp.bfloat16),
            jax.ShapeDtypeStruct((rows, w_keyval.shape[1]), jnp.bfloat16),
            jax.ShapeDtypeStruct((na, nb, ntp, share, width), old_cache.dtype),
        ),
        in_specs=[anywhere, anywhere, vmem, vmem, vmem],
        out_specs=(vmem, vmem, anywhere),
        scratch_shapes=[
            pltpu.VMEM((rows, ntp * cols), tokens.dtype),
            pltpu.SemaphoreType.DMA((4,)),
            pltpu.SemaphoreType.DMA((4,)),
            pltpu.SemaphoreType.DMA((ntp,)),
            pltpu.SemaphoreType.DMA((ntp,)),
            pltpu.SemaphoreType.DMA((2,)),
        ] + _seq_scratch(na, nb, share, width, old_cache.dtype),
        compiler_params=pltpu.CompilerParams(collective_id=0, has_side_effects=True),
    )(tokens, cache4, norm_gain.reshape(1, -1).astype(jnp.float32), w_query, w_keyval)


def _out_kernel(na, nb, ntp, part_ref, share_ref, rs_out, new_out, stage_rs, rsend, rrecv, lsem,
                stage, s1send, s1recv, s2send, s2recv, slocal):
    s = lax.axis_index("seq")
    t = lax.axis_index("tp")
    right = lax.rem(t + 1, ntp)
    left = lax.rem(t + ntp - 1, ntp)
    across = lax.rem(t + 2, ntp)
    rdev = {"seq": s, "tp": right}
    ldev = {"seq": s, "tp": left}
    half = part_ref.shape[1] // 2
    _greet(na, nb, s, t, left, right)

    a2a = SeqAllToAll(na, nb, s, t, share_ref, stage, lambda a_src: new_out.at[a_src],
                      (s1send, s1recv, s2send, s2recv, slocal))
    a2a.first()

    own_part = pltpu.make_async_copy(part_ref.at[t], rs_out.at[t], lsem.at[0])
    own_part.start()
    to_r = _remote(part_ref.at[right], rs_out.at[t], rsend.at[0], rrecv.at[0], rdev)
    to_l = _remote(part_ref.at[left], rs_out.at[t], rsend.at[1], rrecv.at[1], ldev)
    via_r = _remote(part_ref.at[across, pl.ds(0, half)], stage_rs.at[0], rsend.at[2], rrecv.at[2],
                    rdev)
    via_l = _remote(part_ref.at[across, pl.ds(half, half)], stage_rs.at[1], rsend.at[3],
                    rrecv.at[3], ldev)
    for c in (to_r, to_l, via_r, via_l):
        c.start()

    a2a.second()

    _remote(part_ref.at[across, pl.ds(0, half)], stage_rs.at[0], rsend.at[2], rrecv.at[2],
            ldev).wait_recv()
    fwd_r = _remote(stage_rs.at[0], rs_out.at[left, pl.ds(0, half)], rsend.at[4], rrecv.at[4],
                    rdev)
    fwd_r.start()
    _remote(part_ref.at[across, pl.ds(half, half)], stage_rs.at[1], rsend.at[3], rrecv.at[3],
            rdev).wait_recv()
    fwd_l = _remote(stage_rs.at[1], rs_out.at[right, pl.ds(half, half)], rsend.at[5],
                    rrecv.at[5], ldev)
    fwd_l.start()

    a2a.arrived()
    _remote(part_ref.at[t], rs_out.at[left], rsend.at[0], rrecv.at[0], ldev).wait_recv()
    _remote(part_ref.at[t], rs_out.at[right], rsend.at[1], rrecv.at[1], rdev).wait_recv()
    _remote(stage_rs.at[0], rs_out.at[across, pl.ds(0, half)], rsend.at[4], rrecv.at[4],
            ldev).wait_recv()
    _remote(stage_rs.at[1], rs_out.at[across, pl.ds(half, half)], rsend.at[5], rrecv.at[5],
            rdev).wait_recv()
    for c in (to_r, to_l, via_r, via_l, fwd_r, fwd_l):
        c.wait_send()
    a2a.finish()
    own_part.wait()


def scatter_outputs(partial, share, na, nb, ntp):
    _, rows, cols = partial.shape
    _, block, width = share.shape
    share4 = share.reshape(na, nb, block, width)
    rs, new = pl.pallas_call(
        functools.partial(_out_kernel, na, nb, ntp),
        out_shape=(
            jax.ShapeDtypeStruct(partial.shape, partial.dtype),
            jax.ShapeDtypeStruct(share4.shape, share.dtype),
        ),
        in_specs=[pl.BlockSpec(memory_space=pl.ANY)] * 2,
        out_specs=(pl.BlockSpec(memory_space=pl.ANY), pl.BlockSpec(memory_space=pl.ANY)),
        scratch_shapes=[
            pltpu.VMEM((2, rows // 2, cols), partial.dtype),
            pltpu.SemaphoreType.DMA((6,)),
            pltpu.SemaphoreType.DMA((6,)),
            pltpu.SemaphoreType.DMA((1,)),
        ] + _seq_scratch(na, nb, block, width, share.dtype),
        compiler_params=pltpu.CompilerParams(collective_id=1, has_side_effects=True),
    )(partial, share4)
    return rs, new.reshape(share.shape)


def _attend_kernel(scale, lens_ref, q_ref, k_ref, v_ref, o_ref):
    chunk = q_ref.shape[0]
    capacity = k_ref.shape[0]
    held = lens_ref[0]
    first = pl.program_id(1) * chunk
    scores = lax.dot_general(
        q_ref[...], k_ref[...], (((1,), (1,)), ((), ())), preferred_element_type=jnp.float32
    ) * scale
    row_pos = first + lax.broadcasted_iota(jnp.int32, (chunk, capacity), 0)
    key_pos = lax.broadcasted_iota(jnp.int32, (chunk, capacity), 1)
    scores = jnp.where(key_pos <= held + row_pos, scores, MASKED)
    top = jnp.max(scores, axis=1, keepdims=True)
    weights = jnp.exp(scores - top)
    probs = (weights / jnp.sum(weights, axis=1, keepdims=True)).astype(jnp.bfloat16)
    o_ref[...] = jnp.dot(probs, v_ref[...], preferred_element_type=jnp.float32).astype(o_ref.dtype)


def attend(query, fresh, held_len, head_size, chunk=128):
    rows, qcols = query.shape
    capacity = fresh.shape[0]
    heads = qcols // head_size
    lens = jnp.reshape(held_len, (1,)).astype(jnp.int32)
    return pl.pallas_call(
        functools.partial(_attend_kernel, head_size ** (-0.5)),
        out_shape=jax.ShapeDtypeStruct((rows, qcols), jnp.bfloat16),
        grid_spec=pltpu.PrefetchScalarGridSpec(
            num_scalar_prefetch=1,
            grid=(heads, rows // chunk),
            in_specs=[
                pl.BlockSpec((chunk, head_size), lambda h, r, lens: (r, h)),
                pl.BlockSpec((capacity, head_size), lambda h, r, lens: (0, 0)),
                pl.BlockSpec((capacity, head_size), lambda h, r, lens: (0, 1)),
            ],
            out_specs=pl.BlockSpec((chunk, head_size), lambda h, r, lens: (r, h)),
        ),
        cost_estimate=pl.CostEstimate(
            flops=4 * rows * capacity * qcols,
            transcendentals=rows * capacity * heads,
            bytes_accessed=2 * (2 * rows * qcols + 2 * capacity * head_size),
        ),
    )(lens, query, fresh, fresh)


def _prep_kernel(ntp, held_ref, span_ref, holders_ref, targets_ref, cache_ref, kv_ref, fresh, kt,
                 share_buf, fresh32, sources_ref):
    t = lax.axis_index("tp")
    capacity, width = fresh.shape
    head_size = width // 2
    block_rows = cache_ref.shape[1]
    share = block_rows // ntp
    held = held_ref[0]
    span = span_ref[0]

    def invert(b, carry):
        sources_ref[targets_ref[b]] = b
        return carry

    lax.fori_loop(0, targets_ref.shape[0], invert, 0, unroll=True)

    def place(b, carry):
        fresh32[pl.ds(pl.multiple_of(b * block_rows, block_rows), block_rows), :] = (
            cache_ref[holders_ref[b]].astype(jnp.float32))
        return carry

    lax.fori_loop(0, capacity // block_rows, place, 0, unroll=True)
    padded = jnp.concatenate(
        [kv_ref[...].astype(jnp.float32),
         jnp.zeros((capacity - kv_ref.shape[0], width), jnp.float32)], axis=0)
    shifted = pltpu.roll(padded, held, 0)
    positions = lax.broadcasted_iota(jnp.int32, (capacity, width), 0)
    full = jnp.where(positions < held, fresh32[...],
                     jnp.where(positions < held + span, shifted, 0.0))
    fresh32[...] = full
    fresh[...] = full.astype(fresh.dtype)
    kt[...] = fresh[:, pl.ds(0, head_size)].T

    def pick(d, carry):
        start = pl.multiple_of(sources_ref[d] * block_rows + t * share, share)
        share_buf[d] = fresh32[pl.ds(start, share), :].astype(share_buf.dtype)
        return carry

    lax.fori_loop(0, share_buf.shape[0], pick, 0, unroll=True)


def prepare(cache, keyval, held, span, holders, targets, ntp):
    blocks, block_rows, width = cache.shape
    capacity = blocks * block_rows
    vmem = pl.BlockSpec(memory_space=pltpu.VMEM)
    smem = pl.BlockSpec(memory_space=pltpu.SMEM)
    return pl.pallas_call(
        functools.partial(_prep_kernel, ntp),
        out_shape=(
            jax.ShapeDtypeStruct((capacity, width), cache.dtype),
            jax.ShapeDtypeStruct((width // 2, capacity), cache.dtype),
            jax.ShapeDtypeStruct((blocks, block_rows // ntp, width), cache.dtype),
        ),
        in_specs=[smem, smem, smem, smem, vmem, vmem],
        out_specs=(vmem, vmem, vmem),
        scratch_shapes=[pltpu.VMEM((capacity, width), jnp.float32),
                        pltpu.SMEM((targets.shape[0],), jnp.int32)],
    )(held, span, holders, targets, cache, keyval)


def _tail_kernel(na, nb, ntp, scale, chunk, lens_ref, q_ref, fresh, kt, share_buf, w_ref,
                 rs_out, new_out, ctx, part, psend, precv, plocal, stage, s1send, s1recv, s2send,
                 s2recv, slocal):
    s = lax.axis_index("seq")
    t = lax.axis_index("tp")
    rows, qcols = q_ref.shape
    capacity, width = fresh.shape
    head_size = width // 2
    share = share_buf.shape[1]
    heads = qcols // head_size
    cols = w_ref.shape[1] // ntp
    chunks = rows // chunk
    held = lens_ref[0]

    _greet(na, nb, s, t, *[lax.rem(t + k, ntp) for k in range(1, ntp)])
    sorted4 = share_buf.reshape(na, nb, share, width)
    a2a = SeqAllToAll(na, nb, s, t, sorted4, stage, lambda a_src: new_out.at[a_src],
                      (s1send, s1recv, s2send, s2recv, slocal))
    a2a.first()

    def slice_out(c, k):
        peer = lax.rem(t + k, ntp)
        return _remote(part.at[c, :, pl.ds(pl.multiple_of(peer * cols, cols), cols)],
                       rs_out.at[t, pl.ds(pl.multiple_of(c * chunk, chunk), chunk)],
                       psend.at[c, k], precv.at[c, k], {"seq": s, "tp": peer})

    def slice_in(c, k):
        sender = lax.rem(t + ntp - k, ntp)
        return _remote(part.at[c, :, pl.ds(0, cols)],
                       rs_out.at[sender, pl.ds(pl.multiple_of(c * chunk, chunk), chunk)],
                       psend.at[c, k], precv.at[c, k], {"seq": s, "tp": sender})

    def slice_own(c):
        return pltpu.make_async_copy(
            part.at[c, :, pl.ds(pl.multiple_of(t * cols, cols), cols)],
            rs_out.at[t, pl.ds(pl.multiple_of(c * chunk, chunk), chunk)], plocal.at[c])

    def do_chunk(c):
        first = pl.multiple_of(c * chunk, chunk)
        row_pos = first + lax.broadcasted_iota(jnp.int32, (chunk, capacity), 0)
        key_pos = lax.broadcasted_iota(jnp.int32, (chunk, capacity), 1)
        allowed = key_pos <= held + row_pos
        for h in range(heads):
            q = q_ref[pl.ds(first, chunk), pl.ds(h * head_size, head_size)]
            scores = jnp.dot(q, kt[...], preferred_element_type=jnp.float32) * scale
            scores = jnp.where(allowed, scores, MASKED)
            top = jnp.max(scores, axis=1, keepdims=True)
            weights = jnp.exp(scores - top)
            inv = 1.0 / jnp.sum(weights, axis=1, keepdims=True)
            probs = (weights * inv).astype(jnp.bfloat16)
            ctx[:, pl.ds(h * head_size, head_size)] = jnp.dot(
                probs, fresh[:, pl.ds(head_size, head_size)],
                preferred_element_type=jnp.float32).astype(ctx.dtype)
        part[c] = jnp.dot(ctx[...], w_ref[...], preferred_element_type=jnp.float32).astype(
            part.dtype)
        slice_own(c).start()
        for k in range(1, ntp):
            slice_out(c, k).start()

    do_chunk(0)
    a2a.second()

    def rest(c, carry):
        do_chunk(c)
        return carry

    lax.fori_loop(1, chunks, rest, 0, unroll=True)
    a2a.arrived()

    def drain(c, carry):
        for k in range(1, ntp):
            slice_in(c, k).wait_recv()
            slice_out(c, k).wait_send()
        slice_own(c).wait()
        return carry

    lax.fori_loop(0, chunks, drain, 0)
    a2a.finish()


def attend_and_scatter(query, cache, keyval, held, span, holders, targets, w_out, na, nb, ntp,
                       chunk=128):
    rows, qcols = query.shape
    blocks, block_rows, width = cache.shape
    share = block_rows // ntp
    cols = w_out.shape[1] // ntp
    fresh, keys_t, sorted_share = prepare(cache, keyval, held, span, holders, targets, ntp)
    vmem = pl.BlockSpec(memory_space=pltpu.VMEM)
    smem = pl.BlockSpec(memory_space=pltpu.SMEM)
    rs, new = pl.pallas_call(
        functools.partial(_tail_kernel, na, nb, ntp, (width // 2) ** (-0.5), chunk),
        out_shape=(
            jax.ShapeDtypeStruct((ntp, rows, cols), jnp.bfloat16),
            jax.ShapeDtypeStruct((na, nb, share, width), cache.dtype),
        ),
        in_specs=[smem, vmem, vmem, vmem, vmem, vmem],
        out_specs=(pl.BlockSpec(memory_space=pl.ANY), pl.BlockSpec(memory_space=pl.ANY)),
        scratch_shapes=[
            pltpu.VMEM((chunk, qcols), jnp.bfloat16),
            pltpu.VMEM((rows // chunk, chunk, w_out.shape[1]), jnp.bfloat16),
            pltpu.SemaphoreType.DMA((rows // chunk, ntp)),
            pltpu.SemaphoreType.DMA((rows // chunk, ntp)),
            pltpu.SemaphoreType.DMA((rows // chunk,)),
        ] + _seq_scratch(na, nb, share, width, cache.dtype),
        compiler_params=pltpu.CompilerParams(collective_id=1, has_side_effects=True),
    )(held, query, fresh, keys_t, sorted_share, w_out)
    return rs, new.reshape(blocks, share, width)


def body(
    tokens,
    norm_gain,
    w_query,
    w_keyval,
    w_out,
    span_lens,
    cached_lens,
    old_table,
    new_table,
    old_cache,
):
    groups = lax.axis_size("seq")
    tp_count = lax.axis_size("tp")
    tp_index = lax.axis_index("tp")
    holders = old_table[0]
    held_len = cached_lens[0]
    span_len = span_lens[0]
    tok_rows, tok_cols = tokens.shape
    share = old_cache.shape[1]
    width = old_cache.shape[2]
    block_rows = share * tp_count
    capacity = groups * block_rows

    inner = min(groups, 8)
    outer = groups // inner
    query, keyval, cache_all = gather_inputs(
        tokens, old_cache, norm_gain, w_query, w_keyval, outer, inner, tp_count
    )
    cache_all = cache_all.reshape(groups, tp_count, share, width)

    summed, new_cache = attend_and_scatter(
        query, cache_all.reshape(groups, block_rows, width), keyval, cached_lens, span_lens,
        holders, new_table[0], w_out, outer, inner, tp_count
    )
    row_pos = lax.broadcasted_iota(jnp.int32, (tok_rows, 1), 0)
    total = tokens.astype(jnp.float32)
    for p in range(tp_count):
        total = total + summed[p].astype(jnp.float32)
    mixed = jnp.where(row_pos < span_len, total, jnp.zeros_like(total)).astype(jnp.bfloat16)
    return (mixed, new_cache)


def solution(mesh):
    in_specs = (
        P("seq", "tp"),
        P(),
        P(None, "tp"),
        P(),
        P("tp", None),
        P("seq"),
        P("seq"),
        P("seq", None),
        P("seq", None),
        P("seq", "tp", None),
    )
    out_specs = (P("seq", "tp"), P("seq", "tp", None))
    return jax.shard_map(body, mesh=mesh, in_specs=in_specs, out_specs=out_specs, check_vma=False)
```
